32 devices in a mesh: expert: 8 (over z, x), fsdp: 4 (over y, core).
Axes of the slice: x: 2, y: 2, z: 4, core: 2. Of those that a mesh axis runs over, the one named last changes fastest.
Arguments:
- tokens: bfloat16 [160, 197, 512], P(('expert', 'fsdp')), may hold values from -6 to 6
- ln1_gain: bfloat16 [512], P('fsdp'), may hold values from 0.5 to 1.5
- ln1_bias: bfloat16 [512], P('fsdp'), may hold values from -1.796875 to 1.796875
- w_qkv: bfloat16 [512, 1536], P('fsdp'), may hold values from -0.25 to 0.25
- q_bias: bfloat16 [512], P('fsdp'), may hold values from -1.796875 to 1.796875
- v_bias: bfloat16 [512], P('fsdp'), may hold values from -1.796875 to 1.796875
- w_out: bfloat16 [512, 512], P('fsdp'), may hold values from -1.5 to 1.5
- out_bias: bfloat16 [512], P('fsdp'), may hold values from -1.796875 to 1.796875
- ln2_gain: bfloat16 [512], P('fsdp'), may hold values from 0.5 to 1.5
- ln2_bias: bfloat16 [512], P('fsdp'), may hold values from -1.796875 to 1.796875
- w_router: bfloat16 [512, 8], P('fsdp'), may hold values from -0.1875 to 0.1875
- expert_w1: bfloat16 [8, 512, 2048], P('expert', 'fsdp'), may hold values from -0.25 to 0.25
- expert_b1: bfloat16 [8, 2048], P('expert', 'fsdp'), may hold values from -1.796875 to 1.796875
- expert_w2: bfloat16 [8, 2048, 512], P('expert', 'fsdp'), may hold values from -0.75 to 0.75
- expert_b2: bfloat16 [8, 512], P('expert', 'fsdp'), may hold values from -6 to 6
- route_ids: int32 [31520, 2], P(('expert', 'fsdp')), may hold values from 0 to 7, all different within a row; in each aligned block of 985 rows (0 to 984, 985 to 1969, ...) at most 432 rows name the same one
- clip_threshold: int32 [8], replicated, may hold values from 2 to 4
- grad_output: bfloat16 [160, 197, 512], P(('expert', 'fsdp')), may hold values from -6 to 6
Outputs:
- output: bfloat16 [160, 197, 512], P(('expert', 'fsdp'))
- input_grad: float32 [160, 197, 512], P(('expert', 'fsdp'))
- grad_ln1_gain: float32 [512], P('fsdp')
- grad_ln1_bias: float32 [512], P('fsdp')
- grad_w_qkv: float32 [512, 1536], P('fsdp')
- grad_q_bias: float32 [512], P('fsdp')
- grad_v_bias: float32 [512], P('fsdp')
- grad_w_out: float32 [512, 512], P('fsdp')
- grad_out_bias: float32 [512], P('fsdp')
- grad_ln2_gain: float32 [512], P('fsdp')
- grad_ln2_bias: float32 [512], P('fsdp')
- grad_w_router: float32 [512, 8], P('fsdp')
- grad_expert_w1: float32 [8, 512, 2048], P('expert', 'fsdp')
- grad_expert_b1: float32 [8, 2048], P('expert', 'fsdp')
- grad_expert_w2: float32 [8, 2048, 512], P('expert', 'fsdp')
- grad_expert_b2: float32 [8, 512], P('expert', 'fsdp')
- clipped_qkv: bfloat16 [512, 1536], P('fsdp')
The draws below stay inside these ranges and needn't reach their ends.
Inputs may be any that keep to these rules, and one draw needn't show every extreme that they name: `route_ids`: each row names 2 different experts; among the 985 rows of one device no expert is named by more than 432 rows, and in some device's rows one expert is named by exactly 432.
All inputs are finite; a program needn't handle non-finite values.
Results may differ from the reference program's by a relative error of at most 0.024.
Values may be sent and summed in bfloat16 or wider, within the bound.
No kernel may reach another device: no remote copies, remote signals or barrier semaphores. Data moves between devices by JAX's collectives and lax.ppermute only.
A program may use at most 256 MiB of HBM per device.

```python
import math
import jax
import jax.numpy as jnp
import numpy as np
from jax import lax

D = 512
HEADS = 8
HD = 64
H = 2048
TOP = 2
SEQ = 197
IMG_DEV = 5
EXPERTS = 8
TOK_DEV = 985
IMAGES = 160
TOKENS = 31520
CAP = 432


def touch_ends(values, own_key, smallest, largest):
    longest = values.shape.index(max(values.shape))
    spots = []
    for shift in (0, 1):
        where = [jax.random.randint(jax.random.fold_in(own_key, axis), (), 0, length) for axis, length in enumerate(values.shape)]
        where[longest] = (where[longest] + shift) % values.shape[longest]
        spots.append(tuple(where))
    return values.at[spots[0]].set(smallest).at[spots[1]].set(largest)


def block_scale(rng, extent, pieces, smallest, top_value):
    def one(position, shards_of):
        heights = jax.random.uniform(jax.random.fold_in(jax.random.fold_in(rng, 6), position), (shards_of,), jnp.float32, smallest / len(pieces), top_value / len(pieces))
        return jnp.repeat(jnp.exp(heights), extent[position] // shards_of).reshape((-1,) + (1,) * (len(extent) - position - 1))

    level = one(*pieces[0])
    for cut in pieces[1:]:
        level = level * one(*cut)
    return level


def shared_out(stream_key, own, number, rows, number_of, top, most, skew):
    order = jax.random.permutation(stream_key, number_of)
    heavy_load, common = shares(number_of, rows * top, most, skew, True), shares(number_of, rows * top, most, skew, False)
    places = jnp.arange(number_of)

    def named(sizes, offset_by):
        used = int((sizes > 0).sum())
        fixed = max(1, used // 4)
        moved = fixed + (places - fixed + offset_by * (used - fixed)) % max(1, number_of - fixed)
        return jnp.zeros((number_of,), jnp.int32).at[order[jnp.where(places < fixed, places, moved)]].set(jnp.asarray(sizes, jnp.int32))

    sizes = jnp.where(number % 4 == 0, named(heavy_load, number // 4), named(common, number - number // 4 - 1))
    mixed = jax.random.permutation(jax.random.fold_in(own, 3), number_of)
    giver, taker = mixed[0:number_of // 2 * 2:2], mixed[1:number_of // 2 * 2:2]
    room = jnp.minimum(sizes[giver] - 1, most - sizes[taker]) // 2
    room = jnp.where((giver == order[0]) | (taker == order[0]) | (sizes[taker] == 0), 0, jnp.maximum(room, 0))
    moved = jax.random.randint(jax.random.fold_in(own, 4), (number_of // 2,), 0, 1 << 20) % (room + 1)
    sizes = sizes.at[giver].add(-moved).at[taker].add(moved)
    members = jnp.searchsorted(jnp.cumsum(sizes), jnp.arange(rows * top), side="right").astype(jnp.int32)
    listing = members.reshape(top, rows).T
    listing = listing[jax.random.permutation(jax.random.fold_in(own, 1), rows)]
    offset_by = jax.random.randint(jax.random.fold_in(own, 2), (rows, 1), 0, top)
    return jnp.take_along_axis(listing, (jnp.arange(top)[None, :] + offset_by) % top, axis=1)


def shares(count, total, most, skew, full):
    weights = [(1 << 20) // math.isqrt(standing ** skew) + 1 for standing in range(1, count + 1)]
    largest = most if full else min(most, max(-(-total // count), total * weights[0] // sum(weights)))
    least = 1 if total - largest >= count - 1 else 0
    holding, surplus = [largest] + [least] * (count - 1), total - largest - least * (count - 1)
    while surplus > 0:
        movable = [i for i in range(1, count) if holding[i] < largest] or [i for i in range(1, count) if holding[i] < most]
        mass, budget = sum([weights[i] for i in movable]), surplus
        for i in movable:
            extra = min(most - holding[i], max(1, budget * weights[i] // mass), surplus)
            holding[i] = holding[i] + extra
            surplus = surplus - extra
    return np.array(holding)


def gaussian(key, shape, deviation, most, pieces=(), kind=jnp.bfloat16):
    values = deviation * jax.random.normal(key, shape, jnp.float32)
    if pieces:
        values = values * block_scale(key, shape, pieces, -0.22, 0.18)
    return jnp.clip(values, -most, most).astype(kind)


def setup_inputs(seed: int = 0) -> dict:
    key_list = jax.random.split(jax.random.key(seed), 19)
    tokens = gaussian(key_list[0], (IMAGES, SEQ, D), 1.0, 6.0, ((0, 32),))
    ln1_gain = jnp.clip(1.0 + 0.1 * jax.random.normal(key_list[1], (D,), jnp.float32), 0.5, 1.5).astype(jnp.bfloat16)
    ln1_bias = gaussian(key_list[2], (D,), 0.3, 1.796875, ((0, 4),))
    w_qkv = gaussian(key_list[3], (D, 3 * D), D ** -0.5, 0.25, ((0, 4),))
    q_bias = gaussian(key_list[4], (D,), 0.3, 1.796875, ((0, 4),))
    v_bias = gaussian(key_list[5], (D,), 0.3, 1.796875, ((0, 4),))
    w_out = gaussian(key_list[6], (D, D), (D // 32) ** -0.5, 1.5, ((0, 4),))
    out_bias = gaussian(key_list[7], (D,), 0.3, 1.796875, ((0, 4),))
    ln2_gain = jnp.clip(1.0 + 0.1 * jax.random.normal(key_list[8], (D,), jnp.float32), 0.5, 1.5).astype(jnp.bfloat16)
    ln2_bias = gaussian(key_list[9], (D,), 0.3, 1.796875, ((0, 4),))
    w_router = gaussian(key_list[10], (D, EXPERTS), (2 * D) ** -0.5, 0.1875, ((0, 4),))
    expert_w1 = gaussian(key_list[11], (EXPERTS, D, H), D ** -0.5, 0.25, ((0, 8), (1, 4)))
    expert_b1 = gaussian(key_list[12], (EXPERTS, H), 0.3, 1.796875, ((0, 8), (1, 4)))
    expert_w2 = gaussian(key_list[13], (EXPERTS, H, D), (max(1, 2 * H // (EXPERTS * EXPERTS))) ** -0.5, 0.75, ((0, 8), (1, 4)))
    expert_b2 = gaussian(key_list[14], (EXPERTS, D), 1.0, 6.0, ((0, 8), (1, 4)))
    route_ids_keys = jax.random.split(jax.random.fold_in(key_list[15], 1), TOKENS // TOK_DEV)
    route_ids_turns = jax.random.permutation(jax.random.fold_in(key_list[15], 3), TOKENS // TOK_DEV)
    route_ids = jax.vmap(lambda own, number: shared_out(jax.random.fold_in(key_list[15], 2), own, number, TOK_DEV, EXPERTS, TOP, CAP, 1))(route_ids_keys, route_ids_turns).reshape((TOKENS, TOP))
    clip_threshold = touch_ends(jax.random.randint(key_list[16], (HEADS,), 2, 5), jax.random.fold_in(key_list[16], 1), 2, 4).astype(jnp.int32)
    grad_output = gaussian(key_list[17], (IMAGES, SEQ, D), 1.0, 6.0, ((0, 32),))
    return dict(tokens=tokens, ln1_gain=ln1_gain, ln1_bias=ln1_bias, w_qkv=w_qkv, q_bias=q_bias, v_bias=v_bias, w_out=w_out, out_bias=out_bias, ln2_gain=ln2_gain, ln2_bias=ln2_bias, w_router=w_router, expert_w1=expert_w1, expert_b1=expert_b1, expert_w2=expert_w2, expert_b2=expert_b2, route_ids=route_ids, clip_threshold=clip_threshold, grad_output=grad_output)


norm_eps = 1e-06
highest = lax.Precision.HIGHEST

@jax.custom_vjp
def low(v):
    return lax.optimization_barrier(v.astype(jnp.bfloat16)).astype(jnp.float32)

@jax.custom_vjp
def low_back(v):
    return v

def low_keep(v):
    return (low(v), None)

def low_pass(kept, grad):
    return (grad,)

def back_keep(v):
    return (v, None)

def back_low(kept, grad):
    return (low(grad),)
low.defvjp(low_keep, low_pass)
low_back.defvjp(back_keep, back_low)

def layer_norm(matrix, norm_gain, norm_shift):
    centred = matrix - lax.optimization_barrier(jnp.mean(matrix, axis=1, keepdims=True))
    variance = lax.optimization_barrier(jnp.mean(centred * centred, axis=1, keepdims=True))
    return centred * lax.rsqrt(variance + norm_eps) * norm_gain + norm_shift

def reference(tokens, ln1_gain, ln1_bias, w_qkv, q_bias, v_bias, w_out, out_bias, ln2_gain, ln2_bias, w_router, expert_w1, expert_b1, expert_w2, expert_b2, route_ids, clip_threshold, grad_output):
    blocks = TOKENS // TOK_DEV
    score_scale = HD ** (-0.5)
    flat_ids = route_ids.reshape(blocks, TOK_DEV * TOP)
    onehot = (flat_ids[:, :, None] == jnp.arange(EXPERTS, dtype=jnp.int32)[None, None, :]).astype(jnp.int32)
    slot_rank = lax.optimization_barrier(jnp.sum((jnp.cumsum(onehot, axis=1, dtype=jnp.int32) - onehot) * onehot, axis=2, dtype=jnp.int32))
    block_index = jnp.arange(blocks, dtype=jnp.int32)[:, None]
    targets = (flat_ids * (blocks * CAP) + block_index * CAP + slot_rank).astype(jnp.int32).reshape(TOKENS, TOP)
    sources = jnp.arange(TOP, dtype=jnp.int32)[None, :] * TOKENS + jnp.arange(TOKENS, dtype=jnp.int32)[:, None]
    slot_table = jnp.full((EXPERTS * blocks * CAP,), TOP * TOKENS, jnp.int32).at[targets.reshape(-1)].set(sources.reshape(-1).astype(jnp.int32))

    def attend(group_data):
        group_query, group_key, group_value = group_data
        raw_scores = jnp.einsum('bqhd,bkhd->bhqk', group_query, group_key, precision=highest) * score_scale
        scores = low_back(raw_scores)
        weights = low(jax.nn.softmax(scores, axis=3))
        mixed_group = jnp.einsum('bhqk,bkhd->bqhd', weights, group_value, precision=highest)
        return (mixed_group, lax.optimization_barrier(jnp.max(scores, axis=(0, 2, 3))))

    def expert(group_data):
        rows_in, first_weight, first_bias, second_weight, second_bias = group_data
        pre_act = low_back(jnp.dot(rows_in, first_weight, precision=highest) + first_bias)
        activation = low(jax.nn.gelu(pre_act, approximate=False))
        return jnp.dot(activation, second_weight, precision=highest) + second_bias

    def forward(residual, gain_one, shift_one, qkv_weight, query_bias, value_bias, out_weight, out_shift, gain_two, shift_two, router_weight, first_weights, first_biases, second_weights, second_biases):
        normed_in = low(layer_norm(residual, gain_one, shift_one))
        projected = jnp.dot(normed_in, qkv_weight, precision=highest)
        queries = low_back(low(projected[:, :D] + query_bias))
        key_rows = low_back(low(projected[:, D:2 * D]))
        value_rows = low_back(low(projected[:, 2 * D:] + value_bias))
        head_shape = (blocks, IMG_DEV, SEQ, HEADS, HD)
        mixed_rows, head_peaks = lax.map(jax.checkpoint(attend), (queries.reshape(head_shape), key_rows.reshape(head_shape), value_rows.reshape(head_shape)))
        mixed_rows = low_back(low(mixed_rows.reshape(TOKENS, D)))
        branch = low_back(jnp.dot(mixed_rows, out_weight, precision=highest) + out_shift)
        hidden = residual + branch
        normed_mid = layer_norm(hidden, gain_two, shift_two)
        route_prob = jax.nn.softmax(jnp.dot(normed_mid, router_weight, precision=highest), axis=1)
        gate_values = jnp.take_along_axis(route_prob, route_ids, axis=1)
        mid_low = low(normed_mid)
        copies = [low_back(mid_low) for slot_index in range(TOP)]
        slot_rows = jnp.concatenate(copies + [jnp.zeros((1, D), jnp.float32)], axis=0)
        arrived = jnp.take(slot_rows, slot_table, axis=0).reshape(EXPERTS, blocks * CAP, D)
        produced = lax.map(jax.checkpoint(expert), (arrived, first_weights, first_biases, second_weights, second_biases))
        produced = low_back(low(produced)).reshape(EXPERTS * blocks * CAP, D)
        mixture = jnp.zeros((TOKENS, D), jnp.float32)
        for slot_index in range(TOP):
            mixture = mixture + gate_values[:, slot_index:slot_index + 1] * jnp.take(produced, targets[:, slot_index], axis=0)
        return (hidden + mixture, lax.optimization_barrier(jnp.max(head_peaks, axis=0)))
    weights_in = [item.astype(jnp.float32) for item in (ln1_gain, ln1_bias, w_qkv, q_bias, v_bias, w_out, out_bias, ln2_gain, ln2_bias, w_router, expert_w1, expert_b1, expert_w2, expert_b2)]
    start = tokens.astype(jnp.float32).reshape(TOKENS, D)
    result, pullback, peak_logit = jax.vjp(forward, start, *weights_in, has_aux=True)
    gradients = pullback(grad_output.astype(jnp.float32).reshape(TOKENS, D))
    limit_value = clip_threshold.astype(jnp.float32)
    root_factor = jnp.sqrt(limit_value / jnp.maximum(peak_logit, limit_value))
    column_scale = jnp.concatenate([jnp.repeat(root_factor, HD), jnp.repeat(root_factor, HD), jnp.ones((D,), jnp.float32)])
    clipped_qkv = (w_qkv.astype(jnp.float32) * column_scale).astype(jnp.bfloat16)
    return (result.astype(jnp.bfloat16).reshape(IMAGES, SEQ, D), gradients[0].reshape(IMAGES, SEQ, D), gradients[1], gradients[2], gradients[3], gradients[4], gradients[5], gradients[6], gradients[7], gradients[8], gradients[9], gradients[10], gradients[11], gradients[12], gradients[13], gradients[14], clipped_qkv)
```

```python
import functools

import jax
import jax.numpy as jnp
from jax import lax
from jax.experimental import pallas as pl
from jax.experimental.pallas import tpu as pltpu
from jax.sharding import Mesh
from jax.sharding import PartitionSpec as P

HEADS = 8
EPS = 1e-06
LANES = 128
VEC = 64
TAIL = 16
NEG = -1e30
f32 = jnp.float32
bf16 = jnp.bfloat16
i32 = jnp.int32
NN = (((1,), (0,)), ((), ()))
NT = (((1,), (1,)), ((), ()))
TN = (((0,), (0,)), ((), ()))
DEVICE = ("hi", "lo", "fy", "core")
GROUP = ("lo", "core")
VMEM_LIMIT = 58 << 20


def dot(a, b, dims):
    return lax.dot_general(a, b, dims, preferred_element_type=f32)


def pieces(value, count):
    parts = []
    for _ in range(count):
        part = value.astype(bf16)
        parts.append(part)
        value = value - part.astype(f32)
    return parts


def iota(shape, axis):
    return lax.broadcasted_iota(i32, shape, axis)


def relative_expert(place, shift, experts):
    other = jnp.bitwise_xor(place, shift)
    return (other & 1) * (experts // 2) + (other >> 1)


def router_order(place, experts):
    row, col = iota((LANES, LANES), 0), iota((LANES, LANES), 1)
    return jnp.where((row == relative_expert(place, col, experts)) & (col < experts), 1.0, 0.0).astype(bf16)


def norm_stats(matrix):
    centred = matrix - jnp.mean(matrix, axis=1, keepdims=True)
    inverse = lax.rsqrt(jnp.mean(centred * centred, axis=1, keepdims=True) + EPS)
    return centred * inverse, inverse


def norm_back(upstream, gain, hat, inverse):
    scaled = upstream * gain
    spread = (
        scaled
        - jnp.mean(scaled, axis=1, keepdims=True)
        - hat * jnp.mean(scaled * hat, axis=1, keepdims=True)
    )
    return spread * inverse


def softmax_lanes(logits, experts):
    logits = jnp.where(iota(logits.shape, 1) < experts, logits, NEG)
    top = jnp.max(logits, axis=1, keepdims=True)
    weight = jnp.exp(logits - top)
    return weight / jnp.sum(weight, axis=1, keepdims=True)


def gelu_pair(value):
    bell = jnp.exp(value * value * -0.5)
    t = 1.0 / (1.0 + jnp.abs(value) * (0.3275911 * 0.7071067811865476))
    poly = t * (
        0.127414796 + t * (-0.142248368 + t * (0.7107068705 + t * (-0.7265760135 + t * 0.5307027145)))
    )
    lower = poly * bell
    phi = jnp.where(value >= 0, 1.0 - lower, lower)
    return value * phi, phi + value * (bell * 0.3989422804014327)


def whole(shape):
    return pl.BlockSpec(shape, lambda *_: (0,) * len(shape))


def params(**extra):
    return pltpu.CompilerParams(vmem_limit_bytes=VMEM_LIMIT, **extra)


def cost(flops, moved, trans=0):
    return pl.CostEstimate(flops=int(flops), bytes_accessed=int(moved), transcendentals=int(trans))


def pack_kernel(spot_ref, wqkv, wout, router, *rest):
    vectors, (w2, b1, b2, pack_ref, w2_ref, spread, tail) = rest[:-7], rest[-7:]
    part, wide = wqkv.shape
    width, hidden = wout.shape[1], w2.shape[0]
    pack_ref[:, 0:wide] = wqkv[...]
    pack_ref[:, wide : wide + width] = wout[...]
    spread[...] = jnp.zeros_like(spread)
    for index, ref in enumerate(vectors):
        spread[VEC + index : VEC + index + 1, :] = ref[...].astype(f32)
    columns = spread[...].T
    pack_ref[:, wide + width :] = columns.astype(bf16)
    pack_ref[:, wide + width : wide + width + router.shape[1]] = router[...]
    w2_ref[0:hidden] = w2[...]
    tail[...] = jnp.zeros_like(tail)
    tail[0:1, 0 : b1.shape[1]] = b1[...].astype(f32)
    copies = jnp.concatenate([b2[...].astype(f32)] * (width // part), axis=1)
    tail[1:2] = jnp.where(iota((1, width), 1) // part == spot_ref[0], copies, 0.0)
    w2_ref[hidden : hidden + TAIL] = tail[...].astype(bf16)


def pack_parameters(spot, w_qkv, w_out, w_router, vectors, w2, b1, b2):
    part, width = w_out.shape
    hidden = w2.shape[0]
    operands = [w_qkv, w_out, w_router, *[v.reshape(1, part) for v in vectors], w2, b1, b2]
    return pl.pallas_call(
        pack_kernel,
        grid=(1,),
        in_specs=[pl.BlockSpec(memory_space=pltpu.SMEM)] + [whole(v.shape) for v in operands],
        out_specs=[whole((part, 4 * width + LANES)), whole((hidden + TAIL, width))],
        out_shape=[
            jax.ShapeDtypeStruct((part, 4 * width + LANES), bf16),
            jax.ShapeDtypeStruct((hidden + TAIL, width), bf16),
        ],
        scratch_shapes=[pltpu.VMEM((LANES, part), f32), pltpu.VMEM((TAIL, width), f32)],
        compiler_params=params(),
        cost_estimate=cost(1 << 20, 3 << 20),
        name="pack",
    )(spot, *operands)


def one_hot_rows(row, cap):
    slots = iota((cap, row.shape[1]), 0).astype(f32)
    return jnp.where(slots == row, 1.0, 0.0).astype(bf16)


def one_hot_cols(column, cap):
    slots = iota((column.shape[0], cap), 1).astype(f32)
    return jnp.where(slots == column, 1.0, 0.0).astype(bf16)


def route_kernel(place_ref, ids_ref, up_ref, post_ref, pos_ref, *rest, cap, stride):
    outs, gathered = rest[:-1], rest[-1]
    experts = len(outs)
    images, seq, width = up_ref.shape
    step = pl.program_id(0)

    @pl.when(step == 0)
    def _():
        expert = relative_expert(place_ref[0], iota((experts, stride), 0), experts)
        before = jnp.where(iota((stride, stride), 0) < iota((stride, stride), 1), 1.0, 0.0).astype(bf16)
        carry = jnp.zeros((experts, 1), f32)
        gathered[...] = jnp.zeros_like(gathered)
        for image in range(images):
            ids = ids_ref[:, image * stride : (image + 1) * stride]
            hit = jnp.zeros((experts, stride), jnp.bool_)
            for choice in range(ids_ref.shape[0]):
                hit = hit | (ids[choice : choice + 1] == expert)
            mask = jnp.where(hit, 1.0, 0.0)
            rank = carry + dot(mask.astype(bf16), before, NN)
            carry = carry + jnp.sum(mask, axis=1, keepdims=True)
            slot = jnp.where(hit, rank, -1.0)
            post_ref[:, image * stride : (image + 1) * stride] = slot
            padded = jnp.concatenate([slot, jnp.full((LANES - experts, stride), -1.0, f32)], axis=0)
            pos_ref[image] = padded.T
            gathered[image * stride : image * stride + seq] = up_ref[image]

    hot = one_hot_rows(post_ref[pl.ds(step, 1), :], cap)
    rows = dot(hot, gathered[...], NN).astype(bf16)
    for index in range(experts):

        @pl.when(step == index)
        def _():
            outs[index][...] = rows


def route(place, ids, grad_output, experts, cap, stride):
    images, seq, width = grad_output.shape
    total = images * stride
    return pl.pallas_call(
        functools.partial(route_kernel, cap=cap, stride=stride),
        grid=(experts,),
        in_specs=[
            pl.BlockSpec(memory_space=pltpu.SMEM),
            whole(ids.shape),
            whole(grad_output.shape),
        ],
        out_specs=[whole((experts, total)), whole((images, stride, LANES))] + [whole((cap, width))] * experts,
        out_shape=[
            jax.ShapeDtypeStruct((experts, total), f32),
            jax.ShapeDtypeStruct((images, stride, LANES), f32),
        ]
        + [jax.ShapeDtypeStruct((cap, width), bf16)] * experts,
        scratch_shapes=[pltpu.VMEM((total, width), bf16)],
        compiler_params=params(),
        cost_estimate=cost(2 * experts * cap * total * width, 8 << 20),
        name="route",
    )(place, ids, grad_output)


def forward_kernel(
    place_ref,
    tok_ref,
    wqkv_ref,
    wout_ref,
    misc_ref,
    post_ref,
    *rest,
    cap,
    stride,
    experts,
):
    qkv_ref, mixed_ref, hidden_ref, prob_ref, lse_ref, peak_ref = rest[-10 - experts : -4 - experts]
    outs, (tokens, vectors, router, gathered) = rest[-4 - experts : -4], rest[-4:]
    _, seq, width = tok_ref.shape
    rows = tokens.shape[0]
    head = width // HEADS
    step = pl.program_id(0)
    images = pl.num_programs(0) - experts

    @pl.when(step == 0)
    def _():
        vectors[...] = misc_ref[...].astype(f32).T
        router[...] = dot(misc_ref[...], router_order(place_ref[0], experts), NN).astype(bf16)
        gathered[...] = jnp.zeros_like(gathered)
        tokens[...] = jnp.zeros_like(tokens)
        peak_ref[...] = jnp.full_like(peak_ref, NEG)

    @pl.when(step < images)
    def _():
        def vector(index):
            return vectors[VEC + index : VEC + index + 1, :]

        tokens[0:seq] = tok_ref[0].astype(f32)
        residual = tokens[...]
        hat, _ = norm_stats(residual)
        normed = (hat * vector(0) + vector(1)).astype(bf16)
        projected = dot(normed, wqkv_ref[...], NN)
        qkv_ref[0, :, 0:width] = ((projected[:, 0:width] + vector(2)).astype(bf16).astype(f32) * head**-0.5).astype(
            bf16
        )
        qkv_ref[0, :, width : 2 * width] = projected[:, width : 2 * width].astype(bf16)
        qkv_ref[0, :, 2 * width :] = (projected[:, 2 * width :] + vector(3)).astype(bf16)
        lane = iota((1, LANES), 1)
        first = lane < head
        halves = (jnp.where(first, 1.0, 0.0).astype(bf16), jnp.where(first, 0.0, 1.0).astype(bf16))
        keys = jnp.where(iota((1, rows), 1) < seq, 0.0, NEG)
        valid = iota((rows, 1), 0) < seq

        def pair(index, carry):
            lse, peak = carry
            at = pl.multiple_of(index * LANES, LANES)
            query = qkv_ref[0, :, pl.ds(at, LANES)]
            key = qkv_ref[0, :, pl.ds(width + at, LANES)]
            value = qkv_ref[0, :, pl.ds(2 * width + at, LANES)]
            parts = []
            for half in range(2):
                scores = dot(query * halves[half], key, NT) + keys
                top = jnp.max(scores, axis=1, keepdims=True)
                weight = jnp.exp(scores - top)
                total = jnp.sum(weight, axis=1, keepdims=True)
                number = index * 2 + half
                lse = jnp.where(lane == number, top + jnp.log(total), lse)
                largest = jnp.max(jnp.where(valid, top, NEG), axis=0, keepdims=True)
                peak = jnp.where(lane == number, largest, peak)
                parts.append(dot(weight.astype(bf16), value, NN) * (1.0 / total))
            mixed_ref[0, :, pl.ds(at, LANES)] = jnp.where(first, parts[0], parts[1]).astype(bf16)
            return lse, peak

        lse, peak = lax.fori_loop(
            0, HEADS // 2, pair, (jnp.zeros((rows, LANES), f32), jnp.full((1, LANES), NEG, f32))
        )
        lse_ref[0] = lse
        peak_ref[...] = jnp.maximum(peak_ref[...], peak)
        hidden = residual + dot(mixed_ref[0], wout_ref[...], NN) + vector(4)
        hidden_ref[0] = hidden
        hat, _ = norm_stats(hidden)
        mid = hat * vector(5) + vector(6)
        logits = jnp.zeros((rows, LANES), f32)
        for part in pieces(mid, 3):
            logits = logits + dot(part, router[...], NN)
        prob_ref[0] = softmax_lanes(logits, experts)
        gathered[pl.ds(pl.multiple_of(step * stride, stride), rows)] = mid.astype(bf16)

    @pl.when(step >= images)
    def _():
        hot = one_hot_rows(post_ref[pl.ds(step - images, 1), :], cap)
        sent = dot(hot, gathered[...], NN).astype(bf16)
        for index in range(experts):

            @pl.when(step == images + index)
            def _():
                outs[index][...] = sent


def forward(place, tokens, pack, post, after, experts, cap, stride, rows):
    images, seq, width = tokens.shape
    total = images * stride

    def image(shape):
        return pl.BlockSpec((1,) + shape, lambda i: (jnp.minimum(i, images - 1), 0, 0))

    def struct(shape, kind):
        return jax.ShapeDtypeStruct((images,) + shape, kind)

    return pl.pallas_call(
        functools.partial(forward_kernel, cap=cap, stride=stride, experts=experts),
        grid=(images + experts,),
        in_specs=[
            pl.BlockSpec(memory_space=pltpu.SMEM),
            image((seq, width)),
            pl.BlockSpec((width, 3 * width), lambda i: (0, 0)),
            pl.BlockSpec((width, width), lambda i: (0, 3)),
            pl.BlockSpec((width, LANES), lambda i: (0, 4 * width // LANES)),
            whole(post.shape),
        ]
        + [pl.BlockSpec(memory_space=pl.ANY)] * len(after),
        out_specs=[
            image((rows, 3 * width)),
            image((rows, width)),
            image((rows, width)),
            image((rows, LANES)),
            image((rows, LANES)),
            whole((1, LANES)),
        ]
        + [whole((cap, width))] * experts,
        out_shape=[
            struct((rows, 3 * width), bf16),
            struct((rows, width), bf16),
            struct((rows, width), f32),
            struct((rows, LANES), f32),
            struct((rows, LANES), f32),
            jax.ShapeDtypeStruct((1, LANES), f32),
        ]
        + [jax.ShapeDtypeStruct((cap, width), bf16)] * experts,
        scratch_shapes=[
            pltpu.VMEM((rows, width), f32),
            pltpu.VMEM((LANES, width), f32),
            pltpu.VMEM((width, LANES), bf16),
            pltpu.VMEM((total, width), bf16),
        ],
        compiler_params=params(),
        cost_estimate=cost(2 * images * rows * width * 5 * width + 2 * experts * cap * total * width, 16 << 20),
        name="attend",
    )(place, tokens, pack, pack, pack, post, *after)


def expert_kernel(place_ref, *refs, cap, count, first, last, experts):
    taken = iter(refs)

    def take(number):
        return [next(taken) for _ in range(number)]

    rows_in, ups_in = take(count), take(count)
    w1, w2, b1, b2, misc = take(5)
    old = [] if first else take(2)
    row_back, gated = take(count), take(count)
    grad1, grad2 = take(2)
    rows, ups, gates, acc_row, acc_out, shift2, bias2 = take(7)
    step = pl.program_id(0)
    width = rows.shape[1]
    tile = w1.shape[1]

    @pl.when(step == 0)
    def _():
        for index in range(count):
            rows[index * cap : (index + 1) * cap] = rows_in[index][...]
        router = dot(misc[...], router_order(place_ref[0], experts), NN).astype(bf16)
        gate = softmax_lanes(dot(rows[...], router, NN), experts)[:, 0:1]
        gates[...] = jnp.broadcast_to(gate, gates.shape)
        for index in range(count):
            part = slice(index * cap, (index + 1) * cap)
            ups[part] = (ups_in[index][...].astype(f32) * gate[part]).astype(bf16)
        acc_row[...] = jnp.zeros_like(acc_row)
        acc_out[...] = jnp.zeros_like(acc_out)
        bias2[...] = jnp.zeros_like(bias2)
        shift2[...] = jnp.sum(ups[...].astype(f32), axis=0, keepdims=True)

    tail = b1[0].astype(f32)
    bias2[...] += tail[1:2]
    x, up = rows[...], ups[...]
    value, slope = gelu_pair(dot(x, w1[...], NN) + tail[0:1, 0:tile])
    act = value.astype(bf16)
    acc_out[...] += dot(act, w2[0], NN)
    raw = slope * dot(up, w2[0], NT)
    pre = raw.astype(bf16)
    acc_row[...] += dot(pre, w1[...], NT)
    part1 = dot(x, pre, TN)
    part2 = dot(act, up, TN)
    shift1 = jnp.sum(pre.astype(f32), axis=0, keepdims=True)
    if tile < width:
        shift1 = jnp.concatenate([shift1, jnp.zeros((1, width - tile), f32)], axis=1)
    place = iota((TAIL, width), 0)
    sums = jnp.where(place == 0, shift1, jnp.where(place == 1, shift2[...], 0.0))
    if not first:
        part1, part2, sums = old[0][...] + part1, old[1][0, 0:tile] + part2, old[1][0, tile:] + sums
    grad1[...] = part1.astype(grad1.dtype)
    grad2[0, 0:tile] = part2.astype(grad2.dtype)
    grad2[0, tile:] = sums.astype(grad2.dtype)

    @pl.when(step == pl.num_programs(0) - 1)
    def _():
        for index in range(count):
            part = slice(index * cap, (index + 1) * cap)
            made = acc_out[part] + bias2[...]
            gate = gates[part, 0:1]
            gated[index][...] = (made * gate).astype(bf16)
            row_back[index][0:cap] = acc_row[part].astype(bf16)
            effect = jnp.sum(made * ups_in[index][...].astype(f32), axis=1, keepdims=True) * gate
            effect = jnp.concatenate([effect, jnp.zeros((width - cap, 1), f32)], axis=0)
            line = jnp.broadcast_to(effect, (width, LANES)).T[0:1]
            end = jnp.zeros((TAIL, width), f32)
            for order, piece in enumerate(pieces(line, 3)):
                end = jnp.where(place == order, piece.astype(f32), end)
            row_back[index][cap : cap + TAIL] = end.astype(bf16)


def expert_call(place, rows, ups, weights, pack, old, cap, experts, last):
    count = len(rows)
    first = old is None
    w1, w2 = weights
    width, hidden = w1.shape
    shards_of, tall, _ = w2.shape
    tile = tall - TAIL
    total = count * cap
    kept = bf16 if last else f32
    column = pl.BlockSpec((width, tile), lambda h: (0, h))
    line = pl.BlockSpec((1, tall, width), lambda h: (h, 0, 0))
    unused = pl.BlockSpec((1, TAIL, width), lambda h: (h, tile // TAIL, 0))
    grads = [column, line]
    operands = [place, *rows, *ups, w1, w2, w2, w2, pack] + ([] if first else list(old))
    return pl.pallas_call(
        functools.partial(expert_kernel, cap=cap, count=count, first=first, last=last, experts=experts),
        grid=(shards_of,),
        in_specs=[pl.BlockSpec(memory_space=pltpu.SMEM)]
        + [whole((cap, width))] * (2 * count)
        + [
            column,
            pl.BlockSpec((1, tile, width), lambda h: (h, 0, 0)),
            unused,
            unused,
            pl.BlockSpec((width, LANES), lambda h: (0, 4 * width // LANES)),
        ]
        + ([] if first else grads),
        out_specs=[whole((cap + TAIL, width))] * count + [whole((cap, width))] * count + grads,
        out_shape=[jax.ShapeDtypeStruct((cap + TAIL, width), bf16)] * count
        + [jax.ShapeDtypeStruct((cap, width), bf16)] * count
        + [
            jax.ShapeDtypeStruct((width, hidden), kept),
            jax.ShapeDtypeStruct((shards_of, tall, width), kept),
        ],
        scratch_shapes=[pltpu.VMEM((total, width), bf16)] * 2
        + [pltpu.VMEM((total, LANES), f32)]
        + [pltpu.VMEM((total, width), f32)] * 2
        + [pltpu.VMEM((1, width), f32)] * 2,
        compiler_params=params(),
        cost_estimate=cost(12 * total * width * hidden, 24 << 20),
        name="expert",
    )(*operands)


def middle_kernel(
    place_ref, up_ref, wout_ref, misc_ref, pos_ref, mixed_ref, hidden_ref, prob_ref, *rest, cap, experts
):
    backs = rest[:experts]
    hidden_grad_ref, mixed_grad_ref, sums_ref, padded, vectors, router, shifts, acc_out, acc_router = rest[-9:]
    _, seq, width = up_ref.shape
    rows = padded.shape[0]
    step = pl.program_id(0)

    @pl.when(step == 0)
    def _():
        vectors[...] = misc_ref[...].astype(f32).T
        router[...] = dot(misc_ref[...], router_order(place_ref[0], experts), NN).astype(bf16)
        padded[...] = jnp.zeros_like(padded)
        shifts[...] = jnp.zeros_like(shifts)
        acc_out[...] = jnp.zeros_like(acc_out)
        acc_router[...] = jnp.zeros_like(acc_router)

    def vector(index):
        return vectors[VEC + index : VEC + index + 1, :]

    def shift(index, value):
        shifts[index : index + 1, :] += jnp.sum(value, axis=0, keepdims=True)

    lane = iota((1, LANES), 1)
    places = pos_ref[0, 0:rows, :]
    slot_sum = jnp.zeros((rows, width), f32)
    effect = jnp.zeros((rows, LANES), f32)
    for index in range(experts):
        hot = one_hot_cols(places[:, index : index + 1], cap)
        slot_sum = slot_sum + dot(hot, backs[index][0:cap], NN)
        parts = dot(hot, backs[index][cap : cap + TAIL, 0:cap], NT)
        effect = jnp.where(lane == index, jnp.sum(parts, axis=1, keepdims=True), effect)
    prob = prob_ref[0]
    logit_grad = effect - prob * jnp.sum(effect, axis=1, keepdims=True)
    logit_parts = pieces(logit_grad, 2)
    mid_grad = slot_sum
    for part in logit_parts:
        mid_grad = mid_grad + dot(part, router[...], NT)
    padded[0:seq] = up_ref[0].astype(f32)
    hat, inverse = norm_stats(hidden_ref[0])
    mid_parts = pieces(hat * vector(5) + vector(6), 2)
    acc_router[...] += (
        dot(logit_parts[0], mid_parts[0], TN)
        + dot(logit_parts[0], mid_parts[1], TN)
        + dot(logit_parts[1], mid_parts[0], TN)
    )
    shift(5, mid_grad * hat)
    shift(6, mid_grad)
    hidden_grad = padded[...] + norm_back(mid_grad, vector(5), hat, inverse)
    hidden_grad_ref[0] = hidden_grad
    branch = hidden_grad.astype(bf16)
    shift(4, branch.astype(f32))
    acc_out[...] += dot(mixed_ref[0], branch, TN)
    mixed_grad_ref[0] = dot(branch, wout_ref[...], NT).astype(bf16)

    @pl.when(step == pl.num_programs(0) - 1)
    def _():
        sums_ref[:, 0:width] = acc_out[...]
        ordered = dot(router_order(place_ref[0], experts), acc_router[...].astype(bf16), NN)
        spare = jnp.concatenate(
            [ordered[0:VEC], shifts[...], jnp.zeros((LANES - VEC - shifts.shape[0], width), f32)], axis=0
        )
        sums_ref[:, width:] = spare.T


def middle(place, grad_output, pack, pos, saved, backs, cap, experts):
    images, seq, width = grad_output.shape
    _, mixed, hidden, prob, _ = saved
    rows = mixed.shape[1]

    def image(shape):
        return pl.BlockSpec((1,) + shape, lambda i: (i, 0, 0))

    return pl.pallas_call(
        functools.partial(middle_kernel, cap=cap, experts=experts),
        grid=(images,),
        in_specs=[
            pl.BlockSpec(memory_space=pltpu.SMEM),
            image((seq, width)),
            pl.BlockSpec((width, width), lambda i: (0, 3)),
            pl.BlockSpec((width, LANES), lambda i: (0, 4 * width // LANES)),
            image((pos.shape[1], LANES)),
            image((rows, width)),
            image((rows, width)),
            image((rows, LANES)),
        ]
        + [whole((cap + TAIL, width))] * experts,
        out_specs=[image((rows, width)), image((rows, width)), whole((width, width + LANES))],
        out_shape=[
            jax.ShapeDtypeStruct((images, rows, width), f32),
            jax.ShapeDtypeStruct((images, rows, width), bf16),
            jax.ShapeDtypeStruct((width, width + LANES), f32),
        ],
        scratch_shapes=[
            pltpu.VMEM((rows, width), f32),
            pltpu.VMEM((LANES, width), f32),
            pltpu.VMEM((width, LANES), bf16),
            pltpu.VMEM((8, width), f32),
            pltpu.VMEM((width, width), f32),
            pltpu.VMEM((LANES, width), f32),
        ],
        compiler_params=params(),
        cost_estimate=cost(2 * images * rows * width * (2 * width + experts * cap), 16 << 20),
        name="middle",
    )(place, grad_output, pack, pack, pos, mixed, hidden, prob, *backs)


def backward_kernel(
    spots_ref, tok_ref, qkv_ref, lse_ref, mixed_grad_ref, sums_ref, peak_ref, *rest, head_rows, members
):
    qkv_grad_ref, keep_ref, give_ref, padded, acc_qkv, columns, spare, misc = rest[-8:]
    _, seq, width = tok_ref.shape
    rows = padded.shape[0]
    head = width // HEADS
    wide = 3 * width
    step = pl.program_id(0)
    part = keep_ref.shape[1]

    @pl.when(step == 0)
    def _():
        padded[...] = jnp.zeros_like(padded)
        acc_qkv[...] = jnp.zeros_like(acc_qkv)
        columns[...] = jnp.zeros_like(columns)

    lane = iota((1, LANES), 1)
    first = lane < head
    halves = (jnp.where(first, 1.0, 0.0).astype(bf16), jnp.where(first, 0.0, 1.0).astype(bf16))
    keys = jnp.where(iota((1, rows), 1) < seq, 0.0, NEG)
    lse = lse_ref[0]

    def pair(index, carry):
        at = pl.multiple_of(index * LANES, LANES)
        query = qkv_ref[0, :, pl.ds(at, LANES)]
        key = qkv_ref[0, :, pl.ds(width + at, LANES)]
        value = qkv_ref[0, :, pl.ds(2 * width + at, LANES)]
        up = mixed_grad_ref[0, :, pl.ds(at, LANES)]
        made = []
        for half in range(2):
            total = jnp.sum(jnp.where(lane == index * 2 + half, lse, 0.0), axis=1, keepdims=True)
            weight = jnp.exp(dot(query * halves[half], key, NT) + keys - total)
            value_grad = dot(weight.astype(bf16), up, TN)
            spread = weight * dot(up * halves[half], value, NT)
            score_grad = (spread - weight * jnp.sum(spread, axis=1, keepdims=True)).astype(bf16)
            made.append((dot(score_grad, key, NN) * head**-0.5, dot(score_grad, query, TN), value_grad))
        for index_of, (left, right) in enumerate(zip(*made)):
            qkv_grad_ref[0, :, pl.ds(index_of * width + at, LANES)] = jnp.where(first, left, right).astype(bf16)
        return carry

    lax.fori_loop(0, HEADS // 2, pair, 0)
    columns[...] += jnp.sum(qkv_grad_ref[0].astype(f32), axis=0, keepdims=True)
    padded[0:seq] = tok_ref[0].astype(f32)
    hat, _ = norm_stats(padded[...])
    acc_qkv[...] += dot(hat.astype(bf16), qkv_grad_ref[0], TN)

    @pl.when(step == pl.num_programs(0) - 1)
    def _():
        line = iota((LANES, width), 0)
        flat = columns[...]
        grown = jnp.where(line == VEC + 2, flat[:, 0:width], 0.0)
        grown = jnp.where(line == VEC + 3, flat[:, 2 * width :], grown)
        misc[...] = sums_ref[:, width:] + grown.T
        spare[...] = jnp.zeros_like(spare)
        number = wide // LANES
        for order, piece in enumerate(pieces(flat, 3)):
            value = piece.astype(f32)
            for index in range(number):
                at = order * number + index
                spare[at : at + 1, :] = value[:, index * LANES : (index + 1) * LANES]
        if members:
            top = jnp.where(lane < HEADS, peak_ref[...], 0.0)
            rows_of = jnp.zeros((TAIL, LANES), f32)
            for order, piece in enumerate(pieces(jnp.broadcast_to(top, (TAIL, LANES)), 3)):
                move = jnp.where(iota((LANES, LANES), 1) == iota((LANES, LANES), 0) + order * HEADS, 1.0, 0.0)
                rows_of = rows_of + dot(piece, move.astype(bf16), NN)
            spare[pl.ds(head_rows + spots_ref[1], 1), :] = rows_of[0:1]
        extra = spare[...].astype(bf16)
        for fy in range(keep_ref.shape[0]):
            for ref, core in ((keep_ref, spots_ref[0]), (give_ref, 1 - spots_ref[0])):
                at = pl.multiple_of((2 * fy + core) * part, part)
                ref[fy, :, 0:wide] = acc_qkv[pl.ds(at, part), :].astype(bf16)
                ref[fy, :, wide : wide + width] = sums_ref[pl.ds(at, part), 0:width].astype(bf16)
                ref[fy, :, wide + width : wide + width + LANES] = misc[pl.ds(at, part), :].astype(bf16)
                ref[fy, :, wide + width + LANES :] = extra


def backward(spots, tokens, saved, mixed_grad, sums, peak, after, ways, part, head_rows, members):
    images, seq, width = tokens.shape
    qkv, _, _, _, lse = saved
    rows = qkv.shape[1]
    wide = 4 * width + 2 * LANES

    def image(shape):
        return pl.BlockSpec((1,) + shape, lambda i: (i, 0, 0))

    return pl.pallas_call(
        functools.partial(backward_kernel, head_rows=head_rows, members=members),
        grid=(images,),
        in_specs=[
            pl.BlockSpec(memory_space=pltpu.SMEM),
            image((seq, width)),
            image((rows, 3 * width)),
            image((rows, LANES)),
            image((rows, width)),
            whole(sums.shape),
            whole(peak.shape),
        ]
        + [pl.BlockSpec(memory_space=pl.ANY)] * len(after),
        out_specs=[image((rows, 3 * width)), whole((ways, part, wide)), whole((ways, part, wide))],
        out_shape=[
            jax.ShapeDtypeStruct((images, rows, 3 * width), bf16),
            jax.ShapeDtypeStruct((ways, part, wide), bf16),
            jax.ShapeDtypeStruct((ways, part, wide), bf16),
        ],
        scratch_shapes=[
            pltpu.VMEM((rows, width), f32),
            pltpu.VMEM((width, 3 * width), f32),
            pltpu.VMEM((1, 3 * width), f32),
            pltpu.VMEM((part, LANES), f32),
            pltpu.VMEM((width, LANES), f32),
        ],
        compiler_params=params(),
        cost_estimate=cost(2 * images * rows * width * 8 * width, 24 << 20),
        name="attend_back",
    )(spots, tokens, qkv, lse, mixed_grad, sums, peak, *after)


def first_kernel(tok_ref, qkv_grad_ref, wqkv_ref, misc_ref, hidden_grad_ref, grad_ref, padded, gain):
    _, seq, width = tok_ref.shape

    @pl.when(pl.program_id(0) == 0)
    def _():
        gain[...] = misc_ref[...].astype(f32).T[VEC : VEC + 1]
        padded[...] = jnp.zeros_like(padded)

    in_grad = dot(qkv_grad_ref[0], wqkv_ref[...], NT)
    padded[0:seq] = tok_ref[0].astype(f32)
    hat, inverse = norm_stats(padded[...])
    grad_ref[0] = (hidden_grad_ref[0] + norm_back(in_grad, gain[...], hat, inverse))[0:seq]


def first_norm(tokens, qkv_grad, pack, hidden_grad):
    images, seq, width = tokens.shape
    rows = qkv_grad.shape[1]

    def image(shape):
        return pl.BlockSpec((1,) + shape, lambda i: (i, 0, 0))

    return pl.pallas_call(
        first_kernel,
        grid=(images,),
        in_specs=[
            image((seq, width)),
            image((rows, 3 * width)),
            pl.BlockSpec((width, 3 * width), lambda i: (0, 0)),
            pl.BlockSpec((width, LANES), lambda i: (0, 4 * width // LANES)),
            image((rows, width)),
        ],
        out_specs=image((seq, width)),
        out_shape=jax.ShapeDtypeStruct((images, seq, width), f32),
        scratch_shapes=[pltpu.VMEM((rows, width), f32), pltpu.VMEM((1, width), f32)],
        compiler_params=params(),
        cost_estimate=cost(2 * images * rows * width * 3 * width, 12 << 20),
        name="first_norm",
    )(tokens, qkv_grad, pack, pack, hidden_grad)


def output_kernel(pos_ref, hidden_ref, *rest, cap):
    made, out_ref = rest[:-1], rest[-1]
    seq = out_ref.shape[1]
    total = hidden_ref[0]
    places = pos_ref[0, 0 : total.shape[0], :]
    for index, ref in enumerate(made):
        total = total + dot(one_hot_cols(places[:, index : index + 1], cap), ref[...], NN)
    out_ref[0] = total[0:seq].astype(bf16)


def combine_output(pos, hidden, made, cap, seq):
    images, rows, width = hidden.shape

    def image(shape):
        return pl.BlockSpec((1,) + shape, lambda i: (i, 0, 0))

    return pl.pallas_call(
        functools.partial(output_kernel, cap=cap),
        grid=(images,),
        in_specs=[image((pos.shape[1], LANES)), image((rows, width))] + [whole((cap, width))] * len(made),
        out_specs=image((seq, width)),
        out_shape=jax.ShapeDtypeStruct((images, seq, width), bf16),
        compiler_params=params(),
        cost_estimate=cost(2 * images * rows * width * cap * len(made), 8 << 20),
        name="combine",
    )(pos, hidden, *made)


def finish_kernel(total_ref, own_ref, limit_ref, peak_ref, *rest, head_rows, members):
    qkv_ref, out_ref, misc_ref, vec_ref, clip_ref = rest
    part = own_ref.shape[0]
    width = out_ref.shape[1]
    wide = 3 * width
    number = wide // LANES
    base = total_ref[:, 0:wide].astype(f32)
    extra = total_ref[:, wide + width + LANES :].astype(f32)
    weight = own_ref[:, 0:wide].astype(f32)
    columns = [sum(extra[k * number + i : k * number + i + 1] for k in range(3)) for i in range(number)]
    columns = jnp.concatenate(columns, axis=1)
    own = own_ref[:, wide + width :].astype(f32)
    gain, bias = own[:, VEC : VEC + 1], own[:, VEC + 1 : VEC + 2]
    qkv_ref[...] = base * gain + bias * columns
    out_ref[...] = total_ref[:, wide : wide + width].astype(f32)
    misc = total_ref[:, wide + width : wide + width + LANES].astype(f32)
    misc_ref[...] = misc
    lane = iota((1, LANES), 1)
    misc = jnp.where(lane == VEC, jnp.sum(base * weight, axis=1, keepdims=True), misc)
    misc = jnp.where(lane == VEC + 1, jnp.sum(columns * weight, axis=1, keepdims=True), misc)
    vec_ref[...] = misc.T[VEC : VEC + 8]
    if members:
        move = jnp.where(
            (iota((LANES, LANES), 0) % HEADS == iota((LANES, LANES), 1)) & (iota((LANES, LANES), 0) < 3 * HEADS),
            1.0,
            0.0,
        )
        peaks = dot(total_ref[head_rows : head_rows + members, wide + width + LANES :], move.astype(bf16), NN)
        peak = jnp.max(peaks, axis=0, keepdims=True)
    else:
        peak = peak_ref[...]
    limit = limit_ref[...]
    root = jnp.sqrt(limit / jnp.maximum(peak, limit))
    place = iota((1, width), 1) // (width // HEADS)
    scale = jnp.zeros((1, width), f32)
    for index in range(HEADS):
        scale = jnp.where(place == index, root[:, index : index + 1], scale)
    clip_ref[:, 0:width] = (weight[:, 0:width] * scale).astype(bf16)
    clip_ref[:, width : 2 * width] = (weight[:, width : 2 * width] * scale).astype(bf16)
    clip_ref[:, 2 * width :] = own_ref[:, 2 * width : wide]


def finish(total, own, limit, peak, width, head_rows, members):
    part = own.shape[0]
    operands = [total, own, limit, peak]
    shapes = [(part, 3 * width), (part, width), (part, LANES), (8, part), (part, 3 * width)]
    return pl.pallas_call(
        functools.partial(finish_kernel, head_rows=head_rows, members=members),
        grid=(1,),
        in_specs=[whole(v.shape) for v in operands],
        out_specs=[whole(v) for v in shapes],
        out_shape=[jax.ShapeDtypeStruct(v, bf16 if i == 4 else f32) for i, v in enumerate(shapes)],
        compiler_params=params(),
        cost_estimate=cost(1 << 20, 4 << 20),
        name="finish",
    )(*operands)


def swap(value, axis):
    return lax.ppermute(value, axis, [(0, 1), (1, 0)])


def rotate(values, axis, size):
    if size != 2:
        return jnp.roll(jnp.stack(values), lax.axis_index(axis), axis=0)
    return jnp.where(lax.axis_index(axis) == 0, jnp.stack(values), jnp.stack(values[::-1]))


def around(value, axis, size):
    return [value] + [
        lax.ppermute(value, axis, [((k + step) % size, k) for k in range(size)]) for step in range(1, size)
    ]


def split_sum(value, axis, size):
    if size != 2:
        return lax.psum_scatter(value, axis, scatter_dimension=0, tiled=False)
    place = lax.axis_index(axis)
    sent = lax.dynamic_index_in_dim(value, 1 - place, 0, keepdims=False)
    kept = lax.dynamic_index_in_dim(value, place, 0, keepdims=False)
    return (kept.astype(f32) + swap(sent, axis).astype(f32)).astype(value.dtype)


def exchange(value, shift, experts):
    return lax.ppermute(value, GROUP, [(k, k ^ shift) for k in range(experts)])


def shift_order(experts):
    def key(shift):
        return (shift < 2, bin(shift >> 1).count("1"), shift & 1, shift)

    return sorted(range(experts), key=key)


STRAIGHT = [(0, 0), (1, 2), (2, 1), (3, 3)]
CROSSED = [(0, 2), (1, 0), (2, 3), (3, 1)]
BACK = [(b, a) for a, b in STRAIGHT]
BACK_CROSSED = [(b, a) for a, b in CROSSED]


def shards(
    tokens,
    ln1_gain,
    ln1_bias,
    w_qkv,
    q_bias,
    v_bias,
    w_out,
    out_bias,
    ln2_gain,
    ln2_bias,
    w_router,
    expert_w1,
    expert_b1,
    expert_w2,
    expert_b2,
    route_ids,
    clip_threshold,
    grad_output,
    *,
    experts,
    fsdp,
):
    images, seq, width = tokens.shape
    token_count = images * seq
    ways = fsdp // 2
    cap = (7 * token_count // (2 * experts) + 7) // 8 * 8
    stride = -(-seq // 256) * 256
    rows = -(-seq // 16) * 16
    part = w_qkv.shape[0]
    hidden_part = expert_w2.shape[1]
    high, low, fy, core = (lax.axis_index(name).astype(i32) for name in DEVICE)
    place_ref = (low * 2 + core).reshape(1)
    spot = fy * 2 + core

    vectors = (ln1_gain, ln1_bias, q_bias, v_bias, out_bias, ln2_gain, ln2_bias)
    own, w2_own = pack_parameters(
        spot.reshape(1), w_qkv, w_out, w_router, vectors, expert_w2[0], expert_b1, expert_b2
    )

    def to_places(shard):
        return (
            lax.ppermute(shard, ("hi", "core"), STRAIGHT),
            lax.ppermute(shard, ("hi", "core"), CROSSED),
        )

    def all_rows(pair):
        straight, crossed = (rotate(around(value, "fy", ways), "fy", ways) for value in pair)
        return jnp.where(
            high == 0, jnp.stack([straight, crossed], axis=1), jnp.stack([crossed, straight], axis=1)
        )

    pack = around(own, "fy", ways)
    w1_pair = to_places(expert_w1[0])
    pack = rotate(pack, "fy", ways)
    other = swap(pack, "core")
    pack = jnp.where(core == 0, jnp.stack([pack, other], axis=1), jnp.stack([other, pack], axis=1))
    pack = pack.reshape(width, pack.shape[-1])

    ids = jnp.pad(route_ids.reshape(images, seq, -1), ((0, 0), (0, stride - seq), (0, 0)), constant_values=-1)
    ids = ids.reshape(images * stride, -1).T
    post, pos, *ups = route(place_ref, ids, grad_output, experts, cap, stride)
    order = shift_order(experts)
    ups_in = {shift: ups[shift] if shift == 0 else exchange(ups[shift], shift, experts) for shift in order}

    w2_own, w1_pair = lax.optimization_barrier((w2_own, w1_pair))
    w2_pair = to_places(w2_own)
    outputs = forward(place_ref, tokens, pack, post, w1_pair, experts, cap, stride, rows)
    saved, peak, sent = outputs[:5], outputs[5], outputs[6:]
    w1 = all_rows(w1_pair).reshape(width, -1)
    w2 = all_rows(w2_pair).reshape(fsdp, hidden_part + TAIL, width)

    size = max(1, experts // 4)
    groups = [order[at : at + size] for at in range(0, experts, size)]
    arrived, before = {}, None
    for group in groups:
        pending = [sent[shift] for shift in group]
        if before is not None:
            pending, before = lax.optimization_barrier((pending, before))
        got = [value if shift == 0 else exchange(value, shift, experts) for shift, value in zip(group, pending)]
        before = got
        arrived.update(zip(group, got))

    old = None
    backs, made = {}, {}
    for number, group in enumerate(groups):
        result = expert_call(
            place_ref,
            [arrived[shift] for shift in group],
            [ups_in[shift] for shift in group],
            (w1, w2),
            pack,
            old,
            cap,
            experts,
            number == len(groups) - 1,
        )
        count = len(group)
        old = result[2 * count :]
        for at, shift in enumerate(group):
            backs[shift] = result[at] if shift == 0 else exchange(result[at], shift, experts)
            made[shift] = result[count + at]
    backs = [backs[shift] for shift in range(experts)]
    made = [made[shift] for shift in range(experts)]
    made, backs = lax.optimization_barrier((made, backs))
    made = [value if shift == 0 else exchange(value, shift, experts) for shift, value in enumerate(made)]

    hidden_grad, mixed_grad, sums = middle(place_ref, grad_output, pack, pos, saved, backs, cap, experts)
    head_rows = 3 * (3 * width // LANES) + 4
    devices = 2 * experts // 2 * fsdp
    members = devices if head_rows + devices <= part else 0
    device = ((high * (experts // 2) + low) * ways + fy) * 2 + core
    spots = jnp.stack([core, device])
    qkv_grad, keep, give = backward(
        spots, tokens, saved, mixed_grad, sums, peak, made[: experts // 2], ways, part, head_rows, members
    )

    def return_grad(grad):
        grad = split_sum(grad, "fy", ways)
        straight = lax.dynamic_index_in_dim(grad, high, 0, keepdims=False)
        crossed = lax.dynamic_index_in_dim(grad, 1 - high, 0, keepdims=False)
        straight = lax.ppermute(straight, ("hi", "core"), BACK)
        crossed = lax.ppermute(crossed, ("hi", "core"), BACK_CROSSED)
        return straight.astype(f32) + crossed.astype(f32)

    grad_w1 = return_grad(old[0].reshape(ways, 2, part, -1))[None]
    grad_w2 = return_grad(old[1].reshape(ways, 2, hidden_part + TAIL, width))
    grad_b1 = grad_w2[hidden_part : hidden_part + 1, :hidden_part]
    grad_b2 = lax.dynamic_slice_in_dim(grad_w2[hidden_part + 1 : hidden_part + 2], spot * part, part, axis=1)
    grad_w2 = grad_w2[None, :hidden_part]

    sums = (keep.astype(f32) + swap(give, "core").astype(f32)).astype(bf16)
    sums = split_sum(sums, "fy", ways)
    input_grad = first_norm(tokens, qkv_grad, pack, hidden_grad)
    output = combine_output(pos, saved[2], made, cap, seq)
    sums = sums.reshape(experts, part // experts, -1)
    sums = lax.all_to_all(sums, ("hi", "lo"), split_axis=0, concat_axis=0, tiled=True)
    total = jnp.sum(sums.astype(f32), axis=0, keepdims=True).astype(bf16)
    total = jnp.broadcast_to(total, (experts,) + total.shape[1:])
    total = lax.all_to_all(total, ("hi", "lo"), split_axis=0, concat_axis=0, tiled=True)
    total = total.reshape(part, -1)
    if not members:
        peak = jnp.max(lax.all_gather(peak, DEVICE, axis=0, tiled=True), axis=0, keepdims=True)
    limit = jnp.pad(clip_threshold.astype(f32).reshape(1, HEADS), ((0, 0), (0, LANES - HEADS)), constant_values=1.0)
    grad_qkv, grad_out, grad_misc, grads, clipped = finish(total, own, limit, peak, width, head_rows, members)
    return (
        output,
        input_grad,
        grads[0],
        grads[1],
        grad_qkv,
        grads[2],
        grads[3],
        grad_out,
        grads[4],
        grads[5],
        grads[6],
        grad_misc[:, :experts],
        grad_w1,
        grad_b1,
        grad_w2,
        grad_b2,
        clipped,
    )


def solution(mesh):
    experts, fsdp = mesh.shape["expert"], mesh.shape["fsdp"]
    inner = Mesh(mesh.devices.reshape(2, experts // 2, fsdp // 2, 2), DEVICE)
    token, row, expert = P(DEVICE, None, None), ("fy", "core"), ("hi", "lo")
    vector, matrix = P(row), P(row, None)
    return jax.shard_map(
        functools.partial(shards, experts=experts, fsdp=fsdp),
        mesh=inner,
        in_specs=(
            token,
            vector,
            vector,
            matrix,
            vector,
            vector,
            matrix,
            vector,
            vector,
            vector,
            matrix,
            P(expert, row, None),
            P(expert, row),
            P(expert, row, None),
            P(expert, row),
            P(DEVICE, None),
            P(),
            token,
        ),
        out_specs=(
            token,
            token,
            vector,
            vector,
            matrix,
            vector,
            vector,
            matrix,
            vector,
            vector,
            vector,
            matrix,
            P(expert, row, None),
            P(expert, row),
            P(expert, row, None),
            P(expert, row),
            matrix,
        ),
        check_vma=False,
    )
```

```python
import functools

import jax
import jax.numpy as jnp
from jax import lax
from jax.experimental import pallas as pl
from jax.experimental.pallas import tpu as pltpu
from jax.sharding import Mesh
from jax.sharding import PartitionSpec as P

HEADS = 8
EPS = 1e-06
LANES = 128
VEC = 64
TAIL = 16
NEG = -1e30
f32 = jnp.float32
bf16 = jnp.bfloat16
i32 = jnp.int32
NN = (((1,), (0,)), ((), ()))
NT = (((1,), (1,)), ((), ()))
TN = (((0,), (0,)), ((), ()))
DEVICE = ("hi", "lo", "fy", "core")
GROUP = ("lo", "core")
VMEM_LIMIT = 58 << 20


def dot(a, b, dims):
    return lax.dot_general(a, b, dims, preferred_element_type=f32)


def pieces(value, count):
    parts = []
    for _ in range(count):
        part = value.astype(bf16)
        parts.append(part)
        value = value - part.astype(f32)
    return parts


def iota(shape, axis):
    return lax.broadcasted_iota(i32, shape, axis)


def relative_expert(place, shift, experts):
    other = jnp.bitwise_xor(place, shift)
    return (other & 1) * (experts // 2) + (other >> 1)


def router_order(place, experts):
    row, col = iota((LANES, LANES), 0), iota((LANES, LANES), 1)
    return jnp.where((row == relative_expert(place, col, experts)) & (col < experts), 1.0, 0.0).astype(bf16)


def norm_stats(matrix):
    centred = matrix - jnp.mean(matrix, axis=1, keepdims=True)
    inverse = lax.rsqrt(jnp.mean(centred * centred, axis=1, keepdims=True) + EPS)
    return centred * inverse, inverse


def norm_back(upstream, gain, hat, inverse):
    scaled = upstream * gain
    spread = (
        scaled
        - jnp.mean(scaled, axis=1, keepdims=True)
        - hat * jnp.mean(scaled * hat, axis=1, keepdims=True)
    )
    return spread * inverse


def softmax_lanes(logits, experts):
    logits = jnp.where(iota(logits.shape, 1) < experts, logits, NEG)
    top = jnp.max(logits, axis=1, keepdims=True)
    weight = jnp.exp(logits - top)
    return weight / jnp.sum(weight, axis=1, keepdims=True)


def gelu_pair(value):
    bell = jnp.exp(value * value * -0.5)
    t = 1.0 / (1.0 + jnp.abs(value) * (0.3275911 * 0.7071067811865476))
    poly = t * (
        0.127414796 + t * (-0.142248368 + t * (0.7107068705 + t * (-0.7265760135 + t * 0.5307027145)))
    )
    lower = poly * bell
    phi = jnp.where(value >= 0, 1.0 - lower, lower)
    return value * phi, phi + value * (bell * 0.3989422804014327)


def whole(shape):
    return pl.BlockSpec(shape, lambda *_: (0,) * len(shape))


def params(**extra):
    return pltpu.CompilerParams(vmem_limit_bytes=VMEM_LIMIT, **extra)


def cost(micros):
    return pl.CostEstimate(flops=int(micros * 1e9), bytes_accessed=0, transcendentals=0)


def pack_kernel(spot_ref, wqkv, wout, router, *rest):
    vectors, (w1, w2, b1, b2, pack_ref, pay_ref, spread, tail) = rest[:-8], rest[-8:]
    part, wide = wqkv.shape
    width, hidden = wout.shape[1], w2.shape[0]
    pack_ref[:, 0:wide] = wqkv[...]
    pack_ref[:, wide : wide + width] = wout[...]
    spread[...] = jnp.zeros_like(spread)
    spread[0 : router.shape[0], :] = router[...].astype(f32)
    for index, ref in enumerate(vectors):
        spread[VEC + index : VEC + index + 1, :] = ref[...].astype(f32)
    columns = spread[...].T
    pack_ref[:, wide + width :] = columns.astype(bf16)
    pay_ref[0:hidden] = w2[...]
    tail[...] = jnp.zeros_like(tail)
    tail[0:1, 0 : b1.shape[1]] = b1[...].astype(f32)
    copies = jnp.concatenate([b2[...].astype(f32)] * (width // part), axis=1)
    tail[1:2] = jnp.where(iota((1, width), 1) // part == spot_ref[0], copies, 0.0)
    tall = hidden + TAIL
    pay_ref[hidden:tall] = tail[...].astype(bf16)
    for index in range(width // part):
        block = w1[:, index * hidden : (index + 1) * hidden]
        if hidden < width:
            block = jnp.concatenate([block, jnp.zeros((part, width - hidden), bf16)], axis=1)
        pay_ref[tall + index * part : tall + (index + 1) * part] = block


def pack_parameters(spot, w_qkv, w_out, w_router, vectors, w1, w2, b1, b2):
    part, width = w_out.shape
    hidden = w2.shape[0]
    operands = [w_qkv, w_out, w_router.T, *[v.reshape(1, part) for v in vectors], w1, w2, b1, b2]
    return pl.pallas_call(
        pack_kernel,
        grid=(1,),
        in_specs=[pl.BlockSpec(memory_space=pltpu.SMEM)] + [whole(v.shape) for v in operands],
        out_specs=[whole((part, 4 * width + LANES)), whole((hidden + TAIL + width, width))],
        out_shape=[
            jax.ShapeDtypeStruct((part, 4 * width + LANES), bf16),
            jax.ShapeDtypeStruct((hidden + TAIL + width, width), bf16),
        ],
        scratch_shapes=[pltpu.VMEM((LANES, part), f32), pltpu.VMEM((TAIL, width), f32)],
        compiler_params=params(),
        cost_estimate=cost(0.02),
        name="pack",
    )(spot, *operands)


def one_hot_rows(row, cap):
    slots = iota((cap, row.shape[1]), 0).astype(f32)
    return jnp.where(slots == row, 1.0, 0.0).astype(bf16)


def one_hot_cols(column, cap):
    slots = iota((column.shape[0], cap), 1).astype(f32)
    return jnp.where(slots == column, 1.0, 0.0).astype(bf16)


def route_kernel(place_ref, ids_ref, up_ref, post_ref, pos_ref, *rest, cap, stride):
    outs, gathered = rest[:-1], rest[-1]
    experts = post_ref.shape[0]
    images, seq, width = up_ref.shape
    step = pl.program_id(0)

    @pl.when(step == 0)
    def _():
        expert = relative_expert(place_ref[0], iota((experts, stride), 0), experts)
        before = jnp.where(iota((stride, stride), 0) < iota((stride, stride), 1), 1.0, 0.0).astype(bf16)
        carry = jnp.zeros((experts, 1), f32)
        gathered[...] = jnp.zeros_like(gathered)
        for image in range(images):
            ids = ids_ref[:, image * stride : (image + 1) * stride]
            hit = jnp.zeros((experts, stride), jnp.bool_)
            for choice in range(ids_ref.shape[0]):
                hit = hit | (ids[choice : choice + 1] == expert)
            mask = jnp.where(hit, 1.0, 0.0)
            rank = carry + dot(mask.astype(bf16), before, NN)
            carry = carry + jnp.sum(mask, axis=1, keepdims=True)
            slot = jnp.where(hit, rank, -1.0)
            post_ref[:, image * stride : (image + 1) * stride] = slot
            padded = jnp.concatenate([slot, jnp.full((LANES - experts, stride), -1.0, f32)], axis=0)
            pos_ref[image] = padded.T
            gathered[image * stride : image * stride + seq] = up_ref[image]

    hot = one_hot_rows(post_ref[pl.ds(step, 1), :], cap)
    made = dot(hot, gathered[...], NN).astype(bf16)
    for index in range(experts):

        @pl.when(step == index)
        def _():
            outs[index][...] = made


def route(place, ids, grad_output, experts, cap, stride):
    images, seq, width = grad_output.shape
    total = images * stride
    return pl.pallas_call(
        functools.partial(route_kernel, cap=cap, stride=stride),
        grid=(experts,),
        in_specs=[pl.BlockSpec(memory_space=pltpu.SMEM), whole(ids.shape), whole(grad_output.shape)],
        out_specs=[whole((experts, total)), whole((images, stride, LANES))] + [whole((cap, width))] * experts,
        out_shape=[
            jax.ShapeDtypeStruct((experts, total), f32),
            jax.ShapeDtypeStruct((images, stride, LANES), f32),
        ]
        + [jax.ShapeDtypeStruct((cap, width), bf16)] * experts,
        scratch_shapes=[pltpu.VMEM((total, width), bf16)],
        compiler_params=params(),
        cost_estimate=cost(0.02),
        name="route",
    )(place, ids, grad_output)


def dispatch_kernel(post_ref, rows_ref, *outs, cap):
    step = pl.program_id(0)
    hot = one_hot_rows(post_ref[pl.ds(step, 1), :], cap)
    sent = dot(hot, rows_ref[...], NN).astype(bf16)
    for index in range(len(outs)):

        @pl.when(step == index)
        def _():
            outs[index][...] = sent


def dispatch_after_kernel(post_ref, rows_ref, *rest, cap, skip):
    dispatch_kernel(post_ref, rows_ref, *rest[skip:], cap=cap)


def dispatch(post, rows, after, experts, cap):
    width = rows.shape[1]
    return pl.pallas_call(
        functools.partial(dispatch_after_kernel, cap=cap, skip=len(after)),
        grid=(experts,),
        in_specs=[whole(post.shape), whole(rows.shape)] + [pl.BlockSpec(memory_space=pl.ANY)] * len(after),
        out_specs=[whole((cap, width))] * experts,
        out_shape=[jax.ShapeDtypeStruct((cap, width), bf16)] * experts,
        compiler_params=params(),
        cost_estimate=cost(32),
        name="dispatch",
    )(post, rows, *after)


def forward_kernel(spots_ref, tok_ref, *rest, experts, fsdp, later):
    if later:
        pack_ref, old_peak_ref = rest[:2]
        rest = rest[-10:]
    else:
        shards_of, pack_ref = rest[:fsdp], rest[-4]
        rest = rest[-11:-4] + rest[-3:]
    qkv_ref, mixed_ref, hidden_ref, prob_ref, attn_ref, mid_ref, peak_ref, tokens, vectors, router = rest
    _, seq, width = tok_ref.shape
    rows = tokens.shape[0]
    head = width // HEADS
    step = pl.program_id(0)
    wide = 3 * width

    @pl.when(step == 0)
    def _():
        if not later:
            part = shards_of[0].shape[0]
            for index, ref in enumerate(shards_of):
                pack_ref[pl.ds(pl.multiple_of(spots_ref[1 + index] * part, part), part), :] = ref[...]
        misc = pack_ref[:, wide + width :]
        vectors[...] = misc.astype(f32).T
        router[...] = dot(misc, router_order(spots_ref[0], experts), NN).astype(bf16)
        tokens[...] = jnp.zeros_like(tokens)
        peak_ref[...] = old_peak_ref[...] if later else jnp.full_like(peak_ref, NEG)

    def vector(index):
        return vectors[VEC + index : VEC + index + 1, :]

    tokens[0:seq] = tok_ref[0].astype(f32)
    residual = tokens[...]
    hat, _ = norm_stats(residual)
    normed = (hat * vector(0) + vector(1)).astype(bf16)
    projected = dot(normed, pack_ref[:, 0:wide], NN)
    qkv_ref[0, :, 0:width] = ((projected[:, 0:width] + vector(2)).astype(bf16).astype(f32) * head**-0.5).astype(
        bf16
    )
    qkv_ref[0, :, width : 2 * width] = projected[:, width : 2 * width].astype(bf16)
    qkv_ref[0, :, 2 * width :] = (projected[:, 2 * width :] + vector(3)).astype(bf16)
    lane = iota((1, LANES), 1)
    first = lane < head
    halves = (jnp.where(first, 1.0, 0.0).astype(bf16), jnp.where(first, 0.0, 1.0).astype(bf16))
    keys = jnp.where(iota((1, rows), 1) < seq, 0.0, NEG)
    valid = iota((rows, 1), 0) < seq

    def pair(index, peak):
        at = pl.multiple_of(index * LANES, LANES)
        query = qkv_ref[0, :, pl.ds(at, LANES)]
        key = qkv_ref[0, :, pl.ds(width + at, LANES)]
        value = qkv_ref[0, :, pl.ds(2 * width + at, LANES)]
        parts = []
        for half in range(2):
            scores = dot(query * halves[half], key, NT) + keys
            top = jnp.max(scores, axis=1, keepdims=True)
            weight = jnp.exp(scores - top)
            total = jnp.sum(weight, axis=1, keepdims=True)
            number = index * 2 + half
            largest = jnp.max(jnp.where(valid, top, NEG), axis=0, keepdims=True)
            peak = jnp.where(lane == number, largest, peak)
            low = (weight * (1.0 / total)).astype(bf16)
            attn_ref[0, number] = low
            parts.append(dot(low, value, NN))
        mixed_ref[0, :, pl.ds(at, LANES)] = jnp.where(first, parts[0], parts[1]).astype(bf16)
        return peak

    peak = lax.fori_loop(0, HEADS // 2, pair, jnp.full((1, LANES), NEG, f32))
    peak_ref[...] = jnp.maximum(peak_ref[...], peak)
    hidden = residual + dot(mixed_ref[0], pack_ref[:, wide : wide + width], NN) + vector(4)
    hidden_ref[0] = hidden
    hat, _ = norm_stats(hidden)
    mid = hat * vector(5) + vector(6)
    logits = jnp.zeros((rows, LANES), f32)
    for part in pieces(mid, 3):
        logits = logits + dot(part, router[...], NN)
    prob_ref[0] = softmax_lanes(logits, experts)
    mid_ref[0, 0:rows] = mid.astype(bf16)
    mid_ref[0, rows:] = jnp.zeros((mid_ref.shape[1] - rows, width), bf16)


def forward(spots, tokens, shards_of, old, after, at, count, experts, stride, rows):
    images, seq, width = tokens.shape
    later = old is not None
    far = pl.BlockSpec(memory_space=pl.ANY)
    shapes = [
        ((1, rows, 3 * width), bf16),
        ((1, rows, width), bf16),
        ((1, rows, width), f32),
        ((1, rows, LANES), f32),
        ((1, HEADS, rows, rows), bf16),
        ((1, stride, width), bf16),
    ]

    def image(shape):
        return pl.BlockSpec(shape, lambda i: (at + i,) + (0,) * (len(shape) - 1))

    out_specs = [image(shape) for shape, _ in shapes] + [whole((1, LANES))]
    out_shape = [jax.ShapeDtypeStruct((images,) + shape[1:], kind) for shape, kind in shapes]
    out_shape.append(jax.ShapeDtypeStruct((1, LANES), f32))
    operands = [spots, tokens]
    in_specs = [pl.BlockSpec(memory_space=pltpu.SMEM), image((1, seq, width))]
    if later:
        *arrays, peak, pack = old
        aliases = {len(operands) + 2 + index: index for index in range(len(arrays))}
        operands += [pack, peak, *arrays]
        in_specs += [whole(pack.shape), whole(peak.shape)] + [far] * len(arrays)
    else:
        aliases = {}
        packed = (width, shards_of[0].shape[1])
        operands += shards_of
        in_specs += [whole(v.shape) for v in shards_of]
        out_specs.append(whole(packed))
        out_shape.append(jax.ShapeDtypeStruct(packed, bf16))
    outputs = pl.pallas_call(
        functools.partial(forward_kernel, experts=experts, fsdp=len(shards_of), later=later),
        grid=(count,),
        in_specs=in_specs + [far] * len(after),
        out_specs=out_specs,
        out_shape=out_shape,
        scratch_shapes=[
            pltpu.VMEM((rows, width), f32),
            pltpu.VMEM((LANES, width), f32),
            pltpu.VMEM((width, LANES), bf16),
        ],
        input_output_aliases=aliases,
        compiler_params=params(),
        cost_estimate=cost(20 * count if later else 0.02),
        name="attend",
    )(*operands, *after)
    return [*outputs, pack] if later else outputs


def expert_kernel(place_ref, *refs, cap, group, first, last, experts, fsdp, split, skip):
    taken = iter(refs)

    def take(number):
        return [next(taken) for _ in range(number)]

    count = len(group)
    rows_in, ups_in = take(count), take(count)
    pays, misc = take(fsdp), next(taken)
    old = [] if first else take(3)
    take(skip)
    row_back, made_ref = take(count), next(taken)
    out1, out2, *out3 = take(4 if split else 2) if split or not last else (None, next(taken))
    rows, ups, gates, acc_row, acc_out, shift2, bias2, gated, sems, w1s, w2s, sems_w = take(12)
    step = pl.program_id(0)
    width = rows.shape[1]
    tile = w1s.shape[2]
    tall = tile + TAIL
    chunk = width // fsdp

    @pl.when(step == 0)
    def _():
        loads = []
        for index, ref in enumerate(pays):
            at = place_ref[2 + index]
            loads.append(pltpu.make_async_copy(ref.at[0:tall], w2s.at[at], sems_w.at[index, fsdp]))
            for block in range(fsdp):
                start = tall + block * chunk
                loads.append(
                    pltpu.make_async_copy(
                        ref.at[start : start + chunk, 0:tile],
                        w1s.at[block, pl.ds(pl.multiple_of(at * chunk, chunk), chunk)],
                        sems_w.at[index, block],
                    )
                )
        for load in loads:
            load.start()
        for index in range(count):
            rows[index * cap : (index + 1) * cap] = rows_in[index][...]
        router = dot(misc[...], router_order(place_ref[0], experts), NN).astype(bf16)
        gate = softmax_lanes(dot(rows[...], router, NN), experts)[:, 0:1]
        gates[...] = jnp.broadcast_to(gate, gates.shape)
        for index in range(count):
            part = slice(index * cap, (index + 1) * cap)
            ups[part] = (ups_in[index][...].astype(f32) * gate[part]).astype(bf16)
        acc_row[...] = jnp.zeros_like(acc_row)
        acc_out[...] = jnp.zeros_like(acc_out)
        bias2[...] = jnp.zeros_like(bias2)
        shift2[...] = jnp.sum(ups[...].astype(f32), axis=0, keepdims=True)
        for load in loads:
            load.wait()

    w1, w2 = w1s.at[step], w2s.at[step]
    tail = w2[tile:tall].astype(f32)
    bias2[...] += tail[1:2]
    x, up = rows[...], ups[...]
    value, slope = gelu_pair(dot(x, w1[...], NN) + tail[0:1, 0:tile])
    act = value.astype(bf16)
    acc_out[...] += dot(act, w2[0:tile], NN)
    raw = slope * dot(up, w2[0:tile], NT)
    pre = raw.astype(bf16)
    acc_row[...] += dot(pre, w1[...], NT)
    part1 = dot(x, pre, TN)
    part2 = dot(act, up, TN)
    shift1 = jnp.sum(pre.astype(f32), axis=0, keepdims=True)
    if tile < width:
        shift1 = jnp.concatenate([shift1, jnp.zeros((1, width - tile), f32)], axis=1)
    place = iota((TAIL, width), 0)
    sums = jnp.where(place == 0, shift1, jnp.where(place == 1, shift2[...], 0.0))
    if not first:
        part1, part2, sums = old[1][...] + part1, old[2][0, 0:tile] + part2, old[2][0, tile:] + sums
    if last:
        if tile < width:
            part1 = jnp.concatenate([part1, jnp.zeros((width, width - tile), f32)], axis=1)
        if split:
            for ref, fy in ((out1, place_ref[1]), (out2, 1 - place_ref[1])):

                @pl.when((step >> 1) == fy)
                def _():
                    ref[step & 1, 0:tile] = part2.astype(bf16)
                    ref[step & 1, tile:tall] = sums.astype(bf16)

            at = pl.multiple_of(step * chunk, TAIL)
            for index in range(fsdp):
                block = part1[index * chunk : (index + 1) * chunk].astype(bf16)
                for ref, fy in ((out3[0], place_ref[1]), (out3[1], 1 - place_ref[1])):

                    @pl.when(index // 2 == fy)
                    def _():
                        ref[index % 2, pl.ds(at, chunk), :] = block

        else:
            at = pl.multiple_of(tall + step * chunk, TAIL)
            out2[step, 0:tile] = part2.astype(bf16)
            out2[step, tile:tall] = sums.astype(bf16)
            for index in range(fsdp):
                out2[index, pl.ds(at, chunk), :] = part1[index * chunk : (index + 1) * chunk].astype(bf16)
    else:
        out1[...] = part1
        out2[0, 0:tile] = part2
        out2[0, tile:] = sums

    @pl.when(step == pl.num_programs(0) - 1)
    def _():
        copies = []
        for index, shift in enumerate(group):
            part = slice(index * cap, (index + 1) * cap)
            made = acc_out[part] + bias2[...]
            gate = gates[part, 0:1]
            gated[index] = (made * gate).astype(bf16)
            copies.append(
                pltpu.make_async_copy(gated.at[index], made_ref.at[place_ref[0] ^ shift], sems.at[index])
            )
            copies[-1].start()
            row_back[index][0:cap] = acc_row[part].astype(bf16)
            effect = jnp.sum(made * ups_in[index][...].astype(f32), axis=1, keepdims=True) * gate
            effect = jnp.concatenate([effect, jnp.zeros((width - cap, 1), f32)], axis=0)
            line = jnp.broadcast_to(effect, (width, LANES)).T[0:1]
            end = jnp.zeros((TAIL, width), f32)
            for order, piece in enumerate(pieces(line, 3)):
                end = jnp.where(place == order, piece.astype(f32), end)
            row_back[index][cap : cap + TAIL] = end.astype(bf16)
        for copy in copies:
            copy.wait()


def expert_call(spots, rows, ups, pays, pack, old, after, group, cap, experts, last):
    count = len(group)
    first = old is None
    fsdp = len(pays)
    high, width = pays[0].shape
    tall = high - width
    tile = tall - TAIL
    total = count * cap
    split = last and fsdp == 4
    column = pl.BlockSpec((width, tile), lambda h, _: (0, h))
    line = pl.BlockSpec((1, tall, width), lambda h, _: (h, 0, 0))
    far = pl.BlockSpec(memory_space=pl.ANY)
    if split:
        grads = [(2, tall, width)] * 2 + [(2, width, width)] * 2
    else:
        grads = [(fsdp, high, width)]

    operands = [spots, *rows, *ups, *pays, pack]
    aliases = {}
    if not first:
        aliases = {len(operands): count}
        operands += list(old)
    return pl.pallas_call(
        functools.partial(
            expert_kernel,
            cap=cap,
            group=group,
            first=first,
            last=last,
            experts=experts,
            fsdp=fsdp,
            split=split,
            skip=len(after),
        ),
        grid_spec=pltpu.PrefetchScalarGridSpec(
            num_scalar_prefetch=1,
            grid=(fsdp,),
            in_specs=[whole((cap, width))] * (2 * count)
            + [far] * fsdp
            + [pl.BlockSpec((width, LANES), lambda h, _: (0, 4 * width // LANES))]
            + ([] if first else [far, column, line])
            + [far] * len(after),
            out_specs=[whole((cap + TAIL, width))] * count
            + [far]
            + ([whole(v) for v in grads] if last else [column, line]),
            scratch_shapes=[pltpu.VMEM((total, width), bf16)] * 2
            + [pltpu.VMEM((total, LANES), f32)]
            + [pltpu.VMEM((total, width), f32)] * 2
            + [pltpu.VMEM((1, width), f32)] * 2
            + [pltpu.VMEM((count, cap, width), bf16), pltpu.SemaphoreType.DMA((count,))]
            + [pltpu.VMEM((fsdp, width, tile), bf16), pltpu.VMEM((fsdp, tall, width), bf16)]
            + [pltpu.SemaphoreType.DMA((fsdp, fsdp + 1))],
        ),
        out_shape=[jax.ShapeDtypeStruct((cap + TAIL, width), bf16)] * count
        + [jax.ShapeDtypeStruct((experts, cap, width), bf16)]
        + (
            [jax.ShapeDtypeStruct(v, bf16) for v in grads]
            if last
            else [
                jax.ShapeDtypeStruct((width, tile * fsdp), f32),
                jax.ShapeDtypeStruct((fsdp, tall, width), f32),
            ]
        ),
        input_output_aliases=aliases,
        compiler_params=params(),
        cost_estimate=cost(96),
        name="expert",
    )(*operands, *after)


def middle_kernel(
    place_ref, up_ref, wout_ref, misc_ref, pos_ref, mixed_ref, hidden_ref, prob_ref, *rest, cap, experts
):
    backs = rest[:experts]
    hidden_grad_ref, mixed_grad_ref, sums_ref, padded, vectors, router, shifts, acc_out, acc_router = rest[-9:]
    _, seq, width = up_ref.shape
    rows = padded.shape[0]
    step = pl.program_id(0)

    @pl.when(step == 0)
    def _():
        vectors[...] = misc_ref[...].astype(f32).T
        router[...] = dot(misc_ref[...], router_order(place_ref[0], experts), NN).astype(bf16)
        padded[...] = jnp.zeros_like(padded)
        shifts[...] = jnp.zeros_like(shifts)
        acc_out[...] = jnp.zeros_like(acc_out)
        acc_router[...] = jnp.zeros_like(acc_router)

    def vector(index):
        return vectors[VEC + index : VEC + index + 1, :]

    def shift(index, value):
        shifts[index : index + 1, :] += jnp.sum(value, axis=0, keepdims=True)

    lane = iota((1, LANES), 1)
    places = pos_ref[0, 0:rows, :]
    slot_sum = jnp.zeros((rows, width), f32)
    effect = jnp.zeros((rows, LANES), f32)
    for index in range(experts):
        hot = one_hot_cols(places[:, index : index + 1], cap)
        slot_sum = slot_sum + dot(hot, backs[index][0:cap], NN)
        parts = dot(hot, backs[index][cap : cap + TAIL, 0:cap], NT)
        effect = jnp.where(lane == index, jnp.sum(parts, axis=1, keepdims=True), effect)
    prob = prob_ref[0]
    logit_grad = effect - prob * jnp.sum(effect, axis=1, keepdims=True)
    logit_parts = pieces(logit_grad, 2)
    mid_grad = slot_sum
    for part in logit_parts:
        mid_grad = mid_grad + dot(part, router[...], NT)
    padded[0:seq] = up_ref[0].astype(f32)
    hat, inverse = norm_stats(hidden_ref[0])
    mid_parts = pieces(hat * vector(5) + vector(6), 2)
    acc_router[...] += (
        dot(logit_parts[0], mid_parts[0], TN)
        + dot(logit_parts[0], mid_parts[1], TN)
        + dot(logit_parts[1], mid_parts[0], TN)
    )
    shift(5, mid_grad * hat)
    shift(6, mid_grad)
    hidden_grad = padded[...] + norm_back(mid_grad, vector(5), hat, inverse)
    hidden_grad_ref[0] = hidden_grad
    branch = hidden_grad.astype(bf16)
    shift(4, branch.astype(f32))
    acc_out[...] += dot(mixed_ref[0], branch, TN)
    mixed_grad_ref[0] = dot(branch, wout_ref[...], NT).astype(bf16)

    @pl.when(step == pl.num_programs(0) - 1)
    def _():
        sums_ref[:, 0:width] = acc_out[...]
        ordered = dot(router_order(place_ref[0], experts), acc_router[...].astype(bf16), NN)
        spare = jnp.concatenate(
            [ordered[0:VEC], shifts[...], jnp.zeros((LANES - VEC - shifts.shape[0], width), f32)], axis=0
        )
        sums_ref[:, width:] = spare.T


def middle(place, grad_output, pack, pos, saved, backs, after, cap, experts):
    images, seq, width = grad_output.shape
    _, mixed, hidden, prob, _ = saved
    rows = mixed.shape[1]

    def image(shape):
        return pl.BlockSpec((1,) + shape, lambda i: (i, 0, 0))

    return pl.pallas_call(
        functools.partial(middle_kernel, cap=cap, experts=experts),
        grid=(images,),
        in_specs=[
            pl.BlockSpec(memory_space=pltpu.SMEM),
            image((seq, width)),
            pl.BlockSpec((width, width), lambda i: (0, 3)),
            pl.BlockSpec((width, LANES), lambda i: (0, 4 * width // LANES)),
            image((pos.shape[1], LANES)),
            image((rows, width)),
            image((rows, width)),
            image((rows, LANES)),
        ]
        + [whole((cap + TAIL, width))] * experts
        + [pl.BlockSpec(memory_space=pl.ANY)] * len(after),
        out_specs=[image((rows, width)), image((rows, width)), whole((width, width + LANES))],
        out_shape=[
            jax.ShapeDtypeStruct((images, rows, width), f32),
            jax.ShapeDtypeStruct((images, rows, width), bf16),
            jax.ShapeDtypeStruct((width, width + LANES), f32),
        ],
        scratch_shapes=[
            pltpu.VMEM((rows, width), f32),
            pltpu.VMEM((LANES, width), f32),
            pltpu.VMEM((width, LANES), bf16),
            pltpu.VMEM((8, width), f32),
            pltpu.VMEM((width, width), f32),
            pltpu.VMEM((LANES, width), f32),
        ],
        compiler_params=params(),
        cost_estimate=cost(0.02),
        name="middle",
    )(place, grad_output, pack, pack, pos, mixed, hidden, prob, *backs, *after)


def backward_kernel(
    spots_ref, tok_ref, qkv_ref, attn_ref, mixed_grad_ref, *rest, head_rows, members
):
    sums_ref, peak_ref = rest[:2]
    qkv_grad_ref, keep_ref, give_ref, padded, acc_qkv, columns, spare, misc = rest[-8:]
    _, seq, width = tok_ref.shape
    rows = padded.shape[0]
    head = width // HEADS
    wide = 3 * width
    step = pl.program_id(0)

    @pl.when(step == 0)
    def _():
        padded[...] = jnp.zeros_like(padded)
        acc_qkv[...] = jnp.zeros_like(acc_qkv)
        columns[...] = jnp.zeros_like(columns)

    lane = iota((1, LANES), 1)
    first = lane < head
    halves = (jnp.where(first, 1.0, 0.0).astype(bf16), jnp.where(first, 0.0, 1.0).astype(bf16))

    def pair(index, carry):
        at = pl.multiple_of(index * LANES, LANES)
        query = qkv_ref[0, :, pl.ds(at, LANES)]
        key = qkv_ref[0, :, pl.ds(width + at, LANES)]
        value = qkv_ref[0, :, pl.ds(2 * width + at, LANES)]
        up = mixed_grad_ref[0, :, pl.ds(at, LANES)]
        made = []
        for half in range(2):
            low = attn_ref[0, index * 2 + half]
            weight = low.astype(f32)
            value_grad = dot(low, up, TN)
            spread = weight * dot(up * halves[half], value, NT)
            score_grad = (spread - weight * jnp.sum(spread, axis=1, keepdims=True)).astype(bf16)
            made.append((dot(score_grad, key, NN) * head**-0.5, dot(score_grad, query, TN), value_grad))
        for index_of, (left, right) in enumerate(zip(*made)):
            qkv_grad_ref[0, :, pl.ds(index_of * width + at, LANES)] = jnp.where(first, left, right).astype(bf16)
        return carry

    lax.fori_loop(0, HEADS // 2, pair, 0)
    columns[...] += jnp.sum(qkv_grad_ref[0].astype(f32), axis=0, keepdims=True)
    padded[0:seq] = tok_ref[0].astype(f32)
    hat, _ = norm_stats(padded[...])
    acc_qkv[...] += dot(hat.astype(bf16), qkv_grad_ref[0], TN)
    part = keep_ref.shape[1]

    @pl.when(step == pl.num_programs(0) - 1)
    def _():
        line = iota((LANES, width), 0)
        flat = columns[...]
        grown = jnp.where(line == VEC + 2, flat[:, 0:width], 0.0)
        grown = jnp.where(line == VEC + 3, flat[:, 2 * width :], grown)
        misc[...] = sums_ref[:, width:] + grown.T
        spare[...] = jnp.zeros_like(spare)
        number = wide // LANES
        for order, piece in enumerate(pieces(flat, 3)):
            value = piece.astype(f32)
            for index in range(number):
                at = order * number + index
                spare[at : at + 1, :] = value[:, index * LANES : (index + 1) * LANES]
        if members:
            top = jnp.where(lane < HEADS, peak_ref[...], 0.0)
            rows_of = jnp.zeros((TAIL, LANES), f32)
            for order, piece in enumerate(pieces(jnp.broadcast_to(top, (TAIL, LANES)), 3)):
                move = jnp.where(iota((LANES, LANES), 1) == iota((LANES, LANES), 0) + order * HEADS, 1.0, 0.0)
                rows_of = rows_of + dot(piece, move.astype(bf16), NN)
            spare[pl.ds(head_rows + spots_ref[1], 1), :] = rows_of[0:1]
        extra = spare[...].astype(bf16)
        for fy in range(keep_ref.shape[0]):
            for ref, core in ((keep_ref, spots_ref[0]), (give_ref, 1 - spots_ref[0])):
                at = pl.multiple_of((2 * fy + core) * part, part)
                ref[fy, :, 0:wide] = acc_qkv[pl.ds(at, part), :].astype(bf16)
                ref[fy, :, wide : wide + width] = sums_ref[pl.ds(at, part), 0:width].astype(bf16)
                ref[fy, :, wide + width : wide + width + LANES] = misc[pl.ds(at, part), :].astype(bf16)
                ref[fy, :, wide + width + LANES :] = extra


def backward(spots, tokens, saved, mixed_grad, sums, peak, after, ways, part, head_rows, members):
    images, seq, width = tokens.shape
    qkv, attn = saved[0], saved[-1]
    rows = qkv.shape[1]
    wide = 4 * width + 2 * LANES

    def image(shape):
        return pl.BlockSpec((1,) + shape, lambda i: (i,) + (0,) * len(shape))

    return pl.pallas_call(
        functools.partial(backward_kernel, head_rows=head_rows, members=members),
        grid=(images,),
        in_specs=[
            pl.BlockSpec(memory_space=pltpu.SMEM),
            image((seq, width)),
            image((rows, 3 * width)),
            image((HEADS, rows, rows)),
            image((rows, width)),
            whole(sums.shape),
            whole(peak.shape),
        ]
        + [pl.BlockSpec(memory_space=pl.ANY)] * len(after),
        out_specs=[image((rows, 3 * width)), whole((ways, part, wide)), whole((ways, part, wide))],
        out_shape=[
            jax.ShapeDtypeStruct((images, rows, 3 * width), bf16),
            jax.ShapeDtypeStruct((ways, part, wide), bf16),
            jax.ShapeDtypeStruct((ways, part, wide), bf16),
        ],
        scratch_shapes=[
            pltpu.VMEM((rows, width), f32),
            pltpu.VMEM((width, 3 * width), f32),
            pltpu.VMEM((1, 3 * width), f32),
            pltpu.VMEM((part, LANES), f32),
            pltpu.VMEM((width, LANES), f32),
        ],
        compiler_params=params(),
        cost_estimate=cost(0.05),
        name="attend_back",
    )(spots, tokens, qkv, attn, mixed_grad, sums, peak, *after)


def first_kernel(tok_ref, qkv_grad_ref, wqkv_ref, misc_ref, hidden_grad_ref, grad_ref, padded, gain):
    _, seq, width = tok_ref.shape

    @pl.when(pl.program_id(0) == 0)
    def _():
        gain[...] = misc_ref[...].astype(f32).T[VEC : VEC + 1]
        padded[...] = jnp.zeros_like(padded)

    in_grad = dot(qkv_grad_ref[0], wqkv_ref[...], NT)
    padded[0:seq] = tok_ref[0].astype(f32)
    hat, inverse = norm_stats(padded[...])
    grad_ref[0] = (hidden_grad_ref[0] + norm_back(in_grad, gain[...], hat, inverse))[0:seq]


def first_norm(tokens, qkv_grad, pack, hidden_grad):
    images, seq, width = tokens.shape
    rows = qkv_grad.shape[1]

    def image(shape):
        return pl.BlockSpec((1,) + shape, lambda i: (i, 0, 0))

    return pl.pallas_call(
        first_kernel,
        grid=(images,),
        in_specs=[
            image((seq, width)),
            image((rows, 3 * width)),
            pl.BlockSpec((width, 3 * width), lambda i: (0, 0)),
            pl.BlockSpec((width, LANES), lambda i: (0, 4 * width // LANES)),
            image((rows, width)),
        ],
        out_specs=image((seq, width)),
        out_shape=jax.ShapeDtypeStruct((images, seq, width), f32),
        scratch_shapes=[pltpu.VMEM((rows, width), f32), pltpu.VMEM((1, width), f32)],
        compiler_params=params(),
        cost_estimate=cost(0.02),
        name="first_norm",
    )(tokens, qkv_grad, pack, pack, hidden_grad)


def output_kernel(place_ref, pos_ref, hidden_ref, made_ref, out_ref):
    experts, cap, _ = made_ref.shape
    seq = out_ref.shape[1]
    total = hidden_ref[0]
    places = pos_ref[0, 0 : total.shape[0], :]
    for index in range(experts):
        total = total + dot(one_hot_cols(places[:, index : index + 1], cap), made_ref[place_ref[0] ^ index], NN)
    out_ref[0] = total[0:seq].astype(bf16)


def combine_output(place, pos, hidden, made, seq):
    images, rows, width = hidden.shape

    def image(shape):
        return pl.BlockSpec((1,) + shape, lambda i: (i, 0, 0))

    return pl.pallas_call(
        output_kernel,
        grid=(images,),
        in_specs=[
            pl.BlockSpec(memory_space=pltpu.SMEM),
            image((pos.shape[1], LANES)),
            image((rows, width)),
            whole(made.shape),
        ],
        out_specs=image((seq, width)),
        out_shape=jax.ShapeDtypeStruct((images, seq, width), bf16),
        compiler_params=params(),
        cost_estimate=cost(0.02),
        name="combine",
    )(place, pos, hidden, made)


def finish_kernel(slot_ref, *refs, number, head_rows, members):
    parts, (own_ref, limit_ref, peak_ref) = refs[:number], refs[number : number + 3]
    qkv_ref, out_ref, misc_ref, vec_ref, clip_ref, total_ref = refs[number + 3 :]
    part = own_ref.shape[0]
    for shift, ref in enumerate(parts):
        size = part // number
        total_ref[pl.ds(pl.multiple_of((slot_ref[0] ^ shift) * size, size), size), :] = ref[...]
    width = out_ref.shape[1]
    wide = 3 * width
    number = wide // LANES
    base = total_ref[:, 0:wide].astype(f32)
    extra = total_ref[:, wide + width + LANES :].astype(f32)
    weight = own_ref[:, 0:wide].astype(f32)
    columns = [sum(extra[k * number + i : k * number + i + 1] for k in range(3)) for i in range(number)]
    columns = jnp.concatenate(columns, axis=1)
    own = own_ref[:, wide + width :].astype(f32)
    gain, bias = own[:, VEC : VEC + 1], own[:, VEC + 1 : VEC + 2]
    qkv_ref[...] = base * gain + bias * columns
    out_ref[...] = total_ref[:, wide : wide + width].astype(f32)
    misc = total_ref[:, wide + width : wide + width + LANES].astype(f32)
    lane = iota((1, LANES), 1)
    misc = jnp.where(lane == VEC, jnp.sum(base * weight, axis=1, keepdims=True), misc)
    misc = jnp.where(lane == VEC + 1, jnp.sum(columns * weight, axis=1, keepdims=True), misc)
    misc = misc.T
    vec_ref[...] = misc[VEC : VEC + 8]
    misc_ref[...] = misc[0 : misc_ref.shape[0]]
    if members:
        move = jnp.where(
            (iota((LANES, LANES), 0) % HEADS == iota((LANES, LANES), 1)) & (iota((LANES, LANES), 0) < 3 * HEADS),
            1.0,
            0.0,
        )
        peaks = dot(total_ref[head_rows : head_rows + members, wide + width + LANES :], move.astype(bf16), NN)
        peak = jnp.max(peaks, axis=0, keepdims=True)
    else:
        peak = peak_ref[...]
    limit = limit_ref[...]
    root = jnp.sqrt(limit / jnp.maximum(peak, limit))
    place = iota((1, width), 1) // (width // HEADS)
    scale = jnp.zeros((1, width), f32)
    for index in range(HEADS):
        scale = jnp.where(place == index, root[:, index : index + 1], scale)
    clip_ref[:, 0:width] = (weight[:, 0:width] * scale).astype(bf16)
    clip_ref[:, width : 2 * width] = (weight[:, width : 2 * width] * scale).astype(bf16)
    clip_ref[:, 2 * width :] = own_ref[:, 2 * width : wide]


def finish(slot, total, own, limit, peak, width, experts, head_rows, members):
    part = own.shape[0]
    operands = [*total, own, limit, peak]
    shapes = [(part, 3 * width), (part, width), (experts, part), (8, part), (part, 3 * width)]
    return pl.pallas_call(
        functools.partial(finish_kernel, number=len(total), head_rows=head_rows, members=members),
        grid=(1,),
        in_specs=[pl.BlockSpec(memory_space=pltpu.SMEM)] + [whole(v.shape) for v in operands],
        out_specs=[whole(v) for v in shapes],
        out_shape=[jax.ShapeDtypeStruct(v, bf16 if i == 4 else f32) for i, v in enumerate(shapes)],
        scratch_shapes=[pltpu.VMEM((part, total[0].shape[1]), bf16)],
        compiler_params=params(),
        cost_estimate=cost(0.02),
        name="finish",
    )(slot, *operands)


def half_sums_kernel(high_ref, keep_ref, got_ref, *rest):
    straight_ref, crossed_ref = rest[-2:]
    for ref, core in ((straight_ref, high_ref[0]), (crossed_ref, 1 - high_ref[0])):
        ref[...] = (keep_ref[core].astype(f32) + got_ref[core].astype(f32)).astype(bf16)


def half_sums(high, keep, got, after, micros):
    shape = keep.shape[1:]
    return pl.pallas_call(
        half_sums_kernel,
        grid=(1,),
        in_specs=[pl.BlockSpec(memory_space=pltpu.SMEM), whole(keep.shape), whole(got.shape)]
        + [pl.BlockSpec(memory_space=pl.ANY)] * len(after),
        out_specs=[whole(shape)] * 2,
        out_shape=[jax.ShapeDtypeStruct(shape, bf16)] * 2,
        compiler_params=params(),
        cost_estimate=cost(micros),
        name="half_sums",
    )(high, keep, got, *after)


def home_sums_kernel(spot_ref, one, two, three, four, _, w1_ref, w2_ref, b1_ref, b2_ref):
    tile, width = w2_ref.shape
    part = w1_ref.shape[0]
    w2_ref[...] = one[0:tile].astype(f32) + two[0:tile].astype(f32)
    edge = one[tile:].astype(f32) + two[tile:].astype(f32)
    b1_ref[...] = edge[0:1, 0:tile]
    b2_ref[...] = sum(
        jnp.where(spot_ref[0] == index, edge[1:2, index * part : (index + 1) * part], 0.0)
        for index in range(width // part)
    )
    for index in range(w1_ref.shape[1] // tile):
        rows = slice(index * part, (index + 1) * part)
        total = three[rows].astype(f32) + four[rows].astype(f32)
        w1_ref[:, index * tile : (index + 1) * tile] = total[:, 0:tile]


def home_sums(spot, second, first, after, tile, part, fsdp):
    width = second[0].shape[1]
    shapes = [(part, tile * fsdp), (tile, width), (1, tile), (1, part)]
    operands = [*second, *first]
    return pl.pallas_call(
        home_sums_kernel,
        grid=(1,),
        in_specs=[pl.BlockSpec(memory_space=pltpu.SMEM)]
        + [whole(v.shape) for v in operands]
        + [pl.BlockSpec(memory_space=pl.ANY)],
        out_specs=[whole(v) for v in shapes],
        out_shape=[jax.ShapeDtypeStruct(v, f32) for v in shapes],
        compiler_params=params(),
        cost_estimate=cost(0.02),
        name="home_sums",
    )(spot, *operands, after)


def add_halves_kernel(fy_ref, keep_ref, got_ref, *rest):
    mine_ref, theirs_ref = rest[-2:]
    for ref, half in ((mine_ref, fy_ref[0]), (theirs_ref, 1 - fy_ref[0])):
        ref[...] = (keep_ref[half].astype(f32) + got_ref[half].astype(f32)).astype(bf16)


def add_halves(fy, keep, got, after):
    shape = keep.shape[1:]
    return pl.pallas_call(
        add_halves_kernel,
        grid=(1,),
        in_specs=[pl.BlockSpec(memory_space=pltpu.SMEM), whole(keep.shape), whole(got.shape)]
        + [pl.BlockSpec(memory_space=pl.ANY)] * len(after),
        out_specs=[whole(shape)] * 2,
        out_shape=[jax.ShapeDtypeStruct(shape, bf16)] * 2,
        compiler_params=params(),
        cost_estimate=cost(0.02),
        name="add_halves",
    )(fy, keep, got, *after)


def split_rows_kernel(slot_ref, mine_ref, got_ref, *refs, skip):
    outs, total = refs[skip:-1], refs[-1]
    total[...] = (mine_ref[...].astype(f32) + got_ref[...].astype(f32)).astype(bf16)
    size = outs[0].shape[0]
    for shift, ref in enumerate(outs):
        ref[...] = total[pl.ds(pl.multiple_of((slot_ref[0] ^ shift) * size, size), size), :]


def split_rows(slot, mine, got, after, number):
    part, wide = mine.shape
    shape = (part // number, wide)
    return pl.pallas_call(
        functools.partial(split_rows_kernel, skip=len(after)),
        grid=(1,),
        in_specs=[pl.BlockSpec(memory_space=pltpu.SMEM), whole(mine.shape), whole(got.shape)]
        + [pl.BlockSpec(memory_space=pl.ANY)] * len(after),
        out_specs=[whole(shape)] * number,
        out_shape=[jax.ShapeDtypeStruct(shape, bf16)] * number,
        scratch_shapes=[pltpu.VMEM((part, wide), bf16)],
        compiler_params=params(),
        cost_estimate=cost(0.02),
        name="split_rows",
    )(slot, mine, got, *after)


def add_parts_kernel(*refs):
    parts, out_ref = refs[:-1], refs[-1]
    out_ref[...] = sum(ref[...].astype(f32) for ref in parts).astype(bf16)


def add_parts(parts):
    shape = parts[0].shape
    return pl.pallas_call(
        add_parts_kernel,
        grid=(1,),
        in_specs=[whole(shape)] * len(parts),
        out_specs=whole(shape),
        out_shape=jax.ShapeDtypeStruct(shape, bf16),
        compiler_params=params(),
        cost_estimate=cost(0.02),
        name="add_parts",
    )(*parts)


def swap(value, axis):
    return lax.ppermute(value, axis, [(0, 1), (1, 0)])


def around(value, axis, size):
    return [value] + [
        lax.ppermute(value, axis, [((k + step) % size, k) for k in range(size)]) for step in range(1, size)
    ]


def split_sum(value, axis, size):
    if size != 2:
        return lax.psum_scatter(value, axis, scatter_dimension=0, tiled=False)
    place = lax.axis_index(axis)
    sent = lax.dynamic_index_in_dim(value, 1 - place, 0, keepdims=False)
    kept = lax.dynamic_index_in_dim(value, place, 0, keepdims=False)
    return (kept.astype(f32) + swap(sent, axis).astype(f32)).astype(value.dtype)


def exchange(value, shift, experts):
    return lax.ppermute(value, GROUP, [(k, k ^ shift) for k in range(experts)])


def shift_order(experts):
    def key(shift):
        distance = bin(shift >> 1).count("1")
        return (distance == 0, distance == 1 and shift & 1, distance, shift)

    return sorted(range(experts), key=key)


STRAIGHT = [(0, 0), (1, 2), (2, 1), (3, 3)]
CROSSED = [(0, 2), (1, 0), (2, 3), (3, 1)]
BACK = [(b, a) for a, b in STRAIGHT]
BACK_CROSSED = [(b, a) for a, b in CROSSED]


def shards(
    tokens,
    ln1_gain,
    ln1_bias,
    w_qkv,
    q_bias,
    v_bias,
    w_out,
    out_bias,
    ln2_gain,
    ln2_bias,
    w_router,
    expert_w1,
    expert_b1,
    expert_w2,
    expert_b2,
    route_ids,
    clip_threshold,
    grad_output,
    *,
    experts,
    fsdp,
):
    images, seq, width = tokens.shape
    token_count = images * seq
    ways = fsdp // 2
    cap = (7 * token_count // (2 * experts) + 7) // 8 * 8
    stride = -(-seq // 256) * 256
    rows = -(-seq // 16) * 16
    part = w_qkv.shape[0]
    hidden_part = expert_w2.shape[1]
    high, low, fy, core = (lax.axis_index(name).astype(i32) for name in DEVICE)
    place_ref = (low * 2 + core).reshape(1)
    spot = fy * 2 + core

    vectors = (ln1_gain, ln1_bias, q_bias, v_bias, out_bias, ln2_gain, ln2_bias)
    own, pay = pack_parameters(
        spot.reshape(1), w_qkv, w_out, w_router, vectors, expert_w1[0], expert_w2[0], expert_b1, expert_b2
    )

    near = around(own, "fy", ways)
    far = [swap(own, "core")]
    straight = lax.ppermute(pay, ("hi", "core"), STRAIGHT)

    ids = jnp.pad(route_ids.reshape(images, seq, -1), ((0, 0), (0, stride - seq), (0, 0)), constant_values=-1)
    ids = ids.reshape(images * stride, -1).T
    post, pos, *ups = route(place_ref, ids, grad_output, experts, cap, stride)
    order = shift_order(experts)
    near[1:], post, ups[0] = lax.optimization_barrier((near[1:], post, ups[0]))
    ups = [value if shift == 0 else exchange(value, shift, experts) for shift, value in enumerate(ups)]
    far += [swap(value, "core") for value in near[1:]]
    homes = [((fy + step) % ways) * 2 for step in range(ways)]
    homes = [home + core for home in homes] + [home + 1 - core for home in homes]

    early = max(1, images * 2 // 5)
    spots = jnp.stack([place_ref[0], *homes])
    size = max(1, experts // 4)
    firsts = [ups[shift] for shift in order[:size]]
    begun = list(forward(spots, tokens, near + far, None, [], 0, early, experts, stride, rows))
    pay, straight, begun[0] = lax.optimization_barrier((pay, straight, begun[0]))
    crossed = lax.ppermute(pay, ("hi", "core"), CROSSED)
    pays = around(straight, "fy", ways)
    pay_homes = [((fy + step) % ways) * 2 + high for step in range(ways)]
    *saved, mid, peak, pack = forward(
        spots, tokens, [], begun, [straight, *firsts], early, images - early, experts, stride, rows
    )
    mid = mid.reshape(images * stride, width)
    crossed, mid = lax.optimization_barrier((crossed, mid))
    seconds = [ups[shift] for shift in order[size : 2 * size]]
    sent = dispatch(post, mid, [crossed, *pays[1:], *seconds], experts, cap)
    pays += around(crossed, "fy", ways)
    pay_homes += [((fy + step) % ways) * 2 + 1 - high for step in range(ways)]
    expert_spots = jnp.stack([place_ref[0], fy, *pay_homes])

    groups = [order[at : at + size] for at in range(0, experts, size)]
    arrived = {}

    def send(number, after):
        pending, after = lax.optimization_barrier(([sent[shift] for shift in groups[number]], after))
        for shift, value in zip(groups[number], pending):
            arrived[shift] = value if shift == 0 else exchange(value, shift, experts)
        return after

    send(0, ())
    send(1, [arrived[shift] for shift in groups[0]])
    old, after = None, []
    backs = {}
    for number, group in enumerate(groups):
        result = expert_call(
            expert_spots,
            [arrived[shift] for shift in group],
            [ups[shift] for shift in group],
            pays,
            pack,
            old,
            after,
            group,
            cap,
            experts,
            number == len(groups) - 1,
        )
        old = result[len(group) :]
        after = [backs[shift] for shift in groups[number - 1]] if number else []
        out = result[: len(group)]
        if number + 2 < len(groups):
            out = send(number + 2, out)
        for at, shift in enumerate(group):
            backs[shift] = out[at] if shift == 0 else exchange(out[at], shift, experts)
    backs = [backs[shift] for shift in range(experts)]
    made, *grad = old
    made, backs = lax.optimization_barrier((made, backs))
    made = lax.all_to_all(made, GROUP, split_axis=0, concat_axis=0, tiled=True)

    hidden_grad, mixed_grad, sums = middle(
        place_ref, grad_output, pack, pos, saved, backs, [], cap, experts
    )
    head_rows = 3 * (3 * width // LANES) + 4
    devices = 2 * experts // 2 * fsdp
    members = devices if head_rows + devices <= part else 0
    device = ((high * (experts // 2) + low) * ways + fy) * 2 + core
    spots = jnp.stack([core, device])
    def homeward(straight, crossed):
        return [
            lax.ppermute(straight, ("hi", "core"), BACK),
            lax.ppermute(crossed, ("hi", "core"), BACK_CROSSED),
        ]

    which = high.reshape(1)
    if len(grad) == 4:
        sums_two = list(half_sums(which, grad[0], swap(grad[1], "fy"), [sums], 0.02))
        home_two = homeward(*sums_two)
        grad[3], sums_two[0] = lax.optimization_barrier((grad[3], sums_two[0]))
        got_one = swap(grad[3], "fy")
    else:
        half = split_sum(grad[0].reshape((ways, 2) + grad[0].shape[1:]), "fy", ways)
        home = homeward(*(lax.dynamic_index_in_dim(half, k, 0, keepdims=False) for k in (high, 1 - high)))
        tall = hidden_part + TAIL
        home_two, home_one = [v[:tall] for v in home], [v[tall:] for v in home]
    qkv_grad, keep, give = backward(
        spots, tokens, saved, mixed_grad, sums, peak, [], ways, part, head_rows, members
    )

    got = swap(give, "core")
    after = []
    if len(grad) == 4:
        after = half_sums(which, grad[2], got_one, home_two, 40)
        home_one = homeward(*after)
    output = combine_output(place_ref, pos, saved[2], made, seq)
    near_by = experts // 2
    if ways == 2 and part % (TAIL * near_by) == 0:

        def spread(values):
            return [
                value if k == 0 else lax.ppermute(value, "lo", [(j, j ^ k) for j in range(near_by)])
                for k, value in enumerate(values)
            ]

        mine, theirs = add_halves(fy.reshape(1), keep, got, after)
        theirs, qkv_grad = lax.optimization_barrier((theirs, qkv_grad))
        input_grad = first_norm(tokens, qkv_grad, pack, hidden_grad)
        parts = split_rows(low.reshape(1), mine, swap(theirs, "fy"), [output, input_grad], near_by)
        total = add_parts(spread(parts))
        total = add_parts([total, swap(total, "hi")])
        total = spread([total] * near_by)
    else:
        sums = split_sum((keep.astype(f32) + got.astype(f32)).astype(bf16), "fy", ways)
        total = [lax.psum(sums, ("hi", "lo"))]
        input_grad = first_norm(tokens, qkv_grad, pack, hidden_grad)
    if not members:
        peak = jnp.max(lax.all_gather(peak, DEVICE, axis=0, tiled=True), axis=0, keepdims=True)
    limit = jnp.pad(clip_threshold.astype(f32).reshape(1, HEADS), ((0, 0), (0, LANES - HEADS)), constant_values=1.0)
    grad_qkv, grad_out, grad_router, grads, clipped = finish(
        low.reshape(1), total, own, limit, peak, width, experts, head_rows, members
    )
    grad_w1, grad_w2, grad_b1, grad_b2 = home_sums(
        spot.reshape(1), home_two, home_one, total[0], hidden_part, part, fsdp
    )
    return (
        output,
        input_grad,
        grads[0],
        grads[1],
        grad_qkv,
        grads[2],
        grads[3],
        grad_out,
        grads[4],
        grads[5],
        grads[6],
        grad_router.T,
        grad_w1[None],
        grad_b1,
        grad_w2[None],
        grad_b2,
        clipped,
    )


def solution(mesh):
    experts, fsdp = mesh.shape["expert"], mesh.shape["fsdp"]
    inner = Mesh(mesh.devices.reshape(2, experts // 2, fsdp // 2, 2), DEVICE)
    token, row, expert = P(DEVICE, None, None), ("fy", "core"), ("hi", "lo")
    vector, matrix = P(row), P(row, None)
    return jax.shard_map(
        functools.partial(shards, experts=experts, fsdp=fsdp),
        mesh=inner,
        in_specs=(
            token,
            vector,
            vector,
            matrix,
            vector,
            vector,
            matrix,
            vector,
            vector,
            vector,
            matrix,
            P(expert, row, None),
            P(expert, row),
            P(expert, row, None),
            P(expert, row),
            P(DEVICE, None),
            P(),
            token,
        ),
        out_specs=(
            token,
            token,
            vector,
            vector,
            matrix,
            vector,
            vector,
            matrix,
            vector,
            vector,
            vector,
            matrix,
            P(expert, row, None),
            P(expert, row),
            P(expert, row, None),
            P(expert, row),
            matrix,
        ),
        check_vma=False,
    )
```

```python
import functools

import jax
import jax.numpy as jnp
from jax import lax
from jax.experimental import pallas as pl
from jax.experimental.pallas import tpu as pltpu
from jax.sharding import Mesh
from jax.sharding import PartitionSpec as P

HEADS = 8
EPS = 1e-06
LANES = 128
VEC = 64
TAIL = 16
NEG = -1e30
f32 = jnp.float32
bf16 = jnp.bfloat16
i32 = jnp.int32
NN = (((1,), (0,)), ((), ()))
NT = (((1,), (1,)), ((), ()))
TN = (((0,), (0,)), ((), ()))
DEVICE = ("hi", "lo", "fy", "core")
GROUP = ("lo", "core")
VMEM_LIMIT = 63 << 20


def dot(a, b, dims):
    return lax.dot_general(a, b, dims, preferred_element_type=f32)


def pieces(value, count):
    parts = []
    for _ in range(count):
        part = value.astype(bf16)
        parts.append(part)
        value = value - part.astype(f32)
    return parts


def iota(shape, axis):
    return lax.broadcasted_iota(i32, shape, axis)


def relative_expert(place, shift, experts):
    other = jnp.bitwise_xor(place, shift)
    return (other & 1) * (experts // 2) + (other >> 1)


def router_order(place, experts):
    row, col = iota((LANES, LANES), 0), iota((LANES, LANES), 1)
    return jnp.where((row == relative_expert(place, col, experts)) & (col < experts), 1.0, 0.0).astype(bf16)


def norm_stats(matrix):
    centred = matrix - jnp.mean(matrix, axis=1, keepdims=True)
    inverse = lax.rsqrt(jnp.mean(centred * centred, axis=1, keepdims=True) + EPS)
    return centred * inverse, inverse


def norm_back(upstream, gain, hat, inverse):
    scaled = upstream * gain
    spread = (
        scaled
        - jnp.mean(scaled, axis=1, keepdims=True)
        - hat * jnp.mean(scaled * hat, axis=1, keepdims=True)
    )
    return spread * inverse


def softmax_lanes(logits, experts):
    logits = jnp.where(iota(logits.shape, 1) < experts, logits, NEG)
    top = jnp.max(logits, axis=1, keepdims=True)
    weight = jnp.exp(logits - top)
    return weight / jnp.sum(weight, axis=1, keepdims=True)


def gelu_pair(value):
    def low(number):
        return jnp.asarray(number, bf16)

    value = value.astype(bf16)
    bell = jnp.exp(value * value * low(-0.5))
    t = low(1.0) / (low(1.0) + jnp.abs(value) * low(0.3275911 * 0.7071067811865476))
    poly = low(0.7107068705) + t * (low(-0.7265760135) + t * low(0.5307027145))
    poly = t * (low(0.127414796) + t * (low(-0.142248368) + t * poly))
    lower = poly * bell
    phi = jnp.where(value >= low(0.0), low(1.0) - lower, lower)
    return value * phi, phi + value * (bell * low(0.3989422804014327))


def whole(shape):
    return pl.BlockSpec(shape, lambda *_: (0,) * len(shape))


def params(**extra):
    return pltpu.CompilerParams(vmem_limit_bytes=VMEM_LIMIT, **extra)


def cost(micros):
    return pl.CostEstimate(flops=int(micros * 1e9), bytes_accessed=0, transcendentals=0)


def pack_kernel(spot_ref, wqkv, wout, router, *rest):
    vectors, (w1, w2, b1, b2, pack_ref, pay_ref, spread, tail) = rest[:-8], rest[-8:]
    part, wide = wqkv.shape
    width, hidden = wout.shape[1], w2.shape[0]
    pack_ref[:, 0:wide] = wqkv[...]
    pack_ref[:, wide : wide + width] = wout[...]
    spread[...] = jnp.zeros_like(spread)
    spread[0 : router.shape[0], :] = router[...].astype(f32)
    for index, ref in enumerate(vectors):
        spread[VEC + index : VEC + index + 1, :] = ref[...].astype(f32)
    columns = spread[...].T
    pack_ref[:, wide + width :] = columns.astype(bf16)
    pay_ref[0:hidden] = w2[...]
    tail[...] = jnp.zeros_like(tail)
    tail[0:1, 0 : b1.shape[1]] = b1[...].astype(f32)
    copies = jnp.concatenate([b2[...].astype(f32)] * (width // part), axis=1)
    tail[1:2] = jnp.where(iota((1, width), 1) // part == spot_ref[0], copies, 0.0)
    tall = hidden + TAIL
    pay_ref[hidden:tall] = tail[...].astype(bf16)
    for index in range(width // part):
        block = w1[:, index * hidden : (index + 1) * hidden]
        if hidden < width:
            block = jnp.concatenate([block, jnp.zeros((part, width - hidden), bf16)], axis=1)
        pay_ref[tall + index * part : tall + (index + 1) * part] = block


def pack_parameters(spot, w_qkv, w_out, w_router, vectors, w1, w2, b1, b2):
    part, width = w_out.shape
    hidden = w2.shape[0]
    operands = [w_qkv, w_out, w_router.T, *[v.reshape(1, part) for v in vectors], w1, w2, b1, b2]
    return pl.pallas_call(
        pack_kernel,
        grid=(1,),
        in_specs=[pl.BlockSpec(memory_space=pltpu.SMEM)] + [whole(v.shape) for v in operands],
        out_specs=[whole((part, 4 * width + LANES)), whole((hidden + TAIL + width, width))],
        out_shape=[
            jax.ShapeDtypeStruct((part, 4 * width + LANES), bf16),
            jax.ShapeDtypeStruct((hidden + TAIL + width, width), bf16),
        ],
        scratch_shapes=[pltpu.VMEM((LANES, part), f32), pltpu.VMEM((TAIL, width), f32)],
        compiler_params=params(),
        cost_estimate=cost(0.02),
        name="pack",
    )(spot, *operands)


def one_hot_rows(row, cap):
    slots = iota((cap, row.shape[1]), 0).astype(f32)
    return jnp.where(slots == row, 1.0, 0.0).astype(bf16)


def one_hot_cols(column, cap):
    slots = iota((column.shape[0], cap), 1).astype(f32)
    return jnp.where(slots == column, 1.0, 0.0).astype(bf16)


def route_kernel(place_ref, ids_ref, up_ref, post_ref, pos_ref, *rest, cap, stride):
    outs, gathered = rest[:-1], rest[-1]
    experts = post_ref.shape[0]
    images, seq, width = up_ref.shape
    step = pl.program_id(0)

    @pl.when(step == 0)
    def _():
        expert = relative_expert(place_ref[0], iota((experts, stride), 0), experts)
        before = jnp.where(iota((stride, stride), 0) < iota((stride, stride), 1), 1.0, 0.0).astype(bf16)
        carry = jnp.zeros((experts, 1), f32)
        gathered[...] = jnp.zeros_like(gathered)
        for image in range(images):
            ids = ids_ref[:, image * stride : (image + 1) * stride]
            hit = jnp.zeros((experts, stride), jnp.bool_)
            for choice in range(ids_ref.shape[0]):
                hit = hit | (ids[choice : choice + 1] == expert)
            mask = jnp.where(hit, 1.0, 0.0)
            rank = carry + dot(mask.astype(bf16), before, NN)
            carry = carry + jnp.sum(mask, axis=1, keepdims=True)
            slot = jnp.where(hit, rank, -1.0)
            post_ref[:, image * stride : (image + 1) * stride] = slot
            padded = jnp.concatenate([slot, jnp.full((LANES - experts, stride), -1.0, f32)], axis=0)
            pos_ref[image] = padded.T
            gathered[image * stride : image * stride + seq] = up_ref[image]

    hot = one_hot_rows(post_ref[pl.ds(step, 1), :], cap)
    made = dot(hot, gathered[...], NN).astype(bf16)
    for index in range(experts):

        @pl.when(step == index)
        def _():
            outs[index][...] = made


def route(place, ids, grad_output, experts, cap, stride):
    images, seq, width = grad_output.shape
    total = images * stride
    return pl.pallas_call(
        functools.partial(route_kernel, cap=cap, stride=stride),
        grid=(experts,),
        in_specs=[pl.BlockSpec(memory_space=pltpu.SMEM), whole(ids.shape), whole(grad_output.shape)],
        out_specs=[whole((experts, total)), whole((images, stride, LANES))] + [whole((cap, width))] * experts,
        out_shape=[
            jax.ShapeDtypeStruct((experts, total), f32),
            jax.ShapeDtypeStruct((images, stride, LANES), f32),
        ]
        + [jax.ShapeDtypeStruct((cap, width), bf16)] * experts,
        scratch_shapes=[pltpu.VMEM((total, width), bf16)],
        compiler_params=params(),
        cost_estimate=cost(0.02),
        name="route",
    )(place, ids, grad_output)


def dispatch_kernel(post_ref, rows_ref, *refs, cap, paired, skip):
    ups, outs = refs[: len(paired)], refs[len(paired) + skip :]
    step = pl.program_id(0)
    hot = one_hot_rows(post_ref[pl.ds(step, 1), :], cap)
    sent = dot(hot, rows_ref[...], NN).astype(bf16)
    for index in range(len(outs)):

        @pl.when(step == index)
        def _():
            outs[index][0:cap] = sent
            if index in paired:
                outs[index][cap:] = ups[paired.index(index)][...]


def dispatch(post, rows, ups, paired, after, experts, cap):
    width = rows.shape[1]
    shapes = [((2 if shift in paired else 1) * cap, width) for shift in range(experts)]
    return list(
        pl.pallas_call(
            functools.partial(dispatch_kernel, cap=cap, paired=paired, skip=len(after)),
            grid=(experts,),
            in_specs=[whole(post.shape), whole(rows.shape)]
            + [whole((cap, width))] * len(paired)
            + [pl.BlockSpec(memory_space=pl.ANY)] * len(after),
            out_specs=[whole(v) for v in shapes],
            out_shape=[jax.ShapeDtypeStruct(v, bf16) for v in shapes],
            compiler_params=params(),
            cost_estimate=cost(0.02),
            name="dispatch",
        )(post, rows, *[ups[shift] for shift in paired], *after)
    )


def forward_kernel(spots_ref, tok_ref, *rest, experts, fsdp, later):
    if later:
        pack_ref, old_peak_ref = rest[:2]
        rest = rest[-10:]
    else:
        shards_of, pack_ref = rest[:fsdp], rest[-4]
        rest = rest[-11:-4] + rest[-3:]
    qkv_ref, mixed_ref, hidden_ref, prob_ref, attn_ref, mid_ref, peak_ref, tokens, vectors, router = rest
    _, seq, width = tok_ref.shape
    rows = tokens.shape[0]
    head = width // HEADS
    step = pl.program_id(0)
    wide = 3 * width

    @pl.when(step == 0)
    def _():
        if not later:
            part = shards_of[0].shape[0]
            for index, ref in enumerate(shards_of):
                pack_ref[pl.ds(pl.multiple_of(spots_ref[1 + index] * part, part), part), :] = ref[...]
        misc = pack_ref[:, wide + width :]
        vectors[...] = misc.astype(f32).T
        router[...] = dot(misc, router_order(spots_ref[0], experts), NN).astype(bf16)
        tokens[...] = jnp.zeros_like(tokens)
        peak_ref[...] = old_peak_ref[...] if later else jnp.full_like(peak_ref, NEG)

    def vector(index):
        return vectors[VEC + index : VEC + index + 1, :]

    tokens[0:seq] = tok_ref[0].astype(f32)
    residual = tokens[...]
    hat, _ = norm_stats(residual)
    normed = (hat * vector(0) + vector(1)).astype(bf16)
    projected = dot(normed, pack_ref[:, 0:wide], NN)
    qkv_ref[0, :, 0:width] = ((projected[:, 0:width] + vector(2)).astype(bf16).astype(f32) * head**-0.5).astype(
        bf16
    )
    qkv_ref[0, :, width : 2 * width] = projected[:, width : 2 * width].astype(bf16)
    qkv_ref[0, :, 2 * width :] = (projected[:, 2 * width :] + vector(3)).astype(bf16)
    lane = iota((1, LANES), 1)
    first = lane < head
    halves = (jnp.where(first, 1.0, 0.0).astype(bf16), jnp.where(first, 0.0, 1.0).astype(bf16))
    keys = jnp.where(iota((1, rows), 1) < seq, 0.0, NEG)
    valid = iota((rows, 1), 0) < seq

    def pair(index, peak):
        at = pl.multiple_of(index * LANES, LANES)
        query = qkv_ref[0, :, pl.ds(at, LANES)]
        key = qkv_ref[0, :, pl.ds(width + at, LANES)]
        value = qkv_ref[0, :, pl.ds(2 * width + at, LANES)]
        parts = []
        for half in range(2):
            scores = dot(query * halves[half], key, NT) + keys
            top = jnp.max(scores, axis=1, keepdims=True)
            weight = jnp.exp(scores - top)
            total = jnp.sum(weight, axis=1, keepdims=True)
            number = index * 2 + half
            largest = jnp.max(jnp.where(valid, top, NEG), axis=0, keepdims=True)
            peak = jnp.where(lane == number, largest, peak)
            low = (weight * (1.0 / total)).astype(bf16)
            attn_ref[0, number] = low
            parts.append(dot(low, value, NN))
        mixed_ref[0, :, pl.ds(at, LANES)] = jnp.where(first, parts[0], parts[1]).astype(bf16)
        return peak

    peak = lax.fori_loop(0, HEADS // 2, pair, jnp.full((1, LANES), NEG, f32), unroll=True)
    peak_ref[...] = jnp.maximum(peak_ref[...], peak)
    hidden = residual + dot(mixed_ref[0], pack_ref[:, wide : wide + width], NN) + vector(4)
    hidden_ref[0] = hidden
    hat, _ = norm_stats(hidden)
    mid = hat * vector(5) + vector(6)
    logits = jnp.zeros((rows, LANES), f32)
    for part in pieces(mid, 3):
        logits = logits + dot(part, router[...], NN)
    prob_ref[0] = softmax_lanes(logits, experts)
    mid_ref[0, 0:rows] = mid.astype(bf16)
    mid_ref[0, rows:] = jnp.zeros((mid_ref.shape[1] - rows, width), bf16)


def forward(spots, tokens, shards_of, old, after, at, count, experts, stride, rows):
    images, seq, width = tokens.shape
    later = old is not None
    far = pl.BlockSpec(memory_space=pl.ANY)
    shapes = [
        ((1, rows, 3 * width), bf16),
        ((1, rows, width), bf16),
        ((1, rows, width), f32),
        ((1, rows, LANES), f32),
        ((1, HEADS, rows, rows), bf16),
        ((1, stride, width), bf16),
    ]

    def image(shape):
        return pl.BlockSpec(shape, lambda i: (at + i,) + (0,) * (len(shape) - 1))

    out_specs = [image(shape) for shape, _ in shapes] + [whole((1, LANES))]
    out_shape = [jax.ShapeDtypeStruct((images,) + shape[1:], kind) for shape, kind in shapes]
    out_shape.append(jax.ShapeDtypeStruct((1, LANES), f32))
    operands = [spots, tokens]
    in_specs = [pl.BlockSpec(memory_space=pltpu.SMEM), image((1, seq, width))]
    if later:
        *arrays, peak, pack = old
        aliases = {len(operands) + 2 + index: index for index in range(len(arrays))}
        operands += [pack, peak, *arrays]
        in_specs += [whole(pack.shape), whole(peak.shape)] + [far] * len(arrays)
    else:
        aliases = {}
        packed = (width, shards_of[0].shape[1])
        operands += shards_of
        in_specs += [whole(v.shape) for v in shards_of]
        out_specs.append(whole(packed))
        out_shape.append(jax.ShapeDtypeStruct(packed, bf16))
    outputs = pl.pallas_call(
        functools.partial(forward_kernel, experts=experts, fsdp=len(shards_of), later=later),
        grid=(count,),
        in_specs=in_specs + [far] * len(after),
        out_specs=out_specs,
        out_shape=out_shape,
        scratch_shapes=[
            pltpu.VMEM((rows, width), f32),
            pltpu.VMEM((LANES, width), f32),
            pltpu.VMEM((width, LANES), bf16),
        ],
        input_output_aliases=aliases,
        compiler_params=params(),
        cost_estimate=cost(20 * count if later else 0.02),
        name="attend",
    )(*operands, *after)
    return [*outputs, pack] if later else outputs


def expert_kernel(place_ref, *refs, cap, group, first, last, experts, fsdp, split, skip):
    taken = iter(refs)

    def take(number):
        return [next(taken) for _ in range(number)]

    count = len(group)
    rows_in, ups_in = take(count), take(count)
    pays, misc = take(fsdp), next(taken)
    old = [] if first else take(3)
    take(skip)
    row_back, made_ref = take(count), next(taken)
    out1, out2, *out3 = take(4 if split else 2) if split or not last else (None, next(taken))
    rows, ups, gates, acc_row, acc_out, shift2, bias2, gated, sems, w1s, w2s, sems_w = take(12)
    step = pl.program_id(0)
    width = rows.shape[1]
    tile = w1s.shape[2]
    tall = tile + TAIL
    chunk = width // fsdp

    @pl.when(step == 0)
    def _():
        loads = []
        for index, ref in enumerate(pays):
            at = place_ref[2 + index]
            loads.append(pltpu.make_async_copy(ref.at[0:tall], w2s.at[at], sems_w.at[index, fsdp]))
            for block in range(fsdp):
                start = tall + block * chunk
                loads.append(
                    pltpu.make_async_copy(
                        ref.at[start : start + chunk, 0:tile],
                        w1s.at[block, pl.ds(pl.multiple_of(at * chunk, chunk), chunk)],
                        sems_w.at[index, block],
                    )
                )
        for load in loads:
            load.start()
        for index in range(count):
            rows[index * cap : (index + 1) * cap] = rows_in[index][...]
        router = dot(misc[...], router_order(place_ref[0], experts), NN).astype(bf16)
        gate = softmax_lanes(dot(rows[...], router, NN), experts)[:, 0:1]
        gates[...] = jnp.broadcast_to(gate, gates.shape)
        for index in range(count):
            part = slice(index * cap, (index + 1) * cap)
            ups[part] = (ups_in[index][...].astype(f32) * gate[part]).astype(bf16)
        acc_row[...] = jnp.zeros_like(acc_row)
        acc_out[...] = jnp.zeros_like(acc_out)
        bias2[...] = jnp.zeros_like(bias2)
        shift2[...] = jnp.sum(ups[...].astype(f32), axis=0, keepdims=True)
        for load in loads:
            load.wait()

    w1, w2 = w1s.at[step], w2s.at[step]
    tail = w2[tile:tall].astype(f32)
    bias2[...] += tail[1:2]
    x, up = rows[...], ups[...]
    value, slope = gelu_pair(dot(x, w1[...], NN) + tail[0:1, 0:tile])
    act = value
    acc_out[...] += dot(act, w2[0:tile], NN)
    pre = slope * dot(up, w2[0:tile], NT).astype(bf16)
    acc_row[...] += dot(pre, w1[...], NT)
    part1 = dot(x, pre, TN)
    part2 = dot(act, up, TN)
    shift1 = jnp.sum(pre.astype(f32), axis=0, keepdims=True)
    if tile < width:
        shift1 = jnp.concatenate([shift1, jnp.zeros((1, width - tile), f32)], axis=1)
    place = iota((TAIL, width), 0)
    sums = jnp.where(place == 0, shift1, jnp.where(place == 1, shift2[...], 0.0))
    if not first:
        part1, part2, sums = old[1][...] + part1, old[2][0, 0:tile] + part2, old[2][0, tile:] + sums
    if last:
        if tile < width:
            part1 = jnp.concatenate([part1, jnp.zeros((width, width - tile), f32)], axis=1)
        if split:
            for ref, fy in ((out1, place_ref[1]), (out2, 1 - place_ref[1])):

                @pl.when((step >> 1) == fy)
                def _():
                    ref[step & 1, 0:tile] = part2.astype(bf16)
                    ref[step & 1, tile:tall] = sums.astype(bf16)

            at = pl.multiple_of(step * chunk, TAIL)
            for index in range(fsdp):
                block = part1[index * chunk : (index + 1) * chunk].astype(bf16)
                for ref, fy in ((out3[0], place_ref[1]), (out3[1], 1 - place_ref[1])):

                    @pl.when(index // 2 == fy)
                    def _():
                        ref[index % 2, pl.ds(at, chunk), :] = block

        else:
            at = pl.multiple_of(tall + step * chunk, TAIL)
            out2[step, 0:tile] = part2.astype(bf16)
            out2[step, tile:tall] = sums.astype(bf16)
            for index in range(fsdp):
                out2[index, pl.ds(at, chunk), :] = part1[index * chunk : (index + 1) * chunk].astype(bf16)
    else:
        out1[...] = part1
        out2[0, 0:tile] = part2
        out2[0, tile:] = sums

    @pl.when(step == pl.num_programs(0) - 1)
    def _():
        copies = []
        for index, shift in enumerate(group):
            part = slice(index * cap, (index + 1) * cap)
            made = acc_out[part] + bias2[...]
            gate = gates[part, 0:1]
            gated[index] = (made * gate).astype(bf16)
            copies.append(
                pltpu.make_async_copy(gated.at[index], made_ref.at[place_ref[0] ^ shift], sems.at[index])
            )
            copies[-1].start()
            row_back[index][0:cap] = acc_row[part].astype(bf16)
            effect = jnp.sum(made * ups_in[index][...].astype(f32), axis=1, keepdims=True) * gate
            effect = jnp.concatenate([effect, jnp.zeros((width - cap, 1), f32)], axis=0)
            line = jnp.broadcast_to(effect, (width, LANES)).T[0:1]
            end = jnp.zeros((TAIL, width), f32)
            for order, piece in enumerate(pieces(line, 3)):
                end = jnp.where(place == order, piece.astype(f32), end)
            row_back[index][cap : cap + TAIL] = end.astype(bf16)
        for copy in copies:
            copy.wait()


def expert_call(spots, rows, ups, pays, pack, old, after, group, cap, experts, last):
    count = len(group)
    first = old is None
    fsdp = len(pays)
    high, width = pays[0].shape
    tall = high - width
    tile = tall - TAIL
    total = count * cap
    split = last and fsdp == 4
    column = pl.BlockSpec((width, tile), lambda h, _: (0, h))
    line = pl.BlockSpec((1, tall, width), lambda h, _: (h, 0, 0))
    far = pl.BlockSpec(memory_space=pl.ANY)
    if split:
        grads = [(2, tall, width)] * 2 + [(2, width, width)] * 2
    else:
        grads = [(fsdp, high, width)]

    operands = [spots, *rows, *ups, *pays, pack]
    aliases = {}
    if not first:
        aliases = {len(operands): count}
        operands += list(old)
    return pl.pallas_call(
        functools.partial(
            expert_kernel,
            cap=cap,
            group=group,
            first=first,
            last=last,
            experts=experts,
            fsdp=fsdp,
            split=split,
            skip=len(after),
        ),
        grid_spec=pltpu.PrefetchScalarGridSpec(
            num_scalar_prefetch=1,
            grid=(fsdp,),
            in_specs=[whole((cap, width))] * count
            + [pl.BlockSpec((cap, width), lambda h, _, at=v.shape[0] // cap - 1: (at, 0)) for v in ups]
            + [far] * fsdp
            + [pl.BlockSpec((width, LANES), lambda h, _: (0, 4 * width // LANES))]
            + ([] if first else [far, column, line])
            + [far] * len(after),
            out_specs=[whole((cap + TAIL, width))] * count
            + [far]
            + ([whole(v) for v in grads] if last else [column, line]),
            scratch_shapes=[pltpu.VMEM((total, width), bf16)] * 2
            + [pltpu.VMEM((total, LANES), f32)]
            + [pltpu.VMEM((total, width), f32)] * 2
            + [pltpu.VMEM((1, width), f32)] * 2
            + [pltpu.VMEM((count, cap, width), bf16), pltpu.SemaphoreType.DMA((count,))]
            + [pltpu.VMEM((fsdp, width, tile), bf16), pltpu.VMEM((fsdp, tall, width), bf16)]
            + [pltpu.SemaphoreType.DMA((fsdp, fsdp + 1))],
        ),
        out_shape=[jax.ShapeDtypeStruct((cap + TAIL, width), bf16)] * count
        + [jax.ShapeDtypeStruct((experts, cap, width), bf16)]
        + (
            [jax.ShapeDtypeStruct(v, bf16) for v in grads]
            if last
            else [
                jax.ShapeDtypeStruct((width, tile * fsdp), f32),
                jax.ShapeDtypeStruct((fsdp, tall, width), f32),
            ]
        ),
        input_output_aliases=aliases,
        compiler_params=params(),
        cost_estimate=cost(96),
        name="expert",
    )(*operands, *after)


def gather_back(places, backs, shifts, slot_sum, effect, cap):
    lane = iota((1, LANES), 1)
    for index, ref in zip(shifts, backs):
        hot = one_hot_cols(places[:, index : index + 1], cap)
        slot_sum = slot_sum + dot(hot, ref[0:cap], NN)
        parts = dot(hot, ref[cap : cap + TAIL, 0:cap], NT)
        effect = jnp.where(lane == index, jnp.sum(parts, axis=1, keepdims=True), effect)
    return slot_sum, effect


def returned_kernel(pos_ref, *refs, cap, shifts):
    backs, slot_ref, effect_ref = refs[: len(shifts)], refs[-2], refs[-1]
    _, rows, width = slot_ref.shape
    slot_ref[0], effect_ref[0] = gather_back(
        pos_ref[0, 0:rows, :], backs, shifts, jnp.zeros((rows, width), f32), jnp.zeros((rows, LANES), f32), cap
    )


def returned(pos, backs, shifts, rows, cap):
    images, width = pos.shape[0], backs[0].shape[1]

    def image(shape):
        return pl.BlockSpec((1,) + shape, lambda i: (i, 0, 0))

    return pl.pallas_call(
        functools.partial(returned_kernel, cap=cap, shifts=shifts),
        grid=(images,),
        in_specs=[image((pos.shape[1], LANES))] + [whole((cap + TAIL, width))] * len(backs),
        out_specs=[image((rows, width)), image((rows, LANES))],
        out_shape=[
            jax.ShapeDtypeStruct((images, rows, width), f32),
            jax.ShapeDtypeStruct((images, rows, LANES), f32),
        ],
        compiler_params=params(),
        cost_estimate=cost(100),
        name="returned",
    )(pos, *backs)


def middle_kernel(
    place_ref, up_ref, wout_ref, misc_ref, pos_ref, mixed_ref, hidden_ref, prob_ref, slot_ref, effect_ref, *rest, cap, experts
):
    backs = rest[:2]
    hidden_grad_ref, mixed_grad_ref, sums_ref, padded, vectors, router, shifts, acc_out, acc_router = rest[-9:]
    _, seq, width = up_ref.shape
    rows = padded.shape[0]
    step = pl.program_id(0)

    @pl.when(step == 0)
    def _():
        vectors[...] = misc_ref[...].astype(f32).T
        router[...] = dot(misc_ref[...], router_order(place_ref[0], experts), NN).astype(bf16)
        padded[...] = jnp.zeros_like(padded)
        shifts[...] = jnp.zeros_like(shifts)
        acc_out[...] = jnp.zeros_like(acc_out)
        acc_router[...] = jnp.zeros_like(acc_router)

    def vector(index):
        return vectors[VEC + index : VEC + index + 1, :]

    def shift(index, value):
        shifts[index : index + 1, :] += jnp.sum(value, axis=0, keepdims=True)

    slot_sum, effect = gather_back(pos_ref[0, 0:rows, :], backs, (0, 1), slot_ref[0], effect_ref[0], cap)
    prob = prob_ref[0]
    logit_grad = effect - prob * jnp.sum(effect, axis=1, keepdims=True)
    logit_parts = pieces(logit_grad, 2)
    mid_grad = slot_sum
    for part in logit_parts:
        mid_grad = mid_grad + dot(part, router[...], NT)
    padded[0:seq] = up_ref[0].astype(f32)
    hat, inverse = norm_stats(hidden_ref[0])
    mid_parts = pieces(hat * vector(5) + vector(6), 2)
    acc_router[...] += (
        dot(logit_parts[0], mid_parts[0], TN)
        + dot(logit_parts[0], mid_parts[1], TN)
        + dot(logit_parts[1], mid_parts[0], TN)
    )
    shift(5, mid_grad * hat)
    shift(6, mid_grad)
    hidden_grad = padded[...] + norm_back(mid_grad, vector(5), hat, inverse)
    hidden_grad_ref[0] = hidden_grad
    branch = hidden_grad.astype(bf16)
    shift(4, branch.astype(f32))
    acc_out[...] += dot(mixed_ref[0], branch, TN)
    mixed_grad_ref[0] = dot(branch, wout_ref[...], NT).astype(bf16)

    @pl.when(step == pl.num_programs(0) - 1)
    def _():
        sums_ref[:, 0:width] = acc_out[...]
        ordered = dot(router_order(place_ref[0], experts), acc_router[...].astype(bf16), NN)
        spare = jnp.concatenate(
            [ordered[0:VEC], shifts[...], jnp.zeros((LANES - VEC - shifts.shape[0], width), f32)], axis=0
        )
        sums_ref[:, width:] = spare.T


def middle(place, grad_output, pack, pos, saved, part_sums, backs, cap, experts):
    images, seq, width = grad_output.shape
    _, mixed, hidden, prob, _ = saved
    rows = mixed.shape[1]

    def image(shape):
        return pl.BlockSpec((1,) + shape, lambda i: (i, 0, 0))

    return pl.pallas_call(
        functools.partial(middle_kernel, cap=cap, experts=experts),
        grid=(images,),
        in_specs=[
            pl.BlockSpec(memory_space=pltpu.SMEM),
            image((seq, width)),
            pl.BlockSpec((width, width), lambda i: (0, 3)),
            pl.BlockSpec((width, LANES), lambda i: (0, 4 * width // LANES)),
            image((pos.shape[1], LANES)),
            image((rows, width)),
            image((rows, width)),
            image((rows, LANES)),
            image((rows, width)),
            image((rows, LANES)),
        ]
        + [whole((cap + TAIL, width))] * len(backs),
        out_specs=[image((rows, width)), image((rows, width)), whole((width, width + LANES))],
        out_shape=[
            jax.ShapeDtypeStruct((images, rows, width), f32),
            jax.ShapeDtypeStruct((images, rows, width), bf16),
            jax.ShapeDtypeStruct((width, width + LANES), f32),
        ],
        scratch_shapes=[
            pltpu.VMEM((rows, width), f32),
            pltpu.VMEM((LANES, width), f32),
            pltpu.VMEM((width, LANES), bf16),
            pltpu.VMEM((8, width), f32),
            pltpu.VMEM((width, width), f32),
            pltpu.VMEM((LANES, width), f32),
        ],
        compiler_params=params(),
        cost_estimate=cost(0.02),
        name="middle",
    )(place, grad_output, pack, pack, pos, mixed, hidden, prob, *part_sums, *backs)


def backward_kernel(
    spots_ref, tok_ref, qkv_ref, attn_ref, mixed_grad_ref, *rest, head_rows, members
):
    sums_ref, peak_ref = rest[:2]
    qkv_grad_ref, keep_ref, give_ref, padded, acc_qkv, columns, spare, misc = rest[-8:]
    _, seq, width = tok_ref.shape
    rows = padded.shape[0]
    head = width // HEADS
    wide = 3 * width
    step = pl.program_id(0)

    @pl.when(step == 0)
    def _():
        padded[...] = jnp.zeros_like(padded)
        acc_qkv[...] = jnp.zeros_like(acc_qkv)
        columns[...] = jnp.zeros_like(columns)

    lane = iota((1, LANES), 1)
    first = lane < head
    halves = (jnp.where(first, 1.0, 0.0).astype(bf16), jnp.where(first, 0.0, 1.0).astype(bf16))

    def pair(index, carry):
        at = pl.multiple_of(index * LANES, LANES)
        query = qkv_ref[0, :, pl.ds(at, LANES)]
        key = qkv_ref[0, :, pl.ds(width + at, LANES)]
        value = qkv_ref[0, :, pl.ds(2 * width + at, LANES)]
        up = mixed_grad_ref[0, :, pl.ds(at, LANES)]
        made = []
        for half in range(2):
            low = attn_ref[0, index * 2 + half]
            weight = low.astype(f32)
            value_grad = dot(low, up, TN)
            spread = weight * dot(up * halves[half], value, NT)
            score_grad = (spread - weight * jnp.sum(spread, axis=1, keepdims=True)).astype(bf16)
            made.append((dot(score_grad, key, NN) * head**-0.5, dot(score_grad, query, TN), value_grad))
        for index_of, (left, right) in enumerate(zip(*made)):
            qkv_grad_ref[0, :, pl.ds(index_of * width + at, LANES)] = jnp.where(first, left, right).astype(bf16)
        return carry

    lax.fori_loop(0, HEADS // 2, pair, 0, unroll=True)
    columns[...] += jnp.sum(qkv_grad_ref[0].astype(f32), axis=0, keepdims=True)
    padded[0:seq] = tok_ref[0].astype(f32)
    hat, _ = norm_stats(padded[...])
    acc_qkv[...] += dot(hat.astype(bf16), qkv_grad_ref[0], TN)
    part = keep_ref.shape[1]

    @pl.when(step == pl.num_programs(0) - 1)
    def _():
        line = iota((LANES, width), 0)
        flat = columns[...]
        grown = jnp.where(line == VEC + 2, flat[:, 0:width], 0.0)
        grown = jnp.where(line == VEC + 3, flat[:, 2 * width :], grown)
        misc[...] = sums_ref[:, width:] + grown.T
        spare[...] = jnp.zeros_like(spare)
        number = wide // LANES
        for order, piece in enumerate(pieces(flat, 3)):
            value = piece.astype(f32)
            for index in range(number):
                at = order * number + index
                spare[at : at + 1, :] = value[:, index * LANES : (index + 1) * LANES]
        if members:
            top = jnp.where(lane < HEADS, peak_ref[...], 0.0)
            rows_of = jnp.zeros((TAIL, LANES), f32)
            for order, piece in enumerate(pieces(jnp.broadcast_to(top, (TAIL, LANES)), 3)):
                move = jnp.where(iota((LANES, LANES), 1) == iota((LANES, LANES), 0) + order * HEADS, 1.0, 0.0)
                rows_of = rows_of + dot(piece, move.astype(bf16), NN)
            spare[pl.ds(head_rows + spots_ref[1], 1), :] = rows_of[0:1]
        extra = spare[...].astype(bf16)
        for fy in range(keep_ref.shape[0]):
            for ref, core in ((keep_ref, spots_ref[0]), (give_ref, 1 - spots_ref[0])):
                at = pl.multiple_of((2 * fy + core) * part, part)
                ref[fy, :, 0:wide] = acc_qkv[pl.ds(at, part), :].astype(bf16)
                ref[fy, :, wide : wide + width] = sums_ref[pl.ds(at, part), 0:width].astype(bf16)
                ref[fy, :, wide + width : wide + width + LANES] = misc[pl.ds(at, part), :].astype(bf16)
                ref[fy, :, wide + width + LANES :] = extra


def backward(spots, tokens, saved, mixed_grad, sums, peak, after, ways, part, head_rows, members):
    images, seq, width = tokens.shape
    qkv, attn = saved[0], saved[-1]
    rows = qkv.shape[1]
    wide = 4 * width + 2 * LANES

    def image(shape):
        return pl.BlockSpec((1,) + shape, lambda i: (i,) + (0,) * len(shape))

    return pl.pallas_call(
        functools.partial(backward_kernel, head_rows=head_rows, members=members),
        grid=(images,),
        in_specs=[
            pl.BlockSpec(memory_space=pltpu.SMEM),
            image((seq, width)),
            image((rows, 3 * width)),
            image((HEADS, rows, rows)),
            image((rows, width)),
            whole(sums.shape),
            whole(peak.shape),
        ]
        + [pl.BlockSpec(memory_space=pl.ANY)] * len(after),
        out_specs=[image((rows, 3 * width)), whole((ways, part, wide)), whole((ways, part, wide))],
        out_shape=[
            jax.ShapeDtypeStruct((images, rows, 3 * width), bf16),
            jax.ShapeDtypeStruct((ways, part, wide), bf16),
            jax.ShapeDtypeStruct((ways, part, wide), bf16),
        ],
        scratch_shapes=[
            pltpu.VMEM((rows, width), f32),
            pltpu.VMEM((width, 3 * width), f32),
            pltpu.VMEM((1, 3 * width), f32),
            pltpu.VMEM((part, LANES), f32),
            pltpu.VMEM((width, LANES), f32),
        ],
        compiler_params=params(),
        cost_estimate=cost(0.05),
        name="attend_back",
    )(spots, tokens, qkv, attn, mixed_grad, sums, peak, *after)


def first_kernel(tok_ref, qkv_grad_ref, wqkv_ref, misc_ref, hidden_grad_ref, grad_ref, padded, gain):
    _, seq, width = tok_ref.shape

    @pl.when(pl.program_id(0) == 0)
    def _():
        gain[...] = misc_ref[...].astype(f32).T[VEC : VEC + 1]
        padded[...] = jnp.zeros_like(padded)

    in_grad = dot(qkv_grad_ref[0], wqkv_ref[...], NT)
    padded[0:seq] = tok_ref[0].astype(f32)
    hat, inverse = norm_stats(padded[...])
    grad_ref[0] = (hidden_grad_ref[0] + norm_back(in_grad, gain[...], hat, inverse))[0:seq]


def first_norm(tokens, qkv_grad, pack, hidden_grad):
    images, seq, width = tokens.shape
    rows = qkv_grad.shape[1]

    def image(shape):
        return pl.BlockSpec((1,) + shape, lambda i: (i, 0, 0))

    return pl.pallas_call(
        first_kernel,
        grid=(images,),
        in_specs=[
            image((seq, width)),
            image((rows, 3 * width)),
            pl.BlockSpec((width, 3 * width), lambda i: (0, 0)),
            pl.BlockSpec((width, LANES), lambda i: (0, 4 * width // LANES)),
            image((rows, width)),
        ],
        out_specs=image((seq, width)),
        out_shape=jax.ShapeDtypeStruct((images, seq, width), f32),
        scratch_shapes=[pltpu.VMEM((rows, width), f32), pltpu.VMEM((1, width), f32)],
        compiler_params=params(),
        cost_estimate=cost(0.02),
        name="first_norm",
    )(tokens, qkv_grad, pack, pack, hidden_grad)


def output_kernel(place_ref, pos_ref, hidden_ref, made_ref, out_ref):
    experts, cap, _ = made_ref.shape
    seq = out_ref.shape[1]
    total = hidden_ref[0]
    places = pos_ref[0, 0 : total.shape[0], :]
    for index in range(experts):
        total = total + dot(one_hot_cols(places[:, index : index + 1], cap), made_ref[place_ref[0] ^ index], NN)
    out_ref[0] = total[0:seq].astype(bf16)


def combine_output(place, pos, hidden, made, seq):
    images, rows, width = hidden.shape

    def image(shape):
        return pl.BlockSpec((1,) + shape, lambda i: (i, 0, 0))

    return pl.pallas_call(
        output_kernel,
        grid=(images,),
        in_specs=[
            pl.BlockSpec(memory_space=pltpu.SMEM),
            image((pos.shape[1], LANES)),
            image((rows, width)),
            whole(made.shape),
        ],
        out_specs=image((seq, width)),
        out_shape=jax.ShapeDtypeStruct((images, seq, width), bf16),
        compiler_params=params(),
        cost_estimate=cost(0.02),
        name="combine",
    )(place, pos, hidden, made)


def finish_kernel(slot_ref, *refs, number, head_rows, members):
    parts, (own_ref, limit_ref, peak_ref) = refs[:number], refs[number : number + 3]
    qkv_ref, out_ref, misc_ref, clip_ref, *vec_refs, total_ref = refs[number + 3 :]
    part = own_ref.shape[0]
    for shift, ref in enumerate(parts):
        size = part // number
        total_ref[pl.ds(pl.multiple_of((slot_ref[0] ^ shift) * size, size), size), :] = ref[...]
    width = out_ref.shape[1]
    wide = 3 * width
    number = wide // LANES
    base = total_ref[:, 0:wide].astype(f32)
    extra = total_ref[:, wide + width + LANES :].astype(f32)
    weight = own_ref[:, 0:wide].astype(f32)
    columns = [sum(extra[k * number + i : k * number + i + 1] for k in range(3)) for i in range(number)]
    columns = jnp.concatenate(columns, axis=1)
    own = own_ref[:, wide + width :].astype(f32)
    gain, bias = own[:, VEC : VEC + 1], own[:, VEC + 1 : VEC + 2]
    qkv_ref[...] = base * gain + bias * columns
    out_ref[...] = total_ref[:, wide : wide + width].astype(f32)
    misc = total_ref[:, wide + width : wide + width + LANES].astype(f32)
    lane = iota((1, LANES), 1)
    misc = jnp.where(lane == VEC, jnp.sum(base * weight, axis=1, keepdims=True), misc)
    misc = jnp.where(lane == VEC + 1, jnp.sum(columns * weight, axis=1, keepdims=True), misc)
    misc = misc.T
    for index, ref in enumerate(vec_refs):
        ref[...] = misc[VEC + index : VEC + index + 1]
    misc_ref[...] = misc[0 : misc_ref.shape[0]]
    if members:
        move = jnp.where(
            (iota((LANES, LANES), 0) % HEADS == iota((LANES, LANES), 1)) & (iota((LANES, LANES), 0) < 3 * HEADS),
            1.0,
            0.0,
        )
        peaks = dot(total_ref[head_rows : head_rows + members, wide + width + LANES :], move.astype(bf16), NN)
        peak = jnp.max(peaks, axis=0, keepdims=True)
    else:
        peak = peak_ref[...]
    limit = limit_ref[...]
    root = jnp.sqrt(limit / jnp.maximum(peak, limit))
    place = iota((1, width), 1) // (width // HEADS)
    scale = jnp.zeros((1, width), f32)
    for index in range(HEADS):
        scale = jnp.where(place == index, root[:, index : index + 1], scale)
    clip_ref[:, 0:width] = (weight[:, 0:width] * scale).astype(bf16)
    clip_ref[:, width : 2 * width] = (weight[:, width : 2 * width] * scale).astype(bf16)
    clip_ref[:, 2 * width :] = own_ref[:, 2 * width : wide]


def finish(slot, total, own, limit, peak, width, experts, head_rows, members):
    part = own.shape[0]
    operands = [*total, own, limit, peak]
    shapes = [(part, 3 * width), (part, width), (experts, part), (part, 3 * width)] + [(1, part)] * 7
    return pl.pallas_call(
        functools.partial(finish_kernel, number=len(total), head_rows=head_rows, members=members),
        grid=(1,),
        in_specs=[pl.BlockSpec(memory_space=pltpu.SMEM)] + [whole(v.shape) for v in operands],
        out_specs=[whole(v) for v in shapes],
        out_shape=[jax.ShapeDtypeStruct(v, bf16 if i == 3 else f32) for i, v in enumerate(shapes)],
        scratch_shapes=[pltpu.VMEM((part, total[0].shape[1]), bf16)],
        compiler_params=params(),
        cost_estimate=cost(0.02),
        name="finish",
    )(slot, *operands)


def half_sums_kernel(high_ref, keep_ref, got_ref, *rest):
    straight_ref, crossed_ref = rest[-2:]
    for ref, core in ((straight_ref, high_ref[0]), (crossed_ref, 1 - high_ref[0])):
        ref[...] = (keep_ref[core].astype(f32) + got_ref[core].astype(f32)).astype(bf16)


def half_sums(high, keep, got, after, micros):
    shape = keep.shape[1:]
    return pl.pallas_call(
        half_sums_kernel,
        grid=(1,),
        in_specs=[pl.BlockSpec(memory_space=pltpu.SMEM), whole(keep.shape), whole(got.shape)]
        + [pl.BlockSpec(memory_space=pl.ANY)] * len(after),
        out_specs=[whole(shape)] * 2,
        out_shape=[jax.ShapeDtypeStruct(shape, bf16)] * 2,
        compiler_params=params(),
        cost_estimate=cost(micros),
        name="half_sums",
    )(high, keep, got, *after)


def home_second_kernel(spot_ref, one, two, _, w2_ref, b1_ref, b2_ref):
    tile, width = w2_ref.shape
    part = b2_ref.shape[1]
    w2_ref[...] = one[0:tile].astype(f32) + two[0:tile].astype(f32)
    edge = one[tile:].astype(f32) + two[tile:].astype(f32)
    b1_ref[...] = edge[0:1, 0:tile]
    b2_ref[...] = sum(
        jnp.where(spot_ref[0] == index, edge[1:2, index * part : (index + 1) * part], 0.0)
        for index in range(width // part)
    )


def home_first_kernel(_, one, two, __, w1_ref):
    part, hidden = w1_ref.shape
    number = one.shape[0] // part
    tile = hidden // number
    for index in range(number):
        rows = slice(index * part, (index + 1) * part)
        total = one[rows].astype(f32) + two[rows].astype(f32)
        w1_ref[:, index * tile : (index + 1) * tile] = total[:, 0:tile]


def home_sums(kernel, spot, pair, after, shapes):
    return pl.pallas_call(
        kernel,
        grid=(1,),
        in_specs=[pl.BlockSpec(memory_space=pltpu.SMEM)]
        + [whole(v.shape) for v in pair]
        + [pl.BlockSpec(memory_space=pl.ANY)],
        out_specs=[whole(v) for v in shapes],
        out_shape=[jax.ShapeDtypeStruct(v, f32) for v in shapes],
        compiler_params=params(),
        cost_estimate=cost(0.02),
        name="home_sums",
    )(spot, *pair, after)


def add_halves_kernel(fy_ref, keep_ref, got_ref, *rest):
    mine_ref, theirs_ref = rest[-2:]
    for ref, half in ((mine_ref, fy_ref[0]), (theirs_ref, 1 - fy_ref[0])):
        ref[...] = (keep_ref[half].astype(f32) + got_ref[half].astype(f32)).astype(bf16)


def add_halves(fy, keep, got, after):
    shape = keep.shape[1:]
    return pl.pallas_call(
        add_halves_kernel,
        grid=(1,),
        in_specs=[pl.BlockSpec(memory_space=pltpu.SMEM), whole(keep.shape), whole(got.shape)]
        + [pl.BlockSpec(memory_space=pl.ANY)] * len(after),
        out_specs=[whole(shape)] * 2,
        out_shape=[jax.ShapeDtypeStruct(shape, bf16)] * 2,
        compiler_params=params(),
        cost_estimate=cost(0.02),
        name="add_halves",
    )(fy, keep, got, *after)


def split_rows_kernel(slot_ref, mine_ref, got_ref, *refs, skip):
    outs, total = refs[skip:-1], refs[-1]
    total[...] = (mine_ref[...].astype(f32) + got_ref[...].astype(f32)).astype(bf16)
    size = outs[0].shape[0]
    for shift, ref in enumerate(outs):
        ref[...] = total[pl.ds(pl.multiple_of((slot_ref[0] ^ shift) * size, size), size), :]


def split_rows(slot, mine, got, after, number):
    part, wide = mine.shape
    shape = (part // number, wide)
    return pl.pallas_call(
        functools.partial(split_rows_kernel, skip=len(after)),
        grid=(1,),
        in_specs=[pl.BlockSpec(memory_space=pltpu.SMEM), whole(mine.shape), whole(got.shape)]
        + [pl.BlockSpec(memory_space=pl.ANY)] * len(after),
        out_specs=[whole(shape)] * number,
        out_shape=[jax.ShapeDtypeStruct(shape, bf16)] * number,
        scratch_shapes=[pltpu.VMEM((part, wide), bf16)],
        compiler_params=params(),
        cost_estimate=cost(0.02),
        name="split_rows",
    )(slot, mine, got, *after)


def add_parts_kernel(*refs, number):
    parts, out_ref = refs[:number], refs[-1]
    out_ref[...] = sum(ref[...].astype(f32) for ref in parts).astype(bf16)


def add_parts(parts, after=()):
    shape = parts[0].shape
    return pl.pallas_call(
        functools.partial(add_parts_kernel, number=len(parts)),
        grid=(1,),
        in_specs=[whole(shape)] * len(parts) + [pl.BlockSpec(memory_space=pl.ANY)] * len(after),
        out_specs=whole(shape),
        out_shape=jax.ShapeDtypeStruct(shape, bf16),
        compiler_params=params(),
        cost_estimate=cost(0.02),
        name="add_parts",
    )(*parts, *after)


def swap(value, axis):
    return lax.ppermute(value, axis, [(0, 1), (1, 0)])


def around(value, axis, size):
    return [value] + [
        lax.ppermute(value, axis, [((k + step) % size, k) for k in range(size)]) for step in range(1, size)
    ]


def split_sum(value, axis, size):
    if size != 2:
        return lax.psum_scatter(value, axis, scatter_dimension=0, tiled=False)
    place = lax.axis_index(axis)
    sent = lax.dynamic_index_in_dim(value, 1 - place, 0, keepdims=False)
    kept = lax.dynamic_index_in_dim(value, place, 0, keepdims=False)
    return (kept.astype(f32) + swap(sent, axis).astype(f32)).astype(value.dtype)


def exchange(value, shift, experts):
    return lax.ppermute(value, GROUP, [(k, k ^ shift) for k in range(experts)])


def shift_order(experts):
    def key(shift):
        distance = bin(shift >> 1).count("1")
        return (shift & 1, distance, shift)

    order = sorted(range(2, experts), key=key)
    half = len(order) // 2
    return [order[:half], order[half:], [0, 1]]


STRAIGHT = [(0, 0), (1, 2), (2, 1), (3, 3)]
CROSSED = [(0, 2), (1, 0), (2, 3), (3, 1)]
BACK = [(b, a) for a, b in STRAIGHT]
BACK_CROSSED = [(b, a) for a, b in CROSSED]


def shards(
    tokens,
    ln1_gain,
    ln1_bias,
    w_qkv,
    q_bias,
    v_bias,
    w_out,
    out_bias,
    ln2_gain,
    ln2_bias,
    w_router,
    expert_w1,
    expert_b1,
    expert_w2,
    expert_b2,
    route_ids,
    clip_threshold,
    grad_output,
    *,
    experts,
    fsdp,
):
    images, seq, width = tokens.shape
    token_count = images * seq
    ways = fsdp // 2
    cap = (7 * token_count // (2 * experts) + 7) // 8 * 8
    stride = -(-seq // 256) * 256
    rows = -(-seq // 16) * 16
    part = w_qkv.shape[0]
    hidden_part = expert_w2.shape[1]
    high, low, fy, core = (lax.axis_index(name).astype(i32) for name in DEVICE)
    place_ref = (low * 2 + core).reshape(1)
    spot = fy * 2 + core

    vectors = (ln1_gain, ln1_bias, q_bias, v_bias, out_bias, ln2_gain, ln2_bias)
    own, pay = pack_parameters(
        spot.reshape(1), w_qkv, w_out, w_router, vectors, expert_w1[0], expert_w2[0], expert_b1, expert_b2
    )

    near = around(own, "fy", ways)
    far = [swap(own, "core")]
    straight = lax.ppermute(pay, ("hi", "core"), STRAIGHT)

    ids = jnp.pad(route_ids.reshape(images, seq, -1), ((0, 0), (0, stride - seq), (0, 0)), constant_values=-1)
    ids = ids.reshape(images * stride, -1).T
    post, pos, *ups = route(place_ref, ids, grad_output, experts, cap, stride)
    groups = shift_order(experts)
    near[1:], post, ups[0] = lax.optimization_barrier((near[1:], post, ups[0]))
    for shift in groups[0]:
        ups[shift] = exchange(ups[shift], shift, experts)
    far += [swap(value, "core") for value in near[1:]]
    homes = [((fy + step) % ways) * 2 for step in range(ways)]
    homes = [home + core for home in homes] + [home + 1 - core for home in homes]

    early = 1
    spots = jnp.stack([place_ref[0], *homes])
    firsts = [ups[shift] for shift in groups[0]]
    begun = list(forward(spots, tokens, near + far, None, [], 0, early, experts, stride, rows))
    pay, straight, begun[0] = lax.optimization_barrier((pay, straight, begun[0]))
    crossed = lax.ppermute(pay, ("hi", "core"), CROSSED)
    pays = around(straight, "fy", ways)
    pay_homes = [((fy + step) % ways) * 2 + high for step in range(ways)]
    *saved, mid, peak, pack = forward(
        spots, tokens, [], begun, [straight], early, images - early, experts, stride, rows
    )
    mid = mid.reshape(images * stride, width)
    paired = tuple(shift for group in groups[1:] for shift in group)
    sent = dispatch(post, mid, ups, paired, [], experts, cap)
    crossed, sent[0], firsts, *pays[1:] = lax.optimization_barrier((crossed, sent[0], firsts, *pays[1:]))
    for shift, value in zip(groups[0], firsts):
        ups[shift] = value
    pays += around(crossed, "fy", ways)
    pay_homes += [((fy + step) % ways) * 2 + 1 - high for step in range(ways)]
    expert_spots = jnp.stack([place_ref[0], fy, *pay_homes])

    arrived = {}

    def send(number, after):
        pending, after = lax.optimization_barrier(([sent[shift] for shift in groups[number]], after))
        for shift, value in zip(groups[number], pending):
            arrived[shift] = value if shift == 0 else exchange(value, shift, experts)
        return after

    send(0, [sent[0]])
    first = send(1, [arrived[shift] for shift in groups[0]])
    arrived.update(zip(groups[0], first))
    old, after = None, []
    backs = {}
    for number, group in enumerate(groups):
        result = expert_call(
            expert_spots,
            [arrived[shift] for shift in group],
            [arrived[shift] if shift in paired else ups[shift] for shift in group],
            pays,
            pack,
            old,
            after,
            group,
            cap,
            experts,
            number == len(groups) - 1,
        )
        old = result[len(group) :]
        after = [backs[shift] for shift in groups[number - 1]] if number else []
        out = result[: len(group)]
        if number + 2 < len(groups):
            out = send(number + 2, out)
        for at, shift in enumerate(group):
            backs[shift] = out[at] if shift == 0 else exchange(out[at], shift, experts)
    backs = [backs[shift] for shift in range(experts)]
    made, *grad = old
    made = lax.all_to_all(made, GROUP, split_axis=0, concat_axis=0, tiled=True)

    shifts = tuple(range(2, experts))
    part_sums = returned(pos, backs[2:], shifts, rows, cap)
    hidden_grad, mixed_grad, sums = middle(
        place_ref, grad_output, pack, pos, saved, part_sums, backs[:2], cap, experts
    )
    head_rows = 3 * (3 * width // LANES) + 4
    devices = 2 * experts // 2 * fsdp
    members = devices if head_rows + devices <= part else 0
    device = ((high * (experts // 2) + low) * ways + fy) * 2 + core
    spots = jnp.stack([core, device])
    def homeward(straight, crossed):
        return [
            lax.ppermute(straight, ("hi", "core"), BACK),
            lax.ppermute(crossed, ("hi", "core"), BACK_CROSSED),
        ]

    which = high.reshape(1)
    if len(grad) == 4:
        sums_two = list(half_sums(which, grad[0], swap(grad[1], "fy"), [sums], 0.02))
        home_two = homeward(*sums_two)
        grad[3], sums_two[0] = lax.optimization_barrier((grad[3], sums_two[0]))
        got_one = swap(grad[3], "fy")
    else:
        half = split_sum(grad[0].reshape((ways, 2) + grad[0].shape[1:]), "fy", ways)
        home = homeward(*(lax.dynamic_index_in_dim(half, k, 0, keepdims=False) for k in (high, 1 - high)))
        tall = hidden_part + TAIL
        home_two, home_one = [v[:tall] for v in home], [v[tall:] for v in home]
    qkv_grad, keep, give = backward(
        spots, tokens, saved, mixed_grad, sums, peak, [], ways, part, head_rows, members
    )

    got = swap(give, "core")
    after = []
    if len(grad) == 4:
        after = half_sums(which, grad[2], got_one, home_two, 40)
        home_one = homeward(*after)
    output = combine_output(place_ref, pos, saved[2], made, seq)
    near_by = experts // 2
    if ways == 2 and part % (TAIL * near_by) == 0:

        def spread(values):
            return [
                value if k == 0 else lax.ppermute(value, "lo", [(j, j ^ k) for j in range(near_by)])
                for k, value in enumerate(values)
            ]

        mine, theirs = add_halves(fy.reshape(1), keep, got, after)
        theirs, qkv_grad = lax.optimization_barrier((theirs, qkv_grad))
        input_grad = first_norm(tokens, qkv_grad, pack, hidden_grad)
        parts = split_rows(low.reshape(1), mine, swap(theirs, "fy"), [input_grad, output, *home_one], near_by)
        total = add_parts(spread(parts))
        shapes = [(hidden_part, width), (1, hidden_part), (1, part)]
        grad_w2, grad_b1, grad_b2 = home_sums(home_second_kernel, spot.reshape(1), home_two, total, shapes)
        shapes = [(part, hidden_part * fsdp)]
        (grad_w1,) = home_sums(home_first_kernel, spot.reshape(1), home_one, total, shapes)
        total = add_parts([total, swap(total, "hi")], [grad_w2, grad_w1])
        total = spread([total] * near_by)
    else:
        sums = split_sum((keep.astype(f32) + got.astype(f32)).astype(bf16), "fy", ways)
        total = [lax.psum(sums, ("hi", "lo"))]
        shapes = [(hidden_part, width), (1, hidden_part), (1, part)]
        grad_w2, grad_b1, grad_b2 = home_sums(home_second_kernel, spot.reshape(1), home_two, total[0], shapes)
        shapes = [(part, hidden_part * fsdp)]
        (grad_w1,) = home_sums(home_first_kernel, spot.reshape(1), home_one, total[0], shapes)
        input_grad = first_norm(tokens, qkv_grad, pack, hidden_grad)
    if not members:
        peak = jnp.max(lax.all_gather(peak, DEVICE, axis=0, tiled=True), axis=0, keepdims=True)
    limit = jnp.pad(clip_threshold.astype(f32).reshape(1, HEADS), ((0, 0), (0, LANES - HEADS)), constant_values=1.0)
    grad_qkv, grad_out, grad_router, clipped, *grads = finish(
        low.reshape(1), total, own, limit, peak, width, experts, head_rows, members
    )
    grads = [v.reshape(part) for v in grads]
    return (
        output,
        input_grad,
        grads[0],
        grads[1],
        grad_qkv,
        grads[2],
        grads[3],
        grad_out,
        grads[4],
        grads[5],
        grads[6],
        grad_router.T,
        grad_w1[None],
        grad_b1,
        grad_w2[None],
        grad_b2,
        clipped,
    )


def solution(mesh):
    experts, fsdp = mesh.shape["expert"], mesh.shape["fsdp"]
    inner = Mesh(mesh.devices.reshape(2, experts // 2, fsdp // 2, 2), DEVICE)
    token, row, expert = P(DEVICE, None, None), ("fy", "core"), ("hi", "lo")
    vector, matrix = P(row), P(row, None)
    return jax.shard_map(
        functools.partial(shards, experts=experts, fsdp=fsdp),
        mesh=inner,
        in_specs=(
            token,
            vector,
            vector,
            matrix,
            vector,
            vector,
            matrix,
            vector,
            vector,
            vector,
            matrix,
            P(expert, row, None),
            P(expert, row),
            P(expert, row, None),
            P(expert, row),
            P(DEVICE, None),
            P(),
            token,
        ),
        out_specs=(
            token,
            token,
            vector,
            vector,
            matrix,
            vector,
            vector,
            matrix,
            vector,
            vector,
            vector,
            matrix,
            P(expert, row, None),
            P(expert, row),
            P(expert, row, None),
            P(expert, row),
            matrix,
        ),
        check_vma=False,
    )
```

```python
import functools

import jax
import jax.numpy as jnp
from jax import lax
from jax.experimental import pallas as pl
from jax.experimental.pallas import tpu as pltpu
from jax.sharding import Mesh
from jax.sharding import PartitionSpec as P

HEADS = 8
EPS = 1e-06
LANES = 128
VEC = 64
TAIL = 16
NEG = -1e30
f32 = jnp.float32
bf16 = jnp.bfloat16
i32 = jnp.int32
NN = (((1,), (0,)), ((), ()))
NT = (((1,), (1,)), ((), ()))
TN = (((0,), (0,)), ((), ()))
DEVICE = ("hi", "lo", "fy", "core")
GROUP = ("lo", "core")
PLACE, FY, CORE, NUMBER, HIGH, SPOT, SAME, LOW, HOMES = range(9)
VMEM_LIMIT = 64 << 20


def dot(a, b, dims):
    return lax.dot_general(a, b, dims, preferred_element_type=f32)


def pieces(value, count):
    parts = []
    for _ in range(count):
        part = value.astype(bf16)
        parts.append(part)
        value = value - part.astype(f32)
    return parts


def iota(shape, axis):
    return lax.broadcasted_iota(i32, shape, axis)


def relative_expert(place, shift, experts):
    other = jnp.bitwise_xor(place, shift)
    return (other & 1) * (experts // 2) + (other >> 1)


def router_order(place, experts):
    row, col = iota((LANES, LANES), 0), iota((LANES, LANES), 1)
    return jnp.where((row == relative_expert(place, col, experts)) & (col < experts), 1.0, 0.0).astype(bf16)


def norm_stats(matrix):
    centred = matrix - jnp.mean(matrix, axis=1, keepdims=True)
    inverse = lax.rsqrt(jnp.mean(centred * centred, axis=1, keepdims=True) + EPS)
    return centred * inverse, inverse


def norm_back(upstream, gain, hat, inverse):
    scaled = upstream * gain
    spread = (
        scaled
        - jnp.mean(scaled, axis=1, keepdims=True)
        - hat * jnp.mean(scaled * hat, axis=1, keepdims=True)
    )
    return spread * inverse


def softmax_lanes(logits, experts):
    logits = jnp.where(iota(logits.shape, 1) < experts, logits, NEG)
    top = jnp.max(logits, axis=1, keepdims=True)
    weight = jnp.exp(logits - top)
    return weight / jnp.sum(weight, axis=1, keepdims=True)


def gelu_pair(value):
    def low(number):
        return jnp.asarray(number, bf16)

    value = value.astype(bf16)
    bell = jnp.exp(value * value * low(-0.5))
    t = low(1.0) / (low(1.0) + jnp.abs(value) * low(0.3275911 * 0.7071067811865476))
    poly = low(0.7107068705) + t * (low(-0.7265760135) + t * low(0.5307027145))
    poly = t * (low(0.127414796) + t * (low(-0.142248368) + t * poly))
    lower = poly * bell
    phi = jnp.where(value >= low(0.0), low(1.0) - lower, lower)
    return value * phi, phi + value * (bell * low(0.3989422804014327))


def whole(shape):
    return pl.BlockSpec(shape, lambda *_: (0,) * len(shape))


def params(**extra):
    return pltpu.CompilerParams(vmem_limit_bytes=VMEM_LIMIT, **extra)


def cost(micros):
    return pl.CostEstimate(flops=int(micros * 1e9), bytes_accessed=0, transcendentals=0)


def pack_kernel(spot_ref, wqkv, wout, router, *rest):
    vectors, (w1, w2, b1, b2, pack_ref, pay_ref, spread, tail) = rest[:-8], rest[-8:]
    part, wide = wqkv.shape
    width, hidden = wout.shape[1], w2.shape[0]
    pack_ref[:, 0:wide] = wqkv[...]
    pack_ref[:, wide : wide + width] = wout[...]
    spread[...] = jnp.zeros_like(spread)
    spread[0 : router.shape[0], :] = router[...].astype(f32)
    for index, ref in enumerate(vectors):
        spread[VEC + index : VEC + index + 1, :] = ref[...].astype(f32)
    columns = spread[...].T
    pack_ref[:, wide + width :] = columns.astype(bf16)
    pay_ref[0:hidden] = w2[...]
    tail[...] = jnp.zeros_like(tail)
    tail[0:1, 0 : b1.shape[1]] = b1[...].astype(f32)
    copies = jnp.concatenate([b2[...].astype(f32)] * (width // part), axis=1)
    tail[1:2] = jnp.where(iota((1, width), 1) // part == spot_ref[SPOT], copies, 0.0)
    tall = hidden + TAIL
    pay_ref[hidden:tall] = tail[...].astype(bf16)
    for index in range(width // part):
        block = w1[:, index * hidden : (index + 1) * hidden]
        if hidden < width:
            block = jnp.concatenate([block, jnp.zeros((part, width - hidden), bf16)], axis=1)
        pay_ref[tall + index * part : tall + (index + 1) * part] = block


def pack_parameters(spot, w_qkv, w_out, w_router, vectors, w1, w2, b1, b2):
    part, width = w_out.shape
    hidden = w2.shape[0]
    operands = [w_qkv, w_out, w_router.T, *[v.reshape(1, part) for v in vectors], w1, w2, b1, b2]
    return pl.pallas_call(
        pack_kernel,
        grid=(1,),
        in_specs=[pl.BlockSpec(memory_space=pltpu.SMEM)] + [whole(v.shape) for v in operands],
        out_specs=[whole((part, 4 * width + LANES)), whole((hidden + TAIL + width, width))],
        out_shape=[
            jax.ShapeDtypeStruct((part, 4 * width + LANES), bf16),
            jax.ShapeDtypeStruct((hidden + TAIL + width, width), bf16),
        ],
        scratch_shapes=[pltpu.VMEM((LANES, part), f32), pltpu.VMEM((TAIL, width), f32)],
        compiler_params=params(),
        cost_estimate=cost(0.02),
        name="pack",
    )(spot, *operands)


def one_hot_rows(row, cap):
    slots = iota((cap, row.shape[1]), 0).astype(f32)
    return jnp.where(slots == row, 1.0, 0.0).astype(bf16)


def one_hot_cols(column, cap):
    slots = iota((column.shape[0], cap), 1).astype(f32)
    return jnp.where(slots == column, 1.0, 0.0).astype(bf16)


def route_kernel(place_ref, ids_ref, up_ref, hot_ref, pos_ref, *rest, cap, stride):
    outs, gathered, post_ref = rest[:-2], rest[-2], rest[-1]
    experts = post_ref.shape[0]
    images, seq, width = up_ref.shape
    step = pl.program_id(0)

    @pl.when(step == 0)
    def _():
        expert = relative_expert(place_ref[0], iota((experts, stride), 0), experts)
        before = jnp.where(iota((stride, stride), 0) < iota((stride, stride), 1), 1.0, 0.0).astype(bf16)
        carry = jnp.zeros((experts, 1), f32)
        gathered[...] = jnp.zeros_like(gathered)
        for image in range(images):
            ids = ids_ref[:, image * seq : (image + 1) * seq]
            ids = jnp.concatenate([ids, jnp.full((ids.shape[0], stride - seq), -1, i32)], axis=1)
            hit = jnp.zeros((experts, stride), jnp.bool_)
            for choice in range(ids_ref.shape[0]):
                hit = hit | (ids[choice : choice + 1] == expert)
            mask = jnp.where(hit, 1.0, 0.0)
            rank = carry + dot(mask.astype(bf16), before, NN)
            carry = carry + jnp.sum(mask, axis=1, keepdims=True)
            slot = jnp.where(hit, rank, -1.0)
            post_ref[:, image * stride : (image + 1) * stride] = slot
            padded = jnp.concatenate([slot, jnp.full((LANES - experts, stride), -1.0, f32)], axis=0)
            pos_ref[image] = padded.T
            gathered[image * stride : image * stride + seq] = up_ref[image]

    hot = one_hot_rows(post_ref[pl.ds(step, 1), :], cap)
    hot_ref[0] = hot
    made = dot(hot, gathered[...], NN).astype(bf16)
    for index in range(experts):

        @pl.when(step == index)
        def _():
            outs[index][...] = made


def route(place, ids, grad_output, experts, cap, stride):
    images, seq, width = grad_output.shape
    total = images * stride
    return pl.pallas_call(
        functools.partial(route_kernel, cap=cap, stride=stride),
        grid=(experts,),
        in_specs=[pl.BlockSpec(memory_space=pltpu.SMEM), whole(ids.shape), whole(grad_output.shape)],
        out_specs=[pl.BlockSpec((1, cap, total), lambda s: (s, 0, 0)), whole((images, stride, LANES))]
        + [whole((cap, width))] * experts,
        out_shape=[
            jax.ShapeDtypeStruct((experts, cap, total), bf16),
            jax.ShapeDtypeStruct((images, stride, LANES), f32),
        ]
        + [jax.ShapeDtypeStruct((cap, width), bf16)] * experts,
        scratch_shapes=[pltpu.VMEM((total, width), bf16), pltpu.VMEM((experts, total), f32)],
        compiler_params=params(),
        cost_estimate=cost(0.02),
        name="route",
    )(place, ids, grad_output)


def dispatch_kernel(_, hot_ref, rows_ref, *refs, cap, shifts, paired):
    pairs = [shift for shift in shifts if shift in paired]
    ups, outs = refs[: len(pairs)], refs[len(pairs) :]
    step = pl.program_id(0)
    sent = dot(hot_ref[0], rows_ref[...], NN).astype(bf16)
    for index, shift in enumerate(shifts):

        @pl.when(step == index)
        def _():
            outs[index][0:cap] = sent
            if shift in pairs:
                outs[index][cap:] = ups[pairs.index(shift)][...]


def dispatch(hot, rows, ups, shifts, paired):
    _, cap, total = hot.shape
    width = rows.shape[1]
    shapes = [((2 if shift in paired else 1) * cap, width) for shift in shifts]
    pairs = [ups[shift] for shift in shifts if shift in paired]
    outs = pl.pallas_call(
        functools.partial(dispatch_kernel, cap=cap, shifts=tuple(shifts), paired=paired),
        grid_spec=pltpu.PrefetchScalarGridSpec(
            num_scalar_prefetch=1,
            grid=(len(shifts),),
            in_specs=[pl.BlockSpec((1, cap, total), lambda s, table: (table[s], 0, 0)), whole(rows.shape)]
            + [whole((cap, width))] * len(pairs),
            out_specs=[whole(v) for v in shapes],
        ),
        out_shape=[jax.ShapeDtypeStruct(v, bf16) for v in shapes],
        compiler_params=params(),
        cost_estimate=cost(0.02),
        name="dispatch",
    )(jnp.array(shifts, i32), hot, rows, *pairs)
    return dict(zip(shifts, outs))


def forward_kernel(spots_ref, tok_ref, *rest, experts, fsdp, later):
    if later:
        pack_ref, old_peak_ref = rest[:2]
        rest = rest[-10:]
    else:
        shards_of, pack_ref = rest[:fsdp], rest[-4]
        rest = rest[-11:-4] + rest[-3:]
    qkv_ref, mixed_ref, hidden_ref, prob_ref, attn_ref, mid_ref, peak_ref, tokens, vectors, router = rest
    _, seq, width = tok_ref.shape
    rows = tokens.shape[0]
    head = width // HEADS
    step = pl.program_id(0)
    wide = 3 * width

    @pl.when(step == 0)
    def _():
        if not later:
            part = shards_of[0].shape[0]
            for index, ref in enumerate(shards_of):
                pack_ref[pl.ds(pl.multiple_of(spots_ref[HOMES + fsdp + index] * part, part), part), :] = ref[...]
        misc = pack_ref[:, wide + width :]
        vectors[...] = misc.astype(f32).T
        router[...] = dot(misc, router_order(spots_ref[0], experts), NN).astype(bf16)
        tokens[...] = jnp.zeros_like(tokens)
        peak_ref[...] = old_peak_ref[...] if later else jnp.full_like(peak_ref, NEG)

    def vector(index):
        return vectors[VEC + index : VEC + index + 1, :]

    tokens[0:seq] = tok_ref[0].astype(f32)
    residual = tokens[...]
    hat, _ = norm_stats(residual)
    normed = (hat * vector(0) + vector(1)).astype(bf16)
    projected = dot(normed, pack_ref[:, 0:wide], NN)
    qkv_ref[0, :, 0:width] = ((projected[:, 0:width] + vector(2)).astype(bf16).astype(f32) * head**-0.5).astype(
        bf16
    )
    qkv_ref[0, :, width : 2 * width] = projected[:, width : 2 * width].astype(bf16)
    qkv_ref[0, :, 2 * width :] = (projected[:, 2 * width :] + vector(3)).astype(bf16)
    lane = iota((1, LANES), 1)
    first = lane < head
    halves = (jnp.where(first, 1.0, 0.0).astype(bf16), jnp.where(first, 0.0, 1.0).astype(bf16))
    keys = jnp.where(iota((1, rows), 1) < seq, 0.0, NEG)
    valid = iota((rows, 1), 0) < seq

    def pair(index, peak):
        at = pl.multiple_of(index * LANES, LANES)
        query = qkv_ref[0, :, pl.ds(at, LANES)]
        key = qkv_ref[0, :, pl.ds(width + at, LANES)]
        value = qkv_ref[0, :, pl.ds(2 * width + at, LANES)]
        parts = []
        for half in range(2):
            scores = dot(query * halves[half], key, NT) + keys
            top = jnp.max(scores, axis=1, keepdims=True)
            weight = jnp.exp(scores - top)
            total = jnp.sum(weight, axis=1, keepdims=True)
            number = index * 2 + half
            largest = jnp.max(jnp.where(valid, top, NEG), axis=0, keepdims=True)
            peak = jnp.where(lane == number, largest, peak)
            low = (weight * (1.0 / total)).astype(bf16)
            attn_ref[0, number] = low
            parts.append(dot(low, value, NN))
        mixed_ref[0, :, pl.ds(at, LANES)] = jnp.where(first, parts[0], parts[1]).astype(bf16)
        return peak

    peak = lax.fori_loop(0, HEADS // 2, pair, jnp.full((1, LANES), NEG, f32), unroll=True)
    peak_ref[...] = jnp.maximum(peak_ref[...], peak)
    hidden = residual + dot(mixed_ref[0], pack_ref[:, wide : wide + width], NN) + vector(4)
    hidden_ref[0] = hidden
    hat, _ = norm_stats(hidden)
    mid = hat * vector(5) + vector(6)
    logits = jnp.zeros((rows, LANES), f32)
    for part in pieces(mid, 3):
        logits = logits + dot(part, router[...], NN)
    prob_ref[0] = softmax_lanes(logits, experts)
    mid_ref[0, 0:rows] = mid.astype(bf16)
    mid_ref[0, rows:] = jnp.zeros((mid_ref.shape[1] - rows, width), bf16)


def forward(spots, tokens, shards_of, old, after, at, count, experts, stride, rows):
    images, seq, width = tokens.shape
    later = old is not None
    far = pl.BlockSpec(memory_space=pl.ANY)
    shapes = [
        ((1, rows, 3 * width), bf16),
        ((1, rows, width), bf16),
        ((1, rows, width), f32),
        ((1, rows, LANES), f32),
        ((1, HEADS, rows, rows), bf16),
        ((1, stride, width), bf16),
    ]

    def image(shape):
        return pl.BlockSpec(shape, lambda i: (at + i,) + (0,) * (len(shape) - 1))

    out_specs = [image(shape) for shape, _ in shapes] + [whole((1, LANES))]
    out_shape = [jax.ShapeDtypeStruct((images,) + shape[1:], kind) for shape, kind in shapes]
    out_shape.append(jax.ShapeDtypeStruct((1, LANES), f32))
    operands = [spots, tokens]
    in_specs = [pl.BlockSpec(memory_space=pltpu.SMEM), image((1, seq, width))]
    if later:
        *arrays, peak, pack = old
        aliases = {len(operands) + 2 + index: index for index in range(len(arrays))}
        operands += [pack, peak, *arrays]
        in_specs += [whole(pack.shape), whole(peak.shape)] + [far] * len(arrays)
    else:
        aliases = {}
        packed = (width, shards_of[0].shape[1])
        operands += shards_of
        in_specs += [whole(v.shape) for v in shards_of]
        out_specs.append(whole(packed))
        out_shape.append(jax.ShapeDtypeStruct(packed, bf16))
    outputs = pl.pallas_call(
        functools.partial(forward_kernel, experts=experts, fsdp=len(shards_of), later=later),
        grid=(count,),
        in_specs=in_specs + [far] * len(after),
        out_specs=out_specs,
        out_shape=out_shape,
        scratch_shapes=[
            pltpu.VMEM((rows, width), f32),
            pltpu.VMEM((LANES, width), f32),
            pltpu.VMEM((width, LANES), bf16),
        ],
        input_output_aliases=aliases,
        compiler_params=params(),
        cost_estimate=cost(20 * count if later else 0.02),
        name="attend",
    )(*operands, *after)
    return [*outputs, pack] if later else outputs


def expert_kernel(place_ref, *refs, cap, group, first, last, experts, fsdp, split, skip):
    taken = iter(refs)

    def take(number):
        return [next(taken) for _ in range(number)]

    count = len(group)
    rows_in, ups_in = take(count), take(count)
    pays, misc = take(fsdp), next(taken)
    old = [] if first else take(3)
    take(skip)
    row_back, made_ref = take(count), next(taken)
    out1, out2, *out3 = take(4 if split else 2) if split or not last else (None, next(taken))
    rows, ups, gates, acc_row, acc_out, shift2, bias2, gated, sems, w1s, w2s, sems_w = take(12)
    step = pl.program_id(0)
    width = rows.shape[1]
    tile = w1s.shape[2]
    tall = tile + TAIL
    chunk = width // fsdp

    @pl.when(step == 0)
    def _():
        loads = []
        for index, ref in enumerate(pays):
            at = place_ref[HOMES + index]
            loads.append(pltpu.make_async_copy(ref.at[0:tall], w2s.at[at], sems_w.at[index, fsdp]))
            for block in range(fsdp):
                start = tall + block * chunk
                loads.append(
                    pltpu.make_async_copy(
                        ref.at[start : start + chunk, 0:tile],
                        w1s.at[block, pl.ds(pl.multiple_of(at * chunk, chunk), chunk)],
                        sems_w.at[index, block],
                    )
                )
        for load in loads:
            load.start()
        for index in range(count):
            rows[index * cap : (index + 1) * cap] = rows_in[index][...]
        router = dot(misc[...], router_order(place_ref[0], experts), NN).astype(bf16)
        gate = softmax_lanes(dot(rows[...], router, NN), experts)[:, 0:1]
        gates[...] = jnp.broadcast_to(gate, gates.shape)
        for index in range(count):
            part = slice(index * cap, (index + 1) * cap)
            ups[part] = (ups_in[index][...].astype(f32) * gate[part]).astype(bf16)
        acc_row[...] = jnp.zeros_like(acc_row)
        acc_out[...] = jnp.zeros_like(acc_out)
        bias2[...] = jnp.zeros_like(bias2)
        shift2[...] = jnp.sum(ups[...].astype(f32), axis=0, keepdims=True)
        for load in loads:
            load.wait()

    w1, w2 = w1s.at[step], w2s.at[step]
    tail = w2[tile:tall].astype(f32)
    bias2[...] += tail[1:2]
    x, up = rows[...], ups[...]
    value, slope = gelu_pair(dot(x, w1[...], NN) + tail[0:1, 0:tile])
    act = value
    acc_out[...] += dot(act, w2[0:tile], NN)
    pre = slope * dot(up, w2[0:tile], NT).astype(bf16)
    acc_row[...] += dot(pre, w1[...], NT)
    part1 = dot(x, pre, TN)
    part2 = dot(act, up, TN)
    shift1 = jnp.sum(pre.astype(f32), axis=0, keepdims=True)
    if tile < width:
        shift1 = jnp.concatenate([shift1, jnp.zeros((1, width - tile), f32)], axis=1)
    place = iota((TAIL, width), 0)
    sums = jnp.where(place == 0, shift1, jnp.where(place == 1, shift2[...], 0.0))
    if not first:
        part1, part2, sums = old[1][...] + part1, old[2][0, 0:tile] + part2, old[2][0, tile:] + sums
    if last:
        if tile < width:
            part1 = jnp.concatenate([part1, jnp.zeros((width, width - tile), f32)], axis=1)
        if split:
            for ref, fy in ((out1, place_ref[FY]), (out2, 1 - place_ref[FY])):

                @pl.when((step >> 1) == fy)
                def _():
                    ref[step & 1, 0:tile] = part2.astype(bf16)
                    ref[step & 1, tile:tall] = sums.astype(bf16)

            at = pl.multiple_of(step * chunk, TAIL)
            for index in range(fsdp):
                block = part1[index * chunk : (index + 1) * chunk].astype(bf16)
                for ref, fy in ((out3[0], place_ref[FY]), (out3[1], 1 - place_ref[FY])):

                    @pl.when(index // 2 == fy)
                    def _():
                        ref[index % 2, pl.ds(at, chunk), :] = block

        else:
            at = pl.multiple_of(tall + step * chunk, TAIL)
            out2[step, 0:tile] = part2.astype(bf16)
            out2[step, tile:tall] = sums.astype(bf16)
            for index in range(fsdp):
                out2[index, pl.ds(at, chunk), :] = part1[index * chunk : (index + 1) * chunk].astype(bf16)
    else:
        out1[...] = part1
        out2[0, 0:tile] = part2
        out2[0, tile:] = sums

    @pl.when(step == pl.num_programs(0) - 1)
    def _():
        copies = []
        for index, shift in enumerate(group):
            part = slice(index * cap, (index + 1) * cap)
            made = acc_out[part] + bias2[...]
            gate = gates[part, 0:1]
            gated[index] = (made * gate).astype(bf16)
            copies.append(
                pltpu.make_async_copy(gated.at[index], made_ref.at[place_ref[0] ^ shift], sems.at[index])
            )
            copies[-1].start()
            row_back[index][0:cap] = acc_row[part].astype(bf16)
            effect = jnp.sum(made * ups_in[index][...].astype(f32), axis=1, keepdims=True) * gate
            effect = jnp.concatenate([effect, jnp.zeros((width - cap, 1), f32)], axis=0)
            line = jnp.broadcast_to(effect, (width, LANES)).T[0:1]
            end = jnp.zeros((TAIL, width), f32)
            for order, piece in enumerate(pieces(line, 3)):
                end = jnp.where(place == order, piece.astype(f32), end)
            row_back[index][cap : cap + TAIL] = end.astype(bf16)
        for copy in copies:
            copy.wait()


def expert_call(spots, rows, ups, pays, pack, old, after, group, cap, experts, last):
    count = len(group)
    first = old is None
    fsdp = len(pays)
    high, width = pays[0].shape
    tall = high - width
    tile = tall - TAIL
    total = count * cap
    split = last and fsdp == 4
    column = pl.BlockSpec((width, tile), lambda h, _: (0, h))
    line = pl.BlockSpec((1, tall, width), lambda h, _: (h, 0, 0))
    far = pl.BlockSpec(memory_space=pl.ANY)
    if split:
        grads = [(2, tall, width)] * 2 + [(2, width, width)] * 2
    else:
        grads = [(fsdp, high, width)]

    operands = [spots, *rows, *ups, *pays, pack]
    aliases = {}
    if not first:
        aliases = {len(operands): count}
        operands += list(old)
    return pl.pallas_call(
        functools.partial(
            expert_kernel,
            cap=cap,
            group=group,
            first=first,
            last=last,
            experts=experts,
            fsdp=fsdp,
            split=split,
            skip=len(after),
        ),
        grid_spec=pltpu.PrefetchScalarGridSpec(
            num_scalar_prefetch=1,
            grid=(fsdp,),
            in_specs=[whole((cap, width))] * count
            + [pl.BlockSpec((cap, width), lambda h, _, at=v.shape[0] // cap - 1: (at, 0)) for v in ups]
            + [far] * fsdp
            + [pl.BlockSpec((width, LANES), lambda h, _: (0, 4 * width // LANES))]
            + ([] if first else [far, column, line])
            + [far] * len(after),
            out_specs=[whole((cap + TAIL, width))] * count
            + [far]
            + ([whole(v) for v in grads] if last else [column, line]),
            scratch_shapes=[pltpu.VMEM((total, width), bf16)] * 2
            + [pltpu.VMEM((total, LANES), f32)]
            + [pltpu.VMEM((total, width), f32)] * 2
            + [pltpu.VMEM((1, width), f32)] * 2
            + [pltpu.VMEM((count, cap, width), bf16), pltpu.SemaphoreType.DMA((count,))]
            + [pltpu.VMEM((fsdp, width, tile), bf16), pltpu.VMEM((fsdp, tall, width), bf16)]
            + [pltpu.SemaphoreType.DMA((fsdp, fsdp + 1))],
        ),
        out_shape=[jax.ShapeDtypeStruct((cap + TAIL, width), bf16)] * count
        + [jax.ShapeDtypeStruct((experts, cap, width), bf16)]
        + (
            [jax.ShapeDtypeStruct(v, bf16) for v in grads]
            if last
            else [
                jax.ShapeDtypeStruct((width, tile * fsdp), f32),
                jax.ShapeDtypeStruct((fsdp, tall, width), f32),
            ]
        ),
        input_output_aliases=aliases,
        compiler_params=params(),
        cost_estimate=cost(96),
        name="expert",
    )(*operands, *after)


def gather_back(places, backs, shifts, slot_sum, effect, cap):
    lane = iota((1, LANES), 1)
    for index, ref in zip(shifts, backs):
        hot = one_hot_cols(places[:, index : index + 1], cap)
        slot_sum = slot_sum + dot(hot, ref[0:cap], NN)
        parts = dot(hot, ref[cap : cap + TAIL, 0:cap], NT)
        effect = jnp.where(lane == index, jnp.sum(parts, axis=1, keepdims=True), effect)
    return slot_sum, effect


def returned_kernel(pos_ref, *refs, cap, shifts):
    backs, slot_ref, effect_ref = refs[: len(shifts)], refs[-2], refs[-1]
    _, rows, width = slot_ref.shape
    slot_ref[0], effect_ref[0] = gather_back(
        pos_ref[0, 0:rows, :], backs, shifts, jnp.zeros((rows, width), f32), jnp.zeros((rows, LANES), f32), cap
    )


def returned(pos, backs, shifts, rows, cap):
    images, width = pos.shape[0], backs[0].shape[1]

    def image(shape):
        return pl.BlockSpec((1,) + shape, lambda i: (i, 0, 0))

    return pl.pallas_call(
        functools.partial(returned_kernel, cap=cap, shifts=shifts),
        grid=(images,),
        in_specs=[image((pos.shape[1], LANES))] + [whole((cap + TAIL, width))] * len(backs),
        out_specs=[image((rows, width)), image((rows, LANES))],
        out_shape=[
            jax.ShapeDtypeStruct((images, rows, width), f32),
            jax.ShapeDtypeStruct((images, rows, LANES), f32),
        ],
        compiler_params=params(),
        cost_estimate=cost(100),
        name="returned",
    )(pos, *backs)


def middle_kernel(
    place_ref, up_ref, wout_ref, misc_ref, pos_ref, mixed_ref, hidden_ref, prob_ref, slot_ref, effect_ref, *rest, cap, experts
):
    backs = rest[:2]
    hidden_grad_ref, mixed_grad_ref, sums_ref, padded, vectors, router, shifts, acc_out, acc_router = rest[-9:]
    _, seq, width = up_ref.shape
    rows = padded.shape[0]
    step = pl.program_id(0)

    @pl.when(step == 0)
    def _():
        vectors[...] = misc_ref[...].astype(f32).T
        router[...] = dot(misc_ref[...], router_order(place_ref[0], experts), NN).astype(bf16)
        padded[...] = jnp.zeros_like(padded)
        shifts[...] = jnp.zeros_like(shifts)
        acc_out[...] = jnp.zeros_like(acc_out)
        acc_router[...] = jnp.zeros_like(acc_router)

    def vector(index):
        return vectors[VEC + index : VEC + index + 1, :]

    def shift(index, value):
        shifts[index : index + 1, :] += jnp.sum(value, axis=0, keepdims=True)

    slot_sum, effect = gather_back(pos_ref[0, 0:rows, :], backs, (0, 1), slot_ref[0], effect_ref[0], cap)
    prob = prob_ref[0]
    logit_grad = effect - prob * jnp.sum(effect, axis=1, keepdims=True)
    logit_parts = pieces(logit_grad, 2)
    mid_grad = slot_sum
    for part in logit_parts:
        mid_grad = mid_grad + dot(part, router[...], NT)
    padded[0:seq] = up_ref[0].astype(f32)
    hat, inverse = norm_stats(hidden_ref[0])
    mid_parts = pieces(hat * vector(5) + vector(6), 2)
    acc_router[...] += (
        dot(logit_parts[0], mid_parts[0], TN)
        + dot(logit_parts[0], mid_parts[1], TN)
        + dot(logit_parts[1], mid_parts[0], TN)
    )
    shift(5, mid_grad * hat)
    shift(6, mid_grad)
    hidden_grad = padded[...] + norm_back(mid_grad, vector(5), hat, inverse)
    hidden_grad_ref[0] = hidden_grad
    branch = hidden_grad.astype(bf16)
    shift(4, branch.astype(f32))
    acc_out[...] += dot(mixed_ref[0], branch, TN)
    mixed_grad_ref[0] = dot(branch, wout_ref[...], NT).astype(bf16)

    @pl.when(step == pl.num_programs(0) - 1)
    def _():
        sums_ref[:, 0:width] = acc_out[...]
        ordered = dot(router_order(place_ref[0], experts), acc_router[...].astype(bf16), NN)
        spare = jnp.concatenate(
            [ordered[0:VEC], shifts[...], jnp.zeros((LANES - VEC - shifts.shape[0], width), f32)], axis=0
        )
        sums_ref[:, width:] = spare.T


def middle(place, grad_output, pack, pos, saved, part_sums, backs, cap, experts):
    images, seq, width = grad_output.shape
    _, mixed, hidden, prob, _ = saved
    rows = mixed.shape[1]

    def image(shape):
        return pl.BlockSpec((1,) + shape, lambda i: (i, 0, 0))

    return pl.pallas_call(
        functools.partial(middle_kernel, cap=cap, experts=experts),
        grid=(images,),
        in_specs=[
            pl.BlockSpec(memory_space=pltpu.SMEM),
            image((seq, width)),
            pl.BlockSpec((width, width), lambda i: (0, 3)),
            pl.BlockSpec((width, LANES), lambda i: (0, 4 * width // LANES)),
            image((pos.shape[1], LANES)),
            image((rows, width)),
            image((rows, width)),
            image((rows, LANES)),
            image((rows, width)),
            image((rows, LANES)),
        ]
        + [whole((cap + TAIL, width))] * len(backs),
        out_specs=[image((rows, width)), image((rows, width)), whole((width, width + LANES))],
        out_shape=[
            jax.ShapeDtypeStruct((images, rows, width), f32),
            jax.ShapeDtypeStruct((images, rows, width), bf16),
            jax.ShapeDtypeStruct((width, width + LANES), f32),
        ],
        scratch_shapes=[
            pltpu.VMEM((rows, width), f32),
            pltpu.VMEM((LANES, width), f32),
            pltpu.VMEM((width, LANES), bf16),
            pltpu.VMEM((8, width), f32),
            pltpu.VMEM((width, width), f32),
            pltpu.VMEM((LANES, width), f32),
        ],
        compiler_params=params(),
        cost_estimate=cost(0.02),
        name="middle",
    )(place, grad_output, pack, pack, pos, mixed, hidden, prob, *part_sums, *backs)


def backward_kernel(
    spots_ref, tok_ref, qkv_ref, attn_ref, mixed_grad_ref, *rest, head_rows, members
):
    sums_ref, peak_ref = rest[:2]
    qkv_grad_ref, keep_ref, give_ref, padded, acc_qkv, columns, spare, misc = rest[-8:]
    _, seq, width = tok_ref.shape
    rows = padded.shape[0]
    head = width // HEADS
    wide = 3 * width
    step = pl.program_id(0)

    @pl.when(step == 0)
    def _():
        padded[...] = jnp.zeros_like(padded)
        acc_qkv[...] = jnp.zeros_like(acc_qkv)
        columns[...] = jnp.zeros_like(columns)

    lane = iota((1, LANES), 1)
    first = lane < head
    halves = (jnp.where(first, 1.0, 0.0).astype(bf16), jnp.where(first, 0.0, 1.0).astype(bf16))

    def pair(index, carry):
        at = pl.multiple_of(index * LANES, LANES)
        query = qkv_ref[0, :, pl.ds(at, LANES)]
        key = qkv_ref[0, :, pl.ds(width + at, LANES)]
        value = qkv_ref[0, :, pl.ds(2 * width + at, LANES)]
        up = mixed_grad_ref[0, :, pl.ds(at, LANES)]
        made = []
        for half in range(2):
            low = attn_ref[0, index * 2 + half]
            weight = low.astype(f32)
            value_grad = dot(low, up, TN)
            spread = weight * dot(up * halves[half], value, NT)
            score_grad = (spread - weight * jnp.sum(spread, axis=1, keepdims=True)).astype(bf16)
            made.append((dot(score_grad, key, NN) * head**-0.5, dot(score_grad, query, TN), value_grad))
        for index_of, (left, right) in enumerate(zip(*made)):
            qkv_grad_ref[0, :, pl.ds(index_of * width + at, LANES)] = jnp.where(first, left, right).astype(bf16)
        return carry

    lax.fori_loop(0, HEADS // 2, pair, 0, unroll=True)
    columns[...] += jnp.sum(qkv_grad_ref[0].astype(f32), axis=0, keepdims=True)
    padded[0:seq] = tok_ref[0].astype(f32)
    hat, _ = norm_stats(padded[...])
    acc_qkv[...] += dot(hat.astype(bf16), qkv_grad_ref[0], TN)
    part = keep_ref.shape[1]

    @pl.when(step == pl.num_programs(0) - 1)
    def _():
        line = iota((LANES, width), 0)
        flat = columns[...]
        grown = jnp.where(line == VEC + 2, flat[:, 0:width], 0.0)
        grown = jnp.where(line == VEC + 3, flat[:, 2 * width :], grown)
        misc[...] = sums_ref[:, width:] + grown.T
        spare[...] = jnp.zeros_like(spare)
        number = wide // LANES
        for order, piece in enumerate(pieces(flat, 3)):
            value = piece.astype(f32)
            for index in range(number):
                at = order * number + index
                spare[at : at + 1, :] = value[:, index * LANES : (index + 1) * LANES]
        if members:
            top = jnp.where(lane < HEADS, peak_ref[...], 0.0)
            rows_of = jnp.zeros((TAIL, LANES), f32)
            for order, piece in enumerate(pieces(jnp.broadcast_to(top, (TAIL, LANES)), 3)):
                move = jnp.where(iota((LANES, LANES), 1) == iota((LANES, LANES), 0) + order * HEADS, 1.0, 0.0)
                rows_of = rows_of + dot(piece, move.astype(bf16), NN)
            spare[pl.ds(head_rows + spots_ref[NUMBER], 1), :] = rows_of[0:1]
        extra = spare[...].astype(bf16)
        for fy in range(keep_ref.shape[0]):
            for ref, core in ((keep_ref, spots_ref[CORE]), (give_ref, 1 - spots_ref[CORE])):
                at = pl.multiple_of((2 * fy + core) * part, part)
                ref[fy, :, 0:wide] = acc_qkv[pl.ds(at, part), :].astype(bf16)
                ref[fy, :, wide : wide + width] = sums_ref[pl.ds(at, part), 0:width].astype(bf16)
                ref[fy, :, wide + width : wide + width + LANES] = misc[pl.ds(at, part), :].astype(bf16)
                ref[fy, :, wide + width + LANES :] = extra


def backward(spots, tokens, saved, mixed_grad, sums, peak, after, ways, part, head_rows, members):
    images, seq, width = tokens.shape
    qkv, attn = saved[0], saved[-1]
    rows = qkv.shape[1]
    wide = 4 * width + 2 * LANES

    def image(shape):
        return pl.BlockSpec((1,) + shape, lambda i: (i,) + (0,) * len(shape))

    return pl.pallas_call(
        functools.partial(backward_kernel, head_rows=head_rows, members=members),
        grid=(images,),
        in_specs=[
            pl.BlockSpec(memory_space=pltpu.SMEM),
            image((seq, width)),
            image((rows, 3 * width)),
            image((HEADS, rows, rows)),
            image((rows, width)),
            whole(sums.shape),
            whole(peak.shape),
        ]
        + [pl.BlockSpec(memory_space=pl.ANY)] * len(after),
        out_specs=[image((rows, 3 * width)), whole((ways, part, wide)), whole((ways, part, wide))],
        out_shape=[
            jax.ShapeDtypeStruct((images, rows, 3 * width), bf16),
            jax.ShapeDtypeStruct((ways, part, wide), bf16),
            jax.ShapeDtypeStruct((ways, part, wide), bf16),
        ],
        scratch_shapes=[
            pltpu.VMEM((rows, width), f32),
            pltpu.VMEM((width, 3 * width), f32),
            pltpu.VMEM((1, 3 * width), f32),
            pltpu.VMEM((part, LANES), f32),
            pltpu.VMEM((width, LANES), f32),
        ],
        compiler_params=params(),
        cost_estimate=cost(0.05),
        name="attend_back",
    )(spots, tokens, qkv, attn, mixed_grad, sums, peak, *after)


def first_kernel(tok_ref, qkv_grad_ref, wqkv_ref, misc_ref, hidden_grad_ref, grad_ref, padded, gain):
    _, seq, width = tok_ref.shape

    @pl.when(pl.program_id(0) == 0)
    def _():
        gain[...] = misc_ref[...].astype(f32).T[VEC : VEC + 1]
        padded[...] = jnp.zeros_like(padded)

    in_grad = dot(qkv_grad_ref[0], wqkv_ref[...], NT)
    padded[0:seq] = tok_ref[0].astype(f32)
    hat, inverse = norm_stats(padded[...])
    grad_ref[0] = (hidden_grad_ref[0] + norm_back(in_grad, gain[...], hat, inverse))[0:seq]


def first_norm(tokens, qkv_grad, pack, hidden_grad):
    images, seq, width = tokens.shape
    rows = qkv_grad.shape[1]

    def image(shape):
        return pl.BlockSpec((1,) + shape, lambda i: (i, 0, 0))

    return pl.pallas_call(
        first_kernel,
        grid=(images,),
        in_specs=[
            image((seq, width)),
            image((rows, 3 * width)),
            pl.BlockSpec((width, 3 * width), lambda i: (0, 0)),
            pl.BlockSpec((width, LANES), lambda i: (0, 4 * width // LANES)),
            image((rows, width)),
        ],
        out_specs=image((seq, width)),
        out_shape=jax.ShapeDtypeStruct((images, seq, width), f32),
        scratch_shapes=[pltpu.VMEM((rows, width), f32), pltpu.VMEM((1, width), f32)],
        compiler_params=params(),
        cost_estimate=cost(0.02),
        name="first_norm",
    )(tokens, qkv_grad, pack, pack, hidden_grad)


def output_kernel(place_ref, pos_ref, hidden_ref, made_ref, out_ref):
    experts, cap, _ = made_ref.shape
    seq = out_ref.shape[1]
    total = hidden_ref[0]
    places = pos_ref[0, 0 : total.shape[0], :]
    for index in range(experts):
        total = total + dot(one_hot_cols(places[:, index : index + 1], cap), made_ref[place_ref[0] ^ index], NN)
    out_ref[0] = total[0:seq].astype(bf16)


def combine_output(place, pos, hidden, made, seq):
    images, rows, width = hidden.shape

    def image(shape):
        return pl.BlockSpec((1,) + shape, lambda i: (i, 0, 0))

    return pl.pallas_call(
        output_kernel,
        grid=(images,),
        in_specs=[
            pl.BlockSpec(memory_space=pltpu.SMEM),
            image((pos.shape[1], LANES)),
            image((rows, width)),
            whole(made.shape),
        ],
        out_specs=image((seq, width)),
        out_shape=jax.ShapeDtypeStruct((images, seq, width), bf16),
        compiler_params=params(),
        cost_estimate=cost(0.02),
        name="combine",
    )(place, pos, hidden, made)


def finish_kernel(slot_ref, *refs, number, head_rows, members):
    parts, (own_ref, limit_ref, peak_ref) = refs[:number], refs[number : number + 3]
    qkv_ref, out_ref, misc_ref, clip_ref, *vec_refs, total_ref = refs[number + 3 :]
    part = own_ref.shape[0]
    for shift, ref in enumerate(parts):
        size = part // number
        total_ref[pl.ds(pl.multiple_of((slot_ref[LOW] ^ shift) * size, size), size), :] = ref[...]
    width = out_ref.shape[1]
    wide = 3 * width
    number = wide // LANES
    base = total_ref[:, 0:wide].astype(f32)
    extra = total_ref[:, wide + width + LANES :].astype(f32)
    weight = own_ref[:, 0:wide].astype(f32)
    columns = [sum(extra[k * number + i : k * number + i + 1] for k in range(3)) for i in range(number)]
    columns = jnp.concatenate(columns, axis=1)
    own = own_ref[:, wide + width :].astype(f32)
    gain, bias = own[:, VEC : VEC + 1], own[:, VEC + 1 : VEC + 2]
    qkv_ref[...] = base * gain + bias * columns
    out_ref[...] = total_ref[:, wide : wide + width].astype(f32)
    misc = total_ref[:, wide + width : wide + width + LANES].astype(f32)
    lane = iota((1, LANES), 1)
    misc = jnp.where(lane == VEC, jnp.sum(base * weight, axis=1, keepdims=True), misc)
    misc = jnp.where(lane == VEC + 1, jnp.sum(columns * weight, axis=1, keepdims=True), misc)
    misc = misc.T
    for index, ref in enumerate(vec_refs):
        ref[...] = misc[VEC + index : VEC + index + 1]
    misc_ref[...] = misc[0 : misc_ref.shape[0]]
    if members:
        move = jnp.where(
            (iota((LANES, LANES), 0) % HEADS == iota((LANES, LANES), 1)) & (iota((LANES, LANES), 0) < 3 * HEADS),
            1.0,
            0.0,
        )
        peaks = dot(total_ref[head_rows : head_rows + members, wide + width + LANES :], move.astype(bf16), NN)
        peak = jnp.max(peaks, axis=0, keepdims=True)
    else:
        peak = peak_ref[...]
    limit = jnp.concatenate([limit_ref[...].astype(f32), jnp.ones((1, LANES - HEADS), f32)], axis=1)
    root = jnp.sqrt(limit / jnp.maximum(peak, limit))
    place = iota((1, width), 1) // (width // HEADS)
    scale = jnp.zeros((1, width), f32)
    for index in range(HEADS):
        scale = jnp.where(place == index, root[:, index : index + 1], scale)
    clip_ref[:, 0:width] = (weight[:, 0:width] * scale).astype(bf16)
    clip_ref[:, width : 2 * width] = (weight[:, width : 2 * width] * scale).astype(bf16)
    clip_ref[:, 2 * width :] = own_ref[:, 2 * width : wide]


def finish(slot, total, own, limit, peak, width, experts, head_rows, members):
    part = own.shape[0]
    operands = [*total, own, limit, peak]
    shapes = [(part, 3 * width), (part, width), (experts, part), (part, 3 * width)] + [(1, part)] * 7
    return pl.pallas_call(
        functools.partial(finish_kernel, number=len(total), head_rows=head_rows, members=members),
        grid=(1,),
        in_specs=[pl.BlockSpec(memory_space=pltpu.SMEM)] + [whole(v.shape) for v in operands],
        out_specs=[whole(v) for v in shapes],
        out_shape=[jax.ShapeDtypeStruct(v, bf16 if i == 3 else f32) for i, v in enumerate(shapes)],
        scratch_shapes=[pltpu.VMEM((part, total[0].shape[1]), bf16)],
        compiler_params=params(),
        cost_estimate=cost(0.02),
        name="finish",
    )(slot, *operands)


def half_sums_kernel(high_ref, keep_ref, got_ref, *rest):
    straight_ref, crossed_ref = rest[-2:]
    for ref, core in ((straight_ref, high_ref[HIGH]), (crossed_ref, 1 - high_ref[HIGH])):
        ref[...] = (keep_ref[core].astype(f32) + got_ref[core].astype(f32)).astype(bf16)


def half_sums(high, keep, got, after, micros):
    shape = keep.shape[1:]
    return pl.pallas_call(
        half_sums_kernel,
        grid=(1,),
        in_specs=[pl.BlockSpec(memory_space=pltpu.SMEM), whole(keep.shape), whole(got.shape)]
        + [pl.BlockSpec(memory_space=pl.ANY)] * len(after),
        out_specs=[whole(shape)] * 2,
        out_shape=[jax.ShapeDtypeStruct(shape, bf16)] * 2,
        compiler_params=params(),
        cost_estimate=cost(micros),
        name="half_sums",
    )(high, keep, got, *after)


def both_halves(spot_ref, one, two, own, rows):
    straight = jnp.where(spot_ref[SAME] == 1, own[rows].astype(f32), one[rows].astype(f32))
    return straight + two[rows].astype(f32)


def home_second_kernel(spot_ref, one, two, own, _, w2_ref, b1_ref, b2_ref):
    tile, width = w2_ref.shape
    part = b2_ref.shape[1]
    w2_ref[...] = both_halves(spot_ref, one, two, own, slice(0, tile))
    edge = both_halves(spot_ref, one, two, own, slice(tile, tile + TAIL))
    b1_ref[...] = edge[0:1, 0:tile]
    b2_ref[...] = sum(
        jnp.where(spot_ref[SPOT] == index, edge[1:2, index * part : (index + 1) * part], 0.0)
        for index in range(width // part)
    )


def home_first_kernel(spot_ref, one, two, own, _, w1_ref):
    part, hidden = w1_ref.shape
    number = one.shape[0] // part
    tile = hidden // number
    for index in range(number):
        total = both_halves(spot_ref, one, two, own, slice(index * part, (index + 1) * part))
        w1_ref[:, index * tile : (index + 1) * tile] = total[:, 0:tile]


def home_sums(kernel, spot, pair, after, shapes):
    return pl.pallas_call(
        kernel,
        grid=(1,),
        in_specs=[pl.BlockSpec(memory_space=pltpu.SMEM)]
        + [whole(v.shape) for v in pair]
        + [pl.BlockSpec(memory_space=pl.ANY)],
        out_specs=[whole(v) for v in shapes],
        out_shape=[jax.ShapeDtypeStruct(v, f32) for v in shapes],
        compiler_params=params(),
        cost_estimate=cost(0.02),
        name="home_sums",
    )(spot, *pair, after)


def add_halves_kernel(fy_ref, keep_ref, got_ref, *rest):
    mine_ref, theirs_ref = rest[-2:]
    for ref, half in ((mine_ref, fy_ref[FY]), (theirs_ref, 1 - fy_ref[FY])):
        ref[...] = (keep_ref[half].astype(f32) + got_ref[half].astype(f32)).astype(bf16)


def add_halves(fy, keep, got, after):
    shape = keep.shape[1:]
    return pl.pallas_call(
        add_halves_kernel,
        grid=(1,),
        in_specs=[pl.BlockSpec(memory_space=pltpu.SMEM), whole(keep.shape), whole(got.shape)]
        + [pl.BlockSpec(memory_space=pl.ANY)] * len(after),
        out_specs=[whole(shape)] * 2,
        out_shape=[jax.ShapeDtypeStruct(shape, bf16)] * 2,
        compiler_params=params(),
        cost_estimate=cost(0.02),
        name="add_halves",
    )(fy, keep, got, *after)


def split_rows_kernel(slot_ref, mine_ref, got_ref, *refs, skip):
    outs, total = refs[skip:-1], refs[-1]
    total[...] = (mine_ref[...].astype(f32) + got_ref[...].astype(f32)).astype(bf16)
    size = outs[0].shape[0]
    for shift, ref in enumerate(outs):
        ref[...] = total[pl.ds(pl.multiple_of((slot_ref[LOW] ^ shift) * size, size), size), :]


def split_rows(slot, mine, got, after, number):
    part, wide = mine.shape
    shape = (part // number, wide)
    return pl.pallas_call(
        functools.partial(split_rows_kernel, skip=len(after)),
        grid=(1,),
        in_specs=[pl.BlockSpec(memory_space=pltpu.SMEM), whole(mine.shape), whole(got.shape)]
        + [pl.BlockSpec(memory_space=pl.ANY)] * len(after),
        out_specs=[whole(shape)] * number,
        out_shape=[jax.ShapeDtypeStruct(shape, bf16)] * number,
        scratch_shapes=[pltpu.VMEM((part, wide), bf16)],
        compiler_params=params(),
        cost_estimate=cost(0.02),
        name="split_rows",
    )(slot, mine, got, *after)


def add_parts_kernel(*refs, number):
    parts, out_ref = refs[:number], refs[-1]
    out_ref[...] = sum(ref[...].astype(f32) for ref in parts).astype(bf16)


def add_parts(parts, after=()):
    shape = parts[0].shape
    return pl.pallas_call(
        functools.partial(add_parts_kernel, number=len(parts)),
        grid=(1,),
        in_specs=[whole(shape)] * len(parts) + [pl.BlockSpec(memory_space=pl.ANY)] * len(after),
        out_specs=whole(shape),
        out_shape=jax.ShapeDtypeStruct(shape, bf16),
        compiler_params=params(),
        cost_estimate=cost(0.02),
        name="add_parts",
    )(*parts, *after)


def swap(value, axis):
    return lax.ppermute(value, axis, [(0, 1), (1, 0)])


def around(value, axis, size):
    return [value] + [
        lax.ppermute(value, axis, [((k + step) % size, k) for k in range(size)]) for step in range(1, size)
    ]


def split_sum(value, axis, size):
    if size != 2:
        return lax.psum_scatter(value, axis, scatter_dimension=0, tiled=False)
    place = lax.axis_index(axis)
    sent = lax.dynamic_index_in_dim(value, 1 - place, 0, keepdims=False)
    kept = lax.dynamic_index_in_dim(value, place, 0, keepdims=False)
    return (kept.astype(f32) + swap(sent, axis).astype(f32)).astype(value.dtype)


def exchange(value, shift, experts):
    return lax.ppermute(value, GROUP, [(k, k ^ shift) for k in range(experts)])


def shift_order(experts):
    def key(shift):
        distance = bin(shift >> 1).count("1")
        return (shift & 1, -distance, shift)

    order = sorted(range(2, experts), key=key)
    half = len(order) // 2
    return [order[:half], order[half:], [0, 1]]


STRAIGHT = [(1, 2), (2, 1)]
CROSSED = [(0, 2), (1, 0), (2, 3), (3, 1)]
BACK = [(b, a) for a, b in STRAIGHT]
BACK_CROSSED = [(b, a) for a, b in CROSSED]


def shards(
    tokens,
    ln1_gain,
    ln1_bias,
    w_qkv,
    q_bias,
    v_bias,
    w_out,
    out_bias,
    ln2_gain,
    ln2_bias,
    w_router,
    expert_w1,
    expert_b1,
    expert_w2,
    expert_b2,
    route_ids,
    clip_threshold,
    grad_output,
    *,
    experts,
    fsdp,
):
    images, seq, width = tokens.shape
    token_count = images * seq
    ways = fsdp // 2
    cap = (7 * token_count // (2 * experts) + 7) // 8 * 8
    stride = -(-seq // 256) * 256
    rows = -(-seq // 16) * 16
    part = w_qkv.shape[0]
    hidden_part = expert_w2.shape[1]
    high, low, fy, core = (lax.axis_index(name).astype(i32) for name in DEVICE)
    spot = fy * 2 + core
    homes = [((fy + step) % ways) * 2 for step in range(ways)]
    spots = jnp.stack(
        [
            low * 2 + core,
            fy,
            core,
            ((high * (experts // 2) + low) * ways + fy) * 2 + core,
            high,
            spot,
            (high == core).astype(i32),
            low,
            *[home + high for home in homes],
            *[home + 1 - high for home in homes],
            *[home + core for home in homes],
            *[home + 1 - core for home in homes],
        ]
    )

    vectors = (ln1_gain, ln1_bias, q_bias, v_bias, out_bias, ln2_gain, ln2_bias)
    own, pay = pack_parameters(
        spots, w_qkv, w_out, w_router, vectors, expert_w1[0], expert_w2[0], expert_b1, expert_b2
    )

    near = around(own, "fy", ways)
    far = [swap(own, "core")]
    straight = lax.ppermute(pay, ("hi", "core"), STRAIGHT)

    hot, pos, *ups = route(spots, route_ids.T, grad_output, experts, cap, stride)
    groups = shift_order(experts)
    near[1:], hot, ups[0] = lax.optimization_barrier((near[1:], hot, ups[0]))
    for shift in groups[0]:
        ups[shift] = exchange(ups[shift], shift, experts)
    far += [swap(value, "core") for value in near[1:]]
    early = 1
    firsts = [ups[shift] for shift in groups[0]]
    begun = list(forward(spots, tokens, near + far, None, [], 0, early, experts, stride, rows))
    pay, straight, begun[0] = lax.optimization_barrier((pay, straight, begun[0]))
    straight = jnp.where(high == core, pay, straight)
    crossed = lax.ppermute(pay, ("hi", "core"), CROSSED)
    pays = around(straight, "fy", ways)
    *saved, mid, peak, pack = forward(
        spots, tokens, [], begun, [straight], early, images - early, experts, stride, rows
    )
    mid = mid.reshape(images * stride, width)
    paired = tuple(shift for group in groups[1:] for shift in group)
    sent = dispatch(hot, mid, ups, groups[0], paired)
    sent.update(dispatch(hot, mid, ups, [shift for group in groups[1:] for shift in group], paired))
    ready = [sent[shift] for shift in groups[0]]
    crossed, ready, firsts, *pays[1:] = lax.optimization_barrier((crossed, ready, firsts, *pays[1:]))
    sent.update(zip(groups[0], ready))
    for shift, value in zip(groups[0], firsts):
        ups[shift] = value
    pays += around(crossed, "fy", ways)

    arrived = {}

    def send(number, after):
        pending, after = lax.optimization_barrier(([sent[shift] for shift in groups[number]], after))
        for shift, value in zip(groups[number], pending):
            arrived[shift] = value if shift == 0 else exchange(value, shift, experts)
        return after

    send(0, ())
    first = send(1, [arrived[shift] for shift in groups[0]])
    arrived.update(zip(groups[0], first))
    old, after = None, []
    backs = {}
    for number, group in enumerate(groups):
        result = expert_call(
            spots,
            [arrived[shift] for shift in group],
            [arrived[shift] if shift in paired else ups[shift] for shift in group],
            pays,
            pack,
            old,
            after,
            group,
            cap,
            experts,
            number == len(groups) - 1,
        )
        old = result[len(group) :]
        after = [backs[shift] for shift in groups[number - 1]] if number else []
        out = result[: len(group)]
        if number + 2 < len(groups):
            out = send(number + 2, out)
        for at, shift in enumerate(group):
            backs[shift] = out[at] if shift == 0 else exchange(out[at], shift, experts)
    backs = [backs[shift] for shift in range(experts)]
    made, *grad = old
    made = lax.all_to_all(made, GROUP, split_axis=0, concat_axis=0, tiled=True)

    shifts = tuple(range(2, experts))
    part_sums = returned(pos, backs[2:], shifts, rows, cap)
    hidden_grad, mixed_grad, sums = middle(
        spots, grad_output, pack, pos, saved, part_sums, backs[:2], cap, experts
    )
    head_rows = 3 * (3 * width // LANES) + 4
    devices = 2 * experts // 2 * fsdp
    members = devices if head_rows + devices <= part else 0

    def homeward(straight, crossed):
        return [
            lax.ppermute(straight, ("hi", "core"), BACK),
            lax.ppermute(crossed, ("hi", "core"), BACK_CROSSED),
            straight,
        ]

    if len(grad) == 4:
        sums_two = list(half_sums(spots, grad[0], swap(grad[1], "fy"), [sums], 0.02))
        home_two = homeward(*sums_two)
        grad[3], sums_two[0] = lax.optimization_barrier((grad[3], sums_two[0]))
        got_one = swap(grad[3], "fy")
    else:
        half = split_sum(grad[0].reshape((ways, 2) + grad[0].shape[1:]), "fy", ways)
        home = homeward(*(lax.dynamic_index_in_dim(half, k, 0, keepdims=False) for k in (high, 1 - high)))
        tall = hidden_part + TAIL
        home_two, home_one = [v[:tall] for v in home], [v[tall:] for v in home]
    qkv_grad, keep, give = backward(
        spots, tokens, saved, mixed_grad, sums, peak, [], ways, part, head_rows, members
    )

    got = swap(give, "core")
    after = []
    if len(grad) == 4:
        after = half_sums(spots, grad[2], got_one, home_two[:2], 40)
        home_one = homeward(*after)
    output = combine_output(spots, pos, saved[2], made, seq)
    near_by = experts // 2
    if ways == 2 and part % (TAIL * near_by) == 0:

        def spread(values):
            return [
                value if k == 0 else lax.ppermute(value, "lo", [(j, j ^ k) for j in range(near_by)])
                for k, value in enumerate(values)
            ]

        mine, theirs = add_halves(spots, keep, got, after)
        theirs, qkv_grad = lax.optimization_barrier((theirs, qkv_grad))
        input_grad = first_norm(tokens, qkv_grad, pack, hidden_grad)
        parts = split_rows(spots, mine, swap(theirs, "fy"), [input_grad, output, *home_one[:2]], near_by)
        total = add_parts(spread(parts))
        shapes = [(hidden_part, width), (1, hidden_part), (1, part)]
        grad_w2, grad_b1, grad_b2 = home_sums(home_second_kernel, spots, home_two, total, shapes)
        shapes = [(part, hidden_part * fsdp)]
        (grad_w1,) = home_sums(home_first_kernel, spots, home_one, total, shapes)
        total = add_parts([total, swap(total, "hi")], [grad_w2, grad_w1])
        total = spread([total] * near_by)
    else:
        sums = split_sum((keep.astype(f32) + got.astype(f32)).astype(bf16), "fy", ways)
        total = [lax.psum(sums, ("hi", "lo"))]
        shapes = [(hidden_part, width), (1, hidden_part), (1, part)]
        grad_w2, grad_b1, grad_b2 = home_sums(home_second_kernel, spots, home_two, total[0], shapes)
        shapes = [(part, hidden_part * fsdp)]
        (grad_w1,) = home_sums(home_first_kernel, spots, home_one, total[0], shapes)
        input_grad = first_norm(tokens, qkv_grad, pack, hidden_grad)
    if not members:
        peak = jnp.max(lax.all_gather(peak, DEVICE, axis=0, tiled=True), axis=0, keepdims=True)
    limit = clip_threshold.reshape(1, HEADS)
    grad_qkv, grad_out, grad_router, clipped, *grads = finish(
        spots, total, own, limit, peak, width, experts, head_rows, members
    )
    grads = [v.reshape(part) for v in grads]
    return (
        output,
        input_grad,
        grads[0],
        grads[1],
        grad_qkv,
        grads[2],
        grads[3],
        grad_out,
        grads[4],
        grads[5],
        grads[6],
        grad_router.T,
        grad_w1[None],
        grad_b1,
        grad_w2[None],
        grad_b2,
        clipped,
    )


def solution(mesh):
    experts, fsdp = mesh.shape["expert"], mesh.shape["fsdp"]
    inner = Mesh(mesh.devices.reshape(2, experts // 2, fsdp // 2, 2), DEVICE)
    token, row, expert = P(DEVICE, None, None), ("fy", "core"), ("hi", "lo")
    vector, matrix = P(row), P(row, None)
    return jax.shard_map(
        functools.partial(shards, experts=experts, fsdp=fsdp),
        mesh=inner,
        in_specs=(
            token,
            vector,
            vector,
            matrix,
            vector,
            vector,
            matrix,
            vector,
            vector,
            vector,
            matrix,
            P(expert, row, None),
            P(expert, row),
            P(expert, row, None),
            P(expert, row),
            P(DEVICE, None),
            P(),
            token,
        ),
        out_specs=(
            token,
            token,
            vector,
            vector,
            matrix,
            vector,
            vector,
            matrix,
            vector,
            vector,
            vector,
            matrix,
            P(expert, row, None),
            P(expert, row),
            P(expert, row, None),
            P(expert, row),
            matrix,
        ),
        check_vma=False,
    )
```

```python
import functools

import jax
import jax.numpy as jnp
from jax import lax
from jax.experimental import pallas as pl
from jax.experimental.pallas import tpu as pltpu
from jax.sharding import Mesh
from jax.sharding import PartitionSpec as P

HEADS = 8
EPS = 1e-06
LANES = 128
VEC = 64
TAIL = 16
NEG = -1e30
f32 = jnp.float32
bf16 = jnp.bfloat16
i32 = jnp.int32
NN = (((1,), (0,)), ((), ()))
NT = (((1,), (1,)), ((), ()))
TN = (((0,), (0,)), ((), ()))
DEVICE = ("hi", "lo", "fy", "core")
GROUP = ("lo", "core")
PLACE, FY, CORE, NUMBER, HIGH, SPOT, SAME, LOW, HOMES = range(9)
VMEM_LIMIT = 64 << 20


def dot(a, b, dims):
    return lax.dot_general(a, b, dims, preferred_element_type=f32)


def pieces(value, count):
    parts = []
    for _ in range(count):
        part = value.astype(bf16)
        parts.append(part)
        value = value - part.astype(f32)
    return parts


def iota(shape, axis):
    return lax.broadcasted_iota(i32, shape, axis)


def relative_expert(place, shift, experts):
    other = jnp.bitwise_xor(place, shift)
    return (other & 1) * (experts // 2) + (other >> 1)


def router_order(place, experts):
    row, col = iota((LANES, LANES), 0), iota((LANES, LANES), 1)
    return jnp.where((row == relative_expert(place, col, experts)) & (col < experts), 1.0, 0.0).astype(bf16)


def norm_stats(matrix):
    centred = matrix - jnp.mean(matrix, axis=1, keepdims=True)
    inverse = lax.rsqrt(jnp.mean(centred * centred, axis=1, keepdims=True) + EPS)
    return centred * inverse, inverse


def norm_back(upstream, gain, hat, inverse):
    scaled = upstream * gain
    spread = (
        scaled
        - jnp.mean(scaled, axis=1, keepdims=True)
        - hat * jnp.mean(scaled * hat, axis=1, keepdims=True)
    )
    return spread * inverse


def softmax_lanes(logits, experts):
    logits = jnp.where(iota(logits.shape, 1) < experts, logits, NEG)
    top = jnp.max(logits, axis=1, keepdims=True)
    weight = jnp.exp(logits - top)
    return weight / jnp.sum(weight, axis=1, keepdims=True)


def gelu_pair(value):
    def low(number):
        return jnp.asarray(number, bf16)

    value = value.astype(bf16)
    bell = jnp.exp(value * value * low(-0.5))
    t = low(1.0) / (low(1.0) + jnp.abs(value) * low(0.3275911 * 0.7071067811865476))
    poly = low(0.7107068705) + t * (low(-0.7265760135) + t * low(0.5307027145))
    poly = t * (low(0.127414796) + t * (low(-0.142248368) + t * poly))
    lower = poly * bell
    phi = jnp.where(value >= low(0.0), low(1.0) - lower, lower)
    return value * phi, phi + value * (bell * low(0.3989422804014327))


def whole(shape):
    return pl.BlockSpec(shape, lambda *_: (0,) * len(shape))


def params(**extra):
    return pltpu.CompilerParams(vmem_limit_bytes=VMEM_LIMIT, **extra)


def cost(micros):
    return pl.CostEstimate(flops=int(micros * 1e9), bytes_accessed=0, transcendentals=0)


def pack_kernel(spot_ref, wqkv, wout, router, *rest):
    vectors, (w1, w2, b1, b2, pack_ref, pay_ref, spread, tail) = rest[:-8], rest[-8:]
    part, wide = wqkv.shape
    width, hidden = wout.shape[1], w2.shape[0]
    pack_ref[:, 0:wide] = wqkv[...]
    pack_ref[:, wide : wide + width] = wout[...]
    spread[...] = jnp.zeros_like(spread)
    spread[0 : router.shape[0], :] = router[...].astype(f32)
    for index, ref in enumerate(vectors):
        spread[VEC + index : VEC + index + 1, :] = ref[...].astype(f32)
    columns = spread[...].T
    pack_ref[:, wide + width :] = columns.astype(bf16)
    pay_ref[0:hidden] = w2[...]
    tail[...] = jnp.zeros_like(tail)
    tail[0:1, 0 : b1.shape[1]] = b1[...].astype(f32)
    copies = jnp.concatenate([b2[...].astype(f32)] * (width // part), axis=1)
    tail[1:2] = jnp.where(iota((1, width), 1) // part == spot_ref[SPOT], copies, 0.0)
    tall = hidden + TAIL
    pay_ref[hidden:tall] = tail[...].astype(bf16)
    for index in range(width // part):
        block = w1[:, index * hidden : (index + 1) * hidden]
        if hidden < width:
            block = jnp.concatenate([block, jnp.zeros((part, width - hidden), bf16)], axis=1)
        pay_ref[tall + index * part : tall + (index + 1) * part] = block


def pack_parameters(spot, w_qkv, w_out, w_router, vectors, w1, w2, b1, b2):
    part, width = w_out.shape
    hidden = w2.shape[0]
    operands = [w_qkv, w_out, w_router.T, *[v.reshape(1, part) for v in vectors], w1, w2, b1, b2]
    return pl.pallas_call(
        pack_kernel,
        grid=(1,),
        in_specs=[pl.BlockSpec(memory_space=pltpu.SMEM)] + [whole(v.shape) for v in operands],
        out_specs=[whole((part, 4 * width + LANES)), whole((hidden + TAIL + width, width))],
        out_shape=[
            jax.ShapeDtypeStruct((part, 4 * width + LANES), bf16),
            jax.ShapeDtypeStruct((hidden + TAIL + width, width), bf16),
        ],
        scratch_shapes=[pltpu.VMEM((LANES, part), f32), pltpu.VMEM((TAIL, width), f32)],
        compiler_params=params(),
        cost_estimate=cost(0.02),
        name="pack",
    )(spot, *operands)


def one_hot_rows(row, cap):
    slots = iota((cap, row.shape[1]), 0).astype(f32)
    return jnp.where(slots == row, 1.0, 0.0).astype(bf16)


def one_hot_cols(column, cap):
    slots = iota((column.shape[0], cap), 1).astype(f32)
    return jnp.where(slots == column, 1.0, 0.0).astype(bf16)


def listed(shifts):
    step, shift = pl.program_id(0), shifts[0]
    for index, value in enumerate(shifts[1:]):
        shift = jnp.where(step > index, value, shift)
    return shift


def route_kernel(place_ref, ids_ref, up_ref, hot_ref, pos_ref, post_ref, *rest, cap, stride, shifts):
    outs, gathered = rest[:-1], rest[-1]
    experts = post_ref.shape[0]
    images, seq, width = up_ref.shape
    step = pl.program_id(0)

    @pl.when(step == 0)
    def _():
        expert = relative_expert(place_ref[0], iota((experts, stride), 0), experts)
        before = jnp.where(iota((stride, stride), 0) < iota((stride, stride), 1), 1.0, 0.0).astype(bf16)
        carry = jnp.zeros((experts, 1), f32)
        gathered[...] = jnp.zeros_like(gathered)
        for image in range(images):
            ids = ids_ref[:, image * seq : (image + 1) * seq]
            ids = jnp.concatenate([ids, jnp.full((ids.shape[0], stride - seq), -1, i32)], axis=1)
            hit = jnp.zeros((experts, stride), jnp.bool_)
            for choice in range(ids_ref.shape[0]):
                hit = hit | (ids[choice : choice + 1] == expert)
            mask = jnp.where(hit, 1.0, 0.0)
            rank = carry + dot(mask.astype(bf16), before, NN)
            carry = carry + jnp.sum(mask, axis=1, keepdims=True)
            slot = jnp.where(hit, rank, -1.0)
            post_ref[:, image * stride : (image + 1) * stride] = slot
            padded = jnp.concatenate([slot, jnp.full((LANES - experts, stride), -1.0, f32)], axis=0)
            pos_ref[image] = padded.T
            gathered[image * stride : image * stride + seq] = up_ref[image]

    hot = one_hot_rows(post_ref[pl.ds(listed(shifts), 1), :], cap)
    hot_ref[0] = hot
    made = dot(hot, gathered[...], NN).astype(bf16)
    for index in range(len(outs)):

        @pl.when(step == index)
        def _():
            outs[index][...] = made


def route(place, ids, grad_output, shifts, experts, cap, stride):
    images, seq, width = grad_output.shape
    total = images * stride
    count = len(shifts)
    return pl.pallas_call(
        functools.partial(route_kernel, cap=cap, stride=stride, shifts=tuple(shifts)),
        grid=(count,),
        in_specs=[pl.BlockSpec(memory_space=pltpu.SMEM), whole(ids.shape), whole(grad_output.shape)],
        out_specs=[
            pl.BlockSpec((1, cap, total), lambda s: (s, 0, 0)),
            whole((images, stride, LANES)),
            whole((experts, total)),
        ]
        + [whole((cap, width))] * count,
        out_shape=[
            jax.ShapeDtypeStruct((count, cap, total), bf16),
            jax.ShapeDtypeStruct((images, stride, LANES), f32),
            jax.ShapeDtypeStruct((experts, total), f32),
        ]
        + [jax.ShapeDtypeStruct((cap, width), bf16)] * count,
        scratch_shapes=[pltpu.VMEM((total, width), bf16)],
        compiler_params=params(),
        cost_estimate=cost(0.02),
        name="route",
    )(place, ids, grad_output)


def dispatch_kernel(hot_ref, rows_ref, *outs):
    sent = dot(hot_ref[0], rows_ref[...], NN).astype(bf16)
    for index, ref in enumerate(outs):

        @pl.when(pl.program_id(0) == index)
        def _():
            ref[...] = sent


def dispatch(hot, rows):
    count, cap, total = hot.shape
    width = rows.shape[1]
    return pl.pallas_call(
        dispatch_kernel,
        grid=(count,),
        in_specs=[pl.BlockSpec((1, cap, total), lambda s: (s, 0, 0)), whole(rows.shape)],
        out_specs=[whole((cap, width))] * count,
        out_shape=[jax.ShapeDtypeStruct((cap, width), bf16)] * count,
        compiler_params=params(),
        cost_estimate=cost(0.02),
        name="dispatch",
    )(hot, rows)


def dispatch_both_kernel(post_ref, rows_ref, up_ref, *rest, cap, stride, shifts):
    outs, gathered = rest[-1 - len(shifts) : -1], rest[-1]
    images, seq, width = up_ref.shape
    step = pl.program_id(0)

    @pl.when(step == 0)
    def _():
        gathered[...] = jnp.zeros_like(gathered)
        for image in range(images):
            gathered[image * stride : image * stride + seq] = up_ref[image]

    hot = one_hot_rows(post_ref[pl.ds(listed(shifts), 1), :], cap)
    sent = dot(hot, rows_ref[...], NN).astype(bf16)
    up = dot(hot, gathered[...], NN).astype(bf16)
    for index, ref in enumerate(outs):

        @pl.when(step == index)
        def _():
            ref[0:cap] = sent
            ref[cap:] = up


def dispatch_both(post, rows, grad_output, after, shifts, cap, stride):
    width = rows.shape[1]
    shape = (2 * cap, width)
    return pl.pallas_call(
        functools.partial(dispatch_both_kernel, cap=cap, stride=stride, shifts=tuple(shifts)),
        grid=(len(shifts),),
        in_specs=[whole(post.shape), whole(rows.shape), whole(grad_output.shape)]
        + [pl.BlockSpec(memory_space=pl.ANY)] * len(after),
        out_specs=[whole(shape)] * len(shifts),
        out_shape=[jax.ShapeDtypeStruct(shape, bf16)] * len(shifts),
        scratch_shapes=[pltpu.VMEM(rows.shape, bf16)],
        compiler_params=params(),
        cost_estimate=cost(40),
        name="dispatch",
    )(post, rows, grad_output, *after)


def forward_kernel(spots_ref, tok_ref, *rest, experts, fsdp, later):
    if later:
        pack_ref, old_peak_ref = rest[:2]
        rest = rest[-10:]
    else:
        shards_of, pack_ref = rest[:fsdp], rest[-4]
        rest = rest[-11:-4] + rest[-3:]
    qkv_ref, mixed_ref, hidden_ref, prob_ref, attn_ref, mid_ref, peak_ref, tokens, vectors, router = rest
    _, seq, width = tok_ref.shape
    rows = tokens.shape[0]
    head = width // HEADS
    step = pl.program_id(0)
    wide = 3 * width

    @pl.when(step == 0)
    def _():
        if not later:
            part = shards_of[0].shape[0]
            for index, ref in enumerate(shards_of):
                pack_ref[pl.ds(pl.multiple_of(spots_ref[HOMES + fsdp + index] * part, part), part), :] = ref[...]
        misc = pack_ref[:, wide + width :]
        vectors[...] = misc.astype(f32).T
        router[...] = dot(misc, router_order(spots_ref[0], experts), NN).astype(bf16)
        tokens[...] = jnp.zeros_like(tokens)
        peak_ref[...] = old_peak_ref[...] if later else jnp.full_like(peak_ref, NEG)

    def vector(index):
        return vectors[VEC + index : VEC + index + 1, :]

    tokens[0:seq] = tok_ref[0].astype(f32)
    residual = tokens[...]
    hat, _ = norm_stats(residual)
    normed = (hat * vector(0) + vector(1)).astype(bf16)
    projected = dot(normed, pack_ref[:, 0:wide], NN)
    qkv_ref[0, :, 0:width] = ((projected[:, 0:width] + vector(2)).astype(bf16).astype(f32) * head**-0.5).astype(
        bf16
    )
    qkv_ref[0, :, width : 2 * width] = projected[:, width : 2 * width].astype(bf16)
    qkv_ref[0, :, 2 * width :] = (projected[:, 2 * width :] + vector(3)).astype(bf16)
    lane = iota((1, LANES), 1)
    first = lane < head
    halves = (jnp.where(first, 1.0, 0.0).astype(bf16), jnp.where(first, 0.0, 1.0).astype(bf16))
    keys = jnp.where(iota((1, rows), 1) < seq, 0.0, NEG)
    valid = iota((rows, 1), 0) < seq

    def pair(index, peak):
        at = pl.multiple_of(index * LANES, LANES)
        query = qkv_ref[0, :, pl.ds(at, LANES)]
        key = qkv_ref[0, :, pl.ds(width + at, LANES)]
        value = qkv_ref[0, :, pl.ds(2 * width + at, LANES)]
        parts = []
        for half in range(2):
            scores = dot(query * halves[half], key, NT) + keys
            top = jnp.max(scores, axis=1, keepdims=True)
            weight = jnp.exp(scores - top)
            total = jnp.sum(weight, axis=1, keepdims=True)
            number = index * 2 + half
            largest = jnp.max(jnp.where(valid, top, NEG), axis=0, keepdims=True)
            peak = jnp.where(lane == number, largest, peak)
            low = (weight * (1.0 / total)).astype(bf16)
            attn_ref[0, number] = low
            parts.append(dot(low, value, NN))
        mixed_ref[0, :, pl.ds(at, LANES)] = jnp.where(first, parts[0], parts[1]).astype(bf16)
        return peak

    peak = lax.fori_loop(0, HEADS // 2, pair, jnp.full((1, LANES), NEG, f32), unroll=later)
    peak_ref[...] = jnp.maximum(peak_ref[...], peak)
    hidden = residual + dot(mixed_ref[0], pack_ref[:, wide : wide + width], NN) + vector(4)
    hidden_ref[0] = hidden
    hat, _ = norm_stats(hidden)
    mid = hat * vector(5) + vector(6)
    logits = jnp.zeros((rows, LANES), f32)
    for part in pieces(mid, 3):
        logits = logits + dot(part, router[...], NN)
    prob_ref[0] = softmax_lanes(logits, experts)
    mid_ref[0, 0:rows] = mid.astype(bf16)
    mid_ref[0, rows:] = jnp.zeros((mid_ref.shape[1] - rows, width), bf16)


def forward(spots, tokens, shards_of, old, after, at, count, experts, stride, rows):
    images, seq, width = tokens.shape
    later = old is not None
    far = pl.BlockSpec(memory_space=pl.ANY)
    shapes = [
        ((1, rows, 3 * width), bf16),
        ((1, rows, width), bf16),
        ((1, rows, width), f32),
        ((1, rows, LANES), f32),
        ((1, HEADS, rows, rows), bf16),
        ((1, stride, width), bf16),
    ]

    def image(shape):
        return pl.BlockSpec(shape, lambda i: (at + i,) + (0,) * (len(shape) - 1))

    out_specs = [image(shape) for shape, _ in shapes] + [whole((1, LANES))]
    out_shape = [jax.ShapeDtypeStruct((images,) + shape[1:], kind) for shape, kind in shapes]
    out_shape.append(jax.ShapeDtypeStruct((1, LANES), f32))
    operands = [spots, tokens]
    in_specs = [pl.BlockSpec(memory_space=pltpu.SMEM), image((1, seq, width))]
    if later:
        *arrays, peak, pack = old
        aliases = {len(operands) + 2 + index: index for index in range(len(arrays))}
        operands += [pack, peak, *arrays]
        in_specs += [whole(pack.shape), whole(peak.shape)] + [far] * len(arrays)
    else:
        aliases = {}
        packed = (width, shards_of[0].shape[1])
        operands += shards_of
        in_specs += [whole(v.shape) for v in shards_of]
        out_specs.append(whole(packed))
        out_shape.append(jax.ShapeDtypeStruct(packed, bf16))
    outputs = pl.pallas_call(
        functools.partial(forward_kernel, experts=experts, fsdp=len(shards_of), later=later),
        grid=(count,),
        in_specs=in_specs + [far] * len(after),
        out_specs=out_specs,
        out_shape=out_shape,
        scratch_shapes=[
            pltpu.VMEM((rows, width), f32),
            pltpu.VMEM((LANES, width), f32),
            pltpu.VMEM((width, LANES), bf16),
        ],
        input_output_aliases=aliases,
        compiler_params=params(),
        cost_estimate=cost(20 * count if later else 0.02),
        name="attend",
    )(*operands, *after)
    return [*outputs, pack] if later else outputs


def expert_kernel(place_ref, *refs, cap, group, first, last, experts, fsdp, split, skip):
    taken = iter(refs)

    def take(number):
        return [next(taken) for _ in range(number)]

    count = len(group)
    rows_in, ups_in = take(count), take(count)
    pays, misc = take(fsdp), next(taken)
    old = [] if first else take(3)
    take(skip)
    row_back, made_ref = take(count), next(taken)
    out1, out2, *out3 = take(4 if split else 2) if split or not last else (None, next(taken))
    rows, ups, gates, acc_row, acc_out, shift2, bias2, gated, sems, w1s, w2s, sems_w = take(12)
    step = pl.program_id(0)
    width = rows.shape[1]
    tile = w1s.shape[2]
    tall = tile + TAIL
    chunk = width // fsdp

    @pl.when(step == 0)
    def _():
        loads = []
        for index, ref in enumerate(pays):
            at = place_ref[HOMES + index]
            loads.append(pltpu.make_async_copy(ref.at[0:tall], w2s.at[at], sems_w.at[index, fsdp]))
            for block in range(fsdp):
                start = tall + block * chunk
                loads.append(
                    pltpu.make_async_copy(
                        ref.at[start : start + chunk, 0:tile],
                        w1s.at[block, pl.ds(pl.multiple_of(at * chunk, chunk), chunk)],
                        sems_w.at[index, block],
                    )
                )
        for load in loads:
            load.start()
        for index in range(count):
            rows[index * cap : (index + 1) * cap] = rows_in[index][...]
        router = dot(misc[...], router_order(place_ref[0], experts), NN).astype(bf16)
        gate = softmax_lanes(dot(rows[...], router, NN), experts)[:, 0:1]
        gates[...] = jnp.broadcast_to(gate, gates.shape)
        for index in range(count):
            part = slice(index * cap, (index + 1) * cap)
            ups[part] = (ups_in[index][...].astype(f32) * gate[part]).astype(bf16)
        acc_row[...] = jnp.zeros_like(acc_row)
        acc_out[...] = jnp.zeros_like(acc_out)
        bias2[...] = jnp.zeros_like(bias2)
        shift2[...] = jnp.sum(ups[...].astype(f32), axis=0, keepdims=True)
        for load in loads:
            load.wait()

    w1, w2 = w1s.at[step], w2s.at[step]
    tail = w2[tile:tall].astype(f32)
    bias2[...] += tail[1:2]
    x, up = rows[...], ups[...]
    value, slope = gelu_pair(dot(x, w1[...], NN) + tail[0:1, 0:tile])
    act = value
    acc_out[...] += dot(act, w2[0:tile], NN)
    pre = slope * dot(up, w2[0:tile], NT).astype(bf16)
    acc_row[...] += dot(pre, w1[...], NT)
    part1 = dot(x, pre, TN)
    part2 = dot(act, up, TN)
    shift1 = jnp.sum(pre.astype(f32), axis=0, keepdims=True)
    if tile < width:
        shift1 = jnp.concatenate([shift1, jnp.zeros((1, width - tile), f32)], axis=1)
    place = iota((TAIL, width), 0)
    sums = jnp.where(place == 0, shift1, jnp.where(place == 1, shift2[...], 0.0))
    if not first:
        part1, part2, sums = old[1][...] + part1, old[2][0, 0:tile] + part2, old[2][0, tile:] + sums
    if last:
        if tile < width:
            part1 = jnp.concatenate([part1, jnp.zeros((width, width - tile), f32)], axis=1)
        if split:
            for ref, fy in ((out1, place_ref[FY]), (out2, 1 - place_ref[FY])):

                @pl.when((step >> 1) == fy)
                def _():
                    ref[step & 1, 0:tile] = part2.astype(bf16)
                    ref[step & 1, tile:tall] = sums.astype(bf16)

            at = pl.multiple_of(step * chunk, TAIL)
            for index in range(fsdp):
                block = part1[index * chunk : (index + 1) * chunk].astype(bf16)
                for ref, fy in ((out3[0], place_ref[FY]), (out3[1], 1 - place_ref[FY])):

                    @pl.when(index // 2 == fy)
                    def _():
                        ref[index % 2, pl.ds(at, chunk), :] = block

        else:
            at = pl.multiple_of(tall + step * chunk, TAIL)
            out2[step, 0:tile] = part2.astype(bf16)
            out2[step, tile:tall] = sums.astype(bf16)
            for index in range(fsdp):
                out2[index, pl.ds(at, chunk), :] = part1[index * chunk : (index + 1) * chunk].astype(bf16)
    else:
        out1[...] = part1
        out2[0, 0:tile] = part2
        out2[0, tile:] = sums

    @pl.when(step == pl.num_programs(0) - 1)
    def _():
        copies = []
        for index, shift in enumerate(group):
            part = slice(index * cap, (index + 1) * cap)
            made = acc_out[part] + bias2[...]
            gate = gates[part, 0:1]
            gated[index] = (made * gate).astype(bf16)
            copies.append(
                pltpu.make_async_copy(gated.at[index], made_ref.at[place_ref[0] ^ shift], sems.at[index])
            )
            copies[-1].start()
            row_back[index][0:cap] = acc_row[part].astype(bf16)
            effect = jnp.sum(made * ups_in[index][...].astype(f32), axis=1, keepdims=True) * gate
            effect = jnp.concatenate([effect, jnp.zeros((width - cap, 1), f32)], axis=0)
            line = jnp.broadcast_to(effect, (width, LANES)).T[0:1]
            end = jnp.zeros((TAIL, width), f32)
            for order, piece in enumerate(pieces(line, 3)):
                end = jnp.where(place == order, piece.astype(f32), end)
            row_back[index][cap : cap + TAIL] = end.astype(bf16)
        for copy in copies:
            copy.wait()


def expert_call(spots, rows, ups, pays, pack, old, after, group, cap, experts, last):
    count = len(group)
    first = old is None
    fsdp = len(pays)
    high, width = pays[0].shape
    tall = high - width
    tile = tall - TAIL
    total = count * cap
    split = last and fsdp == 4
    column = pl.BlockSpec((width, tile), lambda h, _: (0, h))
    line = pl.BlockSpec((1, tall, width), lambda h, _: (h, 0, 0))
    far = pl.BlockSpec(memory_space=pl.ANY)
    if split:
        grads = [(2, tall, width)] * 2 + [(2, width, width)] * 2
    else:
        grads = [(fsdp, high, width)]

    operands = [spots, *rows, *ups, *pays, pack]
    aliases = {}
    if not first:
        aliases = {len(operands): count}
        operands += list(old)
    return pl.pallas_call(
        functools.partial(
            expert_kernel,
            cap=cap,
            group=group,
            first=first,
            last=last,
            experts=experts,
            fsdp=fsdp,
            split=split,
            skip=len(after),
        ),
        grid_spec=pltpu.PrefetchScalarGridSpec(
            num_scalar_prefetch=1,
            grid=(fsdp,),
            in_specs=[whole((cap, width))] * count
            + [pl.BlockSpec((cap, width), lambda h, _, at=v.shape[0] // cap - 1: (at, 0)) for v in ups]
            + [far] * fsdp
            + [pl.BlockSpec((width, LANES), lambda h, _: (0, 4 * width // LANES))]
            + ([] if first else [far, column, line])
            + [far] * len(after),
            out_specs=[whole((cap + TAIL, width))] * count
            + [far]
            + ([whole(v) for v in grads] if last else [column, line]),
            scratch_shapes=[pltpu.VMEM((total, width), bf16)] * 2
            + [pltpu.VMEM((total, LANES), f32)]
            + [pltpu.VMEM((total, width), f32)] * 2
            + [pltpu.VMEM((1, width), f32)] * 2
            + [pltpu.VMEM((count, cap, width), bf16), pltpu.SemaphoreType.DMA((count,))]
            + [pltpu.VMEM((fsdp, width, tile), bf16), pltpu.VMEM((fsdp, tall, width), bf16)]
            + [pltpu.SemaphoreType.DMA((fsdp, fsdp + 1))],
        ),
        out_shape=[jax.ShapeDtypeStruct((cap + TAIL, width), bf16)] * count
        + [jax.ShapeDtypeStruct((experts, cap, width), bf16)]
        + (
            [jax.ShapeDtypeStruct(v, bf16) for v in grads]
            if last
            else [
                jax.ShapeDtypeStruct((width, tile * fsdp), f32),
                jax.ShapeDtypeStruct((fsdp, tall, width), f32),
            ]
        ),
        input_output_aliases=aliases,
        compiler_params=params(),
        cost_estimate=cost(96),
        name="expert",
    )(*operands, *after)


def gather_back(places, backs, shifts, slot_sum, effect, cap):
    lane = iota((1, LANES), 1)
    for index, ref in zip(shifts, backs):
        hot = one_hot_cols(places[:, index : index + 1], cap)
        slot_sum = slot_sum + dot(hot, ref[0:cap], NN)
        parts = dot(hot, ref[cap : cap + TAIL, 0:cap], NT)
        effect = jnp.where(lane == index, jnp.sum(parts, axis=1, keepdims=True), effect)
    return slot_sum, effect


def returned_kernel(pos_ref, *refs, cap, shifts):
    backs, slot_ref, effect_ref = refs[: len(shifts)], refs[-2], refs[-1]
    _, rows, width = slot_ref.shape
    slot_ref[0], effect_ref[0] = gather_back(
        pos_ref[0, 0:rows, :], backs, shifts, jnp.zeros((rows, width), f32), jnp.zeros((rows, LANES), f32), cap
    )


def returned(pos, backs, shifts, rows, cap):
    images, width = pos.shape[0], backs[0].shape[1]

    def image(shape):
        return pl.BlockSpec((1,) + shape, lambda i: (i, 0, 0))

    return pl.pallas_call(
        functools.partial(returned_kernel, cap=cap, shifts=shifts),
        grid=(images,),
        in_specs=[image((pos.shape[1], LANES))] + [whole((cap + TAIL, width))] * len(backs),
        out_specs=[image((rows, width)), image((rows, LANES))],
        out_shape=[
            jax.ShapeDtypeStruct((images, rows, width), f32),
            jax.ShapeDtypeStruct((images, rows, LANES), f32),
        ],
        compiler_params=params(),
        cost_estimate=cost(100),
        name="returned",
    )(pos, *backs)


def middle_kernel(
    place_ref, up_ref, wout_ref, misc_ref, pos_ref, mixed_ref, hidden_ref, prob_ref, slot_ref, effect_ref, *rest, cap, experts
):
    backs = rest[:2]
    hidden_grad_ref, mixed_grad_ref, sums_ref, padded, vectors, router, shifts, acc_out, acc_router = rest[-9:]
    _, seq, width = up_ref.shape
    rows = padded.shape[0]
    step = pl.program_id(0)

    @pl.when(step == 0)
    def _():
        vectors[...] = misc_ref[...].astype(f32).T
        router[...] = dot(misc_ref[...], router_order(place_ref[0], experts), NN).astype(bf16)
        padded[...] = jnp.zeros_like(padded)
        shifts[...] = jnp.zeros_like(shifts)
        acc_out[...] = jnp.zeros_like(acc_out)
        acc_router[...] = jnp.zeros_like(acc_router)

    def vector(index):
        return vectors[VEC + index : VEC + index + 1, :]

    def shift(index, value):
        shifts[index : index + 1, :] += jnp.sum(value, axis=0, keepdims=True)

    slot_sum, effect = gather_back(pos_ref[0, 0:rows, :], backs, (0, 1), slot_ref[0], effect_ref[0], cap)
    prob = prob_ref[0]
    logit_grad = effect - prob * jnp.sum(effect, axis=1, keepdims=True)
    logit_parts = pieces(logit_grad, 2)
    mid_grad = slot_sum
    for part in logit_parts:
        mid_grad = mid_grad + dot(part, router[...], NT)
    padded[0:seq] = up_ref[0].astype(f32)
    hat, inverse = norm_stats(hidden_ref[0])
    mid_parts = pieces(hat * vector(5) + vector(6), 2)
    acc_router[...] += (
        dot(logit_parts[0], mid_parts[0], TN)
        + dot(logit_parts[0], mid_parts[1], TN)
        + dot(logit_parts[1], mid_parts[0], TN)
    )
    shift(5, mid_grad * hat)
    shift(6, mid_grad)
    hidden_grad = padded[...] + norm_back(mid_grad, vector(5), hat, inverse)
    hidden_grad_ref[0] = hidden_grad
    branch = hidden_grad.astype(bf16)
    shift(4, branch.astype(f32))
    acc_out[...] += dot(mixed_ref[0], branch, TN)
    mixed_grad_ref[0] = dot(branch, wout_ref[...], NT).astype(bf16)

    @pl.when(step == pl.num_programs(0) - 1)
    def _():
        sums_ref[:, 0:width] = acc_out[...]
        ordered = dot(router_order(place_ref[0], experts), acc_router[...].astype(bf16), NN)
        spare = jnp.concatenate(
            [ordered[0:VEC], shifts[...], jnp.zeros((LANES - VEC - shifts.shape[0], width), f32)], axis=0
        )
        sums_ref[:, width:] = spare.T


def middle(place, grad_output, pack, pos, saved, part_sums, backs, cap, experts):
    images, seq, width = grad_output.shape
    _, mixed, hidden, prob, _ = saved
    rows = mixed.shape[1]

    def image(shape):
        return pl.BlockSpec((1,) + shape, lambda i: (i, 0, 0))

    return pl.pallas_call(
        functools.partial(middle_kernel, cap=cap, experts=experts),
        grid=(images,),
        in_specs=[
            pl.BlockSpec(memory_space=pltpu.SMEM),
            image((seq, width)),
            pl.BlockSpec((width, width), lambda i: (0, 3)),
            pl.BlockSpec((width, LANES), lambda i: (0, 4 * width // LANES)),
            image((pos.shape[1], LANES)),
            image((rows, width)),
            image((rows, width)),
            image((rows, LANES)),
            image((rows, width)),
            image((rows, LANES)),
        ]
        + [whole((cap + TAIL, width))] * len(backs),
        out_specs=[image((rows, width)), image((rows, width)), whole((width, width + LANES))],
        out_shape=[
            jax.ShapeDtypeStruct((images, rows, width), f32),
            jax.ShapeDtypeStruct((images, rows, width), bf16),
            jax.ShapeDtypeStruct((width, width + LANES), f32),
        ],
        scratch_shapes=[
            pltpu.VMEM((rows, width), f32),
            pltpu.VMEM((LANES, width), f32),
            pltpu.VMEM((width, LANES), bf16),
            pltpu.VMEM((8, width), f32),
            pltpu.VMEM((width, width), f32),
            pltpu.VMEM((LANES, width), f32),
        ],
        compiler_params=params(),
        cost_estimate=cost(0.02),
        name="middle",
    )(place, grad_output, pack, pack, pos, mixed, hidden, prob, *part_sums, *backs)


def backward_kernel(
    spots_ref, tok_ref, qkv_ref, attn_ref, mixed_grad_ref, *rest, head_rows, members
):
    sums_ref, peak_ref = rest[:2]
    qkv_grad_ref, keep_ref, give_ref, padded, acc_qkv, columns, spare, misc = rest[-8:]
    _, seq, width = tok_ref.shape
    rows = padded.shape[0]
    head = width // HEADS
    wide = 3 * width
    step = pl.program_id(0)

    @pl.when(step == 0)
    def _():
        padded[...] = jnp.zeros_like(padded)
        acc_qkv[...] = jnp.zeros_like(acc_qkv)
        columns[...] = jnp.zeros_like(columns)

    lane = iota((1, LANES), 1)
    first = lane < head
    halves = (jnp.where(first, 1.0, 0.0).astype(bf16), jnp.where(first, 0.0, 1.0).astype(bf16))

    def pair(index, carry):
        at = pl.multiple_of(index * LANES, LANES)
        query = qkv_ref[0, :, pl.ds(at, LANES)]
        key = qkv_ref[0, :, pl.ds(width + at, LANES)]
        value = qkv_ref[0, :, pl.ds(2 * width + at, LANES)]
        up = mixed_grad_ref[0, :, pl.ds(at, LANES)]
        made = []
        for half in range(2):
            low = attn_ref[0, index * 2 + half]
            weight = low.astype(f32)
            value_grad = dot(low, up, TN)
            spread = weight * dot(up * halves[half], value, NT)
            score_grad = (spread - weight * jnp.sum(spread, axis=1, keepdims=True)).astype(bf16)
            made.append((dot(score_grad, key, NN) * head**-0.5, dot(score_grad, query, TN), value_grad))
        for index_of, (left, right) in enumerate(zip(*made)):
            qkv_grad_ref[0, :, pl.ds(index_of * width + at, LANES)] = jnp.where(first, left, right).astype(bf16)
        return carry

    lax.fori_loop(0, HEADS // 2, pair, 0, unroll=True)
    columns[...] += jnp.sum(qkv_grad_ref[0].astype(f32), axis=0, keepdims=True)
    padded[0:seq] = tok_ref[0].astype(f32)
    hat, _ = norm_stats(padded[...])
    acc_qkv[...] += dot(hat.astype(bf16), qkv_grad_ref[0], TN)
    part = keep_ref.shape[1]

    @pl.when(step == pl.num_programs(0) - 1)
    def _():
        line = iota((LANES, width), 0)
        flat = columns[...]
        grown = jnp.where(line == VEC + 2, flat[:, 0:width], 0.0)
        grown = jnp.where(line == VEC + 3, flat[:, 2 * width :], grown)
        misc[...] = sums_ref[:, width:] + grown.T
        spare[...] = jnp.zeros_like(spare)
        number = wide // LANES
        for order, piece in enumerate(pieces(flat, 3)):
            value = piece.astype(f32)
            for index in range(number):
                at = order * number + index
                spare[at : at + 1, :] = value[:, index * LANES : (index + 1) * LANES]
        if members:
            top = jnp.where(lane < HEADS, peak_ref[...], 0.0)
            rows_of = jnp.zeros((TAIL, LANES), f32)
            for order, piece in enumerate(pieces(jnp.broadcast_to(top, (TAIL, LANES)), 3)):
                move = jnp.where(iota((LANES, LANES), 1) == iota((LANES, LANES), 0) + order * HEADS, 1.0, 0.0)
                rows_of = rows_of + dot(piece, move.astype(bf16), NN)
            spare[pl.ds(head_rows + spots_ref[NUMBER], 1), :] = rows_of[0:1]
        extra = spare[...].astype(bf16)
        for fy in range(keep_ref.shape[0]):
            for ref, core in ((keep_ref, spots_ref[CORE]), (give_ref, 1 - spots_ref[CORE])):
                at = pl.multiple_of((2 * fy + core) * part, part)
                ref[fy, :, 0:wide] = acc_qkv[pl.ds(at, part), :].astype(bf16)
                ref[fy, :, wide : wide + width] = sums_ref[pl.ds(at, part), 0:width].astype(bf16)
                ref[fy, :, wide + width : wide + width + LANES] = misc[pl.ds(at, part), :].astype(bf16)
                ref[fy, :, wide + width + LANES :] = extra


def backward(spots, tokens, saved, mixed_grad, sums, peak, after, ways, part, head_rows, members):
    images, seq, width = tokens.shape
    qkv, attn = saved[0], saved[-1]
    rows = qkv.shape[1]
    wide = 4 * width + 2 * LANES

    def image(shape):
        return pl.BlockSpec((1,) + shape, lambda i: (i,) + (0,) * len(shape))

    return pl.pallas_call(
        functools.partial(backward_kernel, head_rows=head_rows, members=members),
        grid=(images,),
        in_specs=[
            pl.BlockSpec(memory_space=pltpu.SMEM),
            image((seq, width)),
            image((rows, 3 * width)),
            image((HEADS, rows, rows)),
            image((rows, width)),
            whole(sums.shape),
            whole(peak.shape),
        ]
        + [pl.BlockSpec(memory_space=pl.ANY)] * len(after),
        out_specs=[image((rows, 3 * width)), whole((ways, part, wide)), whole((ways, part, wide))],
        out_shape=[
            jax.ShapeDtypeStruct((images, rows, 3 * width), bf16),
            jax.ShapeDtypeStruct((ways, part, wide), bf16),
            jax.ShapeDtypeStruct((ways, part, wide), bf16),
        ],
        scratch_shapes=[
            pltpu.VMEM((rows, width), f32),
            pltpu.VMEM((width, 3 * width), f32),
            pltpu.VMEM((1, 3 * width), f32),
            pltpu.VMEM((part, LANES), f32),
            pltpu.VMEM((width, LANES), f32),
        ],
        compiler_params=params(),
        cost_estimate=cost(0.05),
        name="attend_back",
    )(spots, tokens, qkv, attn, mixed_grad, sums, peak, *after)


def first_kernel(tok_ref, qkv_grad_ref, wqkv_ref, misc_ref, hidden_grad_ref, grad_ref, padded, gain):
    _, seq, width = tok_ref.shape

    @pl.when(pl.program_id(0) == 0)
    def _():
        gain[...] = misc_ref[...].astype(f32).T[VEC : VEC + 1]
        padded[...] = jnp.zeros_like(padded)

    in_grad = dot(qkv_grad_ref[0], wqkv_ref[...], NT)
    padded[0:seq] = tok_ref[0].astype(f32)
    hat, inverse = norm_stats(padded[...])
    grad_ref[0] = (hidden_grad_ref[0] + norm_back(in_grad, gain[...], hat, inverse))[0:seq]


def first_norm(tokens, qkv_grad, pack, hidden_grad):
    images, seq, width = tokens.shape
    rows = qkv_grad.shape[1]

    def image(shape):
        return pl.BlockSpec((1,) + shape, lambda i: (i, 0, 0))

    return pl.pallas_call(
        first_kernel,
        grid=(images,),
        in_specs=[
            image((seq, width)),
            image((rows, 3 * width)),
            pl.BlockSpec((width, 3 * width), lambda i: (0, 0)),
            pl.BlockSpec((width, LANES), lambda i: (0, 4 * width // LANES)),
            image((rows, width)),
        ],
        out_specs=image((seq, width)),
        out_shape=jax.ShapeDtypeStruct((images, seq, width), f32),
        scratch_shapes=[pltpu.VMEM((rows, width), f32), pltpu.VMEM((1, width), f32)],
        compiler_params=params(),
        cost_estimate=cost(0.02),
        name="first_norm",
    )(tokens, qkv_grad, pack, pack, hidden_grad)


def output_kernel(place_ref, pos_ref, hidden_ref, made_ref, out_ref):
    experts, cap, _ = made_ref.shape
    seq = out_ref.shape[1]
    total = hidden_ref[0]
    places = pos_ref[0, 0 : total.shape[0], :]
    for index in range(experts):
        total = total + dot(one_hot_cols(places[:, index : index + 1], cap), made_ref[place_ref[0] ^ index], NN)
    out_ref[0] = total[0:seq].astype(bf16)


def combine_output(place, pos, hidden, made, seq):
    images, rows, width = hidden.shape

    def image(shape):
        return pl.BlockSpec((1,) + shape, lambda i: (i, 0, 0))

    return pl.pallas_call(
        output_kernel,
        grid=(images,),
        in_specs=[
            pl.BlockSpec(memory_space=pltpu.SMEM),
            image((pos.shape[1], LANES)),
            image((rows, width)),
            whole(made.shape),
        ],
        out_specs=image((seq, width)),
        out_shape=jax.ShapeDtypeStruct((images, seq, width), bf16),
        compiler_params=params(),
        cost_estimate=cost(0.02),
        name="combine",
    )(place, pos, hidden, made)


def finish_kernel(slot_ref, *refs, number, head_rows, members):
    parts, (own_ref, limit_ref, peak_ref) = refs[:number], refs[number : number + 3]
    qkv_ref, out_ref, misc_ref, clip_ref, *vec_refs, total_ref = refs[number + 3 :]
    part = own_ref.shape[0]
    for shift, ref in enumerate(parts):
        size = part // number
        total_ref[pl.ds(pl.multiple_of((slot_ref[LOW] ^ shift) * size, size), size), :] = ref[...]
    width = out_ref.shape[1]
    wide = 3 * width
    number = wide // LANES
    base = total_ref[:, 0:wide].astype(f32)
    extra = total_ref[:, wide + width + LANES :].astype(f32)
    weight = own_ref[:, 0:wide].astype(f32)
    columns = [sum(extra[k * number + i : k * number + i + 1] for k in range(3)) for i in range(number)]
    columns = jnp.concatenate(columns, axis=1)
    own = own_ref[:, wide + width :].astype(f32)
    gain, bias = own[:, VEC : VEC + 1], own[:, VEC + 1 : VEC + 2]
    qkv_ref[...] = base * gain + bias * columns
    out_ref[...] = total_ref[:, wide : wide + width].astype(f32)
    misc = total_ref[:, wide + width : wide + width + LANES].astype(f32)
    lane = iota((1, LANES), 1)
    misc = jnp.where(lane == VEC, jnp.sum(base * weight, axis=1, keepdims=True), misc)
    misc = jnp.where(lane == VEC + 1, jnp.sum(columns * weight, axis=1, keepdims=True), misc)
    misc = misc.T
    for index, ref in enumerate(vec_refs):
        ref[...] = misc[VEC + index : VEC + index + 1]
    misc_ref[...] = misc[0 : misc_ref.shape[0]]
    if members:
        move = jnp.where(
            (iota((LANES, LANES), 0) % HEADS == iota((LANES, LANES), 1)) & (iota((LANES, LANES), 0) < 3 * HEADS),
            1.0,
            0.0,
        )
        peaks = dot(total_ref[head_rows : head_rows + members, wide + width + LANES :], move.astype(bf16), NN)
        peak = jnp.max(peaks, axis=0, keepdims=True)
    else:
        peak = peak_ref[...]
    limit = jnp.concatenate([limit_ref[...].astype(f32), jnp.ones((1, LANES - HEADS), f32)], axis=1)
    root = jnp.sqrt(limit / jnp.maximum(peak, limit))
    place = iota((1, width), 1) // (width // HEADS)
    scale = jnp.zeros((1, width), f32)
    for index in range(HEADS):
        scale = jnp.where(place == index, root[:, index : index + 1], scale)
    clip_ref[:, 0:width] = (weight[:, 0:width] * scale).astype(bf16)
    clip_ref[:, width : 2 * width] = (weight[:, width : 2 * width] * scale).astype(bf16)
    clip_ref[:, 2 * width :] = own_ref[:, 2 * width : wide]


def finish(slot, total, own, limit, peak, width, experts, head_rows, members):
    part = own.shape[0]
    operands = [*total, own, limit, peak]
    shapes = [(part, 3 * width), (part, width), (experts, part), (part, 3 * width)] + [(1, part)] * 7
    return pl.pallas_call(
        functools.partial(finish_kernel, number=len(total), head_rows=head_rows, members=members),
        grid=(1,),
        in_specs=[pl.BlockSpec(memory_space=pltpu.SMEM)] + [whole(v.shape) for v in operands],
        out_specs=[whole(v) for v in shapes],
        out_shape=[jax.ShapeDtypeStruct(v, bf16 if i == 3 else f32) for i, v in enumerate(shapes)],
        scratch_shapes=[pltpu.VMEM((part, total[0].shape[1]), bf16)],
        compiler_params=params(),
        cost_estimate=cost(0.02),
        name="finish",
    )(slot, *operands)


def half_sums_kernel(high_ref, keep_ref, got_ref, *rest):
    straight_ref, crossed_ref = rest[-2:]
    for ref, core in ((straight_ref, high_ref[HIGH]), (crossed_ref, 1 - high_ref[HIGH])):
        ref[...] = (keep_ref[core].astype(f32) + got_ref[core].astype(f32)).astype(bf16)


def half_sums(high, keep, got, after, micros):
    shape = keep.shape[1:]
    return pl.pallas_call(
        half_sums_kernel,
        grid=(1,),
        in_specs=[pl.BlockSpec(memory_space=pltpu.SMEM), whole(keep.shape), whole(got.shape)]
        + [pl.BlockSpec(memory_space=pl.ANY)] * len(after),
        out_specs=[whole(shape)] * 2,
        out_shape=[jax.ShapeDtypeStruct(shape, bf16)] * 2,
        compiler_params=params(),
        cost_estimate=cost(micros),
        name="half_sums",
    )(high, keep, got, *after)


def both_halves(spot_ref, one, two, own, rows):
    straight = jnp.where(spot_ref[SAME] == 1, own[rows].astype(f32), one[rows].astype(f32))
    return straight + two[rows].astype(f32)


def home_second_kernel(spot_ref, one, two, own, _, w2_ref, b1_ref, b2_ref):
    tile, width = w2_ref.shape
    part = b2_ref.shape[1]
    w2_ref[...] = both_halves(spot_ref, one, two, own, slice(0, tile))
    edge = both_halves(spot_ref, one, two, own, slice(tile, tile + TAIL))
    b1_ref[...] = edge[0:1, 0:tile]
    b2_ref[...] = sum(
        jnp.where(spot_ref[SPOT] == index, edge[1:2, index * part : (index + 1) * part], 0.0)
        for index in range(width // part)
    )


def home_first_kernel(spot_ref, one, two, own, _, w1_ref):
    part, hidden = w1_ref.shape
    number = one.shape[0] // part
    tile = hidden // number
    for index in range(number):
        total = both_halves(spot_ref, one, two, own, slice(index * part, (index + 1) * part))
        w1_ref[:, index * tile : (index + 1) * tile] = total[:, 0:tile]


def home_sums(kernel, spot, pair, after, shapes):
    return pl.pallas_call(
        kernel,
        grid=(1,),
        in_specs=[pl.BlockSpec(memory_space=pltpu.SMEM)]
        + [whole(v.shape) for v in pair]
        + [pl.BlockSpec(memory_space=pl.ANY)],
        out_specs=[whole(v) for v in shapes],
        out_shape=[jax.ShapeDtypeStruct(v, f32) for v in shapes],
        compiler_params=params(),
        cost_estimate=cost(0.02),
        name="home_sums",
    )(spot, *pair, after)


def add_halves_kernel(fy_ref, keep_ref, got_ref, *rest):
    mine_ref, theirs_ref = rest[-2:]
    for ref, half in ((mine_ref, fy_ref[FY]), (theirs_ref, 1 - fy_ref[FY])):
        ref[...] = (keep_ref[half].astype(f32) + got_ref[half].astype(f32)).astype(bf16)


def add_halves(fy, keep, got, after):
    shape = keep.shape[1:]
    return pl.pallas_call(
        add_halves_kernel,
        grid=(1,),
        in_specs=[pl.BlockSpec(memory_space=pltpu.SMEM), whole(keep.shape), whole(got.shape)]
        + [pl.BlockSpec(memory_space=pl.ANY)] * len(after),
        out_specs=[whole(shape)] * 2,
        out_shape=[jax.ShapeDtypeStruct(shape, bf16)] * 2,
        compiler_params=params(),
        cost_estimate=cost(0.02),
        name="add_halves",
    )(fy, keep, got, *after)


def split_rows_kernel(slot_ref, mine_ref, got_ref, *refs, skip):
    outs, total = refs[skip:-1], refs[-1]
    total[...] = (mine_ref[...].astype(f32) + got_ref[...].astype(f32)).astype(bf16)
    size = outs[0].shape[0]
    for shift, ref in enumerate(outs):
        ref[...] = total[pl.ds(pl.multiple_of((slot_ref[LOW] ^ shift) * size, size), size), :]


def split_rows(slot, mine, got, after, number):
    part, wide = mine.shape
    shape = (part // number, wide)
    return pl.pallas_call(
        functools.partial(split_rows_kernel, skip=len(after)),
        grid=(1,),
        in_specs=[pl.BlockSpec(memory_space=pltpu.SMEM), whole(mine.shape), whole(got.shape)]
        + [pl.BlockSpec(memory_space=pl.ANY)] * len(after),
        out_specs=[whole(shape)] * number,
        out_shape=[jax.ShapeDtypeStruct(shape, bf16)] * number,
        scratch_shapes=[pltpu.VMEM((part, wide), bf16)],
        compiler_params=params(),
        cost_estimate=cost(0.02),
        name="split_rows",
    )(slot, mine, got, *after)


def add_parts_kernel(*refs, number):
    parts, out_ref = refs[:number], refs[-1]
    out_ref[...] = sum(ref[...].astype(f32) for ref in parts).astype(bf16)


def add_parts(parts, after=()):
    shape = parts[0].shape
    return pl.pallas_call(
        functools.partial(add_parts_kernel, number=len(parts)),
        grid=(1,),
        in_specs=[whole(shape)] * len(parts) + [pl.BlockSpec(memory_space=pl.ANY)] * len(after),
        out_specs=whole(shape),
        out_shape=jax.ShapeDtypeStruct(shape, bf16),
        compiler_params=params(),
        cost_estimate=cost(0.02),
        name="add_parts",
    )(*parts, *after)


def swap(value, axis):
    return lax.ppermute(value, axis, [(0, 1), (1, 0)])


def around(value, axis, size):
    return [value] + [
        lax.ppermute(value, axis, [((k + step) % size, k) for k in range(size)]) for step in range(1, size)
    ]


def split_sum(value, axis, size):
    if size != 2:
        return lax.psum_scatter(value, axis, scatter_dimension=0, tiled=False)
    place = lax.axis_index(axis)
    sent = lax.dynamic_index_in_dim(value, 1 - place, 0, keepdims=False)
    kept = lax.dynamic_index_in_dim(value, place, 0, keepdims=False)
    return (kept.astype(f32) + swap(sent, axis).astype(f32)).astype(value.dtype)


def exchange(value, shift, experts):
    return lax.ppermute(value, GROUP, [(k, k ^ shift) for k in range(experts)])


def shift_order(experts):
    def key(shift):
        distance = bin(shift >> 1).count("1")
        return (shift & 1, -distance, shift)

    order = sorted(range(2, experts), key=key)
    half = len(order) // 2
    return [order[:half], order[half:], [0, 1]]


STRAIGHT = [(1, 2), (2, 1)]
CROSSED = [(0, 2), (1, 0), (2, 3), (3, 1)]
BACK = [(b, a) for a, b in STRAIGHT]
BACK_CROSSED = [(b, a) for a, b in CROSSED]


def shards(
    tokens,
    ln1_gain,
    ln1_bias,
    w_qkv,
    q_bias,
    v_bias,
    w_out,
    out_bias,
    ln2_gain,
    ln2_bias,
    w_router,
    expert_w1,
    expert_b1,
    expert_w2,
    expert_b2,
    route_ids,
    clip_threshold,
    grad_output,
    *,
    experts,
    fsdp,
):
    images, seq, width = tokens.shape
    token_count = images * seq
    ways = fsdp // 2
    cap = (7 * token_count // (2 * experts) + 7) // 8 * 8
    stride = -(-seq // 256) * 256
    rows = -(-seq // 16) * 16
    part = w_qkv.shape[0]
    hidden_part = expert_w2.shape[1]
    high, low, fy, core = (lax.axis_index(name).astype(i32) for name in DEVICE)
    spot = fy * 2 + core
    homes = [((fy + step) % ways) * 2 for step in range(ways)]
    spots = jnp.stack(
        [
            low * 2 + core,
            fy,
            core,
            ((high * (experts // 2) + low) * ways + fy) * 2 + core,
            high,
            spot,
            (high == core).astype(i32),
            low,
            *[home + high for home in homes],
            *[home + 1 - high for home in homes],
            *[home + core for home in homes],
            *[home + 1 - core for home in homes],
        ]
    )

    vectors = (ln1_gain, ln1_bias, q_bias, v_bias, out_bias, ln2_gain, ln2_bias)
    own, pay = pack_parameters(
        spots, w_qkv, w_out, w_router, vectors, expert_w1[0], expert_w2[0], expert_b1, expert_b2
    )

    near = around(own, "fy", ways)
    straight = lax.ppermute(pay, ("hi", "core"), STRAIGHT)

    groups = shift_order(experts)
    hot, pos, post, *firsts = route(spots, route_ids.T, grad_output, groups[0], experts, cap, stride)
    near[1:], hot, own_later = lax.optimization_barrier((near[1:], hot, own))
    firsts = [exchange(value, shift, experts) for shift, value in zip(groups[0], firsts)]
    far = [swap(own_later, "core")]
    far += [swap(value, "core") for value in near[1:]]
    early = 1
    begun = list(forward(spots, tokens, near + far, None, [], 0, early, experts, stride, rows))
    pay, straight, begun[0] = lax.optimization_barrier((pay, straight, begun[0]))
    straight = jnp.where(high == core, pay, straight)
    crossed = lax.ppermute(pay, ("hi", "core"), CROSSED)
    pays = around(straight, "fy", ways)
    *saved, mid, peak, pack = forward(
        spots, tokens, [], begun, [straight], early, images - early, experts, stride, rows
    )
    mid = mid.reshape(images * stride, width)
    ready = dispatch(hot, mid)
    rest = [shift for group in groups[1:] for shift in group]
    cut = len(firsts) - len(firsts) // 3
    sent = dict(zip(rest, dispatch_both(post, mid, grad_output, firsts[cut:], rest, cap, stride)))
    crossed, ready, firsts[:cut], *pays[1:] = lax.optimization_barrier(
        (crossed, list(ready), firsts[:cut], *pays[1:])
    )
    sent.update(zip(groups[0], ready))
    ups = dict(zip(groups[0], firsts))
    pays += around(crossed, "fy", ways)

    arrived = {}

    def send(number, after):
        pending, after = lax.optimization_barrier(([sent[shift] for shift in groups[number]], after))
        for shift, value in zip(groups[number], pending):
            arrived[shift] = value if shift == 0 else exchange(value, shift, experts)
        return after

    send(0, ())
    first = send(1, [arrived[shift] for shift in groups[0]])
    arrived.update(zip(groups[0], first))
    old, after = None, []
    backs = {}
    for number, group in enumerate(groups):
        result = expert_call(
            spots,
            [arrived[shift] for shift in group],
            [ups.get(shift, arrived[shift]) for shift in group],
            pays,
            pack,
            old,
            after,
            group,
            cap,
            experts,
            number == len(groups) - 1,
        )
        old = result[len(group) :]
        after = [backs[shift] for shift in groups[number - 1]] if number else []
        out = result[: len(group)]
        if number + 2 < len(groups):
            out = send(number + 2, out)
        for at, shift in enumerate(group):
            backs[shift] = out[at] if shift == 0 else exchange(out[at], shift, experts)
    backs = [backs[shift] for shift in range(experts)]
    made, *grad = old
    made = lax.all_to_all(made, GROUP, split_axis=0, concat_axis=0, tiled=True)

    shifts = tuple(range(2, experts))
    part_sums = returned(pos, backs[2:], shifts, rows, cap)
    hidden_grad, mixed_grad, sums = middle(
        spots, grad_output, pack, pos, saved, part_sums, backs[:2], cap, experts
    )
    head_rows = 3 * (3 * width // LANES) + 4
    devices = 2 * experts // 2 * fsdp
    members = devices if head_rows + devices <= part else 0

    def homeward(straight, crossed):
        return [
            lax.ppermute(straight, ("hi", "core"), BACK),
            lax.ppermute(crossed, ("hi", "core"), BACK_CROSSED),
            straight,
        ]

    if len(grad) == 4:
        sums_two = list(half_sums(spots, grad[0], swap(grad[1], "fy"), [sums], 0.02))
        home_two = homeward(*sums_two)
        grad[3], sums_two[0] = lax.optimization_barrier((grad[3], sums_two[0]))
        got_one = swap(grad[3], "fy")
    else:
        half = split_sum(grad[0].reshape((ways, 2) + grad[0].shape[1:]), "fy", ways)
        home = homeward(*(lax.dynamic_index_in_dim(half, k, 0, keepdims=False) for k in (high, 1 - high)))
        tall = hidden_part + TAIL
        home_two, home_one = [v[:tall] for v in home], [v[tall:] for v in home]
    qkv_grad, keep, give = backward(
        spots, tokens, saved, mixed_grad, sums, peak, [], ways, part, head_rows, members
    )

    got = swap(give, "core")
    after = []
    if len(grad) == 4:
        after = half_sums(spots, grad[2], got_one, home_two[:2], 40)
        home_one = homeward(*after)
    output = combine_output(spots, pos, saved[2], made, seq)
    near_by = experts // 2
    if ways == 2 and part % (TAIL * near_by) == 0:

        def spread(values):
            return [
                value if k == 0 else lax.ppermute(value, "lo", [(j, j ^ k) for j in range(near_by)])
                for k, value in enumerate(values)
            ]

        mine, theirs = add_halves(spots, keep, got, after)
        theirs, qkv_grad = lax.optimization_barrier((theirs, qkv_grad))
        input_grad = first_norm(tokens, qkv_grad, pack, hidden_grad)
        parts = split_rows(spots, mine, swap(theirs, "fy"), [input_grad, output, *home_one[:2]], near_by)
        total = add_parts(spread(parts))
        shapes = [(hidden_part, width), (1, hidden_part), (1, part)]
        grad_w2, grad_b1, grad_b2 = home_sums(home_second_kernel, spots, home_two, total, shapes)
        shapes = [(part, hidden_part * fsdp)]
        (grad_w1,) = home_sums(home_first_kernel, spots, home_one, total, shapes)
        total = add_parts([total, swap(total, "hi")], [grad_w2, grad_w1])
        total = spread([total] * near_by)
    else:
        sums = split_sum((keep.astype(f32) + got.astype(f32)).astype(bf16), "fy", ways)
        total = [lax.psum(sums, ("hi", "lo"))]
        shapes = [(hidden_part, width), (1, hidden_part), (1, part)]
        grad_w2, grad_b1, grad_b2 = home_sums(home_second_kernel, spots, home_two, total[0], shapes)
        shapes = [(part, hidden_part * fsdp)]
        (grad_w1,) = home_sums(home_first_kernel, spots, home_one, total[0], shapes)
        input_grad = first_norm(tokens, qkv_grad, pack, hidden_grad)
    if not members:
        peak = jnp.max(lax.all_gather(peak, DEVICE, axis=0, tiled=True), axis=0, keepdims=True)
    limit = clip_threshold.reshape(1, HEADS)
    grad_qkv, grad_out, grad_router, clipped, *grads = finish(
        spots, total, own, limit, peak, width, experts, head_rows, members
    )
    grads = [v.reshape(part) for v in grads]
    return (
        output,
        input_grad,
        grads[0],
        grads[1],
        grad_qkv,
        grads[2],
        grads[3],
        grad_out,
        grads[4],
        grads[5],
        grads[6],
        grad_router.T,
        grad_w1[None],
        grad_b1,
        grad_w2[None],
        grad_b2,
        clipped,
    )


def solution(mesh):
    experts, fsdp = mesh.shape["expert"], mesh.shape["fsdp"]
    inner = Mesh(mesh.devices.reshape(2, experts // 2, fsdp // 2, 2), DEVICE)
    token, row, expert = P(DEVICE, None, None), ("fy", "core"), ("hi", "lo")
    vector, matrix = P(row), P(row, None)
    return jax.shard_map(
        functools.partial(shards, experts=experts, fsdp=fsdp),
        mesh=inner,
        in_specs=(
            token,
            vector,
            vector,
            matrix,
            vector,
            vector,
            matrix,
            vector,
            vector,
            vector,
            matrix,
            P(expert, row, None),
            P(expert, row),
            P(expert, row, None),
            P(expert, row),
            P(DEVICE, None),
            P(),
            token,
        ),
        out_specs=(
            token,
            token,
            vector,
            vector,
            matrix,
            vector,
            vector,
            matrix,
            vector,
            vector,
            vector,
            matrix,
            P(expert, row, None),
            P(expert, row),
            P(expert, row, None),
            P(expert, row),
            matrix,
        ),
        check_vma=False,
    )
```

```python
import functools

import jax
import jax.numpy as jnp
from jax import lax
from jax.experimental import pallas as pl
from jax.experimental.pallas import tpu as pltpu
from jax.sharding import Mesh
from jax.sharding import PartitionSpec as P

HEADS = 8
EPS = 1e-06
LANES = 128
VEC = 64
TAIL = 16
NEG = -1e30
f32 = jnp.float32
bf16 = jnp.bfloat16
i32 = jnp.int32
NN = (((1,), (0,)), ((), ()))
NT = (((1,), (1,)), ((), ()))
TN = (((0,), (0,)), ((), ()))
DEVICE = ("hi", "lo", "fy", "core")
GROUP = ("lo", "core")
PLACE, FY, CORE, NUMBER, HIGH, SPOT, SAME, LOW, HOMES = range(9)
VMEM_LIMIT = 64 << 20


def dot(a, b, dims):
    return lax.dot_general(a, b, dims, preferred_element_type=f32)


def pieces(value, count):
    parts = []
    for _ in range(count):
        part = value.astype(bf16)
        parts.append(part)
        value = value - part.astype(f32)
    return parts


def iota(shape, axis):
    return lax.broadcasted_iota(i32, shape, axis)


def relative_expert(place, shift, experts):
    other = jnp.bitwise_xor(place, shift)
    return (other & 1) * (experts // 2) + (other >> 1)


def router_order(place, experts):
    row, col = iota((LANES, LANES), 0), iota((LANES, LANES), 1)
    return jnp.where((row == relative_expert(place, col, experts)) & (col < experts), 1.0, 0.0).astype(bf16)


def norm_stats(matrix):
    centred = matrix - jnp.mean(matrix, axis=1, keepdims=True)
    inverse = lax.rsqrt(jnp.mean(centred * centred, axis=1, keepdims=True) + EPS)
    return centred * inverse, inverse


def norm_back(upstream, gain, hat, inverse):
    scaled = upstream * gain
    spread = (
        scaled
        - jnp.mean(scaled, axis=1, keepdims=True)
        - hat * jnp.mean(scaled * hat, axis=1, keepdims=True)
    )
    return spread * inverse


def softmax_lanes(logits, experts):
    logits = jnp.where(iota(logits.shape, 1) < experts, logits, NEG)
    top = jnp.max(logits, axis=1, keepdims=True)
    weight = jnp.exp(logits - top)
    return weight / jnp.sum(weight, axis=1, keepdims=True)


def gelu_pair(value):
    def low(number):
        return jnp.asarray(number, bf16)

    value = value.astype(bf16)
    bell = jnp.exp(value * value * low(-0.5))
    t = low(1.0) / (low(1.0) + jnp.abs(value) * low(0.3275911 * 0.7071067811865476))
    poly = low(0.7107068705) + t * (low(-0.7265760135) + t * low(0.5307027145))
    poly = t * (low(0.127414796) + t * (low(-0.142248368) + t * poly))
    lower = poly * bell
    phi = jnp.where(value >= low(0.0), low(1.0) - lower, lower)
    return value * phi, phi + value * (bell * low(0.3989422804014327))


def whole(shape):
    return pl.BlockSpec(shape, lambda *_: (0,) * len(shape))


def params(**extra):
    return pltpu.CompilerParams(vmem_limit_bytes=VMEM_LIMIT, **extra)


def cost(micros):
    return pl.CostEstimate(flops=int(micros * 1e9), bytes_accessed=0, transcendentals=0)


def pack_kernel(spot_ref, wqkv, wout, router, *rest):
    vectors, (w1, w2, b1, b2, pack_ref, pay_ref, spread, tail) = rest[:-8], rest[-8:]
    part, wide = wqkv.shape
    width, hidden = wout.shape[1], w2.shape[0]
    pack_ref[:, 0:wide] = wqkv[...]
    pack_ref[:, wide : wide + width] = wout[...]
    spread[...] = jnp.zeros_like(spread)
    spread[0 : router.shape[0], :] = router[...].astype(f32)
    for index, ref in enumerate(vectors):
        spread[VEC + index : VEC + index + 1, :] = ref[...].astype(f32)
    columns = spread[...].T
    pack_ref[:, wide + width :] = columns.astype(bf16)
    pay_ref[0:hidden] = w2[...]
    tail[...] = jnp.zeros_like(tail)
    tail[0:1, 0 : b1.shape[1]] = b1[...].astype(f32)
    copies = jnp.concatenate([b2[...].astype(f32)] * (width // part), axis=1)
    tail[1:2] = jnp.where(iota((1, width), 1) // part == spot_ref[SPOT], copies, 0.0)
    tall = hidden + TAIL
    pay_ref[hidden:tall] = tail[...].astype(bf16)
    for index in range(width // part):
        block = w1[:, index * hidden : (index + 1) * hidden]
        if hidden < width:
            block = jnp.concatenate([block, jnp.zeros((part, width - hidden), bf16)], axis=1)
        pay_ref[tall + index * part : tall + (index + 1) * part] = block


def pack_parameters(spot, w_qkv, w_out, w_router, vectors, w1, w2, b1, b2):
    part, width = w_out.shape
    hidden = w2.shape[0]
    operands = [w_qkv, w_out, w_router.T, *[v.reshape(1, part) for v in vectors], w1, w2, b1, b2]
    return pl.pallas_call(
        pack_kernel,
        grid=(1,),
        in_specs=[pl.BlockSpec(memory_space=pltpu.SMEM)] + [whole(v.shape) for v in operands],
        out_specs=[whole((part, 4 * width + LANES)), whole((hidden + TAIL + width, width))],
        out_shape=[
            jax.ShapeDtypeStruct((part, 4 * width + LANES), bf16),
            jax.ShapeDtypeStruct((hidden + TAIL + width, width), bf16),
        ],
        scratch_shapes=[pltpu.VMEM((LANES, part), f32), pltpu.VMEM((TAIL, width), f32)],
        compiler_params=params(),
        cost_estimate=cost(0.02),
        name="pack",
    )(spot, *operands)


def one_hot_rows(row, cap):
    slots = iota((cap, row.shape[1]), 0).astype(f32)
    return jnp.where(slots == row, 1.0, 0.0).astype(bf16)


def one_hot_cols(column, cap):
    slots = iota((column.shape[0], cap), 1).astype(f32)
    return jnp.where(slots == column, 1.0, 0.0).astype(bf16)


def listed(shifts):
    step, shift = pl.program_id(0), shifts[0]
    for index, value in enumerate(shifts[1:]):
        shift = jnp.where(step > index, value, shift)
    return shift


def route_kernel(place_ref, ids_ref, up_ref, hot_ref, pos_ref, post_ref, *rest, cap, stride, shifts):
    outs, gathered = rest[:-1], rest[-1]
    experts = post_ref.shape[0]
    images, seq, width = up_ref.shape
    step = pl.program_id(0)

    @pl.when(step == 0)
    def _():
        expert = relative_expert(place_ref[0], iota((experts, stride), 0), experts)
        before = jnp.where(iota((stride, stride), 0) < iota((stride, stride), 1), 1.0, 0.0).astype(bf16)
        carry = jnp.zeros((experts, 1), f32)
        gathered[...] = jnp.zeros_like(gathered)
        for image in range(images):
            ids = ids_ref[:, image * seq : (image + 1) * seq]
            ids = jnp.concatenate([ids, jnp.full((ids.shape[0], stride - seq), -1, i32)], axis=1)
            hit = jnp.zeros((experts, stride), jnp.bool_)
            for choice in range(ids_ref.shape[0]):
                hit = hit | (ids[choice : choice + 1] == expert)
            mask = jnp.where(hit, 1.0, 0.0)
            rank = carry + dot(mask.astype(bf16), before, NN)
            carry = carry + jnp.sum(mask, axis=1, keepdims=True)
            slot = jnp.where(hit, rank, -1.0)
            post_ref[:, image * stride : (image + 1) * stride] = slot
            padded = jnp.concatenate([slot, jnp.full((LANES - experts, stride), -1.0, f32)], axis=0)
            pos_ref[image] = padded.T
            gathered[image * stride : image * stride + seq] = up_ref[image]

    hot = one_hot_rows(post_ref[pl.ds(listed(shifts), 1), :], cap)
    hot_ref[0] = hot
    made = dot(hot, gathered[...], NN).astype(bf16)
    for index in range(len(outs)):

        @pl.when(step == index)
        def _():
            outs[index][...] = made


def route(place, ids, grad_output, shifts, experts, cap, stride):
    images, seq, width = grad_output.shape
    total = images * stride
    count = len(shifts)
    return pl.pallas_call(
        functools.partial(route_kernel, cap=cap, stride=stride, shifts=tuple(shifts)),
        grid=(count,),
        in_specs=[pl.BlockSpec(memory_space=pltpu.SMEM), whole(ids.shape), whole(grad_output.shape)],
        out_specs=[
            pl.BlockSpec((1, cap, total), lambda s: (s, 0, 0)),
            whole((images, stride, LANES)),
            whole((experts, total)),
        ]
        + [whole((cap, width))] * count,
        out_shape=[
            jax.ShapeDtypeStruct((count, cap, total), bf16),
            jax.ShapeDtypeStruct((images, stride, LANES), f32),
            jax.ShapeDtypeStruct((experts, total), f32),
        ]
        + [jax.ShapeDtypeStruct((cap, width), bf16)] * count,
        scratch_shapes=[pltpu.VMEM((total, width), bf16)],
        compiler_params=params(),
        cost_estimate=cost(0.02),
        name="route",
    )(place, ids, grad_output)


def dispatch_kernel(hot_ref, rows_ref, *outs):
    sent = dot(hot_ref[0], rows_ref[...], NN).astype(bf16)
    for index, ref in enumerate(outs):

        @pl.when(pl.program_id(0) == index)
        def _():
            ref[...] = sent


def dispatch(hot, rows):
    count, cap, total = hot.shape
    width = rows.shape[1]
    return pl.pallas_call(
        dispatch_kernel,
        grid=(count,),
        in_specs=[pl.BlockSpec((1, cap, total), lambda s: (s, 0, 0)), whole(rows.shape)],
        out_specs=[whole((cap, width))] * count,
        out_shape=[jax.ShapeDtypeStruct((cap, width), bf16)] * count,
        compiler_params=params(),
        cost_estimate=cost(0.02),
        name="dispatch",
    )(hot, rows)


def dispatch_both_kernel(post_ref, rows_ref, up_ref, *rest, cap, stride, shifts):
    outs, gathered = rest[-1 - len(shifts) : -1], rest[-1]
    images, seq, width = up_ref.shape
    step = pl.program_id(0)

    @pl.when(step == 0)
    def _():
        gathered[...] = jnp.zeros_like(gathered)
        for image in range(images):
            gathered[image * stride : image * stride + seq] = up_ref[image]

    hot = one_hot_rows(post_ref[pl.ds(listed(shifts), 1), :], cap)
    sent = dot(hot, rows_ref[...], NN).astype(bf16)
    up = dot(hot, gathered[...], NN).astype(bf16)
    for index, ref in enumerate(outs):

        @pl.when(step == index)
        def _():
            ref[0:cap] = sent
            ref[cap:] = up


def dispatch_both(post, rows, grad_output, after, shifts, cap, stride):
    width = rows.shape[1]
    shape = (2 * cap, width)
    return pl.pallas_call(
        functools.partial(dispatch_both_kernel, cap=cap, stride=stride, shifts=tuple(shifts)),
        grid=(len(shifts),),
        in_specs=[whole(post.shape), whole(rows.shape), whole(grad_output.shape)]
        + [pl.BlockSpec(memory_space=pl.ANY)] * len(after),
        out_specs=[whole(shape)] * len(shifts),
        out_shape=[jax.ShapeDtypeStruct(shape, bf16)] * len(shifts),
        scratch_shapes=[pltpu.VMEM(rows.shape, bf16)],
        compiler_params=params(),
        cost_estimate=cost(40),
        name="dispatch",
    )(post, rows, grad_output, *after)


def forward_kernel(spots_ref, tok_ref, *rest, experts, fsdp, later):
    if later:
        pack_ref, old_peak_ref = rest[:2]
        rest = rest[-10:]
    else:
        shards_of, pack_ref = rest[:fsdp], rest[-4]
        rest = rest[-11:-4] + rest[-3:]
    qkv_ref, mixed_ref, hidden_ref, prob_ref, attn_ref, mid_ref, peak_ref, tokens, vectors, router = rest
    _, seq, width = tok_ref.shape
    rows = tokens.shape[0]
    head = width // HEADS
    step = pl.program_id(0)
    wide = 3 * width

    @pl.when(step == 0)
    def _():
        if not later:
            part = shards_of[0].shape[0]
            for index, ref in enumerate(shards_of):
                pack_ref[pl.ds(pl.multiple_of(spots_ref[HOMES + fsdp + index] * part, part), part), :] = ref[...]
        misc = pack_ref[:, wide + width :]
        vectors[...] = misc.astype(f32).T
        router[...] = dot(misc, router_order(spots_ref[0], experts), NN).astype(bf16)
        tokens[...] = jnp.zeros_like(tokens)
        peak_ref[...] = old_peak_ref[...] if later else jnp.full_like(peak_ref, NEG)

    def vector(index):
        return vectors[VEC + index : VEC + index + 1, :]

    tokens[0:seq] = tok_ref[0].astype(f32)
    residual = tokens[...]
    hat, _ = norm_stats(residual)
    normed = (hat * vector(0) + vector(1)).astype(bf16)
    projected = dot(normed, pack_ref[:, 0:wide], NN)
    qkv_ref[0, :, 0:width] = ((projected[:, 0:width] + vector(2)).astype(bf16).astype(f32) * head**-0.5).astype(
        bf16
    )
    qkv_ref[0, :, width : 2 * width] = projected[:, width : 2 * width].astype(bf16)
    qkv_ref[0, :, 2 * width :] = (projected[:, 2 * width :] + vector(3)).astype(bf16)
    lane = iota((1, LANES), 1)
    first = lane < head
    halves = (jnp.where(first, 1.0, 0.0).astype(bf16), jnp.where(first, 0.0, 1.0).astype(bf16))
    keys = jnp.where(iota((1, rows), 1) < seq, 0.0, NEG)
    valid = iota((rows, 1), 0) < seq

    def pair(index, peak):
        at = pl.multiple_of(index * LANES, LANES)
        query = qkv_ref[0, :, pl.ds(at, LANES)]
        key = qkv_ref[0, :, pl.ds(width + at, LANES)]
        value = qkv_ref[0, :, pl.ds(2 * width + at, LANES)]
        parts = []
        for half in range(2):
            scores = dot(query * halves[half], key, NT) + keys
            top = jnp.max(scores, axis=1, keepdims=True)
            weight = jnp.exp(scores - top)
            total = jnp.sum(weight, axis=1, keepdims=True)
            number = index * 2 + half
            largest = jnp.max(jnp.where(valid, top, NEG), axis=0, keepdims=True)
            peak = jnp.where(lane == number, largest, peak)
            low = (weight * (1.0 / total)).astype(bf16)
            attn_ref[0, number] = low
            parts.append(dot(low, value, NN))
        mixed_ref[0, :, pl.ds(at, LANES)] = jnp.where(first, parts[0], parts[1]).astype(bf16)
        return peak

    peak = lax.fori_loop(0, HEADS // 2, pair, jnp.full((1, LANES), NEG, f32), unroll=True)
    peak_ref[...] = jnp.maximum(peak_ref[...], peak)
    hidden = residual + dot(mixed_ref[0], pack_ref[:, wide : wide + width], NN) + vector(4)
    hidden_ref[0] = hidden
    hat, _ = norm_stats(hidden)
    mid = hat * vector(5) + vector(6)
    logits = jnp.zeros((rows, LANES), f32)
    for part in pieces(mid, 3):
        logits = logits + dot(part, router[...], NN)
    prob_ref[0] = softmax_lanes(logits, experts)
    mid_ref[0, 0:rows] = mid.astype(bf16)
    mid_ref[0, rows:] = jnp.zeros((mid_ref.shape[1] - rows, width), bf16)


def forward(spots, tokens, shards_of, old, after, at, count, experts, stride, rows):
    images, seq, width = tokens.shape
    later = old is not None
    far = pl.BlockSpec(memory_space=pl.ANY)
    shapes = [
        ((1, rows, 3 * width), bf16),
        ((1, rows, width), bf16),
        ((1, rows, width), f32),
        ((1, rows, LANES), f32),
        ((1, HEADS, rows, rows), bf16),
        ((1, stride, width), bf16),
    ]

    def image(shape):
        return pl.BlockSpec(shape, lambda i: (at + i,) + (0,) * (len(shape) - 1))

    out_specs = [image(shape) for shape, _ in shapes] + [whole((1, LANES))]
    out_shape = [jax.ShapeDtypeStruct((images,) + shape[1:], kind) for shape, kind in shapes]
    out_shape.append(jax.ShapeDtypeStruct((1, LANES), f32))
    operands = [spots, tokens]
    in_specs = [pl.BlockSpec(memory_space=pltpu.SMEM), image((1, seq, width))]
    if later:
        *arrays, peak, pack = old
        aliases = {len(operands) + 2 + index: index for index in range(len(arrays))}
        operands += [pack, peak, *arrays]
        in_specs += [whole(pack.shape), whole(peak.shape)] + [far] * len(arrays)
    else:
        aliases = {}
        packed = (width, shards_of[0].shape[1])
        operands += shards_of
        in_specs += [whole(v.shape) for v in shards_of]
        out_specs.append(whole(packed))
        out_shape.append(jax.ShapeDtypeStruct(packed, bf16))
    outputs = pl.pallas_call(
        functools.partial(forward_kernel, experts=experts, fsdp=len(shards_of), later=later),
        grid=(count,),
        in_specs=in_specs + [far] * len(after),
        out_specs=out_specs,
        out_shape=out_shape,
        scratch_shapes=[
            pltpu.VMEM((rows, width), f32),
            pltpu.VMEM((LANES, width), f32),
            pltpu.VMEM((width, LANES), bf16),
        ],
        input_output_aliases=aliases,
        compiler_params=params(),
        cost_estimate=cost(20 * count if later else 0.02),
        name="attend",
    )(*operands, *after)
    return [*outputs, pack] if later else outputs


def expert_kernel(place_ref, *refs, cap, group, first, last, experts, fsdp, split, skip):
    taken = iter(refs)

    def take(number):
        return [next(taken) for _ in range(number)]

    count = len(group)
    rows_in, ups_in = take(count), take(count)
    pays, misc = take(fsdp), next(taken)
    old = [] if first else take(3)
    take(skip)
    row_back, made_ref = take(count), next(taken)
    out1, out2, *out3 = take(4 if split else 2) if split or not last else (None, next(taken))
    rows, ups, gates, acc_row, acc_out, shift2, bias2, gated, sems, w1s, w2s, sems_w = take(12)
    step = pl.program_id(0)
    width = rows.shape[1]
    tile = w1s.shape[2]
    tall = tile + TAIL
    chunk = width // fsdp

    @pl.when(step == 0)
    def _():
        loads = []
        for index, ref in enumerate(pays):
            at = place_ref[HOMES + index]
            loads.append(pltpu.make_async_copy(ref.at[0:tall], w2s.at[at], sems_w.at[index, fsdp]))
            for block in range(fsdp):
                start = tall + block * chunk
                loads.append(
                    pltpu.make_async_copy(
                        ref.at[start : start + chunk, 0:tile],
                        w1s.at[block, pl.ds(pl.multiple_of(at * chunk, chunk), chunk)],
                        sems_w.at[index, block],
                    )
                )
        for load in loads:
            load.start()
        for index in range(count):
            rows[index * cap : (index + 1) * cap] = rows_in[index][...]
        router = dot(misc[...], router_order(place_ref[0], experts), NN).astype(bf16)
        gate = softmax_lanes(dot(rows[...], router, NN), experts)[:, 0:1]
        gates[...] = jnp.broadcast_to(gate, gates.shape)
        for index in range(count):
            part = slice(index * cap, (index + 1) * cap)
            ups[part] = (ups_in[index][...].astype(f32) * gate[part]).astype(bf16)
        acc_row[...] = jnp.zeros_like(acc_row)
        acc_out[...] = jnp.zeros_like(acc_out)
        bias2[...] = jnp.zeros_like(bias2)
        shift2[...] = jnp.sum(ups[...].astype(f32), axis=0, keepdims=True)
        for load in loads:
            load.wait()

    w1, w2 = w1s.at[step], w2s.at[step]
    tail = w2[tile:tall].astype(f32)
    bias2[...] += tail[1:2]
    x, up = rows[...], ups[...]
    value, slope = gelu_pair(dot(x, w1[...], NN) + tail[0:1, 0:tile])
    act = value
    acc_out[...] += dot(act, w2[0:tile], NN)
    pre = slope * dot(up, w2[0:tile], NT).astype(bf16)
    acc_row[...] += dot(pre, w1[...], NT)
    part1 = dot(x, pre, TN)
    part2 = dot(act, up, TN)
    shift1 = jnp.sum(pre.astype(f32), axis=0, keepdims=True)
    if tile < width:
        shift1 = jnp.concatenate([shift1, jnp.zeros((1, width - tile), f32)], axis=1)
    place = iota((TAIL, width), 0)
    sums = jnp.where(place == 0, shift1, jnp.where(place == 1, shift2[...], 0.0))
    if not first:
        part1, part2, sums = old[1][...] + part1, old[2][0, 0:tile] + part2, old[2][0, tile:] + sums
    if last:
        if tile < width:
            part1 = jnp.concatenate([part1, jnp.zeros((width, width - tile), f32)], axis=1)
        if split:
            for ref, fy in ((out1, place_ref[FY]), (out2, 1 - place_ref[FY])):

                @pl.when((step >> 1) == fy)
                def _():
                    ref[step & 1, 0:tile] = part2.astype(bf16)
                    ref[step & 1, tile:tall] = sums.astype(bf16)

            at = pl.multiple_of(step * chunk, TAIL)
            for index in range(fsdp):
                block = part1[index * chunk : (index + 1) * chunk].astype(bf16)
                for ref, fy in ((out3[0], place_ref[FY]), (out3[1], 1 - place_ref[FY])):

                    @pl.when(index // 2 == fy)
                    def _():
                        ref[index % 2, pl.ds(at, chunk), :] = block

        else:
            at = pl.multiple_of(tall + step * chunk, TAIL)
            out2[step, 0:tile] = part2.astype(bf16)
            out2[step, tile:tall] = sums.astype(bf16)
            for index in range(fsdp):
                out2[index, pl.ds(at, chunk), :] = part1[index * chunk : (index + 1) * chunk].astype(bf16)
    else:
        out1[...] = part1
        out2[0, 0:tile] = part2
        out2[0, tile:] = sums

    @pl.when(step == pl.num_programs(0) - 1)
    def _():
        copies = []
        for index, shift in enumerate(group):
            part = slice(index * cap, (index + 1) * cap)
            made = acc_out[part] + bias2[...]
            gate = gates[part, 0:1]
            gated[index] = (made * gate).astype(bf16)
            copies.append(
                pltpu.make_async_copy(gated.at[index], made_ref.at[place_ref[0] ^ shift], sems.at[index])
            )
            copies[-1].start()
            row_back[index][0:cap] = acc_row[part].astype(bf16)
            effect = jnp.sum(made * ups_in[index][...].astype(f32), axis=1, keepdims=True) * gate
            effect = jnp.concatenate([effect, jnp.zeros((width - cap, 1), f32)], axis=0)
            line = jnp.broadcast_to(effect, (width, LANES)).T[0:1]
            end = jnp.zeros((TAIL, width), f32)
            for order, piece in enumerate(pieces(line, 3)):
                end = jnp.where(place == order, piece.astype(f32), end)
            row_back[index][cap : cap + TAIL] = end.astype(bf16)
        for copy in copies:
            copy.wait()


def expert_call(spots, rows, ups, pays, pack, old, after, group, cap, experts, last):
    count = len(group)
    first = old is None
    fsdp = len(pays)
    high, width = pays[0].shape
    tall = high - width
    tile = tall - TAIL
    total = count * cap
    split = last and fsdp == 4
    column = pl.BlockSpec((width, tile), lambda h, _: (0, h))
    line = pl.BlockSpec((1, tall, width), lambda h, _: (h, 0, 0))
    far = pl.BlockSpec(memory_space=pl.ANY)
    if split:
        grads = [(2, tall, width)] * 2 + [(2, width, width)] * 2
    else:
        grads = [(fsdp, high, width)]

    operands = [spots, *rows, *ups, *pays, pack]
    aliases = {}
    if not first:
        aliases = {len(operands): count}
        operands += list(old)
    return pl.pallas_call(
        functools.partial(
            expert_kernel,
            cap=cap,
            group=group,
            first=first,
            last=last,
            experts=experts,
            fsdp=fsdp,
            split=split,
            skip=len(after),
        ),
        grid_spec=pltpu.PrefetchScalarGridSpec(
            num_scalar_prefetch=1,
            grid=(fsdp,),
            in_specs=[whole((cap, width))] * count
            + [pl.BlockSpec((cap, width), lambda h, _, at=v.shape[0] // cap - 1: (at, 0)) for v in ups]
            + [far] * fsdp
            + [pl.BlockSpec((width, LANES), lambda h, _: (0, 4 * width // LANES))]
            + ([] if first else [far, column, line])
            + [far] * len(after),
            out_specs=[whole((cap + TAIL, width))] * count
            + [far]
            + ([whole(v) for v in grads] if last else [column, line]),
            scratch_shapes=[pltpu.VMEM((total, width), bf16)] * 2
            + [pltpu.VMEM((total, LANES), f32)]
            + [pltpu.VMEM((total, width), f32)] * 2
            + [pltpu.VMEM((1, width), f32)] * 2
            + [pltpu.VMEM((count, cap, width), bf16), pltpu.SemaphoreType.DMA((count,))]
            + [pltpu.VMEM((fsdp, width, tile), bf16), pltpu.VMEM((fsdp, tall, width), bf16)]
            + [pltpu.SemaphoreType.DMA((fsdp, fsdp + 1))],
        ),
        out_shape=[jax.ShapeDtypeStruct((cap + TAIL, width), bf16)] * count
        + [jax.ShapeDtypeStruct((experts, cap, width), bf16)]
        + (
            [jax.ShapeDtypeStruct(v, bf16) for v in grads]
            if last
            else [
                jax.ShapeDtypeStruct((width, tile * fsdp), f32),
                jax.ShapeDtypeStruct((fsdp, tall, width), f32),
            ]
        ),
        input_output_aliases=aliases,
        compiler_params=params(),
        cost_estimate=cost(96),
        name="expert",
    )(*operands, *after)


def gather_back(places, backs, shifts, slot_sum, effect, cap):
    lane = iota((1, LANES), 1)
    for index, ref in zip(shifts, backs):
        hot = one_hot_cols(places[:, index : index + 1], cap)
        slot_sum = slot_sum + dot(hot, ref[0:cap], NN)
        parts = dot(hot, ref[cap : cap + TAIL, 0:cap], NT)
        effect = jnp.where(lane == index, jnp.sum(parts, axis=1, keepdims=True), effect)
    return slot_sum, effect


def returned_kernel(pos_ref, *refs, cap, shifts):
    backs, slot_ref, effect_ref = refs[: len(shifts)], refs[-2], refs[-1]
    _, rows, width = slot_ref.shape
    slot_ref[0], effect_ref[0] = gather_back(
        pos_ref[0, 0:rows, :], backs, shifts, jnp.zeros((rows, width), f32), jnp.zeros((rows, LANES), f32), cap
    )


def returned(pos, backs, shifts, rows, cap):
    images, width = pos.shape[0], backs[0].shape[1]

    def image(shape):
        return pl.BlockSpec((1,) + shape, lambda i: (i, 0, 0))

    return pl.pallas_call(
        functools.partial(returned_kernel, cap=cap, shifts=shifts),
        grid=(images,),
        in_specs=[image((pos.shape[1], LANES))] + [whole((cap + TAIL, width))] * len(backs),
        out_specs=[image((rows, width)), image((rows, LANES))],
        out_shape=[
            jax.ShapeDtypeStruct((images, rows, width), f32),
            jax.ShapeDtypeStruct((images, rows, LANES), f32),
        ],
        compiler_params=params(),
        cost_estimate=cost(100),
        name="returned",
    )(pos, *backs)


def middle_kernel(
    place_ref, up_ref, wout_ref, misc_ref, pos_ref, mixed_ref, hidden_ref, prob_ref, slot_ref, effect_ref, *rest, cap, experts
):
    backs = rest[:2]
    hidden_grad_ref, mixed_grad_ref, sums_ref, padded, vectors, router, shifts, acc_out, acc_router = rest[-9:]
    _, seq, width = up_ref.shape
    rows = padded.shape[0]
    step = pl.program_id(0)

    @pl.when(step == 0)
    def _():
        vectors[...] = misc_ref[...].astype(f32).T
        router[...] = dot(misc_ref[...], router_order(place_ref[0], experts), NN).astype(bf16)
        padded[...] = jnp.zeros_like(padded)
        shifts[...] = jnp.zeros_like(shifts)
        acc_out[...] = jnp.zeros_like(acc_out)
        acc_router[...] = jnp.zeros_like(acc_router)

    def vector(index):
        return vectors[VEC + index : VEC + index + 1, :]

    def shift(index, value):
        shifts[index : index + 1, :] += jnp.sum(value, axis=0, keepdims=True)

    slot_sum, effect = gather_back(pos_ref[0, 0:rows, :], backs, (0, 1), slot_ref[0], effect_ref[0], cap)
    prob = prob_ref[0]
    logit_grad = effect - prob * jnp.sum(effect, axis=1, keepdims=True)
    logit_parts = pieces(logit_grad, 2)
    mid_grad = slot_sum
    for part in logit_parts:
        mid_grad = mid_grad + dot(part, router[...], NT)
    padded[0:seq] = up_ref[0].astype(f32)
    hat, inverse = norm_stats(hidden_ref[0])
    mid_parts = pieces(hat * vector(5) + vector(6), 2)
    acc_router[...] += (
        dot(logit_parts[0], mid_parts[0], TN)
        + dot(logit_parts[0], mid_parts[1], TN)
        + dot(logit_parts[1], mid_parts[0], TN)
    )
    shift(5, mid_grad * hat)
    shift(6, mid_grad)
    hidden_grad = padded[...] + norm_back(mid_grad, vector(5), hat, inverse)
    hidden_grad_ref[0] = hidden_grad
    branch = hidden_grad.astype(bf16)
    shift(4, branch.astype(f32))
    acc_out[...] += dot(mixed_ref[0], branch, TN)
    mixed_grad_ref[0] = dot(branch, wout_ref[...], NT).astype(bf16)

    @pl.when(step == pl.num_programs(0) - 1)
    def _():
        sums_ref[:, 0:width] = acc_out[...]
        ordered = dot(router_order(place_ref[0], experts), acc_router[...].astype(bf16), NN)
        spare = jnp.concatenate(
            [ordered[0:VEC], shifts[...], jnp.zeros((LANES - VEC - shifts.shape[0], width), f32)], axis=0
        )
        sums_ref[:, width:] = spare.T


def middle(place, grad_output, pack, pos, saved, part_sums, backs, cap, experts):
    images, seq, width = grad_output.shape
    _, mixed, hidden, prob, _ = saved
    rows = mixed.shape[1]

    def image(shape):
        return pl.BlockSpec((1,) + shape, lambda i: (i, 0, 0))

    return pl.pallas_call(
        functools.partial(middle_kernel, cap=cap, experts=experts),
        grid=(images,),
        in_specs=[
            pl.BlockSpec(memory_space=pltpu.SMEM),
            image((seq, width)),
            pl.BlockSpec((width, width), lambda i: (0, 3)),
            pl.BlockSpec((width, LANES), lambda i: (0, 4 * width // LANES)),
            image((pos.shape[1], LANES)),
            image((rows, width)),
            image((rows, width)),
            image((rows, LANES)),
            image((rows, width)),
            image((rows, LANES)),
        ]
        + [whole((cap + TAIL, width))] * len(backs),
        out_specs=[image((rows, width)), image((rows, width)), whole((width, width + LANES))],
        out_shape=[
            jax.ShapeDtypeStruct((images, rows, width), f32),
            jax.ShapeDtypeStruct((images, rows, width), bf16),
            jax.ShapeDtypeStruct((width, width + LANES), f32),
        ],
        scratch_shapes=[
            pltpu.VMEM((rows, width), f32),
            pltpu.VMEM((LANES, width), f32),
            pltpu.VMEM((width, LANES), bf16),
            pltpu.VMEM((8, width), f32),
            pltpu.VMEM((width, width), f32),
            pltpu.VMEM((LANES, width), f32),
        ],
        compiler_params=params(),
        cost_estimate=cost(0.02),
        name="middle",
    )(place, grad_output, pack, pack, pos, mixed, hidden, prob, *part_sums, *backs)


def backward_kernel(
    spots_ref, tok_ref, qkv_ref, attn_ref, mixed_grad_ref, *rest, head_rows, members
):
    sums_ref, peak_ref = rest[:2]
    qkv_grad_ref, keep_ref, give_ref, padded, acc_qkv, columns, spare, misc = rest[-8:]
    _, seq, width = tok_ref.shape
    rows = padded.shape[0]
    head = width // HEADS
    wide = 3 * width
    step = pl.program_id(0)

    @pl.when(step == 0)
    def _():
        padded[...] = jnp.zeros_like(padded)
        acc_qkv[...] = jnp.zeros_like(acc_qkv)
        columns[...] = jnp.zeros_like(columns)

    lane = iota((1, LANES), 1)
    first = lane < head
    halves = (jnp.where(first, 1.0, 0.0).astype(bf16), jnp.where(first, 0.0, 1.0).astype(bf16))

    def pair(index, carry):
        at = pl.multiple_of(index * LANES, LANES)
        query = qkv_ref[0, :, pl.ds(at, LANES)]
        key = qkv_ref[0, :, pl.ds(width + at, LANES)]
        value = qkv_ref[0, :, pl.ds(2 * width + at, LANES)]
        up = mixed_grad_ref[0, :, pl.ds(at, LANES)]
        made = []
        for half in range(2):
            low = attn_ref[0, index * 2 + half]
            weight = low.astype(f32)
            value_grad = dot(low, up, TN)
            spread = weight * dot(up * halves[half], value, NT)
            score_grad = (spread - weight * jnp.sum(spread, axis=1, keepdims=True)).astype(bf16)
            made.append((dot(score_grad, key, NN) * head**-0.5, dot(score_grad, query, TN), value_grad))
        for index_of, (left, right) in enumerate(zip(*made)):
            qkv_grad_ref[0, :, pl.ds(index_of * width + at, LANES)] = jnp.where(first, left, right).astype(bf16)
        return carry

    lax.fori_loop(0, HEADS // 2, pair, 0, unroll=True)
    columns[...] += jnp.sum(qkv_grad_ref[0].astype(f32), axis=0, keepdims=True)
    padded[0:seq] = tok_ref[0].astype(f32)
    hat, _ = norm_stats(padded[...])
    acc_qkv[...] += dot(hat.astype(bf16), qkv_grad_ref[0], TN)
    part = keep_ref.shape[1]

    @pl.when(step == pl.num_programs(0) - 1)
    def _():
        line = iota((LANES, width), 0)
        flat = columns[...]
        grown = jnp.where(line == VEC + 2, flat[:, 0:width], 0.0)
        grown = jnp.where(line == VEC + 3, flat[:, 2 * width :], grown)
        misc[...] = sums_ref[:, width:] + grown.T
        spare[...] = jnp.zeros_like(spare)
        number = wide // LANES
        for order, piece in enumerate(pieces(flat, 3)):
            value = piece.astype(f32)
            for index in range(number):
                at = order * number + index
                spare[at : at + 1, :] = value[:, index * LANES : (index + 1) * LANES]
        if members:
            top = jnp.where(lane < HEADS, peak_ref[...], 0.0)
            rows_of = jnp.zeros((TAIL, LANES), f32)
            for order, piece in enumerate(pieces(jnp.broadcast_to(top, (TAIL, LANES)), 3)):
                move = jnp.where(iota((LANES, LANES), 1) == iota((LANES, LANES), 0) + order * HEADS, 1.0, 0.0)
                rows_of = rows_of + dot(piece, move.astype(bf16), NN)
            spare[pl.ds(head_rows + spots_ref[NUMBER], 1), :] = rows_of[0:1]
        extra = spare[...].astype(bf16)
        for fy in range(keep_ref.shape[0]):
            for ref, core in ((keep_ref, spots_ref[CORE]), (give_ref, 1 - spots_ref[CORE])):
                at = pl.multiple_of((2 * fy + core) * part, part)
                ref[fy, :, 0:wide] = acc_qkv[pl.ds(at, part), :].astype(bf16)
                ref[fy, :, wide : wide + width] = sums_ref[pl.ds(at, part), 0:width].astype(bf16)
                ref[fy, :, wide + width : wide + width + LANES] = misc[pl.ds(at, part), :].astype(bf16)
                ref[fy, :, wide + width + LANES :] = extra


def backward(spots, tokens, saved, mixed_grad, sums, peak, after, ways, part, head_rows, members):
    images, seq, width = tokens.shape
    qkv, attn = saved[0], saved[-1]
    rows = qkv.shape[1]
    wide = 4 * width + 2 * LANES

    def image(shape):
        return pl.BlockSpec((1,) + shape, lambda i: (i,) + (0,) * len(shape))

    return pl.pallas_call(
        functools.partial(backward_kernel, head_rows=head_rows, members=members),
        grid=(images,),
        in_specs=[
            pl.BlockSpec(memory_space=pltpu.SMEM),
            image((seq, width)),
            image((rows, 3 * width)),
            image((HEADS, rows, rows)),
            image((rows, width)),
            whole(sums.shape),
            whole(peak.shape),
        ]
        + [pl.BlockSpec(memory_space=pl.ANY)] * len(after),
        out_specs=[image((rows, 3 * width)), whole((ways, part, wide)), whole((ways, part, wide))],
        out_shape=[
            jax.ShapeDtypeStruct((images, rows, 3 * width), bf16),
            jax.ShapeDtypeStruct((ways, part, wide), bf16),
            jax.ShapeDtypeStruct((ways, part, wide), bf16),
        ],
        scratch_shapes=[
            pltpu.VMEM((rows, width), f32),
            pltpu.VMEM((width, 3 * width), f32),
            pltpu.VMEM((1, 3 * width), f32),
            pltpu.VMEM((part, LANES), f32),
            pltpu.VMEM((width, LANES), f32),
        ],
        compiler_params=params(),
        cost_estimate=cost(0.05),
        name="attend_back",
    )(spots, tokens, qkv, attn, mixed_grad, sums, peak, *after)


def first_kernel(tok_ref, qkv_grad_ref, wqkv_ref, misc_ref, hidden_grad_ref, grad_ref, padded, gain):
    _, seq, width = tok_ref.shape

    @pl.when(pl.program_id(0) == 0)
    def _():
        gain[...] = misc_ref[...].astype(f32).T[VEC : VEC + 1]
        padded[...] = jnp.zeros_like(padded)

    in_grad = dot(qkv_grad_ref[0], wqkv_ref[...], NT)
    padded[0:seq] = tok_ref[0].astype(f32)
    hat, inverse = norm_stats(padded[...])
    grad_ref[0] = (hidden_grad_ref[0] + norm_back(in_grad, gain[...], hat, inverse))[0:seq]


def first_norm(tokens, qkv_grad, pack, hidden_grad):
    images, seq, width = tokens.shape
    rows = qkv_grad.shape[1]

    def image(shape):
        return pl.BlockSpec((1,) + shape, lambda i: (i, 0, 0))

    return pl.pallas_call(
        first_kernel,
        grid=(images,),
        in_specs=[
            image((seq, width)),
            image((rows, 3 * width)),
            pl.BlockSpec((width, 3 * width), lambda i: (0, 0)),
            pl.BlockSpec((width, LANES), lambda i: (0, 4 * width // LANES)),
            image((rows, width)),
        ],
        out_specs=image((seq, width)),
        out_shape=jax.ShapeDtypeStruct((images, seq, width), f32),
        scratch_shapes=[pltpu.VMEM((rows, width), f32), pltpu.VMEM((1, width), f32)],
        compiler_params=params(),
        cost_estimate=cost(0.02),
        name="first_norm",
    )(tokens, qkv_grad, pack, pack, hidden_grad)


def output_kernel(place_ref, pos_ref, hidden_ref, made_ref, out_ref):
    experts, cap, _ = made_ref.shape
    seq = out_ref.shape[1]
    total = hidden_ref[0]
    places = pos_ref[0, 0 : total.shape[0], :]
    for index in range(experts):
        total = total + dot(one_hot_cols(places[:, index : index + 1], cap), made_ref[place_ref[0] ^ index], NN)
    out_ref[0] = total[0:seq].astype(bf16)


def combine_output(place, pos, hidden, made, seq):
    images, rows, width = hidden.shape

    def image(shape):
        return pl.BlockSpec((1,) + shape, lambda i: (i, 0, 0))

    return pl.pallas_call(
        output_kernel,
        grid=(images,),
        in_specs=[
            pl.BlockSpec(memory_space=pltpu.SMEM),
            image((pos.shape[1], LANES)),
            image((rows, width)),
            whole(made.shape),
        ],
        out_specs=image((seq, width)),
        out_shape=jax.ShapeDtypeStruct((images, seq, width), bf16),
        compiler_params=params(),
        cost_estimate=cost(0.02),
        name="combine",
    )(place, pos, hidden, made)


def finish_kernel(slot_ref, *refs, number, head_rows, members):
    parts, (own_ref, limit_ref, peak_ref) = refs[:number], refs[number : number + 3]
    qkv_ref, out_ref, misc_ref, clip_ref, *vec_refs, total_ref = refs[number + 3 :]
    part = own_ref.shape[0]
    for shift, ref in enumerate(parts):
        size = part // number
        total_ref[pl.ds(pl.multiple_of((slot_ref[LOW] ^ shift) * size, size), size), :] = ref[...]
    width = out_ref.shape[1]
    wide = 3 * width
    number = wide // LANES
    base = total_ref[:, 0:wide].astype(f32)
    extra = total_ref[:, wide + width + LANES :].astype(f32)
    weight = own_ref[:, 0:wide].astype(f32)
    columns = [sum(extra[k * number + i : k * number + i + 1] for k in range(3)) for i in range(number)]
    columns = jnp.concatenate(columns, axis=1)
    own = own_ref[:, wide + width :].astype(f32)
    gain, bias = own[:, VEC : VEC + 1], own[:, VEC + 1 : VEC + 2]
    qkv_ref[...] = base * gain + bias * columns
    out_ref[...] = total_ref[:, wide : wide + width].astype(f32)
    misc = total_ref[:, wide + width : wide + width + LANES].astype(f32)
    lane = iota((1, LANES), 1)
    misc = jnp.where(lane == VEC, jnp.sum(base * weight, axis=1, keepdims=True), misc)
    misc = jnp.where(lane == VEC + 1, jnp.sum(columns * weight, axis=1, keepdims=True), misc)
    misc = misc.T
    for index, ref in enumerate(vec_refs):
        ref[...] = misc[VEC + index : VEC + index + 1]
    misc_ref[...] = misc[0 : misc_ref.shape[0]]
    if members:
        move = jnp.where(
            (iota((LANES, LANES), 0) % HEADS == iota((LANES, LANES), 1)) & (iota((LANES, LANES), 0) < 3 * HEADS),
            1.0,
            0.0,
        )
        peaks = dot(total_ref[head_rows : head_rows + members, wide + width + LANES :], move.astype(bf16), NN)
        peak = jnp.max(peaks, axis=0, keepdims=True)
    else:
        peak = peak_ref[...]
    limit = jnp.concatenate([limit_ref[...].astype(f32), jnp.ones((1, LANES - HEADS), f32)], axis=1)
    root = jnp.sqrt(limit / jnp.maximum(peak, limit))
    place = iota((1, width), 1) // (width // HEADS)
    scale = jnp.zeros((1, width), f32)
    for index in range(HEADS):
        scale = jnp.where(place == index, root[:, index : index + 1], scale)
    clip_ref[:, 0:width] = (weight[:, 0:width] * scale).astype(bf16)
    clip_ref[:, width : 2 * width] = (weight[:, width : 2 * width] * scale).astype(bf16)
    clip_ref[:, 2 * width :] = own_ref[:, 2 * width : wide]


def finish(slot, total, own, limit, peak, width, experts, head_rows, members):
    part = own.shape[0]
    operands = [*total, own, limit, peak]
    shapes = [(part, 3 * width), (part, width), (experts, part), (part, 3 * width)] + [(1, part)] * 7
    return pl.pallas_call(
        functools.partial(finish_kernel, number=len(total), head_rows=head_rows, members=members),
        grid=(1,),
        in_specs=[pl.BlockSpec(memory_space=pltpu.SMEM)] + [whole(v.shape) for v in operands],
        out_specs=[whole(v) for v in shapes],
        out_shape=[jax.ShapeDtypeStruct(v, bf16 if i == 3 else f32) for i, v in enumerate(shapes)],
        scratch_shapes=[pltpu.VMEM((part, total[0].shape[1]), bf16)],
        compiler_params=params(),
        cost_estimate=cost(0.02),
        name="finish",
    )(slot, *operands)


def half_sums_kernel(high_ref, keep_ref, got_ref, *rest):
    straight_ref, crossed_ref = rest[-2:]
    for ref, core in ((straight_ref, high_ref[HIGH]), (crossed_ref, 1 - high_ref[HIGH])):
        ref[...] = (keep_ref[core].astype(f32) + got_ref[core].astype(f32)).astype(bf16)


def half_sums(high, keep, got, after, micros):
    shape = keep.shape[1:]
    return pl.pallas_call(
        half_sums_kernel,
        grid=(1,),
        in_specs=[pl.BlockSpec(memory_space=pltpu.SMEM), whole(keep.shape), whole(got.shape)]
        + [pl.BlockSpec(memory_space=pl.ANY)] * len(after),
        out_specs=[whole(shape)] * 2,
        out_shape=[jax.ShapeDtypeStruct(shape, bf16)] * 2,
        compiler_params=params(),
        cost_estimate=cost(micros),
        name="half_sums",
    )(high, keep, got, *after)


def both_halves(spot_ref, one, two, own, rows):
    straight = jnp.where(spot_ref[SAME] == 1, own[rows].astype(f32), one[rows].astype(f32))
    return straight + two[rows].astype(f32)


def home_second_kernel(spot_ref, one, two, own, _, w2_ref, b1_ref, b2_ref):
    tile, width = w2_ref.shape
    part = b2_ref.shape[1]
    w2_ref[...] = both_halves(spot_ref, one, two, own, slice(0, tile))
    edge = both_halves(spot_ref, one, two, own, slice(tile, tile + TAIL))
    b1_ref[...] = edge[0:1, 0:tile]
    b2_ref[...] = sum(
        jnp.where(spot_ref[SPOT] == index, edge[1:2, index * part : (index + 1) * part], 0.0)
        for index in range(width // part)
    )


def home_first_kernel(spot_ref, one, two, own, _, w1_ref):
    part, hidden = w1_ref.shape
    number = one.shape[0] // part
    tile = hidden // number
    for index in range(number):
        total = both_halves(spot_ref, one, two, own, slice(index * part, (index + 1) * part))
        w1_ref[:, index * tile : (index + 1) * tile] = total[:, 0:tile]


def home_sums(kernel, spot, pair, after, shapes):
    return pl.pallas_call(
        kernel,
        grid=(1,),
        in_specs=[pl.BlockSpec(memory_space=pltpu.SMEM)]
        + [whole(v.shape) for v in pair]
        + [pl.BlockSpec(memory_space=pl.ANY)],
        out_specs=[whole(v) for v in shapes],
        out_shape=[jax.ShapeDtypeStruct(v, f32) for v in shapes],
        compiler_params=params(),
        cost_estimate=cost(0.02),
        name="home_sums",
    )(spot, *pair, after)


def add_halves_kernel(fy_ref, keep_ref, got_ref, *rest):
    mine_ref, theirs_ref = rest[-2:]
    for ref, half in ((mine_ref, fy_ref[FY]), (theirs_ref, 1 - fy_ref[FY])):
        ref[...] = (keep_ref[half].astype(f32) + got_ref[half].astype(f32)).astype(bf16)


def add_halves(fy, keep, got, after):
    shape = keep.shape[1:]
    return pl.pallas_call(
        add_halves_kernel,
        grid=(1,),
        in_specs=[pl.BlockSpec(memory_space=pltpu.SMEM), whole(keep.shape), whole(got.shape)]
        + [pl.BlockSpec(memory_space=pl.ANY)] * len(after),
        out_specs=[whole(shape)] * 2,
        out_shape=[jax.ShapeDtypeStruct(shape, bf16)] * 2,
        compiler_params=params(),
        cost_estimate=cost(0.02),
        name="add_halves",
    )(fy, keep, got, *after)


def split_rows_kernel(slot_ref, mine_ref, got_ref, *refs, skip):
    outs, total = refs[skip:-1], refs[-1]
    total[...] = (mine_ref[...].astype(f32) + got_ref[...].astype(f32)).astype(bf16)
    size = outs[0].shape[0]
    for shift, ref in enumerate(outs):
        ref[...] = total[pl.ds(pl.multiple_of((slot_ref[LOW] ^ shift) * size, size), size), :]


def split_rows(slot, mine, got, after, number):
    part, wide = mine.shape
    shape = (part // number, wide)
    return pl.pallas_call(
        functools.partial(split_rows_kernel, skip=len(after)),
        grid=(1,),
        in_specs=[pl.BlockSpec(memory_space=pltpu.SMEM), whole(mine.shape), whole(got.shape)]
        + [pl.BlockSpec(memory_space=pl.ANY)] * len(after),
        out_specs=[whole(shape)] * number,
        out_shape=[jax.ShapeDtypeStruct(shape, bf16)] * number,
        scratch_shapes=[pltpu.VMEM((part, wide), bf16)],
        compiler_params=params(),
        cost_estimate=cost(0.02),
        name="split_rows",
    )(slot, mine, got, *after)


def add_parts_kernel(*refs, number):
    parts, out_ref = refs[:number], refs[-1]
    out_ref[...] = sum(ref[...].astype(f32) for ref in parts).astype(bf16)


def add_parts(parts, after=()):
    shape = parts[0].shape
    return pl.pallas_call(
        functools.partial(add_parts_kernel, number=len(parts)),
        grid=(1,),
        in_specs=[whole(shape)] * len(parts) + [pl.BlockSpec(memory_space=pl.ANY)] * len(after),
        out_specs=whole(shape),
        out_shape=jax.ShapeDtypeStruct(shape, bf16),
        compiler_params=params(),
        cost_estimate=cost(0.02),
        name="add_parts",
    )(*parts, *after)


def swap(value, axis):
    return lax.ppermute(value, axis, [(0, 1), (1, 0)])


def around(value, axis, size):
    return [value] + [
        lax.ppermute(value, axis, [((k + step) % size, k) for k in range(size)]) for step in range(1, size)
    ]


def split_sum(value, axis, size):
    if size != 2:
        return lax.psum_scatter(value, axis, scatter_dimension=0, tiled=False)
    place = lax.axis_index(axis)
    sent = lax.dynamic_index_in_dim(value, 1 - place, 0, keepdims=False)
    kept = lax.dynamic_index_in_dim(value, place, 0, keepdims=False)
    return (kept.astype(f32) + swap(sent, axis).astype(f32)).astype(value.dtype)


def exchange(value, shift, experts):
    return lax.ppermute(value, GROUP, [(k, k ^ shift) for k in range(experts)])


def shift_order(experts):
    def key(shift):
        distance = bin(shift >> 1).count("1")
        return (shift & 1, -distance, shift)

    order = sorted(range(2, experts), key=key)
    half = len(order) // 2
    return [order[:half], order[half:], [0, 1]]


STRAIGHT = [(1, 2), (2, 1)]
CROSSED = [(0, 2), (1, 0), (2, 3), (3, 1)]
BACK = [(b, a) for a, b in STRAIGHT]
BACK_CROSSED = [(b, a) for a, b in CROSSED]


def shards(
    tokens,
    ln1_gain,
    ln1_bias,
    w_qkv,
    q_bias,
    v_bias,
    w_out,
    out_bias,
    ln2_gain,
    ln2_bias,
    w_router,
    expert_w1,
    expert_b1,
    expert_w2,
    expert_b2,
    route_ids,
    clip_threshold,
    grad_output,
    *,
    experts,
    fsdp,
):
    images, seq, width = tokens.shape
    token_count = images * seq
    ways = fsdp // 2
    cap = (7 * token_count // (2 * experts) + 7) // 8 * 8
    stride = -(-seq // 256) * 256
    rows = -(-seq // 16) * 16
    part = w_qkv.shape[0]
    hidden_part = expert_w2.shape[1]
    high, low, fy, core = (lax.axis_index(name).astype(i32) for name in DEVICE)
    spot = fy * 2 + core
    homes = [((fy + step) % ways) * 2 for step in range(ways)]
    spots = jnp.stack(
        [
            low * 2 + core,
            fy,
            core,
            ((high * (experts // 2) + low) * ways + fy) * 2 + core,
            high,
            spot,
            (high == core).astype(i32),
            low,
            *[home + high for home in homes],
            *[home + 1 - high for home in homes],
            *[home + core for home in homes],
            *[home + 1 - core for home in homes],
        ]
    )

    vectors = (ln1_gain, ln1_bias, q_bias, v_bias, out_bias, ln2_gain, ln2_bias)
    own, pay = pack_parameters(
        spots, w_qkv, w_out, w_router, vectors, expert_w1[0], expert_w2[0], expert_b1, expert_b2
    )

    near = around(own, "fy", ways)
    straight = lax.ppermute(pay, ("hi", "core"), STRAIGHT)

    groups = shift_order(experts)
    hot, pos, post, *firsts = route(spots, route_ids.T, grad_output, groups[0], experts, cap, stride)
    near[1:], hot, own_later = lax.optimization_barrier((near[1:], hot, own))
    firsts = [exchange(value, shift, experts) for shift, value in zip(groups[0], firsts)]
    far = [swap(own_later, "core")]
    far += [swap(value, "core") for value in near[1:]]
    early = 1
    begun = list(forward(spots, tokens, near + far, None, [], 0, early, experts, stride, rows))
    pay, straight, begun[0] = lax.optimization_barrier((pay, straight, begun[0]))
    straight = jnp.where(high == core, pay, straight)
    crossed = lax.ppermute(pay, ("hi", "core"), CROSSED)
    pays = around(straight, "fy", ways)
    *saved, mid, peak, pack = forward(
        spots, tokens, [], begun, [straight], early, images - early, experts, stride, rows
    )
    mid = mid.reshape(images * stride, width)
    ready = dispatch(hot, mid)
    rest = [shift for group in groups[1:] for shift in group]
    cut = len(firsts) - len(firsts) // 3
    sent = dict(zip(rest, dispatch_both(post, mid, grad_output, firsts[cut:], rest, cap, stride)))
    crossed, ready, firsts[:cut], *pays[1:] = lax.optimization_barrier(
        (crossed, list(ready), firsts[:cut], *pays[1:])
    )
    sent.update(zip(groups[0], ready))
    ups = dict(zip(groups[0], firsts))
    pays += around(crossed, "fy", ways)

    arrived = {}

    def send(number, after):
        pending, after = lax.optimization_barrier(([sent[shift] for shift in groups[number]], after))
        for shift, value in zip(groups[number], pending):
            arrived[shift] = value if shift == 0 else exchange(value, shift, experts)
        return after

    send(0, ())
    first = send(1, [arrived[shift] for shift in groups[0]])
    arrived.update(zip(groups[0], first))
    old, after = None, []
    backs = {}
    for number, group in enumerate(groups):
        result = expert_call(
            spots,
            [arrived[shift] for shift in group],
            [ups.get(shift, arrived[shift]) for shift in group],
            pays,
            pack,
            old,
            after,
            group,
            cap,
            experts,
            number == len(groups) - 1,
        )
        old = result[len(group) :]
        after = [backs[shift] for shift in groups[number - 1]] if number else []
        out = result[: len(group)]
        if number + 2 < len(groups):
            out = send(number + 2, out)
        for at, shift in enumerate(group):
            backs[shift] = out[at] if shift == 0 else exchange(out[at], shift, experts)
    backs = [backs[shift] for shift in range(experts)]
    made, *grad = old
    made = lax.all_to_all(made, GROUP, split_axis=0, concat_axis=0, tiled=True)

    shifts = tuple(range(2, experts))
    part_sums = returned(pos, backs[2:], shifts, rows, cap)
    hidden_grad, mixed_grad, sums = middle(
        spots, grad_output, pack, pos, saved, part_sums, backs[:2], cap, experts
    )
    head_rows = 3 * (3 * width // LANES) + 4
    devices = 2 * experts // 2 * fsdp
    members = devices if head_rows + devices <= part else 0

    def homeward(straight, crossed):
        return [
            lax.ppermute(straight, ("hi", "core"), BACK),
            lax.ppermute(crossed, ("hi", "core"), BACK_CROSSED),
            straight,
        ]

    if len(grad) == 4:
        sums_two = list(half_sums(spots, grad[0], swap(grad[1], "fy"), [sums], 0.02))
        home_two = homeward(*sums_two)
        grad[3], sums_two[0] = lax.optimization_barrier((grad[3], sums_two[0]))
        got_one = swap(grad[3], "fy")
    else:
        half = split_sum(grad[0].reshape((ways, 2) + grad[0].shape[1:]), "fy", ways)
        home = homeward(*(lax.dynamic_index_in_dim(half, k, 0, keepdims=False) for k in (high, 1 - high)))
        tall = hidden_part + TAIL
        home_two, home_one = [v[:tall] for v in home], [v[tall:] for v in home]
    qkv_grad, keep, give = backward(
        spots, tokens, saved, mixed_grad, sums, peak, [], ways, part, head_rows, members
    )

    got = swap(give, "core")
    after = []
    if len(grad) == 4:
        after = half_sums(spots, grad[2], got_one, home_two[:2], 40)
        home_one = homeward(*after)
    output = combine_output(spots, pos, saved[2], made, seq)
    near_by = experts // 2
    if ways == 2 and part % (TAIL * near_by) == 0:

        def spread(values):
            return [
                value if k == 0 else lax.ppermute(value, "lo", [(j, j ^ k) for j in range(near_by)])
                for k, value in enumerate(values)
            ]

        mine, theirs = add_halves(spots, keep, got, after)
        theirs, qkv_grad = lax.optimization_barrier((theirs, qkv_grad))
        input_grad = first_norm(tokens, qkv_grad, pack, hidden_grad)
        parts = split_rows(spots, mine, swap(theirs, "fy"), [input_grad, output, *home_one[:2]], near_by)
        total = add_parts(spread(parts))
        shapes = [(hidden_part, width), (1, hidden_part), (1, part)]
        grad_w2, grad_b1, grad_b2 = home_sums(home_second_kernel, spots, home_two, total, shapes)
        shapes = [(part, hidden_part * fsdp)]
        (grad_w1,) = home_sums(home_first_kernel, spots, home_one, total, shapes)
        total = add_parts([total, swap(total, "hi")], [grad_w2, grad_w1])
        total = spread([total] * near_by)
    else:
        sums = split_sum((keep.astype(f32) + got.astype(f32)).astype(bf16), "fy", ways)
        total = [lax.psum(sums, ("hi", "lo"))]
        shapes = [(hidden_part, width), (1, hidden_part), (1, part)]
        grad_w2, grad_b1, grad_b2 = home_sums(home_second_kernel, spots, home_two, total[0], shapes)
        shapes = [(part, hidden_part * fsdp)]
        (grad_w1,) = home_sums(home_first_kernel, spots, home_one, total[0], shapes)
        input_grad = first_norm(tokens, qkv_grad, pack, hidden_grad)
    if not members:
        peak = jnp.max(lax.all_gather(peak, DEVICE, axis=0, tiled=True), axis=0, keepdims=True)
    limit = clip_threshold.reshape(1, HEADS)
    grad_qkv, grad_out, grad_router, clipped, *grads = finish(
        spots, total, own, limit, peak, width, experts, head_rows, members
    )
    grads = [v.reshape(part) for v in grads]
    return (
        output,
        input_grad,
        grads[0],
        grads[1],
        grad_qkv,
        grads[2],
        grads[3],
        grad_out,
        grads[4],
        grads[5],
        grads[6],
        grad_router.T,
        grad_w1[None],
        grad_b1,
        grad_w2[None],
        grad_b2,
        clipped,
    )


def solution(mesh):
    experts, fsdp = mesh.shape["expert"], mesh.shape["fsdp"]
    inner = Mesh(mesh.devices.reshape(2, experts // 2, fsdp // 2, 2), DEVICE)
    token, row, expert = P(DEVICE, None, None), ("fy", "core"), ("hi", "lo")
    vector, matrix = P(row), P(row, None)
    return jax.shard_map(
        functools.partial(shards, experts=experts, fsdp=fsdp),
        mesh=inner,
        in_specs=(
            token,
            vector,
            vector,
            matrix,
            vector,
            vector,
            matrix,
            vector,
            vector,
            vector,
            matrix,
            P(expert, row, None),
            P(expert, row),
            P(expert, row, None),
            P(expert, row),
            P(DEVICE, None),
            P(),
            token,
        ),
        out_specs=(
            token,
            token,
            vector,
            vector,
            matrix,
            vector,
            vector,
            matrix,
            vector,
            vector,
            vector,
            matrix,
            P(expert, row, None),
            P(expert, row),
            P(expert, row, None),
            P(expert, row),
            matrix,
        ),
        check_vma=False,
    )
```

```python
import functools

import jax
import jax.numpy as jnp
from jax import lax
from jax.experimental import pallas as pl
from jax.experimental.pallas import tpu as pltpu
from jax.sharding import Mesh
from jax.sharding import PartitionSpec as P

HEADS = 8
EPS = 1e-06
LANES = 128
VEC = 64
TAIL = 16
NEG = -1e30
f32 = jnp.float32
bf16 = jnp.bfloat16
i32 = jnp.int32
NN = (((1,), (0,)), ((), ()))
NT = (((1,), (1,)), ((), ()))
TN = (((0,), (0,)), ((), ()))
DEVICE = ("hi", "lo", "fy", "core")
GROUP = ("lo", "core")
PLACE, FY, CORE, NUMBER, HIGH, SPOT, SAME, LOW, HOMES = range(9)
VMEM_LIMIT = 64 << 20


def dot(a, b, dims):
    return lax.dot_general(a, b, dims, preferred_element_type=f32)


def pieces(value, count):
    parts = []
    for _ in range(count):
        part = value.astype(bf16)
        parts.append(part)
        value = value - part.astype(f32)
    return parts


def iota(shape, axis):
    return lax.broadcasted_iota(i32, shape, axis)


def relative_expert(place, shift, experts):
    other = jnp.bitwise_xor(place, shift)
    return (other & 1) * (experts // 2) + (other >> 1)


def router_order(place, experts):
    row, col = iota((LANES, LANES), 0), iota((LANES, LANES), 1)
    return jnp.where((row == relative_expert(place, col, experts)) & (col < experts), 1.0, 0.0).astype(bf16)


def norm_stats(matrix):
    centred = matrix - jnp.mean(matrix, axis=1, keepdims=True)
    inverse = lax.rsqrt(jnp.mean(centred * centred, axis=1, keepdims=True) + EPS)
    return centred * inverse, inverse


def norm_back(upstream, gain, hat, inverse):
    scaled = upstream * gain
    spread = (
        scaled
        - jnp.mean(scaled, axis=1, keepdims=True)
        - hat * jnp.mean(scaled * hat, axis=1, keepdims=True)
    )
    return spread * inverse


def softmax_lanes(logits, experts):
    logits = jnp.where(iota(logits.shape, 1) < experts, logits, NEG)
    top = jnp.max(logits, axis=1, keepdims=True)
    weight = jnp.exp(logits - top)
    return weight / jnp.sum(weight, axis=1, keepdims=True)


def gelu_pair(value):
    def low(number):
        return jnp.asarray(number, bf16)

    value = value.astype(bf16)
    bell = jnp.exp(value * value * low(-0.5))
    t = low(1.0) / (low(1.0) + jnp.abs(value) * low(0.3275911 * 0.7071067811865476))
    poly = low(0.7107068705) + t * (low(-0.7265760135) + t * low(0.5307027145))
    poly = t * (low(0.127414796) + t * (low(-0.142248368) + t * poly))
    lower = poly * bell
    phi = jnp.where(value >= low(0.0), low(1.0) - lower, lower)
    return value * phi, phi + value * (bell * low(0.3989422804014327))


def whole(shape):
    return pl.BlockSpec(shape, lambda *_: (0,) * len(shape))


def params(**extra):
    return pltpu.CompilerParams(vmem_limit_bytes=VMEM_LIMIT, **extra)


def cost(micros):
    return pl.CostEstimate(flops=int(micros * 1e9), bytes_accessed=0, transcendentals=0)


def pack_kernel(spot_ref, wqkv, wout, router, *rest):
    vectors, (w1, w2, b1, b2, pack_ref, pay_ref, spread, tail) = rest[:-8], rest[-8:]
    part, wide = wqkv.shape
    width, hidden = wout.shape[1], w2.shape[0]
    pack_ref[:, 0:wide] = wqkv[...]
    pack_ref[:, wide : wide + width] = wout[...]
    spread[...] = jnp.zeros_like(spread)
    spread[0 : router.shape[0], :] = router[...].astype(f32)
    for index, ref in enumerate(vectors):
        spread[VEC + index : VEC + index + 1, :] = ref[...].astype(f32)
    columns = spread[...].T
    pack_ref[:, wide + width :] = columns.astype(bf16)
    pay_ref[0:hidden] = w2[...]
    tail[...] = jnp.zeros_like(tail)
    tail[0:1, 0 : b1.shape[1]] = b1[...].astype(f32)
    copies = jnp.concatenate([b2[...].astype(f32)] * (width // part), axis=1)
    tail[1:2] = jnp.where(iota((1, width), 1) // part == spot_ref[SPOT], copies, 0.0)
    tall = hidden + TAIL
    pay_ref[hidden:tall] = tail[...].astype(bf16)
    for index in range(width // part):
        block = w1[:, index * hidden : (index + 1) * hidden]
        if hidden < width:
            block = jnp.concatenate([block, jnp.zeros((part, width - hidden), bf16)], axis=1)
        pay_ref[tall + index * part : tall + (index + 1) * part] = block


def pack_parameters(spot, w_qkv, w_out, w_router, vectors, w1, w2, b1, b2):
    part, width = w_out.shape
    hidden = w2.shape[0]
    operands = [w_qkv, w_out, w_router.T, *[v.reshape(1, part) for v in vectors], w1, w2, b1, b2]
    return pl.pallas_call(
        pack_kernel,
        grid=(1,),
        in_specs=[pl.BlockSpec(memory_space=pltpu.SMEM)] + [whole(v.shape) for v in operands],
        out_specs=[whole((part, 4 * width + LANES)), whole((hidden + TAIL + width, width))],
        out_shape=[
            jax.ShapeDtypeStruct((part, 4 * width + LANES), bf16),
            jax.ShapeDtypeStruct((hidden + TAIL + width, width), bf16),
        ],
        scratch_shapes=[pltpu.VMEM((LANES, part), f32), pltpu.VMEM((TAIL, width), f32)],
        compiler_params=params(),
        cost_estimate=cost(0.02),
        name="pack",
    )(spot, *operands)


def one_hot_rows(row, cap):
    slots = iota((cap, row.shape[1]), 0).astype(f32)
    return jnp.where(slots == row, 1.0, 0.0).astype(bf16)


def one_hot_cols(column, cap):
    slots = iota((column.shape[0], cap), 1).astype(f32)
    return jnp.where(slots == column, 1.0, 0.0).astype(bf16)


def route_kernel(place_ref, ids_ref, up_ref, hot_ref, pos_ref, *rest, cap, stride):
    outs, gathered, post_ref = rest[:-2], rest[-2], rest[-1]
    experts = post_ref.shape[0]
    images, seq, width = up_ref.shape
    step = pl.program_id(0)

    @pl.when(step == 0)
    def _():
        expert = relative_expert(place_ref[0], iota((experts, stride), 0), experts)
        before = jnp.where(iota((stride, stride), 0) < iota((stride, stride), 1), 1.0, 0.0).astype(bf16)
        carry = jnp.zeros((experts, 1), f32)
        gathered[...] = jnp.zeros_like(gathered)
        for image in range(images):
            ids = ids_ref[:, image * seq : (image + 1) * seq]
            ids = jnp.concatenate([ids, jnp.full((ids.shape[0], stride - seq), -1, i32)], axis=1)
            hit = jnp.zeros((experts, stride), jnp.bool_)
            for choice in range(ids_ref.shape[0]):
                hit = hit | (ids[choice : choice + 1] == expert)
            mask = jnp.where(hit, 1.0, 0.0)
            rank = carry + dot(mask.astype(bf16), before, NN)
            carry = carry + jnp.sum(mask, axis=1, keepdims=True)
            slot = jnp.where(hit, rank, -1.0)
            post_ref[:, image * stride : (image + 1) * stride] = slot
            padded = jnp.concatenate([slot, jnp.full((LANES - experts, stride), -1.0, f32)], axis=0)
            pos_ref[image] = padded.T
            gathered[image * stride : image * stride + seq] = up_ref[image]

    hot = one_hot_rows(post_ref[pl.ds(step, 1), :], cap)
    hot_ref[0] = hot
    made = dot(hot, gathered[...], NN).astype(bf16)
    for index in range(experts):

        @pl.when(step == index)
        def _():
            outs[index][...] = made


def route(place, ids, grad_output, experts, cap, stride):
    images, seq, width = grad_output.shape
    total = images * stride
    return pl.pallas_call(
        functools.partial(route_kernel, cap=cap, stride=stride),
        grid=(experts,),
        in_specs=[pl.BlockSpec(memory_space=pltpu.SMEM), whole(ids.shape), whole(grad_output.shape)],
        out_specs=[pl.BlockSpec((1, cap, total), lambda s: (s, 0, 0)), whole((images, stride, LANES))]
        + [whole((cap, width))] * experts,
        out_shape=[
            jax.ShapeDtypeStruct((experts, cap, total), bf16),
            jax.ShapeDtypeStruct((images, stride, LANES), f32),
        ]
        + [jax.ShapeDtypeStruct((cap, width), bf16)] * experts,
        scratch_shapes=[pltpu.VMEM((total, width), bf16), pltpu.VMEM((experts, total), f32)],
        compiler_params=params(),
        cost_estimate=cost(0.02),
        name="route",
    )(place, ids, grad_output)


def dispatch_kernel(_, hot_ref, rows_ref, *refs, cap, shifts, paired):
    pairs = [shift for shift in shifts if shift in paired]
    ups, outs = refs[: len(pairs)], refs[len(pairs) :]
    step = pl.program_id(0)
    sent = dot(hot_ref[0], rows_ref[...], NN).astype(bf16)
    for index, shift in enumerate(shifts):

        @pl.when(step == index)
        def _():
            outs[index][0:cap] = sent
            if shift in pairs:
                outs[index][cap:] = ups[pairs.index(shift)][...]


def dispatch(hot, rows, ups, shifts, paired):
    _, cap, total = hot.shape
    width = rows.shape[1]
    shapes = [((2 if shift in paired else 1) * cap, width) for shift in shifts]
    pairs = [ups[shift] for shift in shifts if shift in paired]
    outs = pl.pallas_call(
        functools.partial(dispatch_kernel, cap=cap, shifts=tuple(shifts), paired=paired),
        grid_spec=pltpu.PrefetchScalarGridSpec(
            num_scalar_prefetch=1,
            grid=(len(shifts),),
            in_specs=[pl.BlockSpec((1, cap, total), lambda s, table: (table[s], 0, 0)), whole(rows.shape)]
            + [whole((cap, width))] * len(pairs),
            out_specs=[whole(v) for v in shapes],
        ),
        out_shape=[jax.ShapeDtypeStruct(v, bf16) for v in shapes],
        compiler_params=params(),
        cost_estimate=cost(0.02),
        name="dispatch",
    )(jnp.array(shifts, i32), hot, rows, *pairs)
    return dict(zip(shifts, outs))


def forward_kernel(spots_ref, tok_ref, *rest, experts, fsdp, later):
    if later:
        pack_ref, old_peak_ref = rest[:2]
        rest = rest[-10:]
    else:
        shards_of, pack_ref = rest[:fsdp], rest[-4]
        rest = rest[-11:-4] + rest[-3:]
    qkv_ref, mixed_ref, hidden_ref, prob_ref, attn_ref, mid_ref, peak_ref, tokens, vectors, router = rest
    _, seq, width = tok_ref.shape
    rows = tokens.shape[0]
    head = width // HEADS
    step = pl.program_id(0)
    wide = 3 * width

    @pl.when(step == 0)
    def _():
        if not later:
            part = shards_of[0].shape[0]
            for index, ref in enumerate(shards_of):
                pack_ref[pl.ds(pl.multiple_of(spots_ref[HOMES + fsdp + index] * part, part), part), :] = ref[...]
        misc = pack_ref[:, wide + width :]
        vectors[...] = misc.astype(f32).T
        router[...] = dot(misc, router_order(spots_ref[0], experts), NN).astype(bf16)
        tokens[...] = jnp.zeros_like(tokens)
        peak_ref[...] = old_peak_ref[...] if later else jnp.full_like(peak_ref, NEG)

    def vector(index):
        return vectors[VEC + index : VEC + index + 1, :]

    tokens[0:seq] = tok_ref[0].astype(f32)
    residual = tokens[...]
    hat, _ = norm_stats(residual)
    normed = (hat * vector(0) + vector(1)).astype(bf16)
    projected = dot(normed, pack_ref[:, 0:wide], NN)
    qkv_ref[0, :, 0:width] = ((projected[:, 0:width] + vector(2)).astype(bf16).astype(f32) * head**-0.5).astype(
        bf16
    )
    qkv_ref[0, :, width : 2 * width] = projected[:, width : 2 * width].astype(bf16)
    qkv_ref[0, :, 2 * width :] = (projected[:, 2 * width :] + vector(3)).astype(bf16)
    lane = iota((1, LANES), 1)
    first = lane < head
    halves = (jnp.where(first, 1.0, 0.0).astype(bf16), jnp.where(first, 0.0, 1.0).astype(bf16))
    keys = jnp.where(iota((1, rows), 1) < seq, 0.0, NEG)
    valid = iota((rows, 1), 0) < seq

    def pair(index, peak):
        at = pl.multiple_of(index * LANES, LANES)
        query = qkv_ref[0, :, pl.ds(at, LANES)]
        key = qkv_ref[0, :, pl.ds(width + at, LANES)]
        value = qkv_ref[0, :, pl.ds(2 * width + at, LANES)]
        parts = []
        for half in range(2):
            scores = dot(query * halves[half], key, NT) + keys
            top = jnp.max(scores, axis=1, keepdims=True)
            weight = jnp.exp(scores - top)
            total = jnp.sum(weight, axis=1, keepdims=True)
            number = index * 2 + half
            largest = jnp.max(jnp.where(valid, top, NEG), axis=0, keepdims=True)
            peak = jnp.where(lane == number, largest, peak)
            low = (weight * (1.0 / total)).astype(bf16)
            attn_ref[0, number] = low
            parts.append(dot(low, value, NN))
        mixed_ref[0, :, pl.ds(at, LANES)] = jnp.where(first, parts[0], parts[1]).astype(bf16)
        return peak

    peak = lax.fori_loop(0, HEADS // 2, pair, jnp.full((1, LANES), NEG, f32), unroll=True)
    peak_ref[...] = jnp.maximum(peak_ref[...], peak)
    hidden = residual + dot(mixed_ref[0], pack_ref[:, wide : wide + width], NN) + vector(4)
    hidden_ref[0] = hidden
    hat, _ = norm_stats(hidden)
    mid = hat * vector(5) + vector(6)
    logits = jnp.zeros((rows, LANES), f32)
    for part in pieces(mid, 3):
        logits = logits + dot(part, router[...], NN)
    prob_ref[0] = softmax_lanes(logits, experts)
    mid_ref[0, 0:rows] = mid.astype(bf16)
    mid_ref[0, rows:] = jnp.zeros((mid_ref.shape[1] - rows, width), bf16)


def forward(spots, tokens, shards_of, old, after, at, count, experts, stride, rows):
    images, seq, width = tokens.shape
    later = old is not None
    far = pl.BlockSpec(memory_space=pl.ANY)
    shapes = [
        ((1, rows, 3 * width), bf16),
        ((1, rows, width), bf16),
        ((1, rows, width), f32),
        ((1, rows, LANES), f32),
        ((1, HEADS, rows, rows), bf16),
        ((1, stride, width), bf16),
    ]

    def image(shape):
        return pl.BlockSpec(shape, lambda i: (at + i,) + (0,) * (len(shape) - 1))

    out_specs = [image(shape) for shape, _ in shapes] + [whole((1, LANES))]
    out_shape = [jax.ShapeDtypeStruct((images,) + shape[1:], kind) for shape, kind in shapes]
    out_shape.append(jax.ShapeDtypeStruct((1, LANES), f32))
    operands = [spots, tokens]
    in_specs = [pl.BlockSpec(memory_space=pltpu.SMEM), image((1, seq, width))]
    if later:
        *arrays, peak, pack = old
        aliases = {len(operands) + 2 + index: index for index in range(len(arrays))}
        operands += [pack, peak, *arrays]
        in_specs += [whole(pack.shape), whole(peak.shape)] + [far] * len(arrays)
    else:
        aliases = {}
        packed = (width, shards_of[0].shape[1])
        operands += shards_of
        in_specs += [whole(v.shape) for v in shards_of]
        out_specs.append(whole(packed))
        out_shape.append(jax.ShapeDtypeStruct(packed, bf16))
    outputs = pl.pallas_call(
        functools.partial(forward_kernel, experts=experts, fsdp=len(shards_of), later=later),
        grid=(count,),
        in_specs=in_specs + [far] * len(after),
        out_specs=out_specs,
        out_shape=out_shape,
        scratch_shapes=[
            pltpu.VMEM((rows, width), f32),
            pltpu.VMEM((LANES, width), f32),
            pltpu.VMEM((width, LANES), bf16),
        ],
        input_output_aliases=aliases,
        compiler_params=params(),
        cost_estimate=cost(20 * count if later else 0.02),
        name="attend",
    )(*operands, *after)
    return [*outputs, pack] if later else outputs


def expert_kernel(place_ref, *refs, cap, group, first, last, experts, fsdp, split, skip):
    taken = iter(refs)

    def take(number):
        return [next(taken) for _ in range(number)]

    count = len(group)
    rows_in, ups_in = take(count), take(count)
    pays, misc = take(fsdp), next(taken)
    old = [] if first else take(3)
    take(skip)
    row_back, made_ref = take(count), next(taken)
    out1, out2, *out3 = take(4 if split else 2) if split or not last else (None, next(taken))
    rows, ups, gates, acc_row, acc_out, shift2, bias2, gated, sems, w1s, w2s, sems_w = take(12)
    step = pl.program_id(0)
    width = rows.shape[1]
    tile = w1s.shape[2]
    tall = tile + TAIL
    chunk = width // fsdp

    @pl.when(step == 0)
    def _():
        loads = []
        for index, ref in enumerate(pays):
            at = place_ref[HOMES + index]
            loads.append(pltpu.make_async_copy(ref.at[0:tall], w2s.at[at], sems_w.at[index, fsdp]))
            for block in range(fsdp):
                start = tall + block * chunk
                loads.append(
                    pltpu.make_async_copy(
                        ref.at[start : start + chunk, 0:tile],
                        w1s.at[block, pl.ds(pl.multiple_of(at * chunk, chunk), chunk)],
                        sems_w.at[index, block],
                    )
                )
        for load in loads:
            load.start()
        for index in range(count):
            rows[index * cap : (index + 1) * cap] = rows_in[index][...]
        router = dot(misc[...], router_order(place_ref[0], experts), NN).astype(bf16)
        gate = softmax_lanes(dot(rows[...], router, NN), experts)[:, 0:1]
        gates[...] = jnp.broadcast_to(gate, gates.shape)
        for index in range(count):
            part = slice(index * cap, (index + 1) * cap)
            ups[part] = (ups_in[index][...].astype(f32) * gate[part]).astype(bf16)
        acc_row[...] = jnp.zeros_like(acc_row)
        acc_out[...] = jnp.zeros_like(acc_out)
        bias2[...] = jnp.zeros_like(bias2)
        shift2[...] = jnp.sum(ups[...].astype(f32), axis=0, keepdims=True)
        for load in loads:
            load.wait()

    w1, w2 = w1s.at[step], w2s.at[step]
    tail = w2[tile:tall].astype(f32)
    bias2[...] += tail[1:2]
    x, up = rows[...], ups[...]
    value, slope = gelu_pair(dot(x, w1[...], NN) + tail[0:1, 0:tile])
    act = value
    acc_out[...] += dot(act, w2[0:tile], NN)
    pre = slope * dot(up, w2[0:tile], NT).astype(bf16)
    acc_row[...] += dot(pre, w1[...], NT)
    part1 = dot(x, pre, TN)
    part2 = dot(act, up, TN)
    shift1 = jnp.sum(pre.astype(f32), axis=0, keepdims=True)
    if tile < width:
        shift1 = jnp.concatenate([shift1, jnp.zeros((1, width - tile), f32)], axis=1)
    place = iota((TAIL, width), 0)
    sums = jnp.where(place == 0, shift1, jnp.where(place == 1, shift2[...], 0.0))
    if not first:
        part1, part2, sums = old[1][...] + part1, old[2][0, 0:tile] + part2, old[2][0, tile:] + sums
    if last:
        if tile < width:
            part1 = jnp.concatenate([part1, jnp.zeros((width, width - tile), f32)], axis=1)
        if split:
            for ref, fy in ((out1, place_ref[FY]), (out2, 1 - place_ref[FY])):

                @pl.when((step >> 1) == fy)
                def _():
                    ref[step & 1, 0:tile] = part2.astype(bf16)
                    ref[step & 1, tile:tall] = sums.astype(bf16)

            at = pl.multiple_of(step * chunk, TAIL)
            for index in range(fsdp):
                block = part1[index * chunk : (index + 1) * chunk].astype(bf16)
                for ref, fy in ((out3[0], place_ref[FY]), (out3[1], 1 - place_ref[FY])):

                    @pl.when(index // 2 == fy)
                    def _():
                        ref[index % 2, pl.ds(at, chunk), :] = block

        else:
            at = pl.multiple_of(tall + step * chunk, TAIL)
            out2[step, 0:tile] = part2.astype(bf16)
            out2[step, tile:tall] = sums.astype(bf16)
            for index in range(fsdp):
                out2[index, pl.ds(at, chunk), :] = part1[index * chunk : (index + 1) * chunk].astype(bf16)
    else:
        out1[...] = part1
        out2[0, 0:tile] = part2
        out2[0, tile:] = sums

    @pl.when(step == pl.num_programs(0) - 1)
    def _():
        copies = []
        for index, shift in enumerate(group):
            part = slice(index * cap, (index + 1) * cap)
            made = acc_out[part] + bias2[...]
            gate = gates[part, 0:1]
            gated[index] = (made * gate).astype(bf16)
            copies.append(
                pltpu.make_async_copy(gated.at[index], made_ref.at[place_ref[0] ^ shift], sems.at[index])
            )
            copies[-1].start()
            row_back[index][0:cap] = acc_row[part].astype(bf16)
            effect = jnp.sum(made * ups_in[index][...].astype(f32), axis=1, keepdims=True) * gate
            effect = jnp.concatenate([effect, jnp.zeros((width - cap, 1), f32)], axis=0)
            line = jnp.broadcast_to(effect, (width, LANES)).T[0:1]
            end = jnp.zeros((TAIL, width), f32)
            for order, piece in enumerate(pieces(line, 3)):
                end = jnp.where(place == order, piece.astype(f32), end)
            row_back[index][cap : cap + TAIL] = end.astype(bf16)
        for copy in copies:
            copy.wait()


def expert_call(spots, rows, ups, pays, pack, old, after, group, cap, experts, last):
    count = len(group)
    first = old is None
    fsdp = len(pays)
    high, width = pays[0].shape
    tall = high - width
    tile = tall - TAIL
    total = count * cap
    split = last and fsdp == 4
    column = pl.BlockSpec((width, tile), lambda h, _: (0, h))
    line = pl.BlockSpec((1, tall, width), lambda h, _: (h, 0, 0))
    far = pl.BlockSpec(memory_space=pl.ANY)
    if split:
        grads = [(2, tall, width)] * 2 + [(2, width, width)] * 2
    else:
        grads = [(fsdp, high, width)]

    operands = [spots, *rows, *ups, *pays, pack]
    aliases = {}
    if not first:
        aliases = {len(operands): count}
        operands += list(old)
    return pl.pallas_call(
        functools.partial(
            expert_kernel,
            cap=cap,
            group=group,
            first=first,
            last=last,
            experts=experts,
            fsdp=fsdp,
            split=split,
            skip=len(after),
        ),
        grid_spec=pltpu.PrefetchScalarGridSpec(
            num_scalar_prefetch=1,
            grid=(fsdp,),
            in_specs=[whole((cap, width))] * count
            + [pl.BlockSpec((cap, width), lambda h, _, at=v.shape[0] // cap - 1: (at, 0)) for v in ups]
            + [far] * fsdp
            + [pl.BlockSpec((width, LANES), lambda h, _: (0, 4 * width // LANES))]
            + ([] if first else [far, column, line])
            + [far] * len(after),
            out_specs=[whole((cap + TAIL, width))] * count
            + [far]
            + ([whole(v) for v in grads] if last else [column, line]),
            scratch_shapes=[pltpu.VMEM((total, width), bf16)] * 2
            + [pltpu.VMEM((total, LANES), f32)]
            + [pltpu.VMEM((total, width), f32)] * 2
            + [pltpu.VMEM((1, width), f32)] * 2
            + [pltpu.VMEM((count, cap, width), bf16), pltpu.SemaphoreType.DMA((count,))]
            + [pltpu.VMEM((fsdp, width, tile), bf16), pltpu.VMEM((fsdp, tall, width), bf16)]
            + [pltpu.SemaphoreType.DMA((fsdp, fsdp + 1))],
        ),
        out_shape=[jax.ShapeDtypeStruct((cap + TAIL, width), bf16)] * count
        + [jax.ShapeDtypeStruct((experts, cap, width), bf16)]
        + (
            [jax.ShapeDtypeStruct(v, bf16) for v in grads]
            if last
            else [
                jax.ShapeDtypeStruct((width, tile * fsdp), f32),
                jax.ShapeDtypeStruct((fsdp, tall, width), f32),
            ]
        ),
        input_output_aliases=aliases,
        compiler_params=params(),
        cost_estimate=cost(96),
        name="expert",
    )(*operands, *after)


def gather_back(places, backs, shifts, slot_sum, effect, cap):
    lane = iota((1, LANES), 1)
    for index, ref in zip(shifts, backs):
        hot = one_hot_cols(places[:, index : index + 1], cap)
        slot_sum = slot_sum + dot(hot, ref[0:cap], NN)
        parts = dot(hot, ref[cap : cap + TAIL, 0:cap], NT)
        effect = jnp.where(lane == index, jnp.sum(parts, axis=1, keepdims=True), effect)
    return slot_sum, effect


def returned_kernel(pos_ref, *refs, cap, shifts):
    backs, slot_ref, effect_ref = refs[: len(shifts)], refs[-2], refs[-1]
    _, rows, width = slot_ref.shape
    slot_ref[0], effect_ref[0] = gather_back(
        pos_ref[0, 0:rows, :], backs, shifts, jnp.zeros((rows, width), f32), jnp.zeros((rows, LANES), f32), cap
    )


def returned(pos, backs, shifts, rows, cap):
    images, width = pos.shape[0], backs[0].shape[1]

    def image(shape):
        return pl.BlockSpec((1,) + shape, lambda i: (i, 0, 0))

    return pl.pallas_call(
        functools.partial(returned_kernel, cap=cap, shifts=shifts),
        grid=(images,),
        in_specs=[image((pos.shape[1], LANES))] + [whole((cap + TAIL, width))] * len(backs),
        out_specs=[image((rows, width)), image((rows, LANES))],
        out_shape=[
            jax.ShapeDtypeStruct((images, rows, width), f32),
            jax.ShapeDtypeStruct((images, rows, LANES), f32),
        ],
        compiler_params=params(),
        cost_estimate=cost(100),
        name="returned",
    )(pos, *backs)


def middle_kernel(
    place_ref, up_ref, wout_ref, misc_ref, pos_ref, mixed_ref, hidden_ref, prob_ref, slot_ref, effect_ref, *rest, cap, experts
):
    backs = rest[:2]
    hidden_grad_ref, mixed_grad_ref, sums_ref, padded, vectors, router, shifts, acc_out, acc_router = rest[-9:]
    _, seq, width = up_ref.shape
    rows = padded.shape[0]
    step = pl.program_id(0)

    @pl.when(step == 0)
    def _():
        vectors[...] = misc_ref[...].astype(f32).T
        router[...] = dot(misc_ref[...], router_order(place_ref[0], experts), NN).astype(bf16)
        padded[...] = jnp.zeros_like(padded)
        shifts[...] = jnp.zeros_like(shifts)
        acc_out[...] = jnp.zeros_like(acc_out)
        acc_router[...] = jnp.zeros_like(acc_router)

    def vector(index):
        return vectors[VEC + index : VEC + index + 1, :]

    def shift(index, value):
        shifts[index : index + 1, :] += jnp.sum(value, axis=0, keepdims=True)

    slot_sum, effect = gather_back(pos_ref[0, 0:rows, :], backs, (0, 1), slot_ref[0], effect_ref[0], cap)
    prob = prob_ref[0]
    logit_grad = effect - prob * jnp.sum(effect, axis=1, keepdims=True)
    logit_parts = pieces(logit_grad, 2)
    mid_grad = slot_sum
    for part in logit_parts:
        mid_grad = mid_grad + dot(part, router[...], NT)
    padded[0:seq] = up_ref[0].astype(f32)
    hat, inverse = norm_stats(hidden_ref[0])
    mid_parts = pieces(hat * vector(5) + vector(6), 2)
    acc_router[...] += (
        dot(logit_parts[0], mid_parts[0], TN)
        + dot(logit_parts[0], mid_parts[1], TN)
        + dot(logit_parts[1], mid_parts[0], TN)
    )
    shift(5, mid_grad * hat)
    shift(6, mid_grad)
    hidden_grad = padded[...] + norm_back(mid_grad, vector(5), hat, inverse)
    hidden_grad_ref[0] = hidden_grad
    branch = hidden_grad.astype(bf16)
    shift(4, branch.astype(f32))
    acc_out[...] += dot(mixed_ref[0], branch, TN)
    mixed_grad_ref[0] = dot(branch, wout_ref[...], NT).astype(bf16)

    @pl.when(step == pl.num_programs(0) - 1)
    def _():
        sums_ref[:, 0:width] = acc_out[...]
        ordered = dot(router_order(place_ref[0], experts), acc_router[...].astype(bf16), NN)
        spare = jnp.concatenate(
            [ordered[0:VEC], shifts[...], jnp.zeros((LANES - VEC - shifts.shape[0], width), f32)], axis=0
        )
        sums_ref[:, width:] = spare.T


def middle(place, grad_output, pack, pos, saved, part_sums, backs, cap, experts):
    images, seq, width = grad_output.shape
    _, mixed, hidden, prob, _ = saved
    rows = mixed.shape[1]

    def image(shape):
        return pl.BlockSpec((1,) + shape, lambda i: (i, 0, 0))

    return pl.pallas_call(
        functools.partial(middle_kernel, cap=cap, experts=experts),
        grid=(images,),
        in_specs=[
            pl.BlockSpec(memory_space=pltpu.SMEM),
            image((seq, width)),
            pl.BlockSpec((width, width), lambda i: (0, 3)),
            pl.BlockSpec((width, LANES), lambda i: (0, 4 * width // LANES)),
            image((pos.shape[1], LANES)),
            image((rows, width)),
            image((rows, width)),
            image((rows, LANES)),
            image((rows, width)),
            image((rows, LANES)),
        ]
        + [whole((cap + TAIL, width))] * len(backs),
        out_specs=[image((rows, width)), image((rows, width)), whole((width, width + LANES))],
        out_shape=[
            jax.ShapeDtypeStruct((images, rows, width), f32),
            jax.ShapeDtypeStruct((images, rows, width), bf16),
            jax.ShapeDtypeStruct((width, width + LANES), f32),
        ],
        scratch_shapes=[
            pltpu.VMEM((rows, width), f32),
            pltpu.VMEM((LANES, width), f32),
            pltpu.VMEM((width, LANES), bf16),
            pltpu.VMEM((8, width), f32),
            pltpu.VMEM((width, width), f32),
            pltpu.VMEM((LANES, width), f32),
        ],
        compiler_params=params(),
        cost_estimate=cost(0.02),
        name="middle",
    )(place, grad_output, pack, pack, pos, mixed, hidden, prob, *part_sums, *backs)


def backward_kernel(
    spots_ref, tok_ref, qkv_ref, attn_ref, mixed_grad_ref, *rest, head_rows, members
):
    sums_ref, peak_ref = rest[:2]
    qkv_grad_ref, keep_ref, give_ref, padded, acc_qkv, columns, spare, misc = rest[-8:]
    _, seq, width = tok_ref.shape
    rows = padded.shape[0]
    head = width // HEADS
    wide = 3 * width
    step = pl.program_id(0)

    @pl.when(step == 0)
    def _():
        padded[...] = jnp.zeros_like(padded)
        acc_qkv[...] = jnp.zeros_like(acc_qkv)
        columns[...] = jnp.zeros_like(columns)

    lane = iota((1, LANES), 1)
    first = lane < head
    halves = (jnp.where(first, 1.0, 0.0).astype(bf16), jnp.where(first, 0.0, 1.0).astype(bf16))

    def pair(index, carry):
        at = pl.multiple_of(index * LANES, LANES)
        query = qkv_ref[0, :, pl.ds(at, LANES)]
        key = qkv_ref[0, :, pl.ds(width + at, LANES)]
        value = qkv_ref[0, :, pl.ds(2 * width + at, LANES)]
        up = mixed_grad_ref[0, :, pl.ds(at, LANES)]
        made = []
        for half in range(2):
            low = attn_ref[0, index * 2 + half]
            weight = low.astype(f32)
            value_grad = dot(low, up, TN)
            spread = weight * dot(up * halves[half], value, NT)
            score_grad = (spread - weight * jnp.sum(spread, axis=1, keepdims=True)).astype(bf16)
            made.append((dot(score_grad, key, NN) * head**-0.5, dot(score_grad, query, TN), value_grad))
        for index_of, (left, right) in enumerate(zip(*made)):
            qkv_grad_ref[0, :, pl.ds(index_of * width + at, LANES)] = jnp.where(first, left, right).astype(bf16)
        return carry

    lax.fori_loop(0, HEADS // 2, pair, 0, unroll=True)
    columns[...] += jnp.sum(qkv_grad_ref[0].astype(f32), axis=0, keepdims=True)
    padded[0:seq] = tok_ref[0].astype(f32)
    hat, _ = norm_stats(padded[...])
    acc_qkv[...] += dot(hat.astype(bf16), qkv_grad_ref[0], TN)
    part = keep_ref.shape[1]

    @pl.when(step == pl.num_programs(0) - 1)
    def _():
        line = iota((LANES, width), 0)
        flat = columns[...]
        grown = jnp.where(line == VEC + 2, flat[:, 0:width], 0.0)
        grown = jnp.where(line == VEC + 3, flat[:, 2 * width :], grown)
        misc[...] = sums_ref[:, width:] + grown.T
        spare[...] = jnp.zeros_like(spare)
        number = wide // LANES
        for order, piece in enumerate(pieces(flat, 3)):
            value = piece.astype(f32)
            for index in range(number):
                at = order * number + index
                spare[at : at + 1, :] = value[:, index * LANES : (index + 1) * LANES]
        if members:
            top = jnp.where(lane < HEADS, peak_ref[...], 0.0)
            rows_of = jnp.zeros((TAIL, LANES), f32)
            for order, piece in enumerate(pieces(jnp.broadcast_to(top, (TAIL, LANES)), 3)):
                move = jnp.where(iota((LANES, LANES), 1) == iota((LANES, LANES), 0) + order * HEADS, 1.0, 0.0)
                rows_of = rows_of + dot(piece, move.astype(bf16), NN)
            spare[pl.ds(head_rows + spots_ref[NUMBER], 1), :] = rows_of[0:1]
        extra = spare[...].astype(bf16)
        for fy in range(keep_ref.shape[0]):
            for ref, core in ((keep_ref, spots_ref[CORE]), (give_ref, 1 - spots_ref[CORE])):
                at = pl.multiple_of((2 * fy + core) * part, part)
                ref[fy, :, 0:wide] = acc_qkv[pl.ds(at, part), :].astype(bf16)
                ref[fy, :, wide : wide + width] = sums_ref[pl.ds(at, part), 0:width].astype(bf16)
                ref[fy, :, wide + width : wide + width + LANES] = misc[pl.ds(at, part), :].astype(bf16)
                ref[fy, :, wide + width + LANES :] = extra


def backward(spots, tokens, saved, mixed_grad, sums, peak, after, ways, part, head_rows, members):
    images, seq, width = tokens.shape
    qkv, attn = saved[0], saved[-1]
    rows = qkv.shape[1]
    wide = 4 * width + 2 * LANES

    def image(shape):
        return pl.BlockSpec((1,) + shape, lambda i: (i,) + (0,) * len(shape))

    return pl.pallas_call(
        functools.partial(backward_kernel, head_rows=head_rows, members=members),
        grid=(images,),
        in_specs=[
            pl.BlockSpec(memory_space=pltpu.SMEM),
            image((seq, width)),
            image((rows, 3 * width)),
            image((HEADS, rows, rows)),
            image((rows, width)),
            whole(sums.shape),
            whole(peak.shape),
        ]
        + [pl.BlockSpec(memory_space=pl.ANY)] * len(after),
        out_specs=[image((rows, 3 * width)), whole((ways, part, wide)), whole((ways, part, wide))],
        out_shape=[
            jax.ShapeDtypeStruct((images, rows, 3 * width), bf16),
            jax.ShapeDtypeStruct((ways, part, wide), bf16),
            jax.ShapeDtypeStruct((ways, part, wide), bf16),
        ],
        scratch_shapes=[
            pltpu.VMEM((rows, width), f32),
            pltpu.VMEM((width, 3 * width), f32),
            pltpu.VMEM((1, 3 * width), f32),
            pltpu.VMEM((part, LANES), f32),
            pltpu.VMEM((width, LANES), f32),
        ],
        compiler_params=params(),
        cost_estimate=cost(0.05),
        name="attend_back",
    )(spots, tokens, qkv, attn, mixed_grad, sums, peak, *after)


def first_kernel(tok_ref, qkv_grad_ref, wqkv_ref, misc_ref, hidden_grad_ref, grad_ref, padded, gain):
    _, seq, width = tok_ref.shape

    @pl.when(pl.program_id(0) == 0)
    def _():
        gain[...] = misc_ref[...].astype(f32).T[VEC : VEC + 1]
        padded[...] = jnp.zeros_like(padded)

    in_grad = dot(qkv_grad_ref[0], wqkv_ref[...], NT)
    padded[0:seq] = tok_ref[0].astype(f32)
    hat, inverse = norm_stats(padded[...])
    grad_ref[0] = (hidden_grad_ref[0] + norm_back(in_grad, gain[...], hat, inverse))[0:seq]


def first_norm(tokens, qkv_grad, pack, hidden_grad):
    images, seq, width = tokens.shape
    rows = qkv_grad.shape[1]

    def image(shape):
        return pl.BlockSpec((1,) + shape, lambda i: (i, 0, 0))

    return pl.pallas_call(
        first_kernel,
        grid=(images,),
        in_specs=[
            image((seq, width)),
            image((rows, 3 * width)),
            pl.BlockSpec((width, 3 * width), lambda i: (0, 0)),
            pl.BlockSpec((width, LANES), lambda i: (0, 4 * width // LANES)),
            image((rows, width)),
        ],
        out_specs=image((seq, width)),
        out_shape=jax.ShapeDtypeStruct((images, seq, width), f32),
        scratch_shapes=[pltpu.VMEM((rows, width), f32), pltpu.VMEM((1, width), f32)],
        compiler_params=params(),
        cost_estimate=cost(0.02),
        name="first_norm",
    )(tokens, qkv_grad, pack, pack, hidden_grad)


def output_kernel(place_ref, pos_ref, hidden_ref, made_ref, out_ref):
    experts, cap, _ = made_ref.shape
    seq = out_ref.shape[1]
    total = hidden_ref[0]
    places = pos_ref[0, 0 : total.shape[0], :]
    for index in range(experts):
        total = total + dot(one_hot_cols(places[:, index : index + 1], cap), made_ref[place_ref[0] ^ index], NN)
    out_ref[0] = total[0:seq].astype(bf16)


def combine_output(place, pos, hidden, made, seq):
    images, rows, width = hidden.shape

    def image(shape):
        return pl.BlockSpec((1,) + shape, lambda i: (i, 0, 0))

    return pl.pallas_call(
        output_kernel,
        grid=(images,),
        in_specs=[
            pl.BlockSpec(memory_space=pltpu.SMEM),
            image((pos.shape[1], LANES)),
            image((rows, width)),
            whole(made.shape),
        ],
        out_specs=image((seq, width)),
        out_shape=jax.ShapeDtypeStruct((images, seq, width), bf16),
        compiler_params=params(),
        cost_estimate=cost(0.02),
        name="combine",
    )(place, pos, hidden, made)


def finish_kernel(slot_ref, *refs, number, head_rows, members):
    parts, (own_ref, limit_ref, peak_ref) = refs[:number], refs[number : number + 3]
    qkv_ref, out_ref, misc_ref, clip_ref, *vec_refs, total_ref = refs[number + 3 :]
    part = own_ref.shape[0]
    for shift, ref in enumerate(parts):
        size = part // number
        at = (slot_ref[LOW] ^ shift) * size if number > 1 else 0
        total_ref[pl.ds(pl.multiple_of(at, size), size), :] = ref[...]
    width = out_ref.shape[1]
    wide = 3 * width
    number = wide // LANES
    base = total_ref[:, 0:wide].astype(f32)
    extra = total_ref[:, wide + width + LANES :].astype(f32)
    weight = own_ref[:, 0:wide].astype(f32)
    columns = [sum(extra[k * number + i : k * number + i + 1] for k in range(3)) for i in range(number)]
    columns = jnp.concatenate(columns, axis=1)
    own = own_ref[:, wide + width :].astype(f32)
    gain, bias = own[:, VEC : VEC + 1], own[:, VEC + 1 : VEC + 2]
    qkv_ref[...] = base * gain + bias * columns
    out_ref[...] = total_ref[:, wide : wide + width].astype(f32)
    misc = total_ref[:, wide + width : wide + width + LANES].astype(f32)
    lane = iota((1, LANES), 1)
    misc = jnp.where(lane == VEC, jnp.sum(base * weight, axis=1, keepdims=True), misc)
    misc = jnp.where(lane == VEC + 1, jnp.sum(columns * weight, axis=1, keepdims=True), misc)
    misc = misc.T
    for index, ref in enumerate(vec_refs):
        ref[...] = misc[VEC + index : VEC + index + 1]
    misc_ref[...] = misc[0 : misc_ref.shape[0]]
    if members:
        move = jnp.where(
            (iota((LANES, LANES), 0) % HEADS == iota((LANES, LANES), 1)) & (iota((LANES, LANES), 0) < 3 * HEADS),
            1.0,
            0.0,
        )
        peaks = dot(total_ref[head_rows : head_rows + members, wide + width + LANES :], move.astype(bf16), NN)
        peak = jnp.max(peaks, axis=0, keepdims=True)
    else:
        peak = peak_ref[...]
    limit = jnp.concatenate([limit_ref[...].astype(f32), jnp.ones((1, LANES - HEADS), f32)], axis=1)
    root = jnp.sqrt(limit / jnp.maximum(peak, limit))
    place = iota((1, width), 1) // (width // HEADS)
    scale = jnp.zeros((1, width), f32)
    for index in range(HEADS):
        scale = jnp.where(place == index, root[:, index : index + 1], scale)
    clip_ref[:, 0:width] = (weight[:, 0:width] * scale).astype(bf16)
    clip_ref[:, width : 2 * width] = (weight[:, width : 2 * width] * scale).astype(bf16)
    clip_ref[:, 2 * width :] = own_ref[:, 2 * width : wide]


def finish(slot, total, own, limit, peak, width, experts, head_rows, members):
    part = own.shape[0]
    operands = [*total, own, limit, peak]
    shapes = [(part, 3 * width), (part, width), (experts, part), (part, 3 * width)] + [(1, part)] * 7
    return pl.pallas_call(
        functools.partial(finish_kernel, number=len(total), head_rows=head_rows, members=members),
        grid=(1,),
        in_specs=[pl.BlockSpec(memory_space=pltpu.SMEM)] + [whole(v.shape) for v in operands],
        out_specs=[whole(v) for v in shapes],
        out_shape=[jax.ShapeDtypeStruct(v, bf16 if i == 3 else f32) for i, v in enumerate(shapes)],
        scratch_shapes=[pltpu.VMEM((part, total[0].shape[1]), bf16)],
        compiler_params=params(),
        cost_estimate=cost(0.02),
        name="finish",
    )(slot, *operands)


def half_sums_kernel(high_ref, keep_ref, got_ref, *rest):
    straight_ref, crossed_ref = rest[-2:]
    for ref, core in ((straight_ref, high_ref[HIGH]), (crossed_ref, 1 - high_ref[HIGH])):
        ref[...] = (keep_ref[core].astype(f32) + got_ref[core].astype(f32)).astype(bf16)


def half_sums(high, keep, got, after, micros):
    shape = keep.shape[1:]
    return pl.pallas_call(
        half_sums_kernel,
        grid=(1,),
        in_specs=[pl.BlockSpec(memory_space=pltpu.SMEM), whole(keep.shape), whole(got.shape)]
        + [pl.BlockSpec(memory_space=pl.ANY)] * len(after),
        out_specs=[whole(shape)] * 2,
        out_shape=[jax.ShapeDtypeStruct(shape, bf16)] * 2,
        compiler_params=params(),
        cost_estimate=cost(micros),
        name="half_sums",
    )(high, keep, got, *after)


def both_halves(spot_ref, one, two, own, rows):
    straight = jnp.where(spot_ref[SAME] == 1, own[rows].astype(f32), one[rows].astype(f32))
    return straight + two[rows].astype(f32)


def home_second_kernel(spot_ref, one, two, own, _, w2_ref, b1_ref, b2_ref):
    tile, width = w2_ref.shape
    part = b2_ref.shape[1]
    w2_ref[...] = both_halves(spot_ref, one, two, own, slice(0, tile))
    edge = both_halves(spot_ref, one, two, own, slice(tile, tile + TAIL))
    b1_ref[...] = edge[0:1, 0:tile]
    b2_ref[...] = sum(
        jnp.where(spot_ref[SPOT] == index, edge[1:2, index * part : (index + 1) * part], 0.0)
        for index in range(width // part)
    )


def home_first_kernel(spot_ref, one, two, own, _, w1_ref):
    part, hidden = w1_ref.shape
    number = one.shape[0] // part
    tile = hidden // number
    for index in range(number):
        total = both_halves(spot_ref, one, two, own, slice(index * part, (index + 1) * part))
        w1_ref[:, index * tile : (index + 1) * tile] = total[:, 0:tile]


def home_sums(kernel, spot, pair, after, shapes):
    return pl.pallas_call(
        kernel,
        grid=(1,),
        in_specs=[pl.BlockSpec(memory_space=pltpu.SMEM)]
        + [whole(v.shape) for v in pair]
        + [pl.BlockSpec(memory_space=pl.ANY)],
        out_specs=[whole(v) for v in shapes],
        out_shape=[jax.ShapeDtypeStruct(v, f32) for v in shapes],
        compiler_params=params(),
        cost_estimate=cost(0.02),
        name="home_sums",
    )(spot, *pair, after)


def add_halves_kernel(fy_ref, keep_ref, got_ref, *rest):
    mine_ref, theirs_ref = rest[-2:]
    for ref, half in ((mine_ref, fy_ref[FY]), (theirs_ref, 1 - fy_ref[FY])):
        ref[...] = (keep_ref[half].astype(f32) + got_ref[half].astype(f32)).astype(bf16)


def add_halves(fy, keep, got, after):
    shape = keep.shape[1:]
    return pl.pallas_call(
        add_halves_kernel,
        grid=(1,),
        in_specs=[pl.BlockSpec(memory_space=pltpu.SMEM), whole(keep.shape), whole(got.shape)]
        + [pl.BlockSpec(memory_space=pl.ANY)] * len(after),
        out_specs=[whole(shape)] * 2,
        out_shape=[jax.ShapeDtypeStruct(shape, bf16)] * 2,
        compiler_params=params(),
        cost_estimate=cost(0.02),
        name="add_halves",
    )(fy, keep, got, *after)


def split_rows_kernel(slot_ref, mine_ref, got_ref, *refs, skip):
    outs, total = refs[skip:-1], refs[-1]
    total[...] = (mine_ref[...].astype(f32) + got_ref[...].astype(f32)).astype(bf16)
    size = outs[0].shape[0]
    for shift, ref in enumerate(outs):
        ref[...] = total[pl.ds(pl.multiple_of((slot_ref[LOW] ^ shift) * size, size), size), :]


def split_rows(slot, mine, got, after, number):
    part, wide = mine.shape
    shape = (part // number, wide)
    return pl.pallas_call(
        functools.partial(split_rows_kernel, skip=len(after)),
        grid=(1,),
        in_specs=[pl.BlockSpec(memory_space=pltpu.SMEM), whole(mine.shape), whole(got.shape)]
        + [pl.BlockSpec(memory_space=pl.ANY)] * len(after),
        out_specs=[whole(shape)] * number,
        out_shape=[jax.ShapeDtypeStruct(shape, bf16)] * number,
        scratch_shapes=[pltpu.VMEM((part, wide), bf16)],
        compiler_params=params(),
        cost_estimate=cost(0.02),
        name="split_rows",
    )(slot, mine, got, *after)


def add_parts_kernel(*refs, number):
    parts, out_ref = refs[:number], refs[-1]
    out_ref[...] = sum(ref[...].astype(f32) for ref in parts).astype(bf16)


def add_parts(parts, after=()):
    shape = parts[0].shape
    return pl.pallas_call(
        functools.partial(add_parts_kernel, number=len(parts)),
        grid=(1,),
        in_specs=[whole(shape)] * len(parts) + [pl.BlockSpec(memory_space=pl.ANY)] * len(after),
        out_specs=whole(shape),
        out_shape=jax.ShapeDtypeStruct(shape, bf16),
        compiler_params=params(),
        cost_estimate=cost(0.02),
        name="add_parts",
    )(*parts, *after)


def swap(value, axis):
    return lax.ppermute(value, axis, [(0, 1), (1, 0)])


def around(value, axis, size):
    return [value] + [
        lax.ppermute(value, axis, [((k + step) % size, k) for k in range(size)]) for step in range(1, size)
    ]


def split_sum(value, axis, size):
    if size != 2:
        return lax.psum_scatter(value, axis, scatter_dimension=0, tiled=False)
    place = lax.axis_index(axis)
    sent = lax.dynamic_index_in_dim(value, 1 - place, 0, keepdims=False)
    kept = lax.dynamic_index_in_dim(value, place, 0, keepdims=False)
    return (kept.astype(f32) + swap(sent, axis).astype(f32)).astype(value.dtype)


def exchange(value, shift, experts):
    return lax.ppermute(value, GROUP, [(k, k ^ shift) for k in range(experts)])


def shift_order(experts):
    def key(shift):
        distance = bin(shift >> 1).count("1")
        return (shift & 1, -distance, shift)

    order = sorted(range(2, experts), key=key)
    half = len(order) // 2
    return [order[:half], order[half:], [0, 1]]


STRAIGHT = [(1, 2), (2, 1)]
CROSSED = [(0, 2), (1, 0), (2, 3), (3, 1)]
BACK = [(b, a) for a, b in STRAIGHT]
BACK_CROSSED = [(b, a) for a, b in CROSSED]


def shards(
    tokens,
    ln1_gain,
    ln1_bias,
    w_qkv,
    q_bias,
    v_bias,
    w_out,
    out_bias,
    ln2_gain,
    ln2_bias,
    w_router,
    expert_w1,
    expert_b1,
    expert_w2,
    expert_b2,
    route_ids,
    clip_threshold,
    grad_output,
    *,
    experts,
    fsdp,
):
    images, seq, width = tokens.shape
    token_count = images * seq
    ways = fsdp // 2
    cap = (7 * token_count // (2 * experts) + 7) // 8 * 8
    stride = -(-seq // 256) * 256
    rows = -(-seq // 16) * 16
    part = w_qkv.shape[0]
    hidden_part = expert_w2.shape[1]
    high, low, fy, core = (lax.axis_index(name).astype(i32) for name in DEVICE)
    spot = fy * 2 + core
    homes = [((fy + step) % ways) * 2 for step in range(ways)]
    spots = jnp.stack(
        [
            low * 2 + core,
            fy,
            core,
            ((high * (experts // 2) + low) * ways + fy) * 2 + core,
            high,
            spot,
            (high == core).astype(i32),
            low,
            *[home + high for home in homes],
            *[home + 1 - high for home in homes],
            *[home + core for home in homes],
            *[home + 1 - core for home in homes],
        ]
    )

    vectors = (ln1_gain, ln1_bias, q_bias, v_bias, out_bias, ln2_gain, ln2_bias)
    own, pay = pack_parameters(
        spots, w_qkv, w_out, w_router, vectors, expert_w1[0], expert_w2[0], expert_b1, expert_b2
    )

    near = around(own, "fy", ways)
    far = [swap(own, "core")]
    straight = lax.ppermute(pay, ("hi", "core"), STRAIGHT)

    hot, pos, *ups = route(spots, route_ids.T, grad_output, experts, cap, stride)
    groups = shift_order(experts)
    near[1:], hot, ups[0] = lax.optimization_barrier((near[1:], hot, ups[0]))
    for shift in groups[0]:
        ups[shift] = exchange(ups[shift], shift, experts)
    far += [swap(value, "core") for value in near[1:]]
    early = 1
    firsts = [ups[shift] for shift in groups[0]]
    begun = list(forward(spots, tokens, near + far, None, [], 0, early, experts, stride, rows))
    pay, straight, begun[0] = lax.optimization_barrier((pay, straight, begun[0]))
    straight = jnp.where(high == core, pay, straight)
    crossed = lax.ppermute(pay, ("hi", "core"), CROSSED)
    pays = around(straight, "fy", ways)
    *saved, mid, peak, pack = forward(
        spots, tokens, [], begun, [straight], early, images - early, experts, stride, rows
    )
    mid = mid.reshape(images * stride, width)
    paired = tuple(shift for group in groups[1:] for shift in group)
    sent = dispatch(hot, mid, ups, groups[0], paired)
    sent.update(dispatch(hot, mid, ups, [shift for group in groups[1:] for shift in group], paired))
    ready = [sent[shift] for shift in groups[0]]
    crossed, ready, firsts, *pays[1:] = lax.optimization_barrier((crossed, ready, firsts, *pays[1:]))
    sent.update(zip(groups[0], ready))
    for shift, value in zip(groups[0], firsts):
        ups[shift] = value
    pays += around(crossed, "fy", ways)

    arrived = {}

    def send(number, after):
        pending, after = lax.optimization_barrier(([sent[shift] for shift in groups[number]], after))
        for shift, value in zip(groups[number], pending):
            arrived[shift] = value if shift == 0 else exchange(value, shift, experts)
        return after

    send(0, ())
    first = send(1, [arrived[shift] for shift in groups[0]])
    arrived.update(zip(groups[0], first))
    old, after = None, []
    backs = {}
    for number, group in enumerate(groups):
        result = expert_call(
            spots,
            [arrived[shift] for shift in group],
            [arrived[shift] if shift in paired else ups[shift] for shift in group],
            pays,
            pack,
            old,
            after,
            group,
            cap,
            experts,
            number == len(groups) - 1,
        )
        old = result[len(group) :]
        after = [backs[shift] for shift in groups[number - 1]] if number else []
        out = result[: len(group)]
        if number + 2 < len(groups):
            out = send(number + 2, out)
        for at, shift in enumerate(group):
            backs[shift] = out[at] if shift == 0 else exchange(out[at], shift, experts)
    backs = [backs[shift] for shift in range(experts)]
    made, *grad = old
    made = lax.all_to_all(made, GROUP, split_axis=0, concat_axis=0, tiled=True)

    shifts = tuple(range(2, experts))
    part_sums = returned(pos, backs[2:], shifts, rows, cap)
    hidden_grad, mixed_grad, sums = middle(
        spots, grad_output, pack, pos, saved, part_sums, backs[:2], cap, experts
    )
    head_rows = 3 * (3 * width // LANES) + 4
    devices = 2 * experts // 2 * fsdp
    members = devices if head_rows + devices <= part else 0

    def homeward(straight, crossed):
        return [
            lax.ppermute(straight, ("hi", "core"), BACK),
            lax.ppermute(crossed, ("hi", "core"), BACK_CROSSED),
            straight,
        ]

    if len(grad) == 4:
        sums_two = list(half_sums(spots, grad[0], swap(grad[1], "fy"), [sums], 0.02))
        home_two = homeward(*sums_two)
        grad[3], sums_two[0] = lax.optimization_barrier((grad[3], sums_two[0]))
        got_one = swap(grad[3], "fy")
    else:
        half = split_sum(grad[0].reshape((ways, 2) + grad[0].shape[1:]), "fy", ways)
        home = homeward(*(lax.dynamic_index_in_dim(half, k, 0, keepdims=False) for k in (high, 1 - high)))
        tall = hidden_part + TAIL
        home_two, home_one = [v[:tall] for v in home], [v[tall:] for v in home]
    qkv_grad, keep, give = backward(
        spots, tokens, saved, mixed_grad, sums, peak, [], ways, part, head_rows, members
    )

    got = swap(give, "core")
    after = []
    if len(grad) == 4:
        after = half_sums(spots, grad[2], got_one, home_two[:2], 40)
        home_one = homeward(*after)
    output = combine_output(spots, pos, saved[2], made, seq)
    near_by = experts // 2
    if ways == 2 and part % (TAIL * near_by) == 0:

        def spread(values):
            return [
                value if k == 0 else lax.ppermute(value, "lo", [(j, j ^ k) for j in range(near_by)])
                for k, value in enumerate(values)
            ]

        mine, theirs = add_halves(spots, keep, got, after)
        theirs, qkv_grad = lax.optimization_barrier((theirs, qkv_grad))
        input_grad = first_norm(tokens, qkv_grad, pack, hidden_grad)
        parts = split_rows(spots, mine, swap(theirs, "fy"), [input_grad, output, *home_one[:2]], near_by)
        total = add_parts(spread(parts))
        shapes = [(hidden_part, width), (1, hidden_part), (1, part)]
        grad_w2, grad_b1, grad_b2 = home_sums(home_second_kernel, spots, home_two, total, shapes)
        shapes = [(part, hidden_part * fsdp)]
        (grad_w1,) = home_sums(home_first_kernel, spots, home_one, total, shapes)
        total = add_parts([total, swap(total, "hi")], [grad_w2, grad_w1])
        total = spread([total] * near_by)
    else:
        sums = split_sum((keep.astype(f32) + got.astype(f32)).astype(bf16), "fy", ways)
        total = [lax.psum(sums, ("hi", "lo"))]
        shapes = [(hidden_part, width), (1, hidden_part), (1, part)]
        grad_w2, grad_b1, grad_b2 = home_sums(home_second_kernel, spots, home_two, total[0], shapes)
        shapes = [(part, hidden_part * fsdp)]
        (grad_w1,) = home_sums(home_first_kernel, spots, home_one, total[0], shapes)
        input_grad = first_norm(tokens, qkv_grad, pack, hidden_grad)
    if not members:
        peak = jnp.max(lax.all_gather(peak, DEVICE, axis=0, tiled=True), axis=0, keepdims=True)
    limit = clip_threshold.reshape(1, HEADS)
    grad_qkv, grad_out, grad_router, clipped, *grads = finish(
        spots, total, own, limit, peak, width, experts, head_rows, members
    )
    grads = [v.reshape(part) for v in grads]
    return (
        output,
        input_grad,
        grads[0],
        grads[1],
        grad_qkv,
        grads[2],
        grads[3],
        grad_out,
        grads[4],
        grads[5],
        grads[6],
        grad_router.T,
        grad_w1[None],
        grad_b1,
        grad_w2[None],
        grad_b2,
        clipped,
    )


def solution(mesh):
    experts, fsdp = mesh.shape["expert"], mesh.shape["fsdp"]
    inner = Mesh(mesh.devices.reshape(2, experts // 2, fsdp // 2, 2), DEVICE)
    token, row, expert = P(DEVICE, None, None), ("fy", "core"), ("hi", "lo")
    vector, matrix = P(row), P(row, None)
    return jax.shard_map(
        functools.partial(shards, experts=experts, fsdp=fsdp),
        mesh=inner,
        in_specs=(
            token,
            vector,
            vector,
            matrix,
            vector,
            vector,
            matrix,
            vector,
            vector,
            vector,
            matrix,
            P(expert, row, None),
            P(expert, row),
            P(expert, row, None),
            P(expert, row),
            P(DEVICE, None),
            P(),
            token,
        ),
        out_specs=(
            token,
            token,
            vector,
            vector,
            matrix,
            vector,
            vector,
            matrix,
            vector,
            vector,
            vector,
            matrix,
            P(expert, row, None),
            P(expert, row),
            P(expert, row, None),
            P(expert, row),
            matrix,
        ),
        check_vma=False,
    )
```
